32 devices in a mesh: ctx: 8 (over z, y), fsdp: 4 (over x, core).
Axes of the slice: x: 2, y: 2, z: 4, core: 2. Of those that a mesh axis runs over, the one named last changes fastest.
Arguments:
- tokens: bfloat16 [4, 2048, 768], P('fsdp', 'ctx'), may hold values from -6 to 6
- cotangent: bfloat16 [4, 2048, 768], P('fsdp', 'ctx'), may hold values from -6 to 6
- lengths: int32 [4], P('fsdp'), may hold values from 512 to 2048, as said below
- position_block: int32 [8], replicated, may hold values from 0 to 7, each once
- routes: int32 [4, 2048, 2], P('fsdp', 'ctx'), may hold values from 0 to 7, all different within a row; in each aligned block of 256 rows (0 to 255, 256 to 511, ..., all dimensions but the last counted through in order) at most 96 rows name the same one
- gain_attn: bfloat16 [768], P('fsdp'), may hold values from 0.099609375 to 1.8984375
- w_qkv: bfloat16 [768, 2304], P('fsdp'), may hold values from -0.21875 to 0.21875
- w_out: bfloat16 [768, 768], P('fsdp'), may hold values from -3.5 to 3.5
- gain_ffn: bfloat16 [768], P('fsdp'), may hold values from 0.099609375 to 1.8984375
- w_router: bfloat16 [768, 8], P('fsdp'), may hold values from -0.15625 to 0.15625
- w_shared_in: bfloat16 [768, 4096], P('fsdp'), may hold values from -0.21875 to 0.21875
- w_shared_out: bfloat16 [2048, 768], P('fsdp'), may hold values from -0.1875 to 0.1875
- w_expert_in: bfloat16 [8, 768, 4096], P('ctx', 'fsdp'), may hold values from -0.21875 to 0.21875
- w_expert_out: bfloat16 [8, 2048, 768], P('ctx', None, 'fsdp'), may hold values from -0.1875 to 0.1875
Outputs:
- output: bfloat16 [4, 2048, 768], P('fsdp', 'ctx')
- grad_tokens: float32 [4, 2048, 768], P('fsdp', 'ctx')
- grad_gain_attn: float32 [768], P('fsdp')
- grad_qkv: float32 [768, 2304], P('fsdp')
- grad_out: float32 [768, 768], P('fsdp')
- grad_gain_ffn: float32 [768], P('fsdp')
- grad_router: float32 [768, 8], P('fsdp')
- grad_shared_in: float32 [768, 4096], P('fsdp')
- grad_shared_out: float32 [2048, 768], P('fsdp')
- grad_expert_in: float32 [8, 768, 4096], P('ctx', 'fsdp')
- grad_expert_out: float32 [8, 2048, 768], P('ctx', None, 'fsdp')
The draws below stay inside these ranges and needn't reach their ends.
Inputs may be any that keep to these rules, and one draw needn't show every extreme that they name: `lengths`: some row has length 2048. `position_block`: each number appears once. `routes`: the two experts of a slot differ; within each row, the two-per-slot choices of an aligned block of 256 slots name no expert more than 96 times, a bound that some block reaches.
All inputs are finite; a program needn't handle non-finite values.
Results may differ from the reference program's by a relative error of at most 0.028.
Values may be sent and summed in bfloat16 or wider, within the bound.
A program may use at most 192 MiB of HBM per device.

```python
import math
import jax
import jax.numpy as jnp
import numpy as np
from jax import lax

D = 768
HEADS = 12
HEAD_DIM = 64
FF = 2048
FS = 2048
TOP = 2
SLOT_DEV = 256
EXPERTS = 8
SLOTS = 2048
ROWS = 4
CAP = 96
N_CTX = 8


def draw_lengths(key, part):
    first_key, second_key = jax.random.split(key)
    drawn = jax.random.randint(first_key, (ROWS,), SLOTS // 4, SLOTS + 1)
    longest = jax.random.randint(second_key, (), 0, ROWS)
    return jnp.where(jnp.arange(ROWS) == longest, SLOTS, drawn).astype(jnp.int32)


def shard_levels(key, dims, shards, smallest, top_value):
    level = 1.0
    for position, parts in shards:
        heights = jax.random.uniform(jax.random.fold_in(jax.random.fold_in(key, 6), position), (parts,), jnp.float32, smallest / len(shards), top_value / len(shards))
        level = level * jnp.repeat(jnp.exp(heights), dims[position] // parts).reshape((-1,) + (1,) * (len(dims) - 1 - position))
    return level


def deal_out(own_key, own, number, rows, count, top, bound, skew):
    order = jax.random.permutation(own_key, count)
    packed, usual = load_shares(count, rows * top, bound, skew, True), load_shares(count, rows * top, bound, skew, False)
    places = jnp.arange(count)

    def named(tallies, offset_by):
        used = int((tallies > 0).sum())
        fixed = max(1, used // 4)
        shifted = fixed + (places - fixed + offset_by * (used - fixed)) % max(1, count - fixed)
        return jnp.zeros((count,), jnp.int32).at[order[jnp.where(places < fixed, places, shifted)]].set(jnp.asarray(tallies, jnp.int32))

    tallies = jnp.where(number % 4 == 0, named(packed, number // 4), named(usual, number - number // 4 - 1))
    mixed = jax.random.permutation(jax.random.fold_in(own, 3), count)
    donor, receiver = mixed[0:count // 2 * 2:2], mixed[1:count // 2 * 2:2]
    slack = jnp.minimum(tallies[donor] - 1, bound - tallies[receiver]) // 2
    slack = jnp.where((donor == order[0]) | (receiver == order[0]) | (tallies[receiver] == 0), 0, jnp.maximum(slack, 0))
    shifted = jax.random.randint(jax.random.fold_in(own, 4), (count // 2,), 0, 1 << 20) % (slack + 1)
    tallies = tallies.at[donor].add(-shifted).at[receiver].add(shifted)
    members = jnp.searchsorted(jnp.cumsum(tallies), jnp.arange(rows * top), side="right").astype(jnp.int32)
    grid = members.reshape(top, rows).T
    grid = grid[jax.random.permutation(jax.random.fold_in(own, 1), rows)]
    offset_by = jax.random.randint(jax.random.fold_in(own, 2), (rows, 1), 0, top)
    return jnp.take_along_axis(grid, (jnp.arange(top)[None, :] + offset_by) % top, axis=1)


def load_shares(number_of, total, limit, lean, full):
    weights = [(1 << 20) // math.isqrt(rank ** lean) + 1 for rank in range(1, number_of + 1)]
    largest = limit if full else min(limit, max(-(-total // number_of), total * weights[0] // sum(weights)))
    least = 1 if total - largest >= number_of - 1 else 0
    counts, spare = [largest] + [least] * (number_of - 1), total - largest - least * (number_of - 1)
    while spare > 0:
        free = [i for i in range(1, number_of) if counts[i] < largest] or [i for i in range(1, number_of) if counts[i] < limit]
        whole, remaining = sum([weights[i] for i in free]), spare
        for i in free:
            addition = min(limit - counts[i], max(1, remaining * weights[i] // whole), spare)
            counts[i] = counts[i] + addition
            spare = spare - addition
    return np.array(counts)


def normal_values(rng, shape, deviation, most, shards=(), held_as=jnp.bfloat16):
    array = jax.random.normal(rng, shape, jnp.float32) * deviation
    if len(shards) > 0:
        array = shard_levels(rng, shape, shards, -0.22, 0.18) * array
    return jnp.clip(array, min=-most, max=most).astype(held_as)


def setup_inputs(seed: int = 0) -> dict:
    key_list = jax.random.split(jax.random.key(seed), 15)
    tokens = normal_values(key_list[0], (ROWS, SLOTS, D), 1.0, 6.0, ((0, 4), (1, 8)))
    cotangent = normal_values(key_list[1], (ROWS, SLOTS, D), 1.0, 6.0, ((0, 4), (1, 8)))
    lengths = draw_lengths(jax.random.fold_in(key_list[14], 71), 0)
    position_block = jax.random.permutation(key_list[3], N_CTX).astype(jnp.int32)
    routes_keys = jax.random.split(jax.random.fold_in(key_list[4], 1), ROWS * SLOTS // SLOT_DEV)
    routes_turns = jax.random.permutation(jax.random.fold_in(key_list[4], 3), ROWS * SLOTS // SLOT_DEV)
    routes = jax.vmap(lambda own, number: deal_out(jax.random.fold_in(key_list[4], 2), own, number, SLOT_DEV, EXPERTS, 2, CAP, 1))(routes_keys, routes_turns).reshape((ROWS, SLOTS, TOP))
    gain_attn = jnp.clip(1.0 + 0.18 * jax.random.normal(key_list[5], (D,), jnp.float32), 0.099609375, 1.8984375).astype(jnp.bfloat16)
    w_qkv = normal_values(key_list[6], (D, 3 * D), D ** -0.5, 0.21875, ((0, 4),))
    w_out = normal_values(key_list[7], (D, D), (max(1, D * 8 // SLOTS)) ** -0.5, 3.5, ((0, 4),))
    gain_ffn = jnp.clip(1.0 + 0.18 * jax.random.normal(key_list[8], (D,), jnp.float32), 0.099609375, 1.8984375).astype(jnp.bfloat16)
    w_router = normal_values(key_list[9], (D, EXPERTS), (2 * D) ** -0.5, 0.15625, ((0, 4),))
    w_shared_in = normal_values(key_list[10], (D, 2 * FS), D ** -0.5, 0.21875, ((0, 4),))
    w_shared_out = normal_values(key_list[11], (FS, D), (FS // 2) ** -0.5, 0.1875, ((0, 4),))
    w_expert_in = normal_values(key_list[12], (EXPERTS, D, 2 * FF), D ** -0.5, 0.21875, ((0, 8), (1, 4)))
    w_expert_out = normal_values(key_list[13], (EXPERTS, FF, D), (FF // 2) ** -0.5, 0.1875, ((0, 8), (2, 4)))
    return {"tokens": tokens, "cotangent": cotangent, "lengths": lengths, "position_block": position_block, "routes": routes, "gain_attn": gain_attn, "w_qkv": w_qkv, "w_out": w_out, "gain_ffn": gain_ffn, "w_router": w_router, "w_shared_in": w_shared_in, "w_shared_out": w_shared_out, "w_expert_in": w_expert_in, "w_expert_out": w_expert_out}


@jax.custom_vjp
def low(v):
    return lax.optimization_barrier(v.astype(jnp.bfloat16)).astype(jnp.float32)

@jax.custom_vjp
def low_back(v):
    return v

def low_keep(v):
    return (low(v), None)

def low_pass(kept, grad):
    return (grad,)

def back_keep(v):
    return (v, None)

def back_low(kept, grad):
    return (low(grad),)
low.defvjp(low_keep, low_pass)
low_back.defvjp(back_keep, back_low)
norm_eps = 1e-06
highest = lax.Precision.HIGHEST

def rms_norm(values, gain):
    return values * lax.rsqrt(lax.optimization_barrier(jnp.mean(values * values, axis=-1, keepdims=True)) + norm_eps) * gain

def rotary(field, positions):
    halves = HEAD_DIM // 2
    inverse = 10000.0 ** (-(jnp.arange(halves, dtype=jnp.float32) * 2.0 / HEAD_DIM))
    angle_grid = positions.astype(jnp.float32)[..., None] * inverse
    cos_part = jnp.cos(angle_grid)[..., None, :]
    sin_part = jnp.sin(angle_grid)[..., None, :]
    first_half = field[..., :halves]
    second_half = field[..., halves:]
    return jnp.concatenate([first_half * cos_part - second_half * sin_part, second_half * cos_part + first_half * sin_part], axis=-1)

@jax.checkpoint
def attend_block(query_block, query_pos, keys, values, key_pos, length):
    scores = jnp.einsum('qhd,khd->hqk', query_block, keys, precision=highest) * HEAD_DIM ** (-0.5)
    scores = low_back(scores)
    allowed = (key_pos[None, :] <= query_pos[:, None]) & (key_pos[None, :] < length)
    scores = jnp.where(allowed[None], scores, -1e+30)
    weights = low(jax.nn.softmax(scores, axis=-1))
    return jnp.einsum('hqk,khd->qhd', weights, values, precision=highest)

def attend_row(operands):
    queries, keys, values, positions, length = operands
    query_rows = min(512, SLOTS)
    block_count = SLOTS // query_rows

    def one_block(pieces):
        return attend_block(pieces[0], pieces[1], keys, values, positions, length)
    result = lax.map(one_block, (queries.reshape(block_count, query_rows, HEADS, HEAD_DIM), positions.reshape(block_count, query_rows)))
    return result.reshape(SLOTS, HEADS, HEAD_DIM)

@jax.checkpoint
def expert_apply(operands):
    rows, weight_in, weight_out = operands
    joined = low_back(jnp.einsum('nd,df->nf', rows, weight_in, precision=highest))
    inner = low(jax.nn.silu(joined[:, :FF]) * joined[:, FF:])
    return low_back(low(jnp.einsum('nf,fd->nd', inner, weight_out, precision=highest)))

def reference(tokens, cotangent, lengths, position_block, routes, gain_attn, w_qkv, w_out, gain_ffn, w_router, w_shared_in, w_shared_out, w_expert_in, w_expert_out):
    positions_row = (position_block[:, None] * SLOT_DEV + jnp.arange(SLOT_DEV, dtype=jnp.int32)[None, :]).reshape(SLOTS)
    positions = jnp.broadcast_to(positions_row[None, :], (ROWS, SLOTS))
    live = (positions < lengths[:, None]).astype(jnp.float32)[..., None]
    pairs = routes.reshape(ROWS, N_CTX, 2 * SLOT_DEV)
    expert_hot = (pairs[..., None] == jnp.arange(EXPERTS, dtype=jnp.int32)).astype(jnp.int32)
    earlier = jnp.cumsum(expert_hot, axis=2) - expert_hot
    slot_index = lax.optimization_barrier(jnp.sum(earlier * expert_hot, axis=-1))
    block_base = jnp.arange(ROWS, dtype=jnp.int32)[:, None] * N_CTX + jnp.arange(N_CTX, dtype=jnp.int32)[None, :]
    targets = ((block_base[..., None] * EXPERTS + pairs) * CAP + slot_index).reshape(-1).astype(jnp.int32)

    def forward(inputs, gain_one, weight_qkv, weight_out, gain_two, weight_router, shared_in, shared_out, expert_in, expert_out):
        attn_in = low(rms_norm(inputs, gain_one))
        projected = low_back(jnp.einsum('rsd,de->rse', attn_in, weight_qkv, precision=highest))
        queries = low_back(low(rotary(projected[..., :D].reshape(ROWS, SLOTS, HEADS, HEAD_DIM), positions)))
        keys = low_back(low(rotary(projected[..., D:2 * D].reshape(ROWS, SLOTS, HEADS, HEAD_DIM), positions)))
        values = low_back(low(projected[..., 2 * D:].reshape(ROWS, SLOTS, HEADS, HEAD_DIM)))
        attended = lax.map(attend_row, (queries, keys, values, positions, lengths))
        attn_rows = low_back(low(attended.reshape(ROWS, SLOTS, D)))
        residual = inputs + low_back(jnp.einsum('rsd,de->rse', attn_rows, weight_out, precision=highest))
        ffn_in = low(rms_norm(residual, gain_two))
        logits = low_back(jnp.einsum('rsd,de->rse', ffn_in, weight_router, precision=highest))
        gates = jax.nn.softmax(jnp.take_along_axis(logits, routes, axis=-1), axis=-1)
        shared_mid = low_back(jnp.einsum('rsd,df->rsf', ffn_in, shared_in, precision=highest))
        shared_act = low(jax.nn.silu(shared_mid[..., :FS]) * shared_mid[..., FS:])
        shared_res = low_back(jnp.einsum('rsf,fd->rsd', shared_act, shared_out, precision=highest))
        pair_in = low_back(jnp.broadcast_to(ffn_in[:, :, None, :], (ROWS, SLOTS, 2, D))).reshape(ROWS * SLOTS * 2, D)
        buffer = jnp.zeros((ROWS * N_CTX * EXPERTS * CAP, D), jnp.float32).at[targets].set(pair_in)
        by_expert = buffer.reshape(ROWS * N_CTX, EXPERTS, CAP, D).transpose(1, 0, 2, 3).reshape(EXPERTS, ROWS * N_CTX * CAP, D)
        expert_res = lax.map(expert_apply, (by_expert, expert_in, expert_out))
        flat_res = expert_res.reshape(EXPERTS, ROWS * N_CTX, CAP, D).transpose(1, 0, 2, 3).reshape(ROWS * N_CTX * EXPERTS * CAP, D)
        pair_res = flat_res[targets].reshape(ROWS, SLOTS, 2, D)
        mixture = lax.optimization_barrier(jnp.sum(gates[..., None] * pair_res, axis=2))
        return live * (residual + shared_res + mixture)
    floats = (tokens.astype(jnp.float32), gain_attn.astype(jnp.float32), w_qkv.astype(jnp.float32), w_out.astype(jnp.float32), gain_ffn.astype(jnp.float32), w_router.astype(jnp.float32), w_shared_in.astype(jnp.float32), w_shared_out.astype(jnp.float32), w_expert_in.astype(jnp.float32), w_expert_out.astype(jnp.float32))
    result, reverse_function = jax.vjp(forward, *floats)
    grads = reverse_function(cotangent.astype(jnp.float32))
    return (result.astype(jnp.bfloat16), grads[0], grads[1], grads[2], grads[3], grads[4], grads[5], grads[6], grads[7], grads[8], grads[9])
```

```python
import functools

import jax
import jax.numpy as jnp
from jax import lax
from jax.experimental import pallas as pl
from jax.experimental.pallas import tpu as pltpu
from jax.sharding import PartitionSpec as P

D = 768
HEADS = 12
HEAD_DIM = 64
FF = 2048
FS = 2048
LANES = 128
CHUNK = 256
PACKED = 3 * D + LANES
norm_eps = 1e-06
F32 = jnp.float32
BF16 = jnp.bfloat16


def dot(a, b):
    return jnp.dot(a, b, preferred_element_type=F32)


def dot_nt(a, b):
    return lax.dot_general(a, b, (((1,), (1,)), ((), ())), preferred_element_type=F32)


def dot_tn(a, b):
    return lax.dot_general(a, b, (((0,), (0,)), ((), ())), preferred_element_type=F32)


def call(kernel, outs, *, flops, nbytes, limit=56, **kw):
    return pl.pallas_call(
        kernel,
        out_shape=outs,
        compiler_params=pltpu.CompilerParams(vmem_limit_bytes=limit << 20),
        cost_estimate=pl.CostEstimate(
            flops=int(flops), bytes_accessed=int(nbytes), transcendentals=0
        ),
        **kw,
    )


def shape(dims, dtype):
    return jax.ShapeDtypeStruct(dims, dtype)


def lanes_of(rows, width=LANES):
    return lax.broadcasted_iota(jnp.int32, (rows, width), 1)


def first_heads(n_ctx, slot_dev):
    share = HEADS * slot_dev // n_ctx
    return [min(share * d // slot_dev, HEADS - 2) for d in range(n_ctx)]


def partner(t, lane):
    return jnp.where(lane % 64 < 32, pltpu.roll(t, 96, 1), pltpu.roll(t, 32, 1))


def in_parts(v):
    high = v.astype(BF16)
    rest = v - high.astype(F32)
    mid = rest.astype(BF16)
    low = (rest - mid.astype(F32)).astype(BF16)
    return high.astype(F32), mid.astype(F32), low.astype(F32)


def part_lanes(v, lane):
    high, mid, low = in_parts(v)
    zero = jnp.zeros((), F32)
    return jnp.where(
        lane == 0, high, jnp.where(lane == 1, mid, jnp.where(lane == 2, low, zero))
    ).astype(BF16)


def picks(target_ref, places):
    rows = target_ref.shape[0]
    place = lanes_of(rows, places)
    return tuple(
        jnp.where(place == target_ref[:, k : k + 1], 1.0, 0.0).astype(BF16) for k in range(2)
    )


def qkv_kernel(heads, experts, x_ref, w_ref, cos_ref, sin_ref, send_ref, in_ref, tail_ref):
    x = x_ref[...].astype(F32)
    tail = w_ref[:, 3 * D :].astype(F32).T
    tail_ref[...] = tail
    inv = lax.rsqrt(jnp.mean(x * x, axis=-1, keepdims=True) + norm_eps)
    attn_in = (x * inv * tail[experts : experts + 1, :]).astype(BF16)
    in_ref[...] = attn_in
    lane = lanes_of(x.shape[0])
    cos, sin = cos_ref[...], sin_ref[...]
    for part in range(3):
        y = dot(attn_in, w_ref[:, part * D : (part + 1) * D])
        groups = []
        for g in range(D // LANES):
            t = y[:, g * LANES : (g + 1) * LANES]
            if part < 2:
                t = t * cos + partner(t, lane) * sin
            groups.append(t)
        turned = [pltpu.roll(t, 64, 1) for t in groups]
        for d, head in enumerate(heads):
            g = head // 2
            if head % 2 == 0:
                packet = groups[g]
            else:
                packet = jnp.where(lane < 64, turned[g], turned[g + 1])
            send_ref[d, :, part * LANES : (part + 1) * LANES] = packet.astype(BF16)


def stack_rows(stack_ref, block, lane):
    rows = block.shape[0]
    zero = jnp.zeros((), block.dtype)
    stack_ref[0:rows, :] = jnp.where(lane < 64, block, zero)
    stack_ref[rows : 2 * rows, :] = jnp.where(lane >= 64, block, zero)


def unstack_rows(stack_ref, block, offset, lane):
    rows = stack_ref.shape[0] // 2
    stack_ref[...] = jnp.zeros_like(stack_ref)
    stack_ref[pl.ds(offset, block.shape[0]), :] = block
    return jnp.where(lane < 64, stack_ref[0:rows, :], stack_ref[rows : 2 * rows, :])


def key_limits(share, rows, q_block, offset, length):
    row = lax.broadcasted_iota(jnp.int32, (1, share), 1) + offset
    row = jnp.where(row >= rows, row - rows, row)
    return jnp.minimum(q_block * rows + row + 1, length)


def attend_kernel(n, share, sc, recv_ref, out_ref, keep_ref, lse_ref, stack, scores, back):
    q_block = pl.program_id(0)
    rows = recv_ref.shape[1]
    offset = pl.multiple_of(sc[n], 64)
    length = sc[n + 1]
    lane = lanes_of(rows)
    stack_rows(stack, recv_ref[sc[q_block], :, 0:LANES] * 0.125, lane)
    query = stack[pl.ds(offset, share), :]
    limit = key_limits(share, rows, q_block, offset, length)
    key_row = lax.broadcasted_iota(jnp.int32, (rows, share), 0)
    blocks = jnp.minimum(q_block + 1, (length + rows - 1) // rows)

    def score_step(j, top):
        keys = recv_ref[sc[j], :, LANES : 2 * LANES]
        s = dot_nt(keys, query)
        s = jnp.where(key_row < limit - j * rows, s, -1e30)
        scores[j] = s
        return jnp.maximum(top, jnp.max(s, axis=0, keepdims=True))

    top = lax.fori_loop(0, blocks, score_step, jnp.full((1, share), -1e30, F32))

    def value_step(j, carry):
        total, acc = carry
        weights = jnp.exp(scores[j] - top)
        total = total + jnp.sum(weights, axis=0, keepdims=True)
        values = recv_ref[sc[j], :, 2 * LANES : 3 * LANES]
        return total, acc + dot_tn(values, weights.astype(BF16))

    total, acc = lax.fori_loop(
        0, blocks, value_step, (jnp.zeros((1, share), F32), jnp.zeros((LANES, share), F32))
    )
    acc = acc / total
    keep_ref[0] = acc
    lse_ref[0] = top + jnp.log(total)
    out_ref[0] = unstack_rows(back, acc.T, offset, lane).astype(BF16)


def attend_back_kernel(
    n, share, sc, recv_ref, grad_ref, keep_ref, lse_ref, out_ref, stack, gstack, dkeys, dvalues, back
):
    q_block = pl.program_id(0)
    rows = recv_ref.shape[1]
    offset = pl.multiple_of(sc[n], 64)
    length = sc[n + 1]
    lane = lanes_of(rows)
    source = sc[q_block]

    @pl.when(q_block == 0)
    def _():
        dkeys[...] = jnp.zeros_like(dkeys)
        dvalues[...] = jnp.zeros_like(dvalues)

    stack_rows(stack, recv_ref[source, :, 0:LANES] * 0.125, lane)
    query = stack[pl.ds(offset, share), :]
    stack_rows(gstack, grad_ref[source], lane)
    grad = gstack[pl.ds(offset, share), :]
    lse = lse_ref[0]
    delta = jnp.sum(grad.astype(F32).T * keep_ref[0], axis=0, keepdims=True)
    limit = key_limits(share, rows, q_block, offset, length)
    key_row = lax.broadcasted_iota(jnp.int32, (rows, share), 0)
    blocks = jnp.minimum(q_block + 1, (length + rows - 1) // rows)

    def step(j, acc):
        keys = recv_ref[sc[j], :, LANES : 2 * LANES]
        values = recv_ref[sc[j], :, 2 * LANES : 3 * LANES]
        s = dot_nt(keys, query)
        weights = jnp.exp(jnp.where(key_row < limit - j * rows, s, -1e30) - lse)
        dweights = dot_nt(values, grad)
        dscores = (weights * (dweights - delta)).astype(BF16)
        dkeys[j] += dot(dscores, query)
        dvalues[j] += dot(weights.astype(BF16), grad)
        return acc + dot_tn(keys, dscores)

    acc = lax.fori_loop(0, blocks, step, jnp.zeros((LANES, share), F32))
    dquery = unstack_rows(back, acc.T * 0.125, offset, lane)
    out_ref[source, :, 0:LANES] = dquery.astype(BF16)

    @pl.when(q_block == n - 1)
    def _():
        def flush(j, carry):
            out_ref[sc[j], :, LANES : 2 * LANES] = dkeys[j].astype(BF16)
            out_ref[sc[j], :, 2 * LANES : 3 * LANES] = dvalues[j].astype(BF16)
            return carry

        lax.fori_loop(0, n, flush, 0)


def middle_kernel(
    heads,
    experts,
    came_ref,
    w_ref,
    x_ref,
    tail_ref,
    routes_ref,
    target_ref,
    residual_ref,
    in_ref,
    gates_ref,
    send_ref,
):
    total = x_ref[...].astype(F32)
    for d, head in enumerate(heads):
        total = total + dot(came_ref[d], w_ref[64 * head : 64 * head + LANES, :])
    residual_ref[...] = total
    inv = lax.rsqrt(jnp.mean(total * total, axis=-1, keepdims=True) + norm_eps)
    ffn_in = (total * inv * tail_ref[experts + 1 : experts + 2, :]).astype(BF16)
    in_ref[...] = ffn_in
    logits = dot_nt(ffn_in, tail_ref[...].astype(BF16))
    lane = lanes_of(logits.shape[0])
    chosen = [
        jnp.sum(jnp.where(lane == routes_ref[:, k : k + 1], logits, 0.0), axis=-1, keepdims=True)
        for k in range(2)
    ]
    top = jnp.maximum(chosen[0], chosen[1])
    raised = [jnp.exp(c - top) for c in chosen]
    gates = [r / (raised[0] + raised[1]) for r in raised]
    gates_ref[...] = jnp.where(lane == 0, gates[0], gates[1])
    pick = picks(target_ref, send_ref.shape[0])
    send_ref[:, 0:D] = dot_tn(pick[0] + pick[1], ffn_in).astype(BF16)
    send_ref[:, D:] = (
        dot_tn(pick[0], part_lanes(gates[0], lane)) + dot_tn(pick[1], part_lanes(gates[1], lane))
    ).astype(BF16)


def gated(g, u, da):
    sig = 1.0 / (1.0 + jnp.exp(-g))
    silu = g * sig
    return silu * u, da * u * sig * (1.0 + g * (1.0 - sig)), da * silu


def shared_kernel(
    x_ref, dy_ref, wg_ref, wu_ref, wo_ref, res_ref, dx_ref, mid_ref, dwo_ref, res_acc, dx_acc
):
    c = pl.program_id(0)

    @pl.when(c == 0)
    def _():
        res_acc[...] = jnp.zeros_like(res_acc)
        dx_acc[...] = jnp.zeros_like(dx_acc)

    x, dy = x_ref[...], dy_ref[...]
    wg, wu, wo = wg_ref[...], wu_ref[...], wo_ref[...]
    act, dg, du = gated(dot(x, wg), dot(x, wu), dot_nt(dy, wo))
    act, dg, du = act.astype(BF16), dg.astype(BF16), du.astype(BF16)
    res_acc[...] += dot(act, wo)
    dx_acc[...] += dot_nt(dg, wg) + dot_nt(du, wu)
    mid_ref[0] = dg
    mid_ref[1] = du
    dwo_ref[...] = dot_tn(act, dy).astype(BF16)

    @pl.when(c == pl.num_programs(0) - 1)
    def _():
        res_ref[...] = res_acc[...]
        dx_ref[...] = dx_acc[...]


def shared_grad_kernel(x_ref, mid_ref, out_ref, xt):
    @pl.when((pl.program_id(0) == 0) & (pl.program_id(1) == 0))
    def _():
        xt[...] = x_ref[...].T

    out_ref[...] = dot(xt[...], mid_ref[0]).astype(BF16)


def expert_kernel(
    x_ref, dy_ref, wg_ref, wu_ref, wt_ref, dx_ref, res_ref, mid_ref, dx_acc, res_acc, dgate
):
    c = pl.program_id(0)

    @pl.when(c == 0)
    def _():
        res_acc[...] = jnp.zeros_like(res_acc)
        dx_acc[...] = jnp.zeros_like(dx_acc)
        dgate[...] = jnp.zeros_like(dgate)

    x, dy = x_ref[:, 0:D], dy_ref[...]
    gate = jnp.sum(x_ref[:, D:].astype(F32), axis=-1, keepdims=True)
    wg, wu, wt = wg_ref[...], wu_ref[...], wt_ref[...]
    da = dot(dy, wt)
    act, dg, du = gated(dot(x, wg), dot(x, wu), da * gate)
    dgate[...] += jnp.sum(act * da, axis=-1, keepdims=True)
    mid_ref[2] = (act * gate).astype(BF16)
    act, dg, du = act.astype(BF16), dg.astype(BF16), du.astype(BF16)
    res_acc[...] += dot_nt(act, wt)
    dx_acc[...] += dot_nt(dg, wg) + dot_nt(du, wu)
    mid_ref[0] = dg
    mid_ref[1] = du

    @pl.when(c == pl.num_programs(0) - 1)
    def _():
        res_ref[...] = res_acc[...].astype(BF16)
        dx_ref[:, 0:D] = dx_acc[...].astype(BF16)
        dx_ref[:, D:] = part_lanes(dgate[:, 0:1], lanes_of(dgate.shape[0]))


def expert_grad_kernel(x_ref, dy_ref, mid_ref, out_ref, xt, dyt):
    @pl.when((pl.program_id(0) == 0) & (pl.program_id(1) == 0))
    def _():
        xt[...] = x_ref[...].T
        dyt[...] = dy_ref[...].T

    @pl.when(pl.program_id(0) < 2)
    def _():
        out_ref[...] = dot(xt[...], mid_ref[0]).astype(BF16)

    @pl.when(pl.program_id(0) == 2)
    def _():
        out_ref[...] = dot(dyt[...], mid_ref[0]).astype(BF16)


def combine_kernel(
    heads,
    experts,
    came_ref,
    dx_ref,
    residual_ref,
    dout_ref,
    gates_ref,
    routes_ref,
    target_ref,
    tail_ref,
    w_ref,
    send_ref,
    dres_ref,
    branch_ref,
    dlogits_ref,
    dgain_ref,
):
    pick = picks(target_ref, came_ref.shape[0])
    gates = [gates_ref[:, k : k + 1] for k in range(2)]
    parts = came_ref[:, D:]
    dgate = [jnp.sum(dot(pick[k], parts), axis=-1, keepdims=True) for k in range(2)]
    mean = gates[0] * dgate[0] + gates[1] * dgate[1]
    lane = lanes_of(pick[0].shape[0])
    dlogits = sum(
        jnp.where(lane == routes_ref[:, k : k + 1], gates[k] * (dgate[k] - mean), 0.0)
        for k in range(2)
    ).astype(BF16)
    dlogits_ref[...] = dlogits
    tail = tail_ref[...]
    dffn = dot(pick[0] + pick[1], came_ref[:, 0:D]) + dx_ref[...] + dot(dlogits, tail.astype(BF16))
    residual = residual_ref[...]
    inv = lax.rsqrt(jnp.mean(residual * residual, axis=-1, keepdims=True) + norm_eps)
    scaled = dffn * tail[experts + 1 : experts + 2, :]
    total = jnp.mean(scaled * residual, axis=-1, keepdims=True)
    dres = dout_ref[...].astype(F32) + inv * scaled - residual * inv * inv * inv * total
    dres_ref[...] = dres
    dgain_ref[...] = jnp.sum(dffn * residual * inv, axis=0, keepdims=True)
    branch = dres.astype(BF16)
    branch_ref[...] = branch
    for d, head in enumerate(heads):
        send_ref[d] = dot_nt(branch, w_ref[64 * head : 64 * head + LANES, :]).astype(BF16)


def dense_grad_kernel(heads, came_ref, branch_ref, in_ref, dlogits_ref, kept_ref, out_ref, router_ref, acc):
    acc[...] = jnp.zeros_like(acc)
    branch = branch_ref[...]
    for d, head in enumerate(heads):
        acc[64 * head : 64 * head + LANES, :] += dot_tn(came_ref[d], branch)
    out_ref[...] = acc[...].astype(BF16)
    router_ref[...] = dot_tn(in_ref[...], dlogits_ref[...])


def last_kernel(
    heads,
    experts,
    recv_ref,
    cos_ref,
    sin_ref,
    in_ref,
    x_ref,
    w_ref,
    tail_ref,
    dres_ref,
    router_ref,
    dgain_ref,
    out_ref,
    pack_ref,
    dproj,
):
    lane = lanes_of(x_ref.shape[0])
    cos, sin = cos_ref[...], sin_ref[...]
    for part in range(3):
        groups = [jnp.zeros(lane.shape, F32) for _ in range(D // LANES)]
        for d, head in enumerate(heads):
            g = head // 2
            packet = recv_ref[d, :, part * LANES : (part + 1) * LANES].astype(F32)
            if head % 2 == 0:
                groups[g] = groups[g] + packet
            else:
                packet = pltpu.roll(packet, 64, 1)
                groups[g] = groups[g] + jnp.where(lane >= 64, packet, 0.0)
                groups[g + 1] = groups[g + 1] + jnp.where(lane < 64, packet, 0.0)
        for g, t in enumerate(groups):
            if part < 2:
                t = t.astype(BF16).astype(F32)
                t = t * cos - partner(t, lane) * sin
            dproj[:, part * D + g * LANES : part * D + (g + 1) * LANES] = t.astype(BF16)
    dnorm = dot_nt(dproj[...], w_ref[:, 0 : 3 * D])
    x = x_ref[...].astype(F32)
    gain = tail_ref[experts : experts + 1, :]
    inv = lax.rsqrt(jnp.mean(x * x, axis=-1, keepdims=True) + norm_eps)
    scaled = dnorm * gain
    total = jnp.mean(scaled * x, axis=-1, keepdims=True)
    out_ref[...] = dres_ref[...] + inv * scaled - x * inv * inv * inv * total
    dgain_one = jnp.sum(dnorm * x * inv, axis=0, keepdims=True)
    row = lax.broadcasted_iota(jnp.int32, (LANES, D), 0)
    gains = jnp.where(row == experts, dgain_one, jnp.where(row == experts + 1, dgain_ref[...], 0.0))
    pack_ref[:, 3 * D :] = (router_ref[...] + gains.T).astype(BF16)
    turned = in_ref[...].T
    for part in range(3):
        pack_ref[:, part * D : (part + 1) * D] = dot(
            turned, dproj[:, part * D : (part + 1) * D]
        ).astype(BF16)


def output_kernel(residual_ref, shared_ref, gates_ref, target_ref, live_ref, came_ref, out_ref):
    pick = picks(target_ref, came_ref.shape[0])
    came = came_ref[...]
    mixture = gates_ref[:, 0:1] * dot(pick[0], came) + gates_ref[:, 1:2] * dot(pick[1], came)
    out_ref[...] = (live_ref[...] * (residual_ref[...] + shared_ref[...] + mixture)).astype(BF16)


def on_device(
    tokens,
    cotangent,
    lengths,
    position_block,
    routes,
    gain_attn,
    w_qkv,
    w_out,
    gain_ffn,
    w_router,
    w_shared_in,
    w_shared_out,
    w_expert_in,
    w_expert_out,
):
    n_ctx = lax.axis_size("ctx")
    ctx_index = lax.axis_index("ctx")
    rows = tokens.shape[1]
    local = w_qkv.shape[0]
    experts = w_router.shape[1]
    capacity = 3 * rows // experts
    places = experts * capacity
    share = HEADS * rows // n_ctx
    heads = first_heads(n_ctx, rows)
    gather = functools.partial(lax.all_gather, axis_name="fsdp", axis=0, tiled=True)
    exchange = functools.partial(
        lax.all_to_all, axis_name="ctx", split_axis=0, concat_axis=0, tiled=True
    )
    x = tokens[0]
    length = lengths[0]

    first_pack = jnp.concatenate(
        [
            w_qkv,
            w_router,
            gain_attn[:, None],
            gain_ffn[:, None],
            jnp.zeros((local, LANES - experts - 2), BF16),
        ],
        axis=1,
    )
    qkv_pack = gather(first_pack)
    mid_pack = gather(jnp.concatenate([w_out, w_shared_in], axis=1))
    shared_out = gather(w_shared_out)
    expert_pack = gather(jnp.concatenate([w_expert_in[0], w_expert_out[0].T], axis=1))

    query_pos = position_block[ctx_index] * rows + jnp.arange(rows, dtype=jnp.int32)
    live = (query_pos < length).astype(F32)[:, None]
    halves = HEAD_DIM // 2
    inverse = 10000.0 ** (-(jnp.arange(halves, dtype=F32) * 2.0 / HEAD_DIM))
    angles = query_pos.astype(F32)[:, None] * inverse[None, :]
    cos, sin = jnp.cos(angles), jnp.sin(angles)
    cos = jnp.concatenate([cos, cos, cos, cos], axis=1)
    sin = jnp.concatenate([-sin, sin, -sin, sin], axis=1)

    order = jnp.sum(
        jnp.where(
            position_block[None, :] == jnp.arange(n_ctx, dtype=jnp.int32)[:, None],
            jnp.arange(n_ctx, dtype=jnp.int32)[None, :],
            0,
        ),
        axis=1,
    )
    head_of = jnp.minimum(share * ctx_index // rows, HEADS - 2)
    offset = share * ctx_index - rows * head_of
    scalars = jnp.concatenate(
        [order, jnp.stack([offset.astype(jnp.int32), length.astype(jnp.int32)])]
    )

    pairs = routes[0].reshape(2 * rows)
    hot = (pairs[:, None] == jnp.arange(experts, dtype=jnp.int32)[None, :]).astype(jnp.int32)
    earlier = jnp.cumsum(hot, axis=0) - hot
    target = (pairs * capacity + jnp.sum(earlier * hot, axis=-1)).reshape(rows, 2)
    dout = (cotangent[0].astype(F32) * live).astype(BF16)
    place = jnp.arange(places, dtype=jnp.int32)
    token_pick = (
        (target[:, 0:1] == place[None, :]) | (target[:, 1:2] == place[None, :])
    ).astype(BF16)
    dy_rows = exchange(dot_tn(token_pick, dout).astype(BF16).reshape(n_ctx, -1, D))
    dy_rows = dy_rows.reshape(places, D)

    send, attn_in, tail = call(
        functools.partial(qkv_kernel, heads, experts),
        (
            shape((n_ctx, rows, 3 * LANES), BF16),
            shape((rows, D), BF16),
            shape((LANES, D), F32),
        ),
        flops=2 * rows * D * 3 * D,
        nbytes=6 << 20,
    )(x, qkv_pack, cos, sin)
    recv = exchange(send)

    packet = pl.BlockSpec((n_ctx, rows, 3 * LANES), lambda i, sc: (0, 0, 0))
    block_of = lambda i, sc: (i, 0, 0)
    attended, kept, lse = call(
        functools.partial(attend_kernel, n_ctx, share),
        (
            shape((n_ctx, rows, LANES), BF16),
            shape((n_ctx, LANES, share), F32),
            shape((n_ctx, 1, share), F32),
        ),
        flops=2 * share * rows * n_ctx * n_ctx * LANES * 2,
        nbytes=5 << 20,
        grid_spec=pltpu.PrefetchScalarGridSpec(
            num_scalar_prefetch=1,
            grid=(n_ctx,),
            in_specs=[packet],
            out_specs=[
                pl.BlockSpec((1, rows, LANES), lambda i, sc: (sc[i], 0, 0)),
                pl.BlockSpec((1, LANES, share), block_of),
                pl.BlockSpec((1, 1, share), block_of),
            ],
            scratch_shapes=[
                pltpu.VMEM((2 * rows, LANES), BF16),
                pltpu.VMEM((n_ctx, rows, share), F32),
                pltpu.VMEM((2 * rows, LANES), F32),
            ],
        ),
    )(scalars, recv)
    came = exchange(attended)

    whole = pl.BlockSpec(memory_space=pltpu.VMEM)
    out_block = pl.BlockSpec((D, D), lambda i: (0, 0))

    def full(*dims):
        return pl.BlockSpec(dims, lambda i: (0,) * len(dims))

    residual, ffn_in, gates, outgoing = call(
        functools.partial(middle_kernel, heads, experts),
        (
            shape((rows, D), F32),
            shape((rows, D), BF16),
            shape((rows, LANES), F32),
            shape((places, D + LANES), BF16),
        ),
        flops=2 * rows * D * (D + 1024 + 2 * places),
        nbytes=5 << 20,
        grid=(1,),
        in_specs=[
            full(n_ctx, rows, LANES),
            out_block,
            full(rows, D),
            full(LANES, D),
            full(rows, 2),
            full(rows, 2),
        ],
        out_specs=[
            full(rows, D),
            full(rows, D),
            full(rows, LANES),
            full(places, D + LANES),
        ],
    )(came, mid_pack, x, tail, routes[0], target)
    x_rows = exchange(outgoing.reshape(n_ctx, -1, D + LANES)).reshape(places, D + LANES)

    lead = D // CHUNK
    steps = FS // CHUNK
    shared_res, shared_dx, shared_mid, grad_so = call(
        shared_kernel,
        (
            shape((rows, D), F32),
            shape((rows, D), F32),
            shape((2, rows, FS), BF16),
            shape((FS, D), BF16),
        ),
        flops=2 * rows * D * FS * 7,
        nbytes=14 << 20,
        grid=(steps,),
        in_specs=[
            full(rows, D),
            full(rows, D),
            pl.BlockSpec((D, CHUNK), lambda c: (0, lead + c)),
            pl.BlockSpec((D, CHUNK), lambda c: (0, lead + steps + c)),
            pl.BlockSpec((CHUNK, D), lambda c: (c, 0)),
        ],
        out_specs=[
            full(rows, D),
            full(rows, D),
            pl.BlockSpec((2, rows, CHUNK), lambda c: (0, 0, c)),
            pl.BlockSpec((CHUNK, D), lambda c: (c, 0)),
        ],
        scratch_shapes=[pltpu.VMEM((rows, D), F32), pltpu.VMEM((rows, D), F32)],
    )(ffn_in, dout, mid_pack, mid_pack, shared_out)
    dense_pack = call(
        shared_grad_kernel,
        shape((D, D + 2 * FS), BF16),
        flops=2 * rows * D * FS * 2,
        nbytes=9 << 20,
        grid=(2, steps),
        in_specs=[
            pl.BlockSpec((rows, D), lambda i, c: (0, 0)),
            pl.BlockSpec((1, rows, CHUNK), lambda i, c: (i, 0, c)),
        ],
        out_specs=pl.BlockSpec((D, CHUNK), lambda i, c: (0, lead + i * steps + c)),
        scratch_shapes=[pltpu.VMEM((D, rows), BF16)],
    )(ffn_in, shared_mid)

    wide = FF // CHUNK
    expert_dx, expert_res, expert_mid = call(
        expert_kernel,
        (
            shape((places, D + LANES), BF16),
            shape((places, D), BF16),
            shape((3, places, FF), BF16),
        ),
        flops=2 * places * D * FF * 6,
        nbytes=24 << 20,
        grid=(wide,),
        in_specs=[
            full(places, D + LANES),
            full(places, D),
            pl.BlockSpec((D, CHUNK), lambda c: (0, c)),
            pl.BlockSpec((D, CHUNK), lambda c: (0, wide + c)),
            pl.BlockSpec((D, CHUNK), lambda c: (0, 2 * wide + c)),
        ],
        out_specs=[
            full(places, D + LANES),
            full(places, D),
            pl.BlockSpec((3, places, CHUNK), lambda c: (0, 0, c)),
        ],
        scratch_shapes=[
            pltpu.VMEM((places, D), F32),
            pltpu.VMEM((places, D), F32),
            pltpu.VMEM((places, LANES), F32),
        ],
    )(x_rows, dy_rows, expert_pack, expert_pack, expert_pack)
    dx_came = exchange(expert_dx.reshape(n_ctx, -1, D + LANES)).reshape(places, D + LANES)
    expert_grad = call(
        expert_grad_kernel,
        shape((D, 3 * FF), BF16),
        flops=2 * places * D * FF * 3,
        nbytes=21 << 20,
        grid=(3, wide),
        in_specs=[
            pl.BlockSpec((places, D), lambda i, c: (0, 0)),
            pl.BlockSpec((places, D), lambda i, c: (0, 0)),
            pl.BlockSpec((1, places, CHUNK), lambda i, c: (i, 0, c)),
        ],
        out_specs=pl.BlockSpec((D, CHUNK), lambda i, c: (0, i * wide + c)),
        scratch_shapes=[pltpu.VMEM((D, places), BF16), pltpu.VMEM((D, places), BF16)],
    )(x_rows, dy_rows, expert_mid)

    branch_send, dres, branch, dlogits, dgain_two = call(
        functools.partial(combine_kernel, heads, experts),
        (
            shape((n_ctx, rows, LANES), BF16),
            shape((rows, D), F32),
            shape((rows, D), BF16),
            shape((rows, LANES), BF16),
            shape((1, D), F32),
        ),
        flops=2 * rows * D * (places + 1024),
        nbytes=6 << 20,
        grid=(1,),
        in_specs=[
            full(places, D + LANES),
            full(rows, D),
            full(rows, D),
            full(rows, D),
            full(rows, LANES),
            full(rows, 2),
            full(rows, 2),
            full(LANES, D),
            out_block,
        ],
        out_specs=[
            full(n_ctx, rows, LANES),
            full(rows, D),
            full(rows, D),
            full(rows, LANES),
            full(1, D),
        ],
    )(dx_came, shared_dx, residual, dout, gates, routes[0], target, tail, mid_pack)
    branch_recv = exchange(branch_send)

    dense_pack, grad_router = call(
        functools.partial(dense_grad_kernel, heads),
        (shape((D, D + 2 * FS), BF16), shape((D, LANES), F32)),
        flops=2 * rows * D * (1024 + LANES),
        nbytes=4 << 20,
        grid=(1,),
        in_specs=[
            full(n_ctx, rows, LANES),
            full(rows, D),
            full(rows, D),
            full(rows, LANES),
            pl.BlockSpec(memory_space=pl.ANY),
        ],
        out_specs=[out_block, full(D, LANES)],
        scratch_shapes=[pltpu.VMEM((D, D), F32)],
        input_output_aliases={4: 0},
    )(came, branch, ffn_in, dlogits, dense_pack)

    dsend = call(
        functools.partial(attend_back_kernel, n_ctx, share),
        shape((n_ctx, rows, 3 * LANES), BF16),
        flops=2 * share * rows * n_ctx * n_ctx * LANES * 3,
        nbytes=8 << 20,
        grid_spec=pltpu.PrefetchScalarGridSpec(
            num_scalar_prefetch=1,
            grid=(n_ctx,),
            in_specs=[
                packet,
                pl.BlockSpec((n_ctx, rows, LANES), lambda i, sc: (0, 0, 0)),
                pl.BlockSpec((1, LANES, share), block_of),
                pl.BlockSpec((1, 1, share), block_of),
            ],
            out_specs=packet,
            scratch_shapes=[
                pltpu.VMEM((2 * rows, LANES), BF16),
                pltpu.VMEM((2 * rows, LANES), BF16),
                pltpu.VMEM((n_ctx, rows, LANES), F32),
                pltpu.VMEM((n_ctx, rows, LANES), F32),
                pltpu.VMEM((2 * rows, LANES), F32),
            ],
        ),
    )(scalars, recv, branch_recv, kept, lse)
    drecv = exchange(dsend)

    grad_x, last_pack = call(
        functools.partial(last_kernel, heads, experts),
        (shape((rows, D), F32), shape((D, PACKED), BF16)),
        flops=2 * rows * D * 3 * D * 2,
        nbytes=14 << 20,
        in_specs=[whole] * 10,
        out_specs=[whole, whole],
        scratch_shapes=[pltpu.VMEM((rows, 3 * D), BF16)],
    )(drecv, cos, sin, attn_in, x, qkv_pack, tail, dres, grad_router, dgain_two)

    res_came = exchange(expert_res.reshape(n_ctx, -1, D)).reshape(places, D)
    output = call(
        output_kernel,
        shape((rows, D), BF16),
        flops=2 * rows * D * places * 2,
        nbytes=5 << 20,
    )(residual, shared_res, gates, target, live, res_came)

    scatter = functools.partial(
        lax.psum_scatter, axis_name="fsdp", scatter_dimension=0, tiled=True
    )
    expert_sum = scatter(expert_grad)
    dense_part, so_part = scatter(dense_pack), scatter(grad_so)
    dense_sum, so_sum = lax.psum((dense_part, so_part), "ctx")
    last_sum = lax.psum(scatter(last_pack), "ctx")
    last_sum = last_sum.astype(F32)
    dense_sum = dense_sum.astype(F32)
    expert_sum = expert_sum.astype(F32)
    small = last_sum[:, 3 * D :]
    return (
        output[None],
        grad_x[None],
        small[:, experts],
        last_sum[:, 0 : 3 * D],
        dense_sum[:, 0:D],
        small[:, experts + 1],
        small[:, 0:experts],
        dense_sum[:, D:],
        so_sum.astype(F32),
        expert_sum[None, :, 0 : 2 * FF],
        expert_sum[:, 2 * FF :].T[None],
    )


def solution(mesh):
    row_spec = P("fsdp", "ctx", None)
    flat = P("fsdp", None)
    return jax.shard_map(
        on_device,
        mesh=mesh,
        in_specs=(
            row_spec,
            row_spec,
            P("fsdp"),
            P(),
            row_spec,
            P("fsdp"),
            flat,
            flat,
            P("fsdp"),
            flat,
            flat,
            flat,
            P("ctx", "fsdp", None),
            P("ctx", None, "fsdp"),
        ),
        out_specs=(
            row_spec,
            row_spec,
            P("fsdp"),
            flat,
            flat,
            P("fsdp"),
            flat,
            flat,
            flat,
            P("ctx", "fsdp", None),
            P("ctx", None, "fsdp"),
        ),
        check_vma=False,
    )
```

```python
import functools

import jax
import jax.numpy as jnp
from jax import lax
from jax.experimental import pallas as pl
from jax.experimental.pallas import tpu as pltpu
from jax.sharding import PartitionSpec as P

D = 768
HEADS = 12
HEAD_DIM = 64
FF = 2048
FS = 2048
LANES = 128
CHUNK = 256
PACKED = 3 * D + LANES
norm_eps = 1e-06
F32 = jnp.float32
BF16 = jnp.bfloat16


def dot(a, b):
    return jnp.dot(a, b, preferred_element_type=F32)


def dot_nt(a, b):
    return lax.dot_general(a, b, (((1,), (1,)), ((), ())), preferred_element_type=F32)


def dot_tn(a, b):
    return lax.dot_general(a, b, (((0,), (0,)), ((), ())), preferred_element_type=F32)


def call(kernel, outs, *, flops, nbytes, limit=56, **kw):
    return pl.pallas_call(
        kernel,
        out_shape=outs,
        compiler_params=pltpu.CompilerParams(vmem_limit_bytes=limit << 20),
        cost_estimate=pl.CostEstimate(
            flops=int(flops), bytes_accessed=int(nbytes), transcendentals=0
        ),
        **kw,
    )


def shape(dims, dtype):
    return jax.ShapeDtypeStruct(dims, dtype)


def lanes_of(rows, width=LANES):
    return lax.broadcasted_iota(jnp.int32, (rows, width), 1)


def first_heads(n_ctx, slot_dev):
    share = HEADS * slot_dev // n_ctx
    return [min(share * d // slot_dev, HEADS - 2) for d in range(n_ctx)]


def partner(t, lane):
    return jnp.where(lane % 64 < 32, pltpu.roll(t, 96, 1), pltpu.roll(t, 32, 1))


def in_parts(v):
    high = v.astype(BF16)
    rest = v - high.astype(F32)
    mid = rest.astype(BF16)
    low = (rest - mid.astype(F32)).astype(BF16)
    return high.astype(F32), mid.astype(F32), low.astype(F32)


def part_lanes(v, lane):
    high, mid, low = in_parts(v)
    zero = jnp.zeros((), F32)
    return jnp.where(
        lane == 0, high, jnp.where(lane == 1, mid, jnp.where(lane == 2, low, zero))
    ).astype(BF16)


def picks(target_ref, places):
    rows = target_ref.shape[0]
    place = lanes_of(rows, places)
    return tuple(
        jnp.where(place == target_ref[:, k : k + 1], 1.0, 0.0).astype(BF16) for k in range(2)
    )


def start_kernel(experts, capacity, routes_ref, cot_ref, live_ref, target_ref, dout_ref, send_ref):
    rows = routes_ref.shape[0]
    lane = lanes_of(rows)
    hot = [jnp.where(lane == routes_ref[:, k : k + 1], 1.0, 0.0) for k in range(2)]
    below = jnp.where(
        lanes_of(rows, rows) < lax.broadcasted_iota(jnp.int32, (rows, rows), 0), 1.0, 0.0
    )
    earlier = dot(below.astype(BF16), (hot[0] + hot[1]).astype(BF16))
    place = [
        routes_ref[:, k : k + 1] * capacity
        + jnp.sum(hot[k] * earlier, axis=-1, keepdims=True).astype(jnp.int32)
        for k in range(2)
    ]
    for k in range(2):
        target_ref[:, k : k + 1] = place[k]
    dout = (cot_ref[...].astype(F32) * live_ref[...]).astype(BF16)
    dout_ref[...] = dout
    spot = lanes_of(rows, send_ref.shape[0])
    pick = jnp.where((spot == place[0]) | (spot == place[1]), 1.0, 0.0).astype(BF16)
    send_ref[...] = dot_tn(pick, dout).astype(BF16)


def qkv_kernel(heads, experts, x_ref, w_ref, cos_ref, sin_ref, send_ref, in_ref, tail_ref):
    x = x_ref[...].astype(F32)
    tail = w_ref[:, 3 * D :].astype(F32).T
    tail_ref[...] = tail
    inv = lax.rsqrt(jnp.mean(x * x, axis=-1, keepdims=True) + norm_eps)
    attn_in = (x * inv * tail[experts : experts + 1, :]).astype(BF16)
    in_ref[...] = attn_in
    lane = lanes_of(x.shape[0])
    cos, sin = cos_ref[...], sin_ref[...]
    for part in range(3):
        y = dot(attn_in, w_ref[:, part * D : (part + 1) * D])
        groups = []
        for g in range(D // LANES):
            t = y[:, g * LANES : (g + 1) * LANES]
            if part < 2:
                t = t * cos + partner(t, lane) * sin
            groups.append(t)
        turned = [pltpu.roll(t, 64, 1) for t in groups]
        for d, head in enumerate(heads):
            g = head // 2
            if head % 2 == 0:
                packet = groups[g]
            else:
                packet = jnp.where(lane < 64, turned[g], turned[g + 1])
            send_ref[d, :, part * LANES : (part + 1) * LANES] = packet.astype(BF16)


def stack_rows(stack_ref, block, lane):
    rows = block.shape[0]
    zero = jnp.zeros((), block.dtype)
    stack_ref[0:rows, :] = jnp.where(lane < 64, block, zero)
    stack_ref[rows : 2 * rows, :] = jnp.where(lane >= 64, block, zero)


def unstack_rows(stack_ref, block, offset, lane):
    rows = stack_ref.shape[0] // 2
    stack_ref[...] = jnp.zeros_like(stack_ref)
    stack_ref[pl.ds(offset, block.shape[0]), :] = block
    return jnp.where(lane < 64, stack_ref[0:rows, :], stack_ref[rows : 2 * rows, :])


def key_limits(share, rows, q_block, offset, length):
    row = lax.broadcasted_iota(jnp.int32, (1, share), 1) + offset
    row = jnp.where(row >= rows, row - rows, row)
    return jnp.minimum(q_block * rows + row + 1, length)


def attend_kernel(n, share, sc, recv_ref, out_ref, keep_ref, lse_ref, stack, scores, back):
    q_block = pl.program_id(0)
    rows = recv_ref.shape[1]
    offset = pl.multiple_of(sc[n], 64)
    length = sc[n + 1]
    lane = lanes_of(rows)
    stack_rows(stack, recv_ref[sc[q_block], :, 0:LANES] * 0.125, lane)
    query = stack[pl.ds(offset, share), :]
    limit = key_limits(share, rows, q_block, offset, length)
    key_row = lax.broadcasted_iota(jnp.int32, (rows, share), 0)
    blocks = jnp.minimum(q_block + 1, (length + rows - 1) // rows)

    def score_step(j, top):
        keys = recv_ref[sc[j], :, LANES : 2 * LANES]
        s = dot_nt(keys, query)
        s = jnp.where(key_row < limit - j * rows, s, -1e30)
        scores[j] = s
        return jnp.maximum(top, jnp.max(s, axis=0, keepdims=True))

    top = lax.fori_loop(0, blocks, score_step, jnp.full((1, share), -1e30, F32))

    def value_step(j, carry):
        total, acc = carry
        weights = jnp.exp(scores[j] - top)
        total = total + jnp.sum(weights, axis=0, keepdims=True)
        values = recv_ref[sc[j], :, 2 * LANES : 3 * LANES]
        return total, acc + dot_tn(values, weights.astype(BF16))

    total, acc = lax.fori_loop(
        0, blocks, value_step, (jnp.zeros((1, share), F32), jnp.zeros((LANES, share), F32))
    )
    acc = acc / total
    keep_ref[0] = acc
    lse_ref[0] = top + jnp.log(total)
    out_ref[0] = unstack_rows(back, acc.T, offset, lane).astype(BF16)


def attend_back_kernel(
    n, share, sc, recv_ref, grad_ref, keep_ref, lse_ref, out_ref, stack, gstack, dkeys, dvalues, back
):
    q_block = pl.program_id(0)
    rows = recv_ref.shape[1]
    offset = pl.multiple_of(sc[n], 64)
    length = sc[n + 1]
    lane = lanes_of(rows)
    source = sc[q_block]

    @pl.when(q_block == 0)
    def _():
        dkeys[...] = jnp.zeros_like(dkeys)
        dvalues[...] = jnp.zeros_like(dvalues)

    stack_rows(stack, recv_ref[source, :, 0:LANES] * 0.125, lane)
    query = stack[pl.ds(offset, share), :]
    stack_rows(gstack, grad_ref[source], lane)
    grad = gstack[pl.ds(offset, share), :]
    lse = lse_ref[0]
    delta = jnp.sum(grad.astype(F32).T * keep_ref[0], axis=0, keepdims=True)
    limit = key_limits(share, rows, q_block, offset, length)
    key_row = lax.broadcasted_iota(jnp.int32, (rows, share), 0)
    blocks = jnp.minimum(q_block + 1, (length + rows - 1) // rows)

    def step(j, acc):
        keys = recv_ref[sc[j], :, LANES : 2 * LANES]
        values = recv_ref[sc[j], :, 2 * LANES : 3 * LANES]
        s = dot_nt(keys, query)
        weights = jnp.exp(jnp.where(key_row < limit - j * rows, s, -1e30) - lse)
        dweights = dot_nt(values, grad)
        dscores = (weights * (dweights - delta)).astype(BF16)
        dkeys[j] += dot(dscores, query)
        dvalues[j] += dot(weights.astype(BF16), grad)
        return acc + dot_tn(keys, dscores)

    acc = lax.fori_loop(0, blocks, step, jnp.zeros((LANES, share), F32))
    dquery = unstack_rows(back, acc.T * 0.125, offset, lane)
    out_ref[source, :, 0:LANES] = dquery.astype(BF16)

    @pl.when(q_block == n - 1)
    def _():
        def flush(j, carry):
            out_ref[sc[j], :, LANES : 2 * LANES] = dkeys[j].astype(BF16)
            out_ref[sc[j], :, 2 * LANES : 3 * LANES] = dvalues[j].astype(BF16)
            return carry

        lax.fori_loop(0, n, flush, 0)


def middle_kernel(
    heads,
    experts,
    came_ref,
    w_ref,
    x_ref,
    tail_ref,
    routes_ref,
    target_ref,
    residual_ref,
    in_ref,
    gates_ref,
    send_ref,
):
    total = x_ref[...].astype(F32)
    for d, head in enumerate(heads):
        total = total + dot(came_ref[d], w_ref[64 * head : 64 * head + LANES, :])
    residual_ref[...] = total
    inv = lax.rsqrt(jnp.mean(total * total, axis=-1, keepdims=True) + norm_eps)
    ffn_in = (total * inv * tail_ref[experts + 1 : experts + 2, :]).astype(BF16)
    in_ref[...] = ffn_in
    logits = dot_nt(ffn_in, tail_ref[...].astype(BF16))
    lane = lanes_of(logits.shape[0])
    chosen = [
        jnp.sum(jnp.where(lane == routes_ref[:, k : k + 1], logits, 0.0), axis=-1, keepdims=True)
        for k in range(2)
    ]
    top = jnp.maximum(chosen[0], chosen[1])
    raised = [jnp.exp(c - top) for c in chosen]
    gates = [r / (raised[0] + raised[1]) for r in raised]
    gates_ref[...] = jnp.where(lane == 0, gates[0], gates[1])
    pick = picks(target_ref, send_ref.shape[0])
    send_ref[:, 0:D] = dot_tn(pick[0] + pick[1], ffn_in).astype(BF16)
    send_ref[:, D:] = (
        dot_tn(pick[0], part_lanes(gates[0], lane)) + dot_tn(pick[1], part_lanes(gates[1], lane))
    ).astype(BF16)


def gated(g, u, da):
    sig = 1.0 / (1.0 + jnp.exp(-g))
    silu = g * sig
    return silu * u, da * u * sig * (1.0 + g * (1.0 - sig)), da * silu


def store_shards(sc, first_row, value, keep_ref, give_ref):
    half, shard, _ = keep_ref.shape
    piece = min(shard, value.shape[0])
    for u in range(value.shape[0] // piece):
        row = first_row + u * piece
        j = sc[row // shard]
        inside = pl.multiple_of(row % shard, piece)

        @pl.when(j < half)
        def _():
            keep_ref[j, pl.ds(inside, piece), :] = value[u * piece : (u + 1) * piece]

        @pl.when(j >= half)
        def _():
            give_ref[j - half, pl.ds(inside, piece), :] = value[u * piece : (u + 1) * piece]


def shared_kernel(
    sc, x_ref, dy_ref, wg_ref, wu_ref, wo_ref, res_ref, dx_ref, mid_ref, keep_ref, give_ref, res_acc, dx_acc
):
    c = pl.program_id(0)

    @pl.when(c == 0)
    def _():
        res_acc[...] = jnp.zeros_like(res_acc)
        dx_acc[...] = jnp.zeros_like(dx_acc)

    x, dy = x_ref[...], dy_ref[...]
    wg, wu, wo = wg_ref[...], wu_ref[...], wo_ref[...]
    act, dg, du = gated(dot(x, wg), dot(x, wu), dot_nt(dy, wo))
    act, dg, du = act.astype(BF16), dg.astype(BF16), du.astype(BF16)
    res_acc[...] += dot(act, wo)
    dx_acc[...] += dot_nt(dg, wg) + dot_nt(du, wu)
    mid_ref[0] = dg
    mid_ref[1] = du
    store_shards(sc, c * CHUNK, dot_tn(act, dy).astype(BF16), keep_ref, give_ref)

    @pl.when(c == pl.num_programs(0) - 1)
    def _():
        res_ref[...] = res_acc[...]
        dx_ref[...] = dx_acc[...]


def turn_shards(sc, x, raw, xt):
    raw[...] = x.T
    shard = raw.shape[0] // sc.shape[0]
    for j in range(sc.shape[0]):
        row = pl.multiple_of(sc[j] * shard, 16)
        xt[j * shard : (j + 1) * shard, :] = raw[pl.ds(row, shard), :]


def split_shards(value, keep_ref, give_ref):
    half, shard, _ = keep_ref.shape
    for j in range(half):
        keep_ref[j] = value[j * shard : (j + 1) * shard]
        give_ref[j] = value[(half + j) * shard : (half + j + 1) * shard]


def shared_grad_kernel(sc, x_ref, mid_ref, keep_ref, give_ref, raw, xt):
    @pl.when((pl.program_id(0) == 0) & (pl.program_id(1) == 0))
    def _():
        turn_shards(sc, x_ref[...], raw, xt)

    split_shards(dot(xt[...], mid_ref[0]).astype(BF16), keep_ref, give_ref)


def expert_kernel(
    x_ref, dy_ref, wg_ref, wu_ref, wt_ref, dx_ref, res_ref, mid_ref, dx_acc, res_acc, dgate
):
    c = pl.program_id(0)

    @pl.when(c == 0)
    def _():
        res_acc[...] = jnp.zeros_like(res_acc)
        dx_acc[...] = jnp.zeros_like(dx_acc)
        dgate[...] = jnp.zeros_like(dgate)

    x, dy = x_ref[:, 0:D], dy_ref[...]
    gate = jnp.sum(x_ref[:, D:].astype(F32), axis=-1, keepdims=True)
    wg, wu, wt = wg_ref[...], wu_ref[...], wt_ref[...]
    da = dot(dy, wt)
    act, dg, du = gated(dot(x, wg), dot(x, wu), da * gate)
    dgate[...] += jnp.sum(act * da, axis=-1, keepdims=True)
    mid_ref[2] = (act * gate).astype(BF16)
    act, dg, du = act.astype(BF16), dg.astype(BF16), du.astype(BF16)
    res_acc[...] += dot_nt(act, wt)
    dx_acc[...] += dot_nt(dg, wg) + dot_nt(du, wu)
    mid_ref[0] = dg
    mid_ref[1] = du

    @pl.when(c == pl.num_programs(0) - 1)
    def _():
        res_ref[...] = res_acc[...].astype(BF16)
        dx_ref[:, 0:D] = dx_acc[...].astype(BF16)
        dx_ref[:, D:] = part_lanes(dgate[:, 0:1], lanes_of(dgate.shape[0]))


def expert_grad_kernel(sc, x_ref, dy_ref, mid_ref, keep_ref, give_ref, raw, xt, dyt):
    @pl.when((pl.program_id(0) == 0) & (pl.program_id(1) == 0))
    def _():
        turn_shards(sc, x_ref[...], raw, xt)
        turn_shards(sc, dy_ref[...], raw, dyt)

    @pl.when(pl.program_id(0) < 2)
    def _():
        split_shards(dot(xt[...], mid_ref[0]).astype(BF16), keep_ref, give_ref)

    @pl.when(pl.program_id(0) == 2)
    def _():
        split_shards(dot(dyt[...], mid_ref[0]).astype(BF16), keep_ref, give_ref)


def combine_kernel(
    heads,
    experts,
    came_ref,
    dx_ref,
    residual_ref,
    dout_ref,
    gates_ref,
    routes_ref,
    target_ref,
    tail_ref,
    w_ref,
    send_ref,
    dres_ref,
    branch_ref,
    dlogits_ref,
    dgain_ref,
):
    pick = picks(target_ref, came_ref.shape[0])
    gates = [gates_ref[:, k : k + 1] for k in range(2)]
    parts = came_ref[:, D:]
    dgate = [jnp.sum(dot(pick[k], parts), axis=-1, keepdims=True) for k in range(2)]
    mean = gates[0] * dgate[0] + gates[1] * dgate[1]
    lane = lanes_of(pick[0].shape[0])
    dlogits = sum(
        jnp.where(lane == routes_ref[:, k : k + 1], gates[k] * (dgate[k] - mean), 0.0)
        for k in range(2)
    ).astype(BF16)
    dlogits_ref[...] = dlogits
    tail = tail_ref[...]
    dffn = dot(pick[0] + pick[1], came_ref[:, 0:D]) + dx_ref[...] + dot(dlogits, tail.astype(BF16))
    residual = residual_ref[...]
    inv = lax.rsqrt(jnp.mean(residual * residual, axis=-1, keepdims=True) + norm_eps)
    scaled = dffn * tail[experts + 1 : experts + 2, :]
    total = jnp.mean(scaled * residual, axis=-1, keepdims=True)
    dres = dout_ref[...].astype(F32) + inv * scaled - residual * inv * inv * inv * total
    dres_ref[...] = dres
    dgain_ref[...] = jnp.sum(dffn * residual * inv, axis=0, keepdims=True)
    branch = dres.astype(BF16)
    branch_ref[...] = branch
    for d, head in enumerate(heads):
        send_ref[d] = dot_nt(branch, w_ref[64 * head : 64 * head + LANES, :]).astype(BF16)


def dense_grad_kernel(
    heads, sc, came_ref, branch_ref, in_ref, dlogits_ref, k_ref, g_ref, keep_ref, give_ref, router_ref, acc
):
    acc[...] = jnp.zeros_like(acc)
    branch = branch_ref[...]
    for d, head in enumerate(heads):
        acc[64 * head : 64 * head + LANES, :] += dot_tn(came_ref[d], branch)
    half, shard, _ = keep_ref.shape
    for j in range(half):
        row = pl.multiple_of(sc[j] * shard, 16)
        keep_ref[j] = acc[pl.ds(row, shard), :].astype(BF16)
        row = pl.multiple_of(sc[half + j] * shard, 16)
        give_ref[j] = acc[pl.ds(row, shard), :].astype(BF16)
    router_ref[...] = dot_tn(in_ref[...], dlogits_ref[...])


def last_kernel(
    heads,
    experts,
    sc,
    recv_ref,
    cos_ref,
    sin_ref,
    in_ref,
    x_ref,
    w_ref,
    tail_ref,
    dres_ref,
    router_ref,
    dgain_ref,
    out_ref,
    pack_ref,
    dproj,
    raw,
    turned,
    small,
):
    lane = lanes_of(x_ref.shape[0])
    cos, sin = cos_ref[...], sin_ref[...]
    for part in range(3):
        groups = [jnp.zeros(lane.shape, F32) for _ in range(D // LANES)]
        for d, head in enumerate(heads):
            g = head // 2
            packet = recv_ref[d, :, part * LANES : (part + 1) * LANES].astype(F32)
            if head % 2 == 0:
                groups[g] = groups[g] + packet
            else:
                packet = pltpu.roll(packet, 64, 1)
                groups[g] = groups[g] + jnp.where(lane >= 64, packet, 0.0)
                groups[g + 1] = groups[g + 1] + jnp.where(lane < 64, packet, 0.0)
        for g, t in enumerate(groups):
            if part < 2:
                t = t.astype(BF16).astype(F32)
                t = t * cos - partner(t, lane) * sin
            dproj[:, part * D + g * LANES : part * D + (g + 1) * LANES] = t.astype(BF16)
    dnorm = dot_nt(dproj[...], w_ref[:, 0 : 3 * D])
    x = x_ref[...].astype(F32)
    gain = tail_ref[experts : experts + 1, :]
    inv = lax.rsqrt(jnp.mean(x * x, axis=-1, keepdims=True) + norm_eps)
    scaled = dnorm * gain
    total = jnp.mean(scaled * x, axis=-1, keepdims=True)
    out_ref[...] = dres_ref[...] + inv * scaled - x * inv * inv * inv * total
    dgain_one = jnp.sum(dnorm * x * inv, axis=0, keepdims=True)
    row = lax.broadcasted_iota(jnp.int32, (LANES, D), 0)
    gains = jnp.where(row == experts, dgain_one, jnp.where(row == experts + 1, dgain_ref[...], 0.0))
    small[...] = router_ref[...] + gains.T
    turn_shards(sc, in_ref[...], raw, turned)
    shards, shard, _ = pack_ref.shape
    for part in range(3):
        value = dot(turned[...], dproj[:, part * D : (part + 1) * D]).astype(BF16)
        for j in range(shards):
            pack_ref[j, :, part * D : (part + 1) * D] = value[j * shard : (j + 1) * shard]
    for j in range(shards):
        row = pl.multiple_of(sc[j] * shard, 16)
        pack_ref[j, :, 3 * D :] = small[pl.ds(row, shard), :].astype(BF16)


def ring_split(rows, columns, pieces):
    down = 1
    while 2 * down <= pieces and rows % (32 * down) == 0:
        down *= 2
    across = pieces // down
    width = -(-columns // (LANES * across)) * LANES
    return down, across, rows // down, width


def ring_place(position, n):
    half = n // 2
    return jnp.where(position < half, 2 * position, 2 * (n - 1 - position) + 1)


def tail_kernel(
    n,
    members,
    splits,
    a_ref,
    b_ref,
    c_ref,
    a_out,
    b_out,
    c_out,
    *scratch,
):
    own, back, full = scratch[0:3], scratch[3:6], scratch[6:9]
    levels = members.bit_length() - 1
    caught, sums = scratch[9 : 9 + levels], scratch[9 + levels : 9 + 2 * levels]
    send_sem, recv_sem, level_send, level_recv = scratch[9 + 2 * levels :]
    ctx, fsdp = lax.axis_index("ctx"), lax.axis_index("fsdp")
    here = jnp.where(ctx % 2 == 0, ctx // 2, n - 1 - ctx // 2)
    ahead = (ring_place(lax.rem(here + 1, n), n), fsdp)
    behind = (ring_place(lax.rem(here + n - 1, n), n), fsdp)
    mates = [(ctx, fsdp + (1 << b) - 2 * (1 << b) * (fsdp // (1 << b) % 2)) for b in range(levels)]

    barrier = pltpu.get_barrier_semaphore()
    for peer in [ahead, behind] + mates:
        pl.semaphore_signal(barrier, inc=1, device_id=peer, device_id_type=pl.DeviceIdType.MESH)
    pl.semaphore_wait(barrier, 2 + levels)

    def level_copy(b):
        count = members >> (b + 1)
        source = c_ref.at[pl.ds(count, count)] if b == 0 else sums[b - 1].at[pl.ds(count, count)]
        return pltpu.make_async_remote_copy(
            src_ref=source,
            dst_ref=caught[b],
            send_sem=level_send.at[b],
            recv_sem=level_recv.at[b],
            device_id=mates[b],
            device_id_type=pl.DeviceIdType.MESH,
        )

    def level_add(b):
        count = members >> (b + 1)
        level_copy(b).wait_recv()
        before = c_ref if b == 0 else sums[b - 1]
        for j in range(count):
            sums[b][j] = (before[j].astype(F32) + caught[b][j].astype(F32)).astype(BF16)

    def load(i, ref):
        down, across, height, width = splits[i]
        for p in range(down * across):
            r, c = p // across, p % across
            have = max(0, min(width, ref.shape[1] - c * width))
            if have > 0:
                own[i][p, :, 0:have] = ref[r * height : (r + 1) * height, c * width : c * width + have]
            if have < width:
                own[i][p, :, have:] = jnp.zeros((height, width - have), BF16)

    def save(i, ref):
        down, across, height, width = splits[i]
        for p in range(down * across):
            r, c = p // across, p % across
            have = max(0, min(width, ref.shape[1] - c * width))
            if have > 0:
                ref[r * height : (r + 1) * height, c * width : c * width + have] = full[i][p, :, 0:have]

    def chunk(direction, steps):
        if direction == 0:
            return lax.rem(here + 4 * n - steps, n)
        return n + lax.rem(here + steps, n)

    def copy(i, direction, step, source, target, slot):
        return pltpu.make_async_remote_copy(
            src_ref=source[i].at[slot],
            dst_ref=target[i].at[slot],
            send_sem=send_sem.at[i, direction, step],
            recv_sem=recv_sem.at[i, direction, step],
            device_id=ahead if direction == 0 else behind,
            device_id_type=pl.DeviceIdType.MESH,
        )

    def first(i):
        for direction in range(2):
            copy(i, direction, 0, own, back, chunk(direction, 1)).start()

    def reduce_step(i, s):
        for direction in range(2):
            slot = chunk(direction, 1 + s)
            copy(i, direction, s - 1, own, back, slot).wait_recv()
            back[i][slot] = (back[i][slot].astype(F32) + own[i][slot].astype(F32)).astype(BF16)
            copy(i, direction, s, back, back, slot).start()

    def turn(i):
        for direction in range(2):
            slot = chunk(direction, n)
            copy(i, direction, n - 2, own, back, slot).wait_recv()
            full[i][slot] = (back[i][slot].astype(F32) + own[i][slot].astype(F32)).astype(BF16)
            copy(i, direction, n - 1, full, full, slot).start()

    def gather_step(i, s):
        for direction in range(2):
            slot = chunk(direction, s)
            copy(i, direction, n - 2 + s, full, full, slot).wait_recv()
            copy(i, direction, n - 1 + s, full, full, slot).start()

    def end(i):
        for direction in range(2):
            slot = chunk(direction, n - 1)
            copy(i, direction, 2 * n - 3, full, full, slot).wait_recv()

    def both(body, low, high):
        lax.fori_loop(low, high, lambda s, carry: (body(s), carry)[1], 0)

    level_copy(0).start()
    load(0, a_ref)
    first(0)
    load(1, b_ref)
    first(1)

    def early(s):
        reduce_step(0, s)
        reduce_step(1, s)

    early(1)
    for b in range(levels):
        level_add(b)
        if b + 1 < levels:
            level_copy(b + 1).start()
            if b == 0:
                both(early, 2, n - 1)
                turn(0)
                turn(1)
    load(2, sums[levels - 1].at[0])
    first(2)

    def joint(s):
        gather_step(0, s)
        gather_step(1, s)
        reduce_step(2, s)

    both(joint, 1, n - 1)
    end(0)
    end(1)
    turn(2)
    save(0, a_out)
    save(1, b_out)
    both(lambda s: gather_step(2, s), 1, n - 1)
    end(2)
    save(2, c_out)
    for b in range(levels):
        level_copy(b).wait_send()

    def drain(s):
        for i in range(3):
            for direction in range(2):
                copy(i, direction, s, own, back, 0).wait_send()

    both(drain, 0, 2 * n - 2)


def output_kernel(residual_ref, shared_ref, gates_ref, target_ref, live_ref, came_ref, out_ref):
    pick = picks(target_ref, came_ref.shape[0])
    came = came_ref[...]
    mixture = gates_ref[:, 0:1] * dot(pick[0], came) + gates_ref[:, 1:2] * dot(pick[1], came)
    out_ref[...] = (live_ref[...] * (residual_ref[...] + shared_ref[...] + mixture)).astype(BF16)


def on_device(
    tokens,
    cotangent,
    lengths,
    position_block,
    routes,
    gain_attn,
    w_qkv,
    w_out,
    gain_ffn,
    w_router,
    w_shared_in,
    w_shared_out,
    w_expert_in,
    w_expert_out,
):
    n_ctx = lax.axis_size("ctx")
    ctx_index = lax.axis_index("ctx")
    rows = tokens.shape[1]
    local = w_qkv.shape[0]
    experts = w_router.shape[1]
    capacity = 3 * rows // experts
    places = experts * capacity
    members = D // local
    share = HEADS * rows // n_ctx
    heads = first_heads(n_ctx, rows)
    gather = functools.partial(lax.all_gather, axis_name="fsdp", axis=0, tiled=True)
    exchange = functools.partial(
        lax.all_to_all, axis_name="ctx", split_axis=0, concat_axis=0, tiled=True
    )
    x = tokens[0]
    length = lengths[0]

    first_pack = jnp.concatenate(
        [
            w_qkv,
            w_router,
            gain_attn[:, None],
            gain_ffn[:, None],
            jnp.zeros((local, LANES - experts - 2), BF16),
        ],
        axis=1,
    )
    qkv_pack = gather(first_pack)
    out_weight = gather(w_out)
    weights = gather(
        jnp.concatenate([w_shared_in, w_expert_in[0], w_expert_out[0].T], axis=1)
    )
    shared_out = gather(w_shared_out)
    fsdp_index = lax.axis_index("fsdp")
    bits = members.bit_length() - 1
    mirrored = [int(format(j, "b").zfill(bits)[::-1], 2) for j in range(members)]
    shard_at = fsdp_index ^ jnp.array(mirrored, jnp.int32)
    spots = fsdp_index ^ jnp.arange(members, dtype=jnp.int32)
    spot_of = sum(((spots >> b) & 1) << (bits - 1 - b) for b in range(bits))

    query_pos = position_block[ctx_index] * rows + jnp.arange(rows, dtype=jnp.int32)
    live = (query_pos < length).astype(F32)[:, None]
    halves = HEAD_DIM // 2
    inverse = 10000.0 ** (-(jnp.arange(halves, dtype=F32) * 2.0 / HEAD_DIM))
    angles = query_pos.astype(F32)[:, None] * inverse[None, :]
    cos, sin = jnp.cos(angles), jnp.sin(angles)
    cos = jnp.concatenate([cos, cos, cos, cos], axis=1)
    sin = jnp.concatenate([-sin, sin, -sin, sin], axis=1)

    order = jnp.sum(
        jnp.where(
            position_block[None, :] == jnp.arange(n_ctx, dtype=jnp.int32)[:, None],
            jnp.arange(n_ctx, dtype=jnp.int32)[None, :],
            0,
        ),
        axis=1,
    )
    head_of = jnp.minimum(share * ctx_index // rows, HEADS - 2)
    offset = share * ctx_index - rows * head_of
    scalars = jnp.concatenate(
        [order, jnp.stack([offset.astype(jnp.int32), length.astype(jnp.int32)])]
    )

    target, dout, dy_send = call(
        functools.partial(start_kernel, experts, capacity),
        (shape((rows, 2), jnp.int32), shape((rows, D), BF16), shape((places, D), BF16)),
        flops=2 * rows * D * places,
        nbytes=3 << 20,
    )(routes[0], cotangent[0], live)
    dy_rows = exchange(dy_send.reshape(n_ctx, -1, D)).reshape(places, D)

    send, attn_in, tail = call(
        functools.partial(qkv_kernel, heads, experts),
        (
            shape((n_ctx, rows, 3 * LANES), BF16),
            shape((rows, D), BF16),
            shape((LANES, D), F32),
        ),
        flops=2 * rows * D * 3 * D,
        nbytes=6 << 20,
    )(x, qkv_pack, cos, sin)
    send, dy_rows = lax.optimization_barrier((send, dy_rows))
    recv = exchange(send)

    packet = pl.BlockSpec((n_ctx, rows, 3 * LANES), lambda i, sc: (0, 0, 0))
    block_of = lambda i, sc: (i, 0, 0)
    attended, kept, lse = call(
        functools.partial(attend_kernel, n_ctx, share),
        (
            shape((n_ctx, rows, LANES), BF16),
            shape((n_ctx, LANES, share), F32),
            shape((n_ctx, 1, share), F32),
        ),
        flops=2 * share * rows * n_ctx * n_ctx * LANES * 2,
        nbytes=5 << 20,
        grid_spec=pltpu.PrefetchScalarGridSpec(
            num_scalar_prefetch=1,
            grid=(n_ctx,),
            in_specs=[packet],
            out_specs=[
                pl.BlockSpec((1, rows, LANES), lambda i, sc: (sc[i], 0, 0)),
                pl.BlockSpec((1, LANES, share), block_of),
                pl.BlockSpec((1, 1, share), block_of),
            ],
            scratch_shapes=[
                pltpu.VMEM((2 * rows, LANES), BF16),
                pltpu.VMEM((n_ctx, rows, share), F32),
                pltpu.VMEM((2 * rows, LANES), F32),
            ],
        ),
    )(scalars, recv)
    came = exchange(attended)

    whole = pl.BlockSpec(memory_space=pltpu.VMEM)
    out_block = pl.BlockSpec((D, D), lambda *at: (0, 0))

    def full(*dims):
        return pl.BlockSpec(dims, lambda *at: (0,) * len(dims))

    residual, ffn_in, gates, outgoing = call(
        functools.partial(middle_kernel, heads, experts),
        (
            shape((rows, D), F32),
            shape((rows, D), BF16),
            shape((rows, LANES), F32),
            shape((places, D + LANES), BF16),
        ),
        flops=2 * rows * D * (D + 1024 + 2 * places),
        nbytes=5 << 20,
        grid=(1,),
        in_specs=[
            full(n_ctx, rows, LANES),
            out_block,
            full(rows, D),
            full(LANES, D),
            full(rows, 2),
            full(rows, 2),
        ],
        out_specs=[
            full(rows, D),
            full(rows, D),
            full(rows, LANES),
            full(places, D + LANES),
        ],
    )(came, out_weight, x, tail, routes[0], target)
    x_rows = exchange(outgoing.reshape(n_ctx, -1, D + LANES)).reshape(places, D + LANES)

    lead = D // CHUNK
    steps = FS // CHUNK
    half = members // 2

    def split(rows_each, columns):
        return (shape((half, rows_each, columns), BF16),) * 2

    shared_res, shared_dx, shared_mid, so_keep, so_give = call(
        shared_kernel,
        (
            shape((rows, D), F32),
            shape((rows, D), F32),
            shape((2, rows, FS), BF16),
        )
        + split(FS // members, D),
        flops=2 * rows * D * FS * 7,
        nbytes=14 << 20,
        grid_spec=pltpu.PrefetchScalarGridSpec(
            num_scalar_prefetch=1,
            grid=(steps,),
            in_specs=[
                full(rows, D),
                full(rows, D),
                pl.BlockSpec((D, CHUNK), lambda c, sc: (0, c)),
                pl.BlockSpec((D, CHUNK), lambda c, sc: (0, steps + c)),
                pl.BlockSpec((CHUNK, D), lambda c, sc: (c, 0)),
            ],
            out_specs=[
                full(rows, D),
                full(rows, D),
                pl.BlockSpec((2, rows, CHUNK), lambda c, sc: (0, 0, c)),
                full(half, FS // members, D),
                full(half, FS // members, D),
            ],
            scratch_shapes=[pltpu.VMEM((rows, D), F32), pltpu.VMEM((rows, D), F32)],
        ),
    )(spot_of, ffn_in, dout, weights, weights, shared_out)
    column = pl.BlockSpec((half, local, CHUNK), lambda i, c, sc: (0, 0, lead + i * steps + c))
    dense_keep, dense_give = call(
        shared_grad_kernel,
        split(local, D + 2 * FS),
        flops=2 * rows * D * FS * 2,
        nbytes=9 << 20,
        grid_spec=pltpu.PrefetchScalarGridSpec(
            num_scalar_prefetch=1,
            grid=(2, steps),
            in_specs=[
                full(rows, D),
                pl.BlockSpec((1, rows, CHUNK), lambda i, c, sc: (i, 0, c)),
            ],
            out_specs=[column, column],
            scratch_shapes=[pltpu.VMEM((D, rows), BF16), pltpu.VMEM((D, rows), BF16)],
        ),
    )(shard_at, ffn_in, shared_mid)

    wide = FF // CHUNK
    expert_dx, expert_res, expert_mid = call(
        expert_kernel,
        (
            shape((places, D + LANES), BF16),
            shape((places, D), BF16),
            shape((3, places, FF), BF16),
        ),
        flops=2 * places * D * FF * 6,
        nbytes=24 << 20,
        grid=(wide,),
        in_specs=[
            full(places, D + LANES),
            full(places, D),
            pl.BlockSpec((D, CHUNK), lambda c: (0, 2 * steps + c)),
            pl.BlockSpec((D, CHUNK), lambda c: (0, 2 * steps + wide + c)),
            pl.BlockSpec((D, CHUNK), lambda c: (0, 2 * steps + 2 * wide + c)),
        ],
        out_specs=[
            full(places, D + LANES),
            full(places, D),
            pl.BlockSpec((3, places, CHUNK), lambda c: (0, 0, c)),
        ],
        scratch_shapes=[
            pltpu.VMEM((places, D), F32),
            pltpu.VMEM((places, D), F32),
            pltpu.VMEM((places, LANES), F32),
        ],
    )(x_rows, dy_rows, weights, weights, weights)
    dx_came = exchange(expert_dx.reshape(n_ctx, -1, D + LANES)).reshape(places, D + LANES)
    wide_column = pl.BlockSpec((half, local, CHUNK), lambda i, c, sc: (0, 0, i * wide + c))
    expert_keep, expert_give = call(
        expert_grad_kernel,
        split(local, 3 * FF),
        flops=2 * places * D * FF * 3,
        nbytes=21 << 20,
        grid_spec=pltpu.PrefetchScalarGridSpec(
            num_scalar_prefetch=1,
            grid=(3, wide),
            in_specs=[
                full(places, D),
                full(places, D),
                pl.BlockSpec((1, places, CHUNK), lambda i, c, sc: (i, 0, c)),
            ],
            out_specs=[wide_column, wide_column],
            scratch_shapes=[pltpu.VMEM((D, places), BF16) for _ in range(3)],
        ),
    )(shard_at, x_rows, dy_rows, expert_mid)

    branch_send, dres, branch, dlogits, dgain_two = call(
        functools.partial(combine_kernel, heads, experts),
        (
            shape((n_ctx, rows, LANES), BF16),
            shape((rows, D), F32),
            shape((rows, D), BF16),
            shape((rows, LANES), BF16),
            shape((1, D), F32),
        ),
        flops=2 * rows * D * (places + 1024),
        nbytes=6 << 20,
        grid=(1,),
        in_specs=[
            full(places, D + LANES),
            full(rows, D),
            full(rows, D),
            full(rows, D),
            full(rows, LANES),
            full(rows, 2),
            full(rows, 2),
            full(LANES, D),
            out_block,
        ],
        out_specs=[
            full(n_ctx, rows, LANES),
            full(rows, D),
            full(rows, D),
            full(rows, LANES),
            full(1, D),
        ],
    )(dx_came, shared_dx, residual, dout, gates, routes[0], target, tail, out_weight)
    branch_recv = exchange(branch_send)

    front = pl.BlockSpec((half, local, D), lambda i, sc: (0, 0, 0))
    dense_keep, dense_give, grad_router = call(
        functools.partial(dense_grad_kernel, heads),
        split(local, D + 2 * FS) + (shape((D, LANES), F32),),
        flops=2 * rows * D * (1024 + LANES),
        nbytes=4 << 20,
        grid_spec=pltpu.PrefetchScalarGridSpec(
            num_scalar_prefetch=1,
            grid=(1,),
            in_specs=[
                full(n_ctx, rows, LANES),
                full(rows, D),
                full(rows, D),
                full(rows, LANES),
                pl.BlockSpec(memory_space=pl.ANY),
                pl.BlockSpec(memory_space=pl.ANY),
            ],
            out_specs=[front, front, full(D, LANES)],
            scratch_shapes=[pltpu.VMEM((D, D), F32)],
        ),
        input_output_aliases={5: 0, 6: 1},
    )(shard_at, came, branch, ffn_in, dlogits, dense_keep, dense_give)

    dsend = call(
        functools.partial(attend_back_kernel, n_ctx, share),
        shape((n_ctx, rows, 3 * LANES), BF16),
        flops=2 * share * rows * n_ctx * n_ctx * LANES * 3,
        nbytes=8 << 20,
        grid_spec=pltpu.PrefetchScalarGridSpec(
            num_scalar_prefetch=1,
            grid=(n_ctx,),
            in_specs=[
                packet,
                pl.BlockSpec((n_ctx, rows, LANES), lambda i, sc: (0, 0, 0)),
                pl.BlockSpec((1, LANES, share), block_of),
                pl.BlockSpec((1, 1, share), block_of),
            ],
            out_specs=packet,
            scratch_shapes=[
                pltpu.VMEM((2 * rows, LANES), BF16),
                pltpu.VMEM((2 * rows, LANES), BF16),
                pltpu.VMEM((n_ctx, rows, LANES), F32),
                pltpu.VMEM((n_ctx, rows, LANES), F32),
                pltpu.VMEM((2 * rows, LANES), F32),
            ],
        ),
    )(scalars, recv, branch_recv, kept, lse)
    drecv = exchange(dsend)

    grad_x, last_pack = call(
        functools.partial(last_kernel, heads, experts),
        (shape((rows, D), F32), shape((members, local, PACKED), BF16)),
        flops=2 * rows * D * 3 * D * 2,
        nbytes=14 << 20,
        grid_spec=pltpu.PrefetchScalarGridSpec(
            num_scalar_prefetch=1,
            grid=(1,),
            in_specs=[
                full(n_ctx, rows, 3 * LANES),
                full(rows, LANES),
                full(rows, LANES),
                full(rows, D),
                full(rows, D),
                full(D, PACKED),
                full(LANES, D),
                full(rows, D),
                full(D, LANES),
                full(1, D),
            ],
            out_specs=[full(rows, D), full(members, local, PACKED)],
            scratch_shapes=[
                pltpu.VMEM((rows, 3 * D), BF16),
                pltpu.VMEM((D, rows), BF16),
                pltpu.VMEM((D, rows), BF16),
                pltpu.VMEM((D, LANES), F32),
            ],
        ),
    )(shard_at, drecv, cos, sin, attn_in, x, qkv_pack, tail, dres, grad_router, dgain_two)

    res_came = exchange(expert_res.reshape(n_ctx, -1, D)).reshape(places, D)
    output = call(
        output_kernel,
        shape((rows, D), BF16),
        flops=2 * rows * D * places * 2,
        nbytes=5 << 20,
    )(residual, shared_res, gates, target, live, res_came)

    def reduce_shards(keep, give):
        terms = [keep]
        for b in range(bits):
            if b > 0:
                count = members >> (b + 1)
                give = sum(t[count:].astype(F32) for t in terms).astype(BF16)
                terms = [t[:count] for t in terms]
            came_in = lax.ppermute(give, "fsdp", [(i, i ^ (1 << b)) for i in range(members)])
            terms.append(came_in)
        return sum(t[0].astype(F32) for t in terms)

    dense_part = reduce_shards(dense_keep, dense_give).astype(BF16)
    so_part = reduce_shards(so_keep, so_give).astype(BF16)
    expert_sum = reduce_shards(expert_keep, expert_give)

    sizes = [dense_part.shape, so_part.shape, (local, PACKED)]
    splits = [ring_split(r, c, 2 * n_ctx) for r, c in sizes]
    tiles = [(2 * n_ctx, height, width) for _, _, height, width in splits]
    levels = [(members >> (b + 1), local, PACKED) for b in range(bits)]
    dense_sum, so_sum, last_sum = pl.pallas_call(
        functools.partial(tail_kernel, n_ctx, members, splits),
        out_shape=tuple(shape(size, BF16) for size in sizes),
        in_specs=[whole] * 3,
        out_specs=[whole] * 3,
        scratch_shapes=[pltpu.VMEM(t, BF16) for t in tiles + tiles + tiles + levels + levels]
        + [
            pltpu.SemaphoreType.DMA((3, 2, 2 * n_ctx - 2)),
            pltpu.SemaphoreType.DMA((3, 2, 2 * n_ctx - 2)),
            pltpu.SemaphoreType.DMA((bits,)),
            pltpu.SemaphoreType.DMA((bits,)),
        ],
        compiler_params=pltpu.CompilerParams(
            collective_id=0, has_side_effects=True, vmem_limit_bytes=56 << 20
        ),
        cost_estimate=pl.CostEstimate(flops=0, bytes_accessed=200 << 20, transcendentals=0),
    )(dense_part, so_part, last_pack)
    last_sum = last_sum.astype(F32)
    dense_sum = dense_sum.astype(F32)
    small = last_sum[:, 3 * D :]
    return (
        output[None],
        grad_x[None],
        small[:, experts],
        last_sum[:, 0 : 3 * D],
        dense_sum[:, 0:D],
        small[:, experts + 1],
        small[:, 0:experts],
        dense_sum[:, D:],
        so_sum.astype(F32),
        expert_sum[None, :, 0 : 2 * FF],
        expert_sum[:, 2 * FF :].T[None],
    )


def solution(mesh):
    row_spec = P("fsdp", "ctx", None)
    flat = P("fsdp", None)
    return jax.shard_map(
        on_device,
        mesh=mesh,
        in_specs=(
            row_spec,
            row_spec,
            P("fsdp"),
            P(),
            row_spec,
            P("fsdp"),
            flat,
            flat,
            P("fsdp"),
            flat,
            flat,
            flat,
            P("ctx", "fsdp", None),
            P("ctx", None, "fsdp"),
        ),
        out_specs=(
            row_spec,
            row_spec,
            P("fsdp"),
            flat,
            flat,
            P("fsdp"),
            flat,
            flat,
            flat,
            P("ctx", "fsdp", None),
            P("ctx", None, "fsdp"),
        ),
        check_vma=False,
    )
```

```python
import functools

import jax
import jax.numpy as jnp
from jax import lax
from jax.experimental import pallas as pl
from jax.experimental.pallas import tpu as pltpu
from jax.sharding import PartitionSpec as P

D = 768
HEADS = 12
HEAD_DIM = 64
FF = 2048
FS = 2048
LANES = 128
CHUNK = 256
PACKED = 3 * D + LANES
norm_eps = 1e-06
F32 = jnp.float32
BF16 = jnp.bfloat16


def dot(a, b):
    return jnp.dot(a, b, preferred_element_type=F32)


def dot_nt(a, b):
    return lax.dot_general(a, b, (((1,), (1,)), ((), ())), preferred_element_type=F32)


def dot_tn(a, b):
    return lax.dot_general(a, b, (((0,), (0,)), ((), ())), preferred_element_type=F32)


def call(kernel, outs, *, flops, nbytes, limit=56, **kw):
    return pl.pallas_call(
        kernel,
        out_shape=outs,
        compiler_params=pltpu.CompilerParams(vmem_limit_bytes=limit << 20),
        cost_estimate=pl.CostEstimate(
            flops=int(flops), bytes_accessed=int(nbytes), transcendentals=0
        ),
        **kw,
    )


def comm_call(kernel, outs, number, *, nbytes, limit=60, **kw):
    return pl.pallas_call(
        kernel,
        out_shape=outs,
        compiler_params=pltpu.CompilerParams(
            collective_id=number, has_side_effects=True, vmem_limit_bytes=limit << 20
        ),
        cost_estimate=pl.CostEstimate(flops=0, bytes_accessed=int(nbytes), transcendentals=0),
        **kw,
    )


def shape(dims, dtype):
    return jax.ShapeDtypeStruct(dims, dtype)


def lanes_of(rows, width=LANES):
    return lax.broadcasted_iota(jnp.int32, (rows, width), 1)


def first_heads(n_ctx, slot_dev):
    share = HEADS * slot_dev // n_ctx
    return [min(share * d // slot_dev, HEADS - 2) for d in range(n_ctx)]


def partner(t, lane):
    return jnp.where(lane % 64 < 32, pltpu.roll(t, 96, 1), pltpu.roll(t, 32, 1))


def in_parts(v):
    high = v.astype(BF16)
    rest = v - high.astype(F32)
    mid = rest.astype(BF16)
    low = (rest - mid.astype(F32)).astype(BF16)
    return high.astype(F32), mid.astype(F32), low.astype(F32)


def part_lanes(v, lane):
    high, mid, low = in_parts(v)
    zero = jnp.zeros((), F32)
    return jnp.where(
        lane == 0, high, jnp.where(lane == 1, mid, jnp.where(lane == 2, low, zero))
    ).astype(BF16)


def picks(target_ref, places):
    rows = target_ref.shape[0]
    place = lanes_of(rows, places)
    return tuple(
        jnp.where(place == target_ref[:, k : k + 1], 1.0, 0.0).astype(BF16) for k in range(2)
    )


def start_kernel(experts, capacity, routes_ref, cot_ref, live_ref, target_ref, dout_ref, send_ref):
    rows = routes_ref.shape[0]
    lane = lanes_of(rows)
    hot = [jnp.where(lane == routes_ref[:, k : k + 1], 1.0, 0.0) for k in range(2)]
    below = jnp.where(
        lanes_of(rows, rows) < lax.broadcasted_iota(jnp.int32, (rows, rows), 0), 1.0, 0.0
    )
    earlier = dot(below.astype(BF16), (hot[0] + hot[1]).astype(BF16))
    place = [
        routes_ref[:, k : k + 1] * capacity
        + jnp.sum(hot[k] * earlier, axis=-1, keepdims=True).astype(jnp.int32)
        for k in range(2)
    ]
    for k in range(2):
        target_ref[:, k : k + 1] = place[k]
    dout = (cot_ref[...].astype(F32) * live_ref[...]).astype(BF16)
    dout_ref[...] = dout
    spot = lanes_of(rows, send_ref.shape[0])
    pick = jnp.where((spot == place[0]) | (spot == place[1]), 1.0, 0.0).astype(BF16)
    send_ref[...] = dot_tn(pick, dout).astype(BF16)


def qkv_kernel(heads, experts, x_ref, w_ref, cos_ref, sin_ref, send_ref, in_ref, tail_ref):
    x = x_ref[...].astype(F32)
    tail = w_ref[:, 3 * D :].astype(F32).T
    tail_ref[...] = tail
    inv = lax.rsqrt(jnp.mean(x * x, axis=-1, keepdims=True) + norm_eps)
    attn_in = (x * inv * tail[experts : experts + 1, :]).astype(BF16)
    in_ref[...] = attn_in
    lane = lanes_of(x.shape[0])
    cos, sin = cos_ref[...], sin_ref[...]
    for part in range(3):
        y = dot(attn_in, w_ref[:, part * D : (part + 1) * D])
        groups = []
        for g in range(D // LANES):
            t = y[:, g * LANES : (g + 1) * LANES]
            if part < 2:
                t = t * cos + partner(t, lane) * sin
            groups.append(t)
        turned = [pltpu.roll(t, 64, 1) for t in groups]
        for d, head in enumerate(heads):
            g = head // 2
            if head % 2 == 0:
                packet = groups[g]
            else:
                packet = jnp.where(lane < 64, turned[g], turned[g + 1])
            send_ref[d, :, part * LANES : (part + 1) * LANES] = packet.astype(BF16)


def stack_rows(stack_ref, block, lane):
    rows = block.shape[0]
    zero = jnp.zeros((), block.dtype)
    stack_ref[0:rows, :] = jnp.where(lane < 64, block, zero)
    stack_ref[rows : 2 * rows, :] = jnp.where(lane >= 64, block, zero)


def unstack_rows(stack_ref, block, offset, lane):
    rows = stack_ref.shape[0] // 2
    stack_ref[...] = jnp.zeros_like(stack_ref)
    stack_ref[pl.ds(offset, block.shape[0]), :] = block
    return jnp.where(lane < 64, stack_ref[0:rows, :], stack_ref[rows : 2 * rows, :])


def key_limits(share, rows, q_block, offset, length):
    row = lax.broadcasted_iota(jnp.int32, (1, share), 1) + offset
    row = jnp.where(row >= rows, row - rows, row)
    return jnp.minimum(q_block * rows + row + 1, length)


def attend_kernel(n, share, sc, recv_ref, out_ref, keep_ref, lse_ref, stack, scores, back):
    q_block = pl.program_id(0)
    rows = recv_ref.shape[1]
    offset = pl.multiple_of(sc[n], 64)
    length = sc[n + 1]
    lane = lanes_of(rows)
    stack_rows(stack, recv_ref[sc[q_block], :, 0:LANES] * 0.125, lane)
    query = stack[pl.ds(offset, share), :]
    limit = key_limits(share, rows, q_block, offset, length)
    key_row = lax.broadcasted_iota(jnp.int32, (rows, share), 0)
    blocks = jnp.minimum(q_block + 1, (length + rows - 1) // rows)

    def score_step(j, top):
        keys = recv_ref[sc[j], :, LANES : 2 * LANES]
        s = dot_nt(keys, query)
        s = jnp.where(key_row < limit - j * rows, s, -1e30)
        scores[j] = s
        return jnp.maximum(top, jnp.max(s, axis=0, keepdims=True))

    top = lax.fori_loop(0, blocks, score_step, jnp.full((1, share), -1e30, F32))

    def value_step(j, carry):
        total, acc = carry
        weights = jnp.exp(scores[j] - top)
        total = total + jnp.sum(weights, axis=0, keepdims=True)
        values = recv_ref[sc[j], :, 2 * LANES : 3 * LANES]
        return total, acc + dot_tn(values, weights.astype(BF16))

    total, acc = lax.fori_loop(
        0, blocks, value_step, (jnp.zeros((1, share), F32), jnp.zeros((LANES, share), F32))
    )
    acc = acc / total
    keep_ref[0] = acc
    lse_ref[0] = top + jnp.log(total)
    out_ref[0] = unstack_rows(back, acc.T, offset, lane).astype(BF16)


def attend_back_kernel(
    n, share, sc, recv_ref, grad_ref, keep_ref, lse_ref, out_ref, stack, gstack, dkeys, dvalues, back
):
    q_block = pl.program_id(0)
    rows = recv_ref.shape[1]
    offset = pl.multiple_of(sc[n], 64)
    length = sc[n + 1]
    lane = lanes_of(rows)
    source = sc[q_block]

    @pl.when(q_block == 0)
    def _():
        dkeys[...] = jnp.zeros_like(dkeys)
        dvalues[...] = jnp.zeros_like(dvalues)

    stack_rows(stack, recv_ref[source, :, 0:LANES] * 0.125, lane)
    query = stack[pl.ds(offset, share), :]
    stack_rows(gstack, grad_ref[source], lane)
    grad = gstack[pl.ds(offset, share), :]
    lse = lse_ref[0]
    delta = jnp.sum(grad.astype(F32).T * keep_ref[0], axis=0, keepdims=True)
    limit = key_limits(share, rows, q_block, offset, length)
    key_row = lax.broadcasted_iota(jnp.int32, (rows, share), 0)
    blocks = jnp.minimum(q_block + 1, (length + rows - 1) // rows)

    def step(j, acc):
        keys = recv_ref[sc[j], :, LANES : 2 * LANES]
        values = recv_ref[sc[j], :, 2 * LANES : 3 * LANES]
        s = dot_nt(keys, query)
        weights = jnp.exp(jnp.where(key_row < limit - j * rows, s, -1e30) - lse)
        dweights = dot_nt(values, grad)
        dscores = (weights * (dweights - delta)).astype(BF16)
        dkeys[j] += dot(dscores, query)
        dvalues[j] += dot(weights.astype(BF16), grad)
        return acc + dot_tn(keys, dscores)

    acc = lax.fori_loop(0, blocks, step, jnp.zeros((LANES, share), F32))
    dquery = unstack_rows(back, acc.T * 0.125, offset, lane)
    out_ref[source, :, 0:LANES] = dquery.astype(BF16)

    @pl.when(q_block == n - 1)
    def _():
        def flush(j, carry):
            out_ref[sc[j], :, LANES : 2 * LANES] = dkeys[j].astype(BF16)
            out_ref[sc[j], :, 2 * LANES : 3 * LANES] = dvalues[j].astype(BF16)
            return carry

        lax.fori_loop(0, n, flush, 0)


def middle_kernel(
    heads,
    experts,
    came_ref,
    w_ref,
    x_ref,
    tail_ref,
    routes_ref,
    target_ref,
    residual_ref,
    in_ref,
    gates_ref,
    send_ref,
):
    total = x_ref[...].astype(F32)
    for d, head in enumerate(heads):
        total = total + dot(came_ref[d], w_ref[64 * head : 64 * head + LANES, :])
    residual_ref[...] = total
    inv = lax.rsqrt(jnp.mean(total * total, axis=-1, keepdims=True) + norm_eps)
    ffn_in = (total * inv * tail_ref[experts + 1 : experts + 2, :]).astype(BF16)
    in_ref[...] = ffn_in
    logits = dot_nt(ffn_in, tail_ref[...].astype(BF16))
    lane = lanes_of(logits.shape[0])
    chosen = [
        jnp.sum(jnp.where(lane == routes_ref[:, k : k + 1], logits, 0.0), axis=-1, keepdims=True)
        for k in range(2)
    ]
    top = jnp.maximum(chosen[0], chosen[1])
    raised = [jnp.exp(c - top) for c in chosen]
    gates = [r / (raised[0] + raised[1]) for r in raised]
    gates_ref[...] = jnp.where(lane == 0, gates[0], gates[1])
    pick = picks(target_ref, send_ref.shape[0])
    send_ref[:, 0:D] = dot_tn(pick[0] + pick[1], ffn_in).astype(BF16)
    send_ref[:, D:] = (
        dot_tn(pick[0], part_lanes(gates[0], lane)) + dot_tn(pick[1], part_lanes(gates[1], lane))
    ).astype(BF16)


def gated(g, u, da):
    sig = 1.0 / (1.0 + jnp.exp(-g))
    silu = g * sig
    return silu * u, da * u * sig * (1.0 + g * (1.0 - sig)), da * silu


def store_shards(sc, first_row, value, keep_ref, give_ref):
    half, shard, _ = keep_ref.shape
    piece = min(shard, value.shape[0])
    for u in range(value.shape[0] // piece):
        row = first_row + u * piece
        j = sc[row // shard]
        inside = pl.multiple_of(row % shard, piece)

        @pl.when(j < half)
        def _():
            keep_ref[j, pl.ds(inside, piece), :] = value[u * piece : (u + 1) * piece]

        @pl.when(j >= half)
        def _():
            give_ref[j - half, pl.ds(inside, piece), :] = value[u * piece : (u + 1) * piece]


def shared_kernel(
    sc, x_ref, dy_ref, wg_ref, wu_ref, wo_ref, res_ref, dx_ref, mid_ref, keep_ref, give_ref, res_acc, dx_acc
):
    c = pl.program_id(0)

    @pl.when(c == 0)
    def _():
        res_acc[...] = jnp.zeros_like(res_acc)
        dx_acc[...] = jnp.zeros_like(dx_acc)

    x, dy = x_ref[...], dy_ref[...]
    wg, wu, wo = wg_ref[...], wu_ref[...], wo_ref[...]
    act, dg, du = gated(dot(x, wg), dot(x, wu), dot_nt(dy, wo))
    act, dg, du = act.astype(BF16), dg.astype(BF16), du.astype(BF16)
    res_acc[...] += dot(act, wo)
    dx_acc[...] += dot_nt(dg, wg) + dot_nt(du, wu)
    mid_ref[0] = dg
    mid_ref[1] = du
    store_shards(sc, c * CHUNK, dot_tn(act, dy).astype(BF16), keep_ref, give_ref)

    @pl.when(c == pl.num_programs(0) - 1)
    def _():
        res_ref[...] = res_acc[...]
        dx_ref[...] = dx_acc[...]


def turn_shards(sc, x, raw, xt):
    raw[...] = x.T
    shard = raw.shape[0] // sc.shape[0]
    for j in range(sc.shape[0]):
        row = pl.multiple_of(sc[j] * shard, 16)
        xt[j * shard : (j + 1) * shard, :] = raw[pl.ds(row, shard), :]


def split_shards(value, keep_ref, give_ref):
    half, shard, _ = keep_ref.shape
    for j in range(half):
        keep_ref[j] = value[j * shard : (j + 1) * shard]
        give_ref[j] = value[(half + j) * shard : (half + j + 1) * shard]


def shared_grad_kernel(sc, x_ref, mid_ref, keep_ref, give_ref, raw, xt):
    @pl.when((pl.program_id(0) == 0) & (pl.program_id(1) == 0))
    def _():
        turn_shards(sc, x_ref[...], raw, xt)

    split_shards(dot(xt[...], mid_ref[0]).astype(BF16), keep_ref, give_ref)


def expert_kernel(
    x_ref, dy_ref, wg_ref, wu_ref, wt_ref, dx_ref, res_ref, mid_ref, dx_acc, res_acc, dgate
):
    c = pl.program_id(0)

    @pl.when(c == 0)
    def _():
        res_acc[...] = jnp.zeros_like(res_acc)
        dx_acc[...] = jnp.zeros_like(dx_acc)
        dgate[...] = jnp.zeros_like(dgate)

    x, dy = x_ref[:, 0:D], dy_ref[...]
    gate = jnp.sum(x_ref[:, D:].astype(F32), axis=-1, keepdims=True)
    wg, wu, wt = wg_ref[...], wu_ref[...], wt_ref[...]
    da = dot(dy, wt)
    act, dg, du = gated(dot(x, wg), dot(x, wu), da * gate)
    dgate[...] += jnp.sum(act * da, axis=-1, keepdims=True)
    mid_ref[2] = (act * gate).astype(BF16)
    act, dg, du = act.astype(BF16), dg.astype(BF16), du.astype(BF16)
    res_acc[...] += dot_nt(act, wt)
    dx_acc[...] += dot_nt(dg, wg) + dot_nt(du, wu)
    mid_ref[0] = dg
    mid_ref[1] = du

    @pl.when(c == pl.num_programs(0) - 1)
    def _():
        res_ref[...] = res_acc[...].astype(BF16)
        dx_ref[:, 0:D] = dx_acc[...].astype(BF16)
        dx_ref[:, D:] = part_lanes(dgate[:, 0:1], lanes_of(dgate.shape[0]))


def combine_kernel(
    heads,
    experts,
    came_ref,
    dx_ref,
    residual_ref,
    dout_ref,
    gates_ref,
    routes_ref,
    target_ref,
    tail_ref,
    w_ref,
    send_ref,
    dres_ref,
    branch_ref,
    dlogits_ref,
    dgain_ref,
):
    pick = picks(target_ref, came_ref.shape[0])
    gates = [gates_ref[:, k : k + 1] for k in range(2)]
    parts = came_ref[:, D:]
    dgate = [jnp.sum(dot(pick[k], parts), axis=-1, keepdims=True) for k in range(2)]
    mean = gates[0] * dgate[0] + gates[1] * dgate[1]
    lane = lanes_of(pick[0].shape[0])
    dlogits = sum(
        jnp.where(lane == routes_ref[:, k : k + 1], gates[k] * (dgate[k] - mean), 0.0)
        for k in range(2)
    ).astype(BF16)
    dlogits_ref[...] = dlogits
    tail = tail_ref[...]
    dffn = dot(pick[0] + pick[1], came_ref[:, 0:D]) + dx_ref[...] + dot(dlogits, tail.astype(BF16))
    residual = residual_ref[...]
    inv = lax.rsqrt(jnp.mean(residual * residual, axis=-1, keepdims=True) + norm_eps)
    scaled = dffn * tail[experts + 1 : experts + 2, :]
    total = jnp.mean(scaled * residual, axis=-1, keepdims=True)
    dres = dout_ref[...].astype(F32) + inv * scaled - residual * inv * inv * inv * total
    dres_ref[...] = dres
    dgain_ref[...] = jnp.sum(dffn * residual * inv, axis=0, keepdims=True)
    branch = dres.astype(BF16)
    branch_ref[...] = branch
    for d, head in enumerate(heads):
        send_ref[d] = dot_nt(branch, w_ref[64 * head : 64 * head + LANES, :]).astype(BF16)


def ring_split(rows, columns, pieces):
    down = 1
    while 2 * down <= pieces and rows % (32 * down) == 0:
        down *= 2
    across = pieces // down
    width = -(-columns // (LANES * across)) * LANES
    return down, across, rows // down, width


def ring_place(position, n):
    half = n // 2
    return jnp.where(position < half, 2 * position, 2 * (n - 1 - position) + 1)


def flipped(index, mask):
    for b in range(mask.bit_length()):
        if mask >> b & 1:
            index = index + (1 << b) - 2 * (1 << b) * (index // (1 << b) % 2)
    return index


def mirrored(members):
    bits = members.bit_length() - 1
    return [int(format(j, "b").zfill(bits)[::-1], 2) for j in range(members)]


def shard_rows(members, shard):
    fsdp = lax.axis_index("fsdp")
    return [pl.multiple_of(flipped(fsdp, m) * shard, 16) for m in mirrored(members)]


def remote(source, target, send_sem, recv_sem, peer):
    return pltpu.make_async_remote_copy(
        src_ref=source,
        dst_ref=target,
        send_sem=send_sem,
        recv_sem=recv_sem,
        device_id=peer,
        device_id_type=pl.DeviceIdType.MESH,
    )


def greet(peers):
    barrier = pltpu.get_barrier_semaphore()
    for peer in peers:
        pl.semaphore_signal(barrier, inc=1, device_id=peer, device_id_type=pl.DeviceIdType.MESH)
    pl.semaphore_wait(barrier, len(peers))


def mates_of(members):
    ctx, fsdp = lax.axis_index("ctx"), lax.axis_index("fsdp")
    return [(ctx, flipped(fsdp, 1 << b)) for b in range(members.bit_length() - 1)]


def row_peers(n):
    ctx, fsdp = lax.axis_index("ctx"), lax.axis_index("fsdp")
    return [(lax.rem(ctx + d, n), fsdp) for d in range(1, n)]


def loop(body, low, high):
    lax.fori_loop(low, high, lambda s, carry: (body(s), carry)[1], 0)


def add_into(target, j, other):
    target[j] = (target[j].astype(F32) + other[j].astype(F32)).astype(BF16)


def back_exchange_kernel(
    n,
    members,
    heads,
    send_ref,
    x_ref,
    dy_ref,
    came_ref,
    branch_ref,
    in_ref,
    dlogits_ref,
    mid_ref,
    recv_ref,
    sum_ref,
    out_grad_ref,
    router_ref,
    give,
    caught,
    crossed,
    raw,
    xt,
    dyt,
    acc,
    mids,
    send_sem,
    recv_sem,
    own_sem,
    give_sem,
    caught_sem,
    cross_sem,
    mid_sem,
):
    ctx = lax.axis_index("ctx")
    peers = row_peers(n)
    mates = mates_of(members)
    mate, far = mates[0], mates[1]
    greet(peers + [mate, far])
    own = pltpu.make_async_copy(send_ref.at[ctx], recv_ref.at[ctx], own_sem)
    own.start()
    copies = [
        remote(send_ref.at[p[0]], recv_ref.at[ctx], send_sem.at[d], recv_sem.at[d], p)
        for d, p in enumerate(peers)
    ]
    for c in copies:
        c.start()

    steps = mid_ref.shape[2] // CHUNK
    parts = mid_ref.shape[0]

    def fetch(i, c, slot):
        column = pl.multiple_of(c * CHUNK, CHUNK)
        return pltpu.make_async_copy(
            mid_ref.at[i, :, pl.ds(column, CHUNK)], mids.at[slot], mid_sem.at[slot]
        )

    fetch(0, 0, 0).start()
    shard = D // members
    half = members // 2
    rows = shard_rows(members, shard)

    def turned(value, target):
        raw[...] = value.T
        for j in range(members):
            target[j * shard : (j + 1) * shard, :] = raw[pl.ds(rows[j], shard), :]

    turned(x_ref[:, 0:D], xt)
    turned(dy_ref[...], dyt)

    def swap(i):
        return remote(give.at[i], caught.at[i], give_sem.at[i], caught_sem.at[i], mate)

    quarter = members // 4
    cross = remote(
        sum_ref.at[0, pl.ds(quarter, quarter)], crossed, cross_sem.at[0], cross_sem.at[1], far
    )
    for i in range(parts):
        left = xt if i < 2 else dyt

        def step(c, left=left, i=i):
            slot = lax.rem(c, 2)
            fetch(i, c, slot).wait()

            @pl.when(c + 1 < steps)
            def _():
                fetch(i, c + 1, 1 - slot).start()

            value = dot(left[...], mids[slot]).astype(BF16)
            column = pl.ds(pl.multiple_of(c * CHUNK, CHUNK), CHUNK)
            for j in range(half):
                sum_ref[i, j, :, column] = value[j * shard : (j + 1) * shard]
                give[i, j, :, column] = value[(half + j) * shard : (half + j + 1) * shard]

        loop(step, 0, steps)
        if i + 1 < parts:
            fetch(i + 1, 0, 0).start()
        swap(i).start()
        if i > 0:
            swap(i - 1).wait_recv()
            for j in range(half):
                add_into(sum_ref.at[i - 1], j, caught.at[i - 1])
        if i == 1:
            cross.start()

    acc[...] = jnp.zeros_like(acc)
    branch = branch_ref[...]
    for d, head in enumerate(heads):
        acc[64 * head : 64 * head + LANES, :] += dot_tn(came_ref[d], branch)
    for j in range(members):
        out_grad_ref[j] = acc[pl.ds(rows[j], shard), :].astype(BF16)
    router_ref[...] = dot_tn(in_ref[...], dlogits_ref[...])
    swap(parts - 1).wait_recv()
    for j in range(half):
        add_into(sum_ref.at[parts - 1], j, caught.at[parts - 1])
    for c in copies:
        c.wait()
    own.wait()
    cross.wait()
    for j in range(quarter):
        add_into(sum_ref.at[0], j, crossed)
    for i in range(parts):
        swap(i).wait_send()


def last_kernel(
    n,
    members,
    heads,
    experts,
    splits,
    recv_ref,
    cos_ref,
    sin_ref,
    in_ref,
    x_ref,
    w_ref,
    tail_ref,
    dres_ref,
    out_grad_ref,
    router_ref,
    dgain_ref,
    a_ref,
    a_other,
    b_ref,
    b_other,
    e_ref,
    x_out,
    a_out,
    b_out,
    c_out,
    e_out,
    *scratch,
):
    bits = members.bit_length() - 1
    streams = len(splits)
    own, back, full = (scratch[k * streams : (k + 1) * streams] for k in range(3))
    scratch = scratch[3 * streams :]
    caught, e_caught = scratch[0:bits], scratch[bits : 2 * bits - 1]
    dproj, raw, turned, small, pack = scratch[2 * bits - 1 : 2 * bits + 4]
    send_sem, recv_sem, level_send, level_recv, e_send, e_recv = scratch[2 * bits + 4 :]
    ctx, fsdp = lax.axis_index("ctx"), lax.axis_index("fsdp")
    here = jnp.where(ctx % 2 == 0, ctx // 2, n - 1 - ctx // 2)
    ahead = (ring_place(lax.rem(here + 1, n), n), fsdp)
    behind = (ring_place(lax.rem(here + n - 1, n), n), fsdp)
    mates = mates_of(members)
    greet([ahead, behind] + mates)
    shard = D // members
    parts = e_ref.shape[0]

    def level_copy(b):
        count = members >> (b + 1)
        return remote(
            pack.at[pl.ds(count, count)], caught[b], level_send.at[b], level_recv.at[b], mates[b]
        )

    def level_add(b):
        level_copy(b).wait_recv()
        for j in range(members >> (b + 1)):
            add_into(pack, j, caught[b])

    def e_copy(i, b):
        count = members >> (b + 1)
        source = e_ref if b == 1 or (b == 2 and i == 0) else e_caught[b - 2]
        return remote(
            source.at[i, pl.ds(count, count)],
            e_caught[b - 1].at[i],
            e_send.at[i, b - 1],
            e_recv.at[i, b - 1],
            mates[b],
        )

    def e_add(i, b):
        e_copy(i, b).wait_recv()
        source = e_ref if b == 1 or (b == 2 and i == 0) else e_caught[b - 2]
        for j in range(members >> (b + 1)):
            total = source[i, j].astype(F32) + e_caught[b - 1][i, j].astype(F32)
            if b == bits - 1:
                e_out[i] = total.astype(BF16)
            else:
                e_caught[b - 1][i, j] = total.astype(BF16)

    def tiles(i):
        down, across, height, width = splits[i][0:4]
        columns = splits[i][4]
        for p in range(down * across):
            r, c = p // across, p % across
            yield p, r * height, height, c * width, max(0, min(width, columns - c * width)), width

    def load(i, ref, skip=0, other=None):
        for p, top, height, start, have, width in tiles(i):
            if have > 0:
                value = ref[top : top + height, skip + start : skip + start + have]
                if other is not None:
                    added = other[top : top + height, skip + start : skip + start + have]
                    value = (value.astype(F32) + added.astype(F32)).astype(BF16)
                own[i][p, :, 0:have] = value
            if have < width:
                own[i][p, :, have:] = jnp.zeros((height, width - have), BF16)

    def save(i, ref, skip=0):
        for p, top, height, start, have, width in tiles(i):
            if have > 0:
                ref[top : top + height, skip + start : skip + start + have] = full[i][p, :, 0:have]

    def chunk(direction, steps):
        if direction == 0:
            return lax.rem(here + 4 * n - steps, n)
        return n + lax.rem(here + steps, n)

    def copy(i, direction, step, source, target, slot):
        return remote(
            source[i].at[slot],
            target[i].at[slot],
            send_sem.at[i, direction, step],
            recv_sem.at[i, direction, step],
            ahead if direction == 0 else behind,
        )

    def first(i):
        for direction in range(2):
            copy(i, direction, 0, own, back, chunk(direction, 1)).start()

    def reduce_step(i, s):
        for direction in range(2):
            slot = chunk(direction, 1 + s)
            copy(i, direction, s - 1, own, back, slot).wait_recv()
            add_into(back[i], slot, own[i])
            copy(i, direction, s, back, back, slot).start()

    def turn(i):
        for direction in range(2):
            slot = chunk(direction, n)
            copy(i, direction, n - 2, own, back, slot).wait_recv()
            full[i][slot] = (back[i][slot].astype(F32) + own[i][slot].astype(F32)).astype(BF16)
            copy(i, direction, n - 1, full, full, slot).start()

    def gather_step(i, s):
        for direction in range(2):
            slot = chunk(direction, s)
            copy(i, direction, n - 2 + s, full, full, slot).wait_recv()
            copy(i, direction, n - 1 + s, full, full, slot).start()

    def end(i):
        for direction in range(2):
            copy(i, direction, 2 * n - 3, full, full, chunk(direction, n - 1)).wait_recv()

    dense, late = [0, 1], list(range(2, streams))
    e_copy(1, 1).start()
    load(0, a_ref, other=a_other)
    first(0)
    load(1, b_ref, other=b_other)
    first(1)

    lane = lanes_of(x_ref.shape[0])
    cos, sin = cos_ref[...], sin_ref[...]
    for part in range(3):
        groups = [jnp.zeros(lane.shape, F32) for _ in range(D // LANES)]
        for d, head in enumerate(heads):
            g = head // 2
            packet = recv_ref[d, :, part * LANES : (part + 1) * LANES].astype(F32)
            if head % 2 == 0:
                groups[g] = groups[g] + packet
            else:
                packet = pltpu.roll(packet, 64, 1)
                groups[g] = groups[g] + jnp.where(lane >= 64, packet, 0.0)
                groups[g + 1] = groups[g + 1] + jnp.where(lane < 64, packet, 0.0)
        for g, t in enumerate(groups):
            if part < 2:
                t = t.astype(BF16).astype(F32)
                t = t * cos - partner(t, lane) * sin
            dproj[:, part * D + g * LANES : part * D + (g + 1) * LANES] = t.astype(BF16)
    rows = shard_rows(members, shard)
    raw[...] = in_ref[...].T
    for j in range(members):
        turned[j * shard : (j + 1) * shard, :] = raw[pl.ds(rows[j], shard), :]
    for part in range(3):
        value = dot(turned[...], dproj[:, part * D : (part + 1) * D]).astype(BF16)
        for j in range(members):
            pack[j, :, part * D : (part + 1) * D] = value[j * shard : (j + 1) * shard]
    dnorm = dot_nt(dproj[...], w_ref[:, 0 : 3 * D])
    x = x_ref[...].astype(F32)
    gain = tail_ref[experts : experts + 1, :]
    inv = lax.rsqrt(jnp.mean(x * x, axis=-1, keepdims=True) + norm_eps)
    dgain_one = jnp.sum(dnorm * x * inv, axis=0, keepdims=True)
    row = lax.broadcasted_iota(jnp.int32, (LANES, D), 0)
    gains = jnp.where(row == experts, dgain_one, jnp.where(row == experts + 1, dgain_ref[...], 0.0))
    small[...] = router_ref[...] + gains.T
    for j in range(members):
        pack[j, :, 3 * D : PACKED] = small[pl.ds(rows[j], shard), :].astype(BF16)
        pack[j, :, PACKED:] = out_grad_ref[j]
    level_copy(0).start()
    scaled = dnorm * gain
    total = jnp.mean(scaled * x, axis=-1, keepdims=True)
    x_out[...] = dres_ref[...] + inv * scaled - x * inv * inv * inv * total

    def early(s):
        for i in dense:
            reduce_step(i, s)

    def dense_gather(s):
        for i in dense:
            gather_step(i, s)

    loop(early, 1, 3)
    level_add(0)
    level_copy(1).start()
    loop(early, 3, n - 1)
    for i in dense:
        turn(i)
    loop(dense_gather, 1, n // 2 + 1)
    for b in range(1, bits):
        level_add(b)
        if b + 1 < bits:
            level_copy(b + 1).start()
    for i in range(2, parts):
        e_copy(i, 1).start()
    skip = 0
    for i in late:
        load(i, pack.at[0], skip)
        skip += splits[i][4]
        first(i)
    rest = n - 2 - n // 2

    def joint(s):
        for i in late:
            reduce_step(i, s)
        for i in dense:
            gather_step(i, s + n // 2)

    def late_reduce(s):
        for i in late:
            reduce_step(i, s)

    loop(joint, 1, rest + 1)
    for i in dense:
        end(i)
    loop(late_reduce, rest + 1, n - 1)
    for i in late:
        turn(i)
    save(0, a_out)
    save(1, b_out)
    e_add(1, 1)

    def finish(s):
        for i in late:
            gather_step(i, s)

    loop(finish, 1, n - 1)
    for i in late:
        end(i)
    skip = 0
    for i in late:
        save(i, c_out, skip)
        skip += splits[i][4]
    for i in range(2, parts):
        e_add(i, 1)
    if bits == 2:
        e_out[0] = e_ref[0, 0]
    for b in range(2, bits):
        for i in range(parts):
            e_copy(i, b).start()
        for i in range(parts):
            e_add(i, b)
    for b in range(bits):
        level_copy(b).wait_send()
    for b in range(1, bits):
        for i in range(1 if b == 1 else 0, parts):
            e_copy(i, b).wait_send()

    def drain(s):
        for i in range(streams):
            for direction in range(2):
                copy(i, direction, s, own, back, 0).wait_send()

    loop(drain, 0, 2 * n - 2)


def widen_kernel(late_ref, a_ref, b_ref, e_ref, qkv_out, w_out, a_out, b_out, in_out, back_out):
    qkv_out[...] = late_ref[:, 0 : 3 * D].astype(F32)
    w_out[...] = late_ref[:, PACKED:].astype(F32)
    a_out[...] = a_ref[...].astype(F32)
    b_out[...] = b_ref[...].astype(F32)
    in_out[:, 0:FF] = e_ref[0].astype(F32)
    in_out[:, FF:] = e_ref[1].astype(F32)
    back_out[...] = e_ref[2].astype(F32).T


def output_kernel(residual_ref, shared_ref, gates_ref, target_ref, live_ref, came_ref, out_ref):
    pick = picks(target_ref, came_ref.shape[0])
    came = came_ref[...]
    mixture = gates_ref[:, 0:1] * dot(pick[0], came) + gates_ref[:, 1:2] * dot(pick[1], came)
    out_ref[...] = (live_ref[...] * (residual_ref[...] + shared_ref[...] + mixture)).astype(BF16)


def on_device(
    tokens,
    cotangent,
    lengths,
    position_block,
    routes,
    gain_attn,
    w_qkv,
    w_out,
    gain_ffn,
    w_router,
    w_shared_in,
    w_shared_out,
    w_expert_in,
    w_expert_out,
):
    n_ctx = lax.axis_size("ctx")
    ctx_index = lax.axis_index("ctx")
    rows = tokens.shape[1]
    local = w_qkv.shape[0]
    experts = w_router.shape[1]
    capacity = 3 * rows // experts
    places = experts * capacity
    members = D // local
    share = HEADS * rows // n_ctx
    heads = first_heads(n_ctx, rows)
    gather = functools.partial(lax.all_gather, axis_name="fsdp", axis=0, tiled=True)
    exchange = functools.partial(
        lax.all_to_all, axis_name="ctx", split_axis=0, concat_axis=0, tiled=True
    )
    x = tokens[0]
    length = lengths[0]

    first_pack = jnp.concatenate(
        [
            w_qkv,
            w_router,
            gain_attn[:, None],
            gain_ffn[:, None],
            jnp.zeros((local, LANES - experts - 2), BF16),
        ],
        axis=1,
    )
    qkv_pack = gather(first_pack)
    out_weight = gather(w_out)
    weights = gather(
        jnp.concatenate([w_shared_in, w_expert_in[0], w_expert_out[0].T], axis=1)
    )
    shared_out = gather(w_shared_out)
    fsdp_index = lax.axis_index("fsdp")
    bits = members.bit_length() - 1
    shard_at = fsdp_index ^ jnp.array(mirrored(members), jnp.int32)
    spots = fsdp_index ^ jnp.arange(members, dtype=jnp.int32)
    spot_of = sum(((spots >> b) & 1) << (bits - 1 - b) for b in range(bits))

    query_pos = position_block[ctx_index] * rows + jnp.arange(rows, dtype=jnp.int32)
    live = (query_pos < length).astype(F32)[:, None]
    halves = HEAD_DIM // 2
    inverse = 10000.0 ** (-(jnp.arange(halves, dtype=F32) * 2.0 / HEAD_DIM))
    angles = query_pos.astype(F32)[:, None] * inverse[None, :]
    cos, sin = jnp.cos(angles), jnp.sin(angles)
    cos = jnp.concatenate([cos, cos, cos, cos], axis=1)
    sin = jnp.concatenate([-sin, sin, -sin, sin], axis=1)

    order = jnp.sum(
        jnp.where(
            position_block[None, :] == jnp.arange(n_ctx, dtype=jnp.int32)[:, None],
            jnp.arange(n_ctx, dtype=jnp.int32)[None, :],
            0,
        ),
        axis=1,
    )
    head_of = jnp.minimum(share * ctx_index // rows, HEADS - 2)
    offset = share * ctx_index - rows * head_of
    scalars = jnp.concatenate(
        [order, jnp.stack([offset.astype(jnp.int32), length.astype(jnp.int32)])]
    )

    target, dout, dy_send = call(
        functools.partial(start_kernel, experts, capacity),
        (shape((rows, 2), jnp.int32), shape((rows, D), BF16), shape((places, D), BF16)),
        flops=2 * rows * D * places,
        nbytes=3 << 20,
    )(routes[0], cotangent[0], live)
    dy_rows = exchange(dy_send.reshape(n_ctx, -1, D)).reshape(places, D)

    send, attn_in, tail = call(
        functools.partial(qkv_kernel, heads, experts),
        (
            shape((n_ctx, rows, 3 * LANES), BF16),
            shape((rows, D), BF16),
            shape((LANES, D), F32),
        ),
        flops=2 * rows * D * 3 * D,
        nbytes=6 << 20,
    )(x, qkv_pack, cos, sin)
    send, dy_rows = lax.optimization_barrier((send, dy_rows))
    recv = exchange(send)

    packet = pl.BlockSpec((n_ctx, rows, 3 * LANES), lambda i, sc: (0, 0, 0))
    block_of = lambda i, sc: (i, 0, 0)
    attended, kept, lse = call(
        functools.partial(attend_kernel, n_ctx, share),
        (
            shape((n_ctx, rows, LANES), BF16),
            shape((n_ctx, LANES, share), F32),
            shape((n_ctx, 1, share), F32),
        ),
        flops=2 * share * rows * n_ctx * n_ctx * LANES * 2,
        nbytes=5 << 20,
        grid_spec=pltpu.PrefetchScalarGridSpec(
            num_scalar_prefetch=1,
            grid=(n_ctx,),
            in_specs=[packet],
            out_specs=[
                pl.BlockSpec((1, rows, LANES), lambda i, sc: (sc[i], 0, 0)),
                pl.BlockSpec((1, LANES, share), block_of),
                pl.BlockSpec((1, 1, share), block_of),
            ],
            scratch_shapes=[
                pltpu.VMEM((2 * rows, LANES), BF16),
                pltpu.VMEM((n_ctx, rows, share), F32),
                pltpu.VMEM((2 * rows, LANES), F32),
            ],
        ),
    )(scalars, recv)
    came = exchange(attended)

    whole = pl.BlockSpec(memory_space=pltpu.VMEM)
    out_block = pl.BlockSpec((D, D), lambda *at: (0, 0))

    def full(*dims):
        return pl.BlockSpec(dims, lambda *at: (0,) * len(dims))

    residual, ffn_in, gates, outgoing = call(
        functools.partial(middle_kernel, heads, experts),
        (
            shape((rows, D), F32),
            shape((rows, D), BF16),
            shape((rows, LANES), F32),
            shape((places, D + LANES), BF16),
        ),
        flops=2 * rows * D * (D + 1024 + 2 * places),
        nbytes=5 << 20,
        grid=(1,),
        in_specs=[
            full(n_ctx, rows, LANES),
            out_block,
            full(rows, D),
            full(LANES, D),
            full(rows, 2),
            full(rows, 2),
        ],
        out_specs=[
            full(rows, D),
            full(rows, D),
            full(rows, LANES),
            full(places, D + LANES),
        ],
    )(came, out_weight, x, tail, routes[0], target)
    x_rows = exchange(outgoing.reshape(n_ctx, -1, D + LANES)).reshape(places, D + LANES)

    steps = FS // CHUNK
    half = members // 2

    def split(rows_each, columns):
        return (shape((half, rows_each, columns), BF16),) * 2

    shared_res, shared_dx, shared_mid, so_keep, so_give = call(
        shared_kernel,
        (
            shape((rows, D), F32),
            shape((rows, D), F32),
            shape((2, rows, FS), BF16),
        )
        + split(FS // members, D),
        flops=2 * rows * D * FS * 7,
        nbytes=14 << 20,
        grid_spec=pltpu.PrefetchScalarGridSpec(
            num_scalar_prefetch=1,
            grid=(steps,),
            in_specs=[
                full(rows, D),
                full(rows, D),
                pl.BlockSpec((D, CHUNK), lambda c, sc: (0, c)),
                pl.BlockSpec((D, CHUNK), lambda c, sc: (0, steps + c)),
                pl.BlockSpec((CHUNK, D), lambda c, sc: (c, 0)),
            ],
            out_specs=[
                full(rows, D),
                full(rows, D),
                pl.BlockSpec((2, rows, CHUNK), lambda c, sc: (0, 0, c)),
                full(half, FS // members, D),
                full(half, FS // members, D),
            ],
            scratch_shapes=[pltpu.VMEM((rows, D), F32), pltpu.VMEM((rows, D), F32)],
        ),
    )(spot_of, ffn_in, dout, weights, weights, shared_out)
    column = pl.BlockSpec((half, local, CHUNK), lambda i, c, sc: (0, 0, i * steps + c))
    dense_keep, dense_give = call(
        shared_grad_kernel,
        split(local, 2 * FS),
        flops=2 * rows * D * FS * 2,
        nbytes=9 << 20,
        grid_spec=pltpu.PrefetchScalarGridSpec(
            num_scalar_prefetch=1,
            grid=(2, steps),
            in_specs=[
                full(rows, D),
                pl.BlockSpec((1, rows, CHUNK), lambda i, c, sc: (i, 0, c)),
            ],
            out_specs=[column, column],
            scratch_shapes=[pltpu.VMEM((D, rows), BF16), pltpu.VMEM((D, rows), BF16)],
        ),
    )(shard_at, ffn_in, shared_mid)

    wide = FF // CHUNK
    expert_dx, expert_res, expert_mid = call(
        expert_kernel,
        (
            shape((places, D + LANES), BF16),
            shape((places, D), BF16),
            shape((3, places, FF), BF16),
        ),
        flops=2 * places * D * FF * 6,
        nbytes=24 << 20,
        grid=(wide,),
        in_specs=[
            full(places, D + LANES),
            full(places, D),
            pl.BlockSpec((D, CHUNK), lambda c: (0, 2 * steps + c)),
            pl.BlockSpec((D, CHUNK), lambda c: (0, 2 * steps + wide + c)),
            pl.BlockSpec((D, CHUNK), lambda c: (0, 2 * steps + 2 * wide + c)),
        ],
        out_specs=[
            full(places, D + LANES),
            full(places, D),
            pl.BlockSpec((3, places, CHUNK), lambda c: (0, 0, c)),
        ],
        scratch_shapes=[
            pltpu.VMEM((places, D), F32),
            pltpu.VMEM((places, D), F32),
            pltpu.VMEM((places, LANES), F32),
        ],
    )(x_rows, dy_rows, weights, weights, weights)
    dx_came = exchange(expert_dx.reshape(n_ctx, -1, D + LANES)).reshape(places, D + LANES)
    shared_dx, dense_keep, dense_give, so_keep, so_give = lax.optimization_barrier(
        (shared_dx, dense_keep, dense_give, so_keep, so_give)
    )
    branch_send, dres, branch, dlogits, dgain_two = call(
        functools.partial(combine_kernel, heads, experts),
        (
            shape((n_ctx, rows, LANES), BF16),
            shape((rows, D), F32),
            shape((rows, D), BF16),
            shape((rows, LANES), BF16),
            shape((1, D), F32),
        ),
        flops=2 * rows * D * (places + 1024),
        nbytes=6 << 20,
        grid=(1,),
        in_specs=[
            full(places, D + LANES),
            full(rows, D),
            full(rows, D),
            full(rows, D),
            full(rows, LANES),
            full(rows, 2),
            full(rows, 2),
            full(LANES, D),
            out_block,
        ],
        out_specs=[
            full(n_ctx, rows, LANES),
            full(rows, D),
            full(rows, D),
            full(rows, LANES),
            full(1, D),
        ],
    )(dx_came, shared_dx, residual, dout, gates, routes[0], target, tail, out_weight)
    branch_recv = exchange(branch_send)

    def halve(terms, give, b):
        count = members >> (b + 1)
        if give is None:
            give = sum(t[count:].astype(F32) for t in terms).astype(BF16)
            terms = [t[:count] for t in terms]
        came_in = lax.ppermute(give, "fsdp", [(i, i ^ (1 << b)) for i in range(members)])
        return terms + [came_in]

    def upper(terms, b):
        count = members >> (b + 1)
        give = sum(t[count:].astype(F32) for t in terms).astype(BF16)
        return [t[:count] for t in terms], give

    def gathered(terms):
        return sum(t.astype(F32) for t in terms).astype(BF16)

    def rest_of(terms, give):
        keep = gathered(terms)
        for b in range(1, bits):
            came_in = halve([], give, b)[0]
            if b + 1 < bits:
                keep, give = (
                    gathered(t) for t in zip(*[(u[: u.shape[0] // 2], u[u.shape[0] // 2 :]) for u in (keep, came_in)])
                )
        return keep[0], came_in[0]

    dense_terms, dense_give = upper(halve([dense_keep], dense_give, 0), 1)
    so_terms, so_give = upper(halve([so_keep], so_give, 0), 1)
    branch_recv, expert_res = lax.optimization_barrier((branch_recv, expert_res))
    recv, dense_give, so_give = lax.optimization_barrier((recv, dense_give, so_give))
    dense_part, dense_other = rest_of(dense_terms, dense_give)
    so_part, so_other = rest_of(so_terms, so_give)

    dsend = call(
        functools.partial(attend_back_kernel, n_ctx, share),
        shape((n_ctx, rows, 3 * LANES), BF16),
        flops=2 * share * rows * n_ctx * n_ctx * LANES * 3,
        nbytes=8 << 20,
        grid_spec=pltpu.PrefetchScalarGridSpec(
            num_scalar_prefetch=1,
            grid=(n_ctx,),
            in_specs=[
                packet,
                pl.BlockSpec((n_ctx, rows, LANES), lambda i, sc: (0, 0, 0)),
                pl.BlockSpec((1, LANES, share), block_of),
                pl.BlockSpec((1, 1, share), block_of),
            ],
            out_specs=packet,
            scratch_shapes=[
                pltpu.VMEM((2 * rows, LANES), BF16),
                pltpu.VMEM((2 * rows, LANES), BF16),
                pltpu.VMEM((n_ctx, rows, LANES), F32),
                pltpu.VMEM((n_ctx, rows, LANES), F32),
                pltpu.VMEM((2 * rows, LANES), F32),
            ],
        ),
    )(scalars, recv, branch_recv, kept, lse)
    drecv, expert_sum, out_grad, grad_router = comm_call(
        functools.partial(back_exchange_kernel, n_ctx, members, heads),
        (
            shape((n_ctx, rows, 3 * LANES), BF16),
            shape((3, half, local, FF), BF16),
            shape((members, local, D), BF16),
            shape((D, LANES), F32),
        ),
        1,
        in_specs=[whole] * 7 + [pl.BlockSpec(memory_space=pl.ANY)],
        out_specs=[whole] * 4,
        scratch_shapes=[
            pltpu.VMEM((3, half, local, FF), BF16),
            pltpu.VMEM((3, half, local, FF), BF16),
            pltpu.VMEM((members // 4, local, FF), BF16),
            pltpu.VMEM((D, places), BF16),
            pltpu.VMEM((D, places), BF16),
            pltpu.VMEM((D, places), BF16),
            pltpu.VMEM((D, D), F32),
            pltpu.VMEM((2, places, CHUNK), BF16),
            pltpu.SemaphoreType.DMA((n_ctx - 1,)),
            pltpu.SemaphoreType.DMA((n_ctx - 1,)),
            pltpu.SemaphoreType.DMA,
            pltpu.SemaphoreType.DMA((3,)),
            pltpu.SemaphoreType.DMA((3,)),
            pltpu.SemaphoreType.DMA((2,)),
            pltpu.SemaphoreType.DMA((2,)),
        ],
        nbytes=120 << 20,
    )(dsend, x_rows, dy_rows, came, branch, ffn_in, dlogits, expert_mid)

    late_width = PACKED + D
    first_width = late_width // 2 // LANES * LANES
    sizes = [(local, 2 * FS), (FS // members, D)]
    sizes += [(local, first_width), (local, late_width - first_width)]
    splits = [ring_split(r, c, 2 * n_ctx) + (c,) for r, c in sizes]
    tiles = [(2 * n_ctx, t[2], t[3]) for t in splits]
    grad_x, dense_sum, so_sum, last_sum, expert_sum = comm_call(
        functools.partial(last_kernel, n_ctx, members, heads, experts, splits),
        (
            shape((rows, D), F32),
            shape((local, 2 * FS), BF16),
            shape((FS // members, D), BF16),
            shape((local, late_width), BF16),
            shape((3, local, FF), BF16),
        ),
        0,
        in_specs=[whole] * 16,
        out_specs=[whole] * 5,
        scratch_shapes=[pltpu.VMEM(t, BF16) for t in tiles * 3]
        + [pltpu.VMEM((members >> (b + 1), local, late_width), BF16) for b in range(bits)]
        + [pltpu.VMEM((3, members >> (b + 1), local, FF), BF16) for b in range(1, bits)]
        + [
            pltpu.VMEM((rows, 3 * D), BF16),
            pltpu.VMEM((D, rows), BF16),
            pltpu.VMEM((D, rows), BF16),
            pltpu.VMEM((D, LANES), F32),
            pltpu.VMEM((members, local, late_width), BF16),
            pltpu.SemaphoreType.DMA((4, 2, 2 * n_ctx - 2)),
            pltpu.SemaphoreType.DMA((4, 2, 2 * n_ctx - 2)),
            pltpu.SemaphoreType.DMA((bits,)),
            pltpu.SemaphoreType.DMA((bits,)),
            pltpu.SemaphoreType.DMA((3, max(1, bits - 1))),
            pltpu.SemaphoreType.DMA((3, max(1, bits - 1))),
        ],
        nbytes=200 << 20,
    )(
        drecv,
        cos,
        sin,
        attn_in,
        x,
        qkv_pack,
        tail,
        dres,
        out_grad,
        grad_router,
        dgain_two,
        dense_part,
        dense_other,
        so_part,
        so_other,
        expert_sum,
    )

    res_came = exchange(expert_res.reshape(n_ctx, -1, D)).reshape(places, D)
    output = call(
        output_kernel,
        shape((rows, D), BF16),
        flops=2 * rows * D * places * 2,
        nbytes=5 << 20,
    )(residual, shared_res, gates, target, live, res_came)

    small = last_sum[:, 3 * D : PACKED].astype(F32)
    grad_qkv, grad_out, grad_si, grad_so, grad_ei, grad_eo = call(
        widen_kernel,
        (
            shape((local, 3 * D), F32),
            shape((local, D), F32),
            shape((local, 2 * FS), F32),
            shape((FS // members, D), F32),
            shape((local, 2 * FF), F32),
            shape((FF, local), F32),
        ),
        flops=0,
        nbytes=21 << 20,
    )(last_sum, dense_sum, so_sum, expert_sum)
    return (
        output[None],
        grad_x[None],
        small[:, experts],
        grad_qkv,
        grad_out,
        small[:, experts + 1],
        small[:, 0:experts],
        grad_si,
        grad_so,
        grad_ei[None],
        grad_eo[None],
    )


def solution(mesh):
    row_spec = P("fsdp", "ctx", None)
    flat = P("fsdp", None)
    return jax.shard_map(
        on_device,
        mesh=mesh,
        in_specs=(
            row_spec,
            row_spec,
            P("fsdp"),
            P(),
            row_spec,
            P("fsdp"),
            flat,
            flat,
            P("fsdp"),
            flat,
            flat,
            flat,
            P("ctx", "fsdp", None),
            P("ctx", None, "fsdp"),
        ),
        out_specs=(
            row_spec,
            row_spec,
            P("fsdp"),
            flat,
            flat,
            P("fsdp"),
            flat,
            flat,
            flat,
            P("ctx", "fsdp", None),
            P("ctx", None, "fsdp"),
        ),
        check_vma=False,
    )
```

```python
import functools

import jax
import jax.numpy as jnp
from jax import lax
from jax.experimental import pallas as pl
from jax.experimental.pallas import tpu as pltpu
from jax.sharding import PartitionSpec as P

D = 768
HEADS = 12
HEAD_DIM = 64
FF = 2048
FS = 2048
LANES = 128
CHUNK = 256
PACKED = 3 * D + LANES
norm_eps = 1e-06
F32 = jnp.float32
BF16 = jnp.bfloat16


def dot(a, b):
    return jnp.dot(a, b, preferred_element_type=F32)


def dot_nt(a, b):
    return lax.dot_general(a, b, (((1,), (1,)), ((), ())), preferred_element_type=F32)


def dot_tn(a, b):
    return lax.dot_general(a, b, (((0,), (0,)), ((), ())), preferred_element_type=F32)


def call(kernel, outs, *, flops, nbytes, limit=56, **kw):
    return pl.pallas_call(
        kernel,
        out_shape=outs,
        compiler_params=pltpu.CompilerParams(vmem_limit_bytes=limit << 20),
        cost_estimate=pl.CostEstimate(
            flops=int(flops), bytes_accessed=int(nbytes), transcendentals=0
        ),
        **kw,
    )


def comm_call(kernel, outs, number, *, nbytes, limit=60, **kw):
    return pl.pallas_call(
        kernel,
        out_shape=outs,
        compiler_params=pltpu.CompilerParams(
            collective_id=number, has_side_effects=True, vmem_limit_bytes=limit << 20
        ),
        cost_estimate=pl.CostEstimate(flops=0, bytes_accessed=int(nbytes), transcendentals=0),
        **kw,
    )


def shape(dims, dtype):
    return jax.ShapeDtypeStruct(dims, dtype)


def lanes_of(rows, width=LANES):
    return lax.broadcasted_iota(jnp.int32, (rows, width), 1)


def first_heads(n_ctx, slot_dev):
    share = HEADS * slot_dev // n_ctx
    return [min(share * d // slot_dev, HEADS - 2) for d in range(n_ctx)]


def partner(t, lane):
    return jnp.where(lane % 64 < 32, pltpu.roll(t, 96, 1), pltpu.roll(t, 32, 1))


def in_parts(v):
    high = v.astype(BF16)
    rest = v - high.astype(F32)
    mid = rest.astype(BF16)
    low = (rest - mid.astype(F32)).astype(BF16)
    return high.astype(F32), mid.astype(F32), low.astype(F32)


def part_lanes(v, lane):
    high, mid, low = in_parts(v)
    zero = jnp.zeros((), F32)
    return jnp.where(
        lane == 0, high, jnp.where(lane == 1, mid, jnp.where(lane == 2, low, zero))
    ).astype(BF16)


def picks(target_ref, places):
    rows = target_ref.shape[0]
    place = lanes_of(rows, places)
    return tuple(
        jnp.where(place == target_ref[:, k : k + 1], 1.0, 0.0).astype(BF16) for k in range(2)
    )


def start_kernel(experts, capacity, routes_ref, cot_ref, live_ref, target_ref, dout_ref, send_ref):
    rows = routes_ref.shape[0]
    lane = lanes_of(rows)
    hot = [jnp.where(lane == routes_ref[:, k : k + 1], 1.0, 0.0) for k in range(2)]
    below = jnp.where(
        lanes_of(rows, rows) < lax.broadcasted_iota(jnp.int32, (rows, rows), 0), 1.0, 0.0
    )
    earlier = dot(below.astype(BF16), (hot[0] + hot[1]).astype(BF16))
    place = [
        routes_ref[:, k : k + 1] * capacity
        + jnp.sum(hot[k] * earlier, axis=-1, keepdims=True).astype(jnp.int32)
        for k in range(2)
    ]
    for k in range(2):
        target_ref[:, k : k + 1] = place[k]
    dout = (cot_ref[...].astype(F32) * live_ref[...]).astype(BF16)
    dout_ref[...] = dout
    spot = lanes_of(rows, send_ref.shape[0])
    pick = jnp.where((spot == place[0]) | (spot == place[1]), 1.0, 0.0).astype(BF16)
    send_ref[...] = dot_tn(pick, dout).astype(BF16)


def qkv_kernel(heads, experts, x_ref, w_ref, cos_ref, sin_ref, send_ref, in_ref, tail_ref):
    x = x_ref[...].astype(F32)
    tail = w_ref[:, 3 * D :].astype(F32).T
    tail_ref[...] = tail
    inv = lax.rsqrt(jnp.mean(x * x, axis=-1, keepdims=True) + norm_eps)
    attn_in = (x * inv * tail[experts : experts + 1, :]).astype(BF16)
    in_ref[...] = attn_in
    lane = lanes_of(x.shape[0])
    cos, sin = cos_ref[...], sin_ref[...]
    for part in range(3):
        y = dot(attn_in, w_ref[:, part * D : (part + 1) * D])
        groups = []
        for g in range(D // LANES):
            t = y[:, g * LANES : (g + 1) * LANES]
            if part < 2:
                t = t * cos + partner(t, lane) * sin
            groups.append(t)
        turned = [pltpu.roll(t, 64, 1) for t in groups]
        for d, head in enumerate(heads):
            g = head // 2
            if head % 2 == 0:
                packet = groups[g]
            else:
                packet = jnp.where(lane < 64, turned[g], turned[g + 1])
            send_ref[d, :, part * LANES : (part + 1) * LANES] = packet.astype(BF16)


def stack_rows(stack_ref, block, lane):
    rows = block.shape[0]
    zero = jnp.zeros((), block.dtype)
    stack_ref[0:rows, :] = jnp.where(lane < 64, block, zero)
    stack_ref[rows : 2 * rows, :] = jnp.where(lane >= 64, block, zero)


def unstack_rows(stack_ref, block, offset, lane):
    rows = stack_ref.shape[0] // 2
    stack_ref[...] = jnp.zeros_like(stack_ref)
    stack_ref[pl.ds(offset, block.shape[0]), :] = block
    return jnp.where(lane < 64, stack_ref[0:rows, :], stack_ref[rows : 2 * rows, :])


def key_limits(share, rows, q_block, offset, length):
    row = lax.broadcasted_iota(jnp.int32, (1, share), 1) + offset
    row = jnp.where(row >= rows, row - rows, row)
    return jnp.minimum(q_block * rows + row + 1, length)


def attend_kernel(n, share, sc, recv_ref, out_ref, keep_ref, lse_ref, stack, scores, back):
    q_block = pl.program_id(0)
    rows = recv_ref.shape[1]
    offset = pl.multiple_of(sc[n], 64)
    length = sc[n + 1]
    lane = lanes_of(rows)
    stack_rows(stack, recv_ref[sc[q_block], :, 0:LANES] * 0.125, lane)
    query = stack[pl.ds(offset, share), :]
    limit = key_limits(share, rows, q_block, offset, length)
    key_row = lax.broadcasted_iota(jnp.int32, (rows, share), 0)
    blocks = jnp.minimum(q_block + 1, (length + rows - 1) // rows)

    def score_step(j, top):
        keys = recv_ref[sc[j], :, LANES : 2 * LANES]
        s = dot_nt(keys, query)
        s = jnp.where(key_row < limit - j * rows, s, -1e30)
        scores[j] = s
        return jnp.maximum(top, jnp.max(s, axis=0, keepdims=True))

    top = lax.fori_loop(0, blocks, score_step, jnp.full((1, share), -1e30, F32))

    def value_step(j, carry):
        total, acc = carry
        weights = jnp.exp(scores[j] - top)
        total = total + jnp.sum(weights, axis=0, keepdims=True)
        values = recv_ref[sc[j], :, 2 * LANES : 3 * LANES]
        return total, acc + dot_tn(values, weights.astype(BF16))

    total, acc = lax.fori_loop(
        0, blocks, value_step, (jnp.zeros((1, share), F32), jnp.zeros((LANES, share), F32))
    )
    acc = acc / total
    keep_ref[0] = acc
    lse_ref[0] = top + jnp.log(total)
    out_ref[0] = unstack_rows(back, acc.T, offset, lane).astype(BF16)


def attend_back_kernel(
    n, share, sc, recv_ref, grad_ref, keep_ref, lse_ref, out_ref, stack, gstack, dkeys, dvalues, back
):
    q_block = pl.program_id(0)
    rows = recv_ref.shape[1]
    offset = pl.multiple_of(sc[n], 64)
    length = sc[n + 1]
    lane = lanes_of(rows)
    source = sc[q_block]

    @pl.when(q_block == 0)
    def _():
        dkeys[...] = jnp.zeros_like(dkeys)
        dvalues[...] = jnp.zeros_like(dvalues)

    stack_rows(stack, recv_ref[source, :, 0:LANES] * 0.125, lane)
    query = stack[pl.ds(offset, share), :]
    stack_rows(gstack, grad_ref[source], lane)
    grad = gstack[pl.ds(offset, share), :]
    lse = lse_ref[0]
    delta = jnp.sum(grad.astype(F32).T * keep_ref[0], axis=0, keepdims=True)
    limit = key_limits(share, rows, q_block, offset, length)
    key_row = lax.broadcasted_iota(jnp.int32, (rows, share), 0)
    blocks = jnp.minimum(q_block + 1, (length + rows - 1) // rows)

    def step(j, acc):
        keys = recv_ref[sc[j], :, LANES : 2 * LANES]
        values = recv_ref[sc[j], :, 2 * LANES : 3 * LANES]
        s = dot_nt(keys, query)
        weights = jnp.exp(jnp.where(key_row < limit - j * rows, s, -1e30) - lse)
        dweights = dot_nt(values, grad)
        dscores = (weights * (dweights - delta)).astype(BF16)
        dkeys[j] += dot(dscores, query)
        dvalues[j] += dot(weights.astype(BF16), grad)
        return acc + dot_tn(keys, dscores)

    acc = lax.fori_loop(0, blocks, step, jnp.zeros((LANES, share), F32))
    dquery = unstack_rows(back, acc.T * 0.125, offset, lane)
    out_ref[source, :, 0:LANES] = dquery.astype(BF16)

    @pl.when(q_block == n - 1)
    def _():
        def flush(j, carry):
            out_ref[sc[j], :, LANES : 2 * LANES] = dkeys[j].astype(BF16)
            out_ref[sc[j], :, 2 * LANES : 3 * LANES] = dvalues[j].astype(BF16)
            return carry

        lax.fori_loop(0, n, flush, 0)


def middle_kernel(
    heads,
    experts,
    came_ref,
    w_ref,
    x_ref,
    tail_ref,
    routes_ref,
    target_ref,
    residual_ref,
    in_ref,
    gates_ref,
    send_ref,
):
    total = x_ref[...].astype(F32)
    for d, head in enumerate(heads):
        total = total + dot(came_ref[d], w_ref[64 * head : 64 * head + LANES, :])
    residual_ref[...] = total
    inv = lax.rsqrt(jnp.mean(total * total, axis=-1, keepdims=True) + norm_eps)
    ffn_in = (total * inv * tail_ref[experts + 1 : experts + 2, :]).astype(BF16)
    in_ref[...] = ffn_in
    logits = dot_nt(ffn_in, tail_ref[...].astype(BF16))
    lane = lanes_of(logits.shape[0])
    chosen = [
        jnp.sum(jnp.where(lane == routes_ref[:, k : k + 1], logits, 0.0), axis=-1, keepdims=True)
        for k in range(2)
    ]
    top = jnp.maximum(chosen[0], chosen[1])
    raised = [jnp.exp(c - top) for c in chosen]
    gates = [r / (raised[0] + raised[1]) for r in raised]
    gates_ref[...] = jnp.where(lane == 0, gates[0], gates[1])
    pick = picks(target_ref, send_ref.shape[0])
    send_ref[:, 0:D] = dot_tn(pick[0] + pick[1], ffn_in).astype(BF16)
    send_ref[:, D:] = (
        dot_tn(pick[0], part_lanes(gates[0], lane)) + dot_tn(pick[1], part_lanes(gates[1], lane))
    ).astype(BF16)


def gated(g, u, da):
    sig = 1.0 / (1.0 + jnp.exp(-g))
    silu = g * sig
    return silu * u, da * u * sig * (1.0 + g * (1.0 - sig)), da * silu


def expert_kernel(
    x_ref, dy_ref, wg_ref, wu_ref, wt_ref, dx_ref, res_ref, mid_ref, dx_acc, res_acc, dgate
):
    c = pl.program_id(0)

    @pl.when(c == 0)
    def _():
        res_acc[...] = jnp.zeros_like(res_acc)
        dx_acc[...] = jnp.zeros_like(dx_acc)
        dgate[...] = jnp.zeros_like(dgate)

    x, dy = x_ref[:, 0:D], dy_ref[...]
    gate = jnp.sum(x_ref[:, D:].astype(F32), axis=-1, keepdims=True)
    wg, wu, wt = wg_ref[...], wu_ref[...], wt_ref[...]
    da = dot(dy, wt)
    act, dg, du = gated(dot(x, wg), dot(x, wu), da * gate)
    dgate[...] += jnp.sum(act * da, axis=-1, keepdims=True)
    mid_ref[2] = (act * gate).astype(BF16)
    act, dg, du = act.astype(BF16), dg.astype(BF16), du.astype(BF16)
    res_acc[...] += dot_nt(act, wt)
    dx_acc[...] += dot_nt(dg, wg) + dot_nt(du, wu)
    mid_ref[0] = dg
    mid_ref[1] = du

    @pl.when(c == pl.num_programs(0) - 1)
    def _():
        res_ref[...] = res_acc[...].astype(BF16)
        dx_ref[:, 0:D] = dx_acc[...].astype(BF16)
        dx_ref[:, D:] = part_lanes(dgate[:, 0:1], lanes_of(dgate.shape[0]))


def ring_split(rows, columns, pieces):
    down = 1
    while 2 * down <= pieces and rows % (32 * down) == 0:
        down *= 2
    across = pieces // down
    width = -(-columns // (LANES * across)) * LANES
    return down, across, rows // down, width


def ring_place(position, n):
    half = n // 2
    return jnp.where(position < half, 2 * position, 2 * (n - 1 - position) + 1)


def flipped(index, mask):
    for b in range(mask.bit_length()):
        if mask >> b & 1:
            index = index + (1 << b) - 2 * (1 << b) * (index // (1 << b) % 2)
    return index


def mirrored(members):
    bits = members.bit_length() - 1
    return [int(format(j, "b").zfill(bits)[::-1], 2) for j in range(members)]


def shard_rows(members, shard):
    fsdp = lax.axis_index("fsdp")
    return [pl.multiple_of(flipped(fsdp, m) * shard, 16) for m in mirrored(members)]


def remote(source, target, send_sem, recv_sem, peer):
    return pltpu.make_async_remote_copy(
        src_ref=source,
        dst_ref=target,
        send_sem=send_sem,
        recv_sem=recv_sem,
        device_id=peer,
        device_id_type=pl.DeviceIdType.MESH,
    )


def greet(peers):
    barrier = pltpu.get_barrier_semaphore()
    for peer in peers:
        pl.semaphore_signal(barrier, inc=1, device_id=peer, device_id_type=pl.DeviceIdType.MESH)
    pl.semaphore_wait(barrier, len(peers))


def mates_of(members):
    ctx, fsdp = lax.axis_index("ctx"), lax.axis_index("fsdp")
    return [(ctx, flipped(fsdp, 1 << b)) for b in range(members.bit_length() - 1)]


def row_peers(n):
    ctx, fsdp = lax.axis_index("ctx"), lax.axis_index("fsdp")
    return [(lax.rem(ctx + d, n), fsdp) for d in range(1, n)]


def loop(body, low, high):
    lax.fori_loop(low, high, lambda s, carry: (body(s), carry)[1], 0)


def add_into(target, j, other):
    target[j] = (target[j].astype(F32) + other[j].astype(F32)).astype(BF16)


def shared_kernel(
    n,
    members,
    heads,
    experts,
    send_ref,
    in_ref,
    dout_ref,
    residual_ref,
    gates_ref,
    routes_ref,
    target_ref,
    tail_ref,
    w_ref,
    wide_ref,
    back_ref,
    recv_ref,
    res_ref,
    dres_ref,
    branch_ref,
    dlogits_ref,
    dgain_ref,
    a_keep,
    a_give,
    b_keep,
    b_give,
    came,
    packets,
    mids,
    dx_acc,
    a_all,
    b_all,
    a_caught,
    b_caught,
    raw,
    xt,
    gate_buf,
    up_buf,
    back_buf,
    send_sem,
    recv_sem,
    own_sem,
    packet_send,
    packet_recv,
    a_sem,
    b_sem,
    w_sem,
):
    ctx, fsdp = lax.axis_index("ctx"), lax.axis_index("fsdp")
    bits = members.bit_length() - 1
    peers = row_peers(n)
    mate = mates_of(members)[0]
    greet(peers + [mate])
    block = send_ref.shape[0] // n

    def block_at(p):
        return pl.ds(pl.multiple_of(p * block, 16), block)

    own = pltpu.make_async_copy(send_ref.at[block_at(ctx)], came.at[block_at(ctx)], own_sem.at[0])
    own.start()
    copies = [
        remote(
            send_ref.at[block_at(p[0])], came.at[block_at(ctx)], send_sem.at[d], recv_sem.at[d], p
        )
        for d, p in enumerate(peers)
    ]
    for c in copies:
        c.start()

    steps = FS // CHUNK

    def fetch(c, slot):
        at = pl.ds(pl.multiple_of(c * CHUNK, CHUNK), CHUNK)
        up = pl.ds(pl.multiple_of(FS + c * CHUNK, CHUNK), CHUNK)
        return [
            pltpu.make_async_copy(wide_ref.at[:, at], gate_buf.at[slot], w_sem.at[slot, 0]),
            pltpu.make_async_copy(wide_ref.at[:, up], up_buf.at[slot], w_sem.at[slot, 1]),
            pltpu.make_async_copy(back_ref.at[at], back_buf.at[slot], w_sem.at[slot, 2]),
        ]

    for f in fetch(0, 0):
        f.start()
    res_ref[...] = jnp.zeros_like(res_ref)
    dx_acc[...] = jnp.zeros_like(dx_acc)
    b_shard = FS // members
    piece = b_all.shape[2]

    def ffn_step(c):
        slot = lax.rem(c, 2)
        for f in fetch(c, slot):
            f.wait()

        @pl.when(c + 1 < steps)
        def _():
            for f in fetch(c + 1, 1 - slot):
                f.start()

        x, dy = in_ref[...], dout_ref[...]
        wg, wu, wo = gate_buf[slot], up_buf[slot], back_buf[slot]
        act, dg, du = gated(dot(x, wg), dot(x, wu), dot_nt(dy, wo))
        act, dg, du = act.astype(BF16), dg.astype(BF16), du.astype(BF16)
        res_ref[...] += dot(act, wo)
        dx_acc[...] += dot_nt(dg, wg) + dot_nt(du, wu)
        mids[c] = dg
        mids[steps + c] = du
        value = dot_tn(act, dy).astype(BF16)
        span = min(piece, CHUNK)
        for u in range(CHUNK // span):
            row = c * CHUNK + u * span
            t = row // b_shard
            j = sum(
                lax.rem(fsdp // (1 << b) + t // (1 << b), 2) * (1 << (bits - 1 - b))
                for b in range(bits)
            )
            inside = lax.rem(row, b_shard)
            top = pl.multiple_of(lax.rem(inside, piece), 16)
            b_all[inside // piece, j, pl.ds(top, span), :] = value[u * span : (u + 1) * span]

    loop(ffn_step, 0, steps)
    half, quarter = members // 2, members // 4

    def a_swap(i):
        return remote(
            a_all.at[i, pl.ds(half, half)], a_caught.at[i], a_sem.at[i, 0], a_sem.at[i, 1], mate
        )

    def b_swap(i):
        return remote(
            b_all.at[i, pl.ds(half, half)], b_caught.at[i], b_sem.at[i, 0], b_sem.at[i, 1], mate
        )

    for i in range(2):
        b_swap(i).start()
    rows = shard_rows(members, D // members)
    shard = D // members
    raw[...] = in_ref[...].T
    for j in range(members):
        xt[j * shard : (j + 1) * shard, :] = raw[pl.ds(rows[j], shard), :]
    for i in range(2):

        def grad_step(c, i=i):
            value = dot(xt[...], mids[i * steps + c]).astype(BF16)
            column = pl.ds(pl.multiple_of(c * CHUNK, CHUNK), CHUNK)
            for j in range(members):
                a_all[i, j, :, column] = value[j * shard : (j + 1) * shard]

        loop(grad_step, 0, steps)
        a_swap(i).start()
    for i in range(2):
        b_swap(i).wait_recv()
        for j in range(half):
            total = (b_all[i, j].astype(F32) + b_caught[i, j].astype(F32)).astype(BF16)
            if j < quarter:
                b_keep[i, j] = total
            else:
                b_give[i, j - quarter] = total
    for c in copies:
        c.wait()
    own.wait()

    pick = picks(target_ref, came.shape[0])
    gates = [gates_ref[:, k : k + 1] for k in range(2)]
    parts = came[:, D:]
    dgate = [jnp.sum(dot(pick[k], parts), axis=-1, keepdims=True) for k in range(2)]
    mean = gates[0] * dgate[0] + gates[1] * dgate[1]
    lane = lanes_of(pick[0].shape[0])
    dlogits = sum(
        jnp.where(lane == routes_ref[:, k : k + 1], gates[k] * (dgate[k] - mean), 0.0)
        for k in range(2)
    ).astype(BF16)
    dlogits_ref[...] = dlogits
    tail = tail_ref[...]
    dffn = dot(pick[0] + pick[1], came[:, 0:D]) + dx_acc[...] + dot(dlogits, tail.astype(BF16))
    residual = residual_ref[...]
    inv = lax.rsqrt(jnp.mean(residual * residual, axis=-1, keepdims=True) + norm_eps)
    scaled = dffn * tail[experts + 1 : experts + 2, :]
    total = jnp.mean(scaled * residual, axis=-1, keepdims=True)
    dres = dout_ref[...].astype(F32) + inv * scaled - residual * inv * inv * inv * total
    branch = dres.astype(BF16)
    branch_ref[...] = branch
    for d, head in enumerate(heads):
        packets[d] = dot_nt(branch, w_ref[64 * head : 64 * head + LANES, :]).astype(BF16)
    own = pltpu.make_async_copy(packets.at[ctx], recv_ref.at[ctx], own_sem.at[1])
    own.start()
    copies = [
        remote(packets.at[p[0]], recv_ref.at[ctx], packet_send.at[d], packet_recv.at[d], p)
        for d, p in enumerate(peers)
    ]
    for c in copies:
        c.start()
    dres_ref[...] = dres
    dgain_ref[...] = jnp.sum(dffn * residual * inv, axis=0, keepdims=True)
    for i in range(2):
        a_swap(i).wait_recv()
        for j in range(half):
            total = (a_all[i, j].astype(F32) + a_caught[i, j].astype(F32)).astype(BF16)
            if j < quarter:
                a_keep[i, j] = total
            else:
                a_give[i, j - quarter] = total
    for c in copies:
        c.wait()
    own.wait()
    for i in range(2):
        a_swap(i).wait_send()
        b_swap(i).wait_send()


def back_exchange_kernel(
    n,
    members,
    heads,
    send_ref,
    x_ref,
    dy_ref,
    came_ref,
    branch_ref,
    in_ref,
    dlogits_ref,
    residual_ref,
    shared_ref,
    gates_ref,
    target_ref,
    live_ref,
    res_ref,
    mid_ref,
    recv_ref,
    sum_ref,
    out_grad_ref,
    router_ref,
    output_ref,
    give,
    caught,
    crossed,
    raw,
    xt,
    dyt,
    acc,
    mids,
    send_sem,
    recv_sem,
    own_sem,
    give_sem,
    caught_sem,
    cross_sem,
    mid_sem,
):
    ctx = lax.axis_index("ctx")
    peers = row_peers(n)
    mates = mates_of(members)
    mate, far = mates[0], mates[1]
    greet(peers + [mate, far])
    own = pltpu.make_async_copy(send_ref.at[ctx], recv_ref.at[ctx], own_sem)
    own.start()
    copies = [
        remote(send_ref.at[p[0]], recv_ref.at[ctx], send_sem.at[d], recv_sem.at[d], p)
        for d, p in enumerate(peers)
    ]
    for c in copies:
        c.start()

    steps = mid_ref.shape[2] // CHUNK
    parts = mid_ref.shape[0]

    def fetch(i, c, slot):
        column = pl.multiple_of(c * CHUNK, CHUNK)
        return pltpu.make_async_copy(
            mid_ref.at[i, :, pl.ds(column, CHUNK)], mids.at[slot], mid_sem.at[slot]
        )

    fetch(0, 0, 0).start()
    shard = D // members
    half = members // 2
    rows = shard_rows(members, shard)

    def turned(value, target):
        raw[...] = value.T
        for j in range(members):
            target[j * shard : (j + 1) * shard, :] = raw[pl.ds(rows[j], shard), :]

    turned(x_ref[:, 0:D], xt)
    turned(dy_ref[...], dyt)

    def swap(i):
        return remote(give.at[i], caught.at[i], give_sem.at[i], caught_sem.at[i], mate)

    quarter = members // 4
    cross = remote(
        sum_ref.at[0, pl.ds(quarter, quarter)], crossed, cross_sem.at[0], cross_sem.at[1], far
    )
    for i in range(parts):
        left = xt if i < 2 else dyt

        def step(c, left=left, i=i):
            slot = lax.rem(c, 2)
            fetch(i, c, slot).wait()

            @pl.when(c + 1 < steps)
            def _():
                fetch(i, c + 1, 1 - slot).start()

            value = dot(left[...], mids[slot]).astype(BF16)
            column = pl.ds(pl.multiple_of(c * CHUNK, CHUNK), CHUNK)
            for j in range(half):
                sum_ref[i, j, :, column] = value[j * shard : (j + 1) * shard]
                give[i, j, :, column] = value[(half + j) * shard : (half + j + 1) * shard]

        loop(step, 0, steps)
        if i + 1 < parts:
            fetch(i + 1, 0, 0).start()
        swap(i).start()
        if i > 0:
            swap(i - 1).wait_recv()
            for j in range(half):
                add_into(sum_ref.at[i - 1], j, caught.at[i - 1])
        if i == 1:
            cross.start()

    acc[...] = jnp.zeros_like(acc)
    branch = branch_ref[...]
    for d, head in enumerate(heads):
        acc[64 * head : 64 * head + LANES, :] += dot_tn(came_ref[d], branch)
    for j in range(members):
        out_grad_ref[j] = acc[pl.ds(rows[j], shard), :].astype(BF16)
    router_ref[...] = dot_tn(in_ref[...], dlogits_ref[...])
    pick = picks(target_ref, res_ref.shape[0])
    came = res_ref[...]
    mixture = gates_ref[:, 0:1] * dot(pick[0], came) + gates_ref[:, 1:2] * dot(pick[1], came)
    output_ref[...] = (live_ref[...] * (residual_ref[...] + shared_ref[...] + mixture)).astype(BF16)
    swap(parts - 1).wait_recv()
    for j in range(half):
        add_into(sum_ref.at[parts - 1], j, caught.at[parts - 1])
    for c in copies:
        c.wait()
    own.wait()
    cross.wait()
    for j in range(quarter):
        add_into(sum_ref.at[0], j, crossed)
    for i in range(parts):
        swap(i).wait_send()


def last_kernel(
    n,
    members,
    heads,
    experts,
    splits,
    recv_ref,
    cos_ref,
    sin_ref,
    in_ref,
    x_ref,
    w_ref,
    tail_ref,
    dres_ref,
    out_grad_ref,
    router_ref,
    dgain_ref,
    a_ref,
    a_other,
    b_ref,
    b_other,
    e_ref,
    x_out,
    a_out,
    b_out,
    c_out,
    e_out,
    *scratch,
):
    bits = members.bit_length() - 1
    streams = len(splits)
    own, full, back_up, back_down = (scratch[k * streams : (k + 1) * streams] for k in range(4))
    back = (back_up, back_down)
    scratch = scratch[4 * streams :]
    packs, scratch = scratch[0:4], scratch[4:]
    caught = [scratch[4 * b : 4 * b + 4] for b in range(bits)]
    scratch = scratch[4 * bits :]
    e_caught, scratch = scratch[0 : bits - 1], scratch[bits - 1 :]
    dproj, raw, turned, small = scratch[0:4]
    send_sem, recv_sem, level_send, level_recv, e_send, e_recv = scratch[4:]
    ctx, fsdp = lax.axis_index("ctx"), lax.axis_index("fsdp")
    here = jnp.where(ctx % 2 == 0, ctx // 2, n - 1 - ctx // 2)
    ahead = (ring_place(lax.rem(here + 1, n), n), fsdp)
    behind = (ring_place(lax.rem(here + n - 1, n), n), fsdp)
    mates = mates_of(members)
    greet([ahead, behind] + mates)
    shard = D // members
    parts = e_ref.shape[0]

    def level_copy(p, b):
        count = members >> (b + 1)
        return remote(
            packs[p].at[pl.ds(count, count)],
            caught[b][p],
            level_send.at[p, b],
            level_recv.at[p, b],
            mates[b],
        )

    def level_add(p, b):
        level_copy(p, b).wait_recv()
        for j in range(members >> (b + 1)):
            add_into(packs[p], j, caught[b][p])

    def level_next(p):
        level_add(p, 0)
        level_copy(p, 1).start()

    def e_copy(i, b):
        count = members >> (b + 1)
        source = e_ref if b == 1 or (b == 2 and i == 0) else e_caught[b - 2]
        return remote(
            source.at[i, pl.ds(count, count)],
            e_caught[b - 1].at[i],
            e_send.at[i, b - 1],
            e_recv.at[i, b - 1],
            mates[b],
        )

    def e_add(i, b):
        e_copy(i, b).wait_recv()
        source = e_ref if b == 1 or (b == 2 and i == 0) else e_caught[b - 2]
        for j in range(members >> (b + 1)):
            total = source[i, j].astype(F32) + e_caught[b - 1][i, j].astype(F32)
            if b == bits - 1:
                e_out[i] = total.astype(BF16)
            else:
                e_caught[b - 1][i, j] = total.astype(BF16)

    def tiles(i):
        down, across, height, width = splits[i][0:4]
        columns = splits[i][4]
        for p in range(down * across):
            r, c = p // across, p % across
            yield p, r * height, height, c * width, max(0, min(width, columns - c * width)), width

    def load(i, ref, skip=0, other=None):
        for p, top, height, start, have, width in tiles(i):
            if have > 0:
                value = ref[top : top + height, skip + start : skip + start + have]
                if other is not None:
                    added = other[top : top + height, skip + start : skip + start + have]
                    value = (value.astype(F32) + added.astype(F32)).astype(BF16)
                own[i][p, :, 0:have] = value
            if have < width:
                own[i][p, :, have:] = jnp.zeros((height, width - have), BF16)

    def save(i, ref, skip=0):
        for p, top, height, start, have, width in tiles(i):
            if have > 0:
                ref[top : top + height, skip + start : skip + start + have] = full[i][p, :, 0:have]

    long, short = n // 2, n - 1 - n // 2

    def hops(i, direction):
        return long if direction == i % 2 else short

    def place(direction, steps):
        return lax.rem(here + (steps if direction == 0 else 2 * n - steps), n)

    def copy(i, direction, step, source, target, slot):
        return remote(
            source.at[slot],
            target.at[slot],
            send_sem.at[i, direction, step],
            recv_sem.at[i, direction, step],
            ahead if direction == 0 else behind,
        )

    def first(i):
        for direction in range(2):
            slot = place(direction, hops(i, direction))
            copy(i, direction, 0, own[i], back[direction][i], slot).start()

    def reduce_step(i, s):
        for direction in range(2):
            count = hops(i, direction)
            if s < count:
                slot = place(direction, count - s)
                buffer = back[direction][i]
                copy(i, direction, s - 1, buffer, buffer, slot).wait_recv()
                add_into(buffer, slot, own[i])
                copy(i, direction, s, buffer, buffer, slot).start()

    def turn(i):
        for direction in range(2):
            buffer = back[direction][i]
            copy(i, direction, hops(i, direction) - 1, buffer, buffer, here).wait_recv()
        full[i][here] = (
            own[i][here].astype(F32) + back_up[i][here].astype(F32) + back_down[i][here].astype(F32)
        ).astype(BF16)
        for direction in range(2):
            copy(i, direction, long, full[i], full[i], here).start()

    def gather_step(i, s):
        for direction in range(2):
            if s < hops(i, direction):
                slot = place(1 - direction, s)
                copy(i, direction, long + s - 1, full[i], full[i], slot).wait_recv()
                copy(i, direction, long + s, full[i], full[i], slot).start()

    def end(i):
        for direction in range(2):
            count = hops(i, direction)
            slot = place(1 - direction, count)
            copy(i, direction, long + count - 1, full[i], full[i], slot).wait_recv()

    def drain(i):
        for direction in range(2):

            def sent(step, direction=direction):
                copy(i, direction, step, own[i], full[i], 0).wait_send()

            loop(sent, 0, hops(i, direction))
            loop(sent, long, long + hops(i, direction))

    def steps_of(i):
        done = [functools.partial(reduce_step, i, s) for s in range(1, long)]
        done.append(functools.partial(turn, i))
        done += [functools.partial(gather_step, i, s) for s in range(1, long)]
        done.append(functools.partial(end, i))
        return done

    for i in range(2):
        load(i, a_ref.at[i], 0, a_other.at[i])
        first(i)
    for i in range(2):
        load(2 + i, b_ref.at[i], 0, b_other.at[i])
        first(2 + i)
    waiting = [steps_of(i) for i in range(4)]

    def dense_step():
        for queue in waiting[0:4]:
            if queue:
                queue.pop(0)()

    rows = shard_rows(members, shard)
    raw[...] = in_ref[...].T
    for j in range(members):
        turned[j * shard : (j + 1) * shard, :] = raw[pl.ds(rows[j], shard), :]
    lane = lanes_of(x_ref.shape[0])
    cos, sin = cos_ref[...], sin_ref[...]
    for part in range(3):
        groups = [jnp.zeros(lane.shape, F32) for _ in range(D // LANES)]
        for d, head in enumerate(heads):
            g = head // 2
            packet = recv_ref[d, :, part * LANES : (part + 1) * LANES].astype(F32)
            if head % 2 == 0:
                groups[g] = groups[g] + packet
            else:
                packet = pltpu.roll(packet, 64, 1)
                groups[g] = groups[g] + jnp.where(lane >= 64, packet, 0.0)
                groups[g + 1] = groups[g + 1] + jnp.where(lane < 64, packet, 0.0)
        for g, t in enumerate(groups):
            if part < 2:
                t = t.astype(BF16).astype(F32)
                t = t * cos - partner(t, lane) * sin
            dproj[:, part * D + g * LANES : part * D + (g + 1) * LANES] = t.astype(BF16)
        value = dot(turned[...], dproj[:, part * D : (part + 1) * D]).astype(BF16)
        for j in range(members):
            packs[part][j] = value[j * shard : (j + 1) * shard]
        level_copy(part, 0).start()
        if part > 0:
            level_next(part - 1)
    dense_step()
    dnorm = dot_nt(dproj[...], w_ref[:, 0 : 3 * D])
    x = x_ref[...].astype(F32)
    gain = tail_ref[experts : experts + 1, :]
    inv = lax.rsqrt(jnp.mean(x * x, axis=-1, keepdims=True) + norm_eps)
    dgain_one = jnp.sum(dnorm * x * inv, axis=0, keepdims=True)
    row = lax.broadcasted_iota(jnp.int32, (LANES, D), 0)
    gains = jnp.where(row == experts, dgain_one, jnp.where(row == experts + 1, dgain_ref[...], 0.0))
    small[...] = router_ref[...] + gains.T
    for j in range(members):
        packs[3][j, :, 0:LANES] = small[pl.ds(rows[j], shard), :].astype(BF16)
        packs[3][j, :, LANES:] = out_grad_ref[j]
    level_copy(3, 0).start()
    level_next(2)
    scaled = dnorm * gain
    total = jnp.mean(scaled * x, axis=-1, keepdims=True)
    x_out[...] = dres_ref[...] + inv * scaled - x * inv * inv * inv * total
    level_next(3)
    for i in range(1, parts):
        e_copy(i, 1).start()

    for p in range(4):
        for b in range(1, bits):
            level_add(p, b)
            if b + 1 < bits:
                level_copy(p, b + 1).start()
        load(4 + p, packs[p].at[0])
        first(4 + p)
        dense_step()
        for queue in waiting[4:]:
            queue.pop(0)()
        waiting.append(steps_of(4 + p))
    while any(waiting):
        for i, queue in enumerate(waiting):
            if queue:
                queue.pop(0)()
                if not queue and i < 4:
                    if i < 2:
                        save(i, a_out, i * splits[0][4])
                    else:
                        height = splits[2][0] * splits[2][2]
                        save(i, b_out.at[pl.ds((i - 2) * height, height)])
        if not any(waiting[0:4]) and parts > 1:
            e_add(1, 1)
            parts = min(parts, 1)
    for p in range(4):
        save(4 + p, c_out, p * D)
    parts = e_ref.shape[0]
    for i in range(2, parts):
        e_add(i, 1)
    if bits == 2:
        e_out[0] = e_ref[0, 0]
    for b in range(2, bits):
        for i in range(parts):
            e_copy(i, b).start()
        for i in range(parts):
            e_add(i, b)
    for b in range(bits):
        for p in range(4):
            level_copy(p, b).wait_send()
    for b in range(1, bits):
        for i in range(1 if b == 1 else 0, parts):
            e_copy(i, b).wait_send()

    for i in range(streams):
        drain(i)


def widen_kernel(
    experts,
    late_ref,
    a_ref,
    b_ref,
    in_ref,
    back_ref,
    x_ref,
    small_ref,
    qkv_out,
    w_out,
    a_out,
    b_out,
    in_out,
    back_out,
    x_out,
    router_out,
    gains_out,
):
    qkv_out[...] = late_ref[:, 0 : 3 * D].astype(F32)
    w_out[...] = late_ref[:, PACKED:].astype(F32)
    a_out[...] = a_ref[...].astype(F32)
    b_out[...] = b_ref[...].astype(F32)
    in_out[:, 0:FF] = in_ref[0].astype(F32)
    in_out[:, FF:] = in_ref[1].astype(F32)
    back_out[...] = back_ref[0].astype(F32)
    x_out[...] = x_ref[...]

    @pl.when(pl.program_id(0) == 0)
    def _():
        small = small_ref[...].astype(F32).T
        router_out[...] = small[0:experts]
        gains_out[...] = small[experts : experts + 2]


def on_device(
    tokens,
    cotangent,
    lengths,
    position_block,
    routes,
    gain_attn,
    w_qkv,
    w_out,
    gain_ffn,
    w_router,
    w_shared_in,
    w_shared_out,
    w_expert_in,
    w_expert_out,
):
    n_ctx = lax.axis_size("ctx")
    ctx_index = lax.axis_index("ctx")
    rows = tokens.shape[1]
    local = w_qkv.shape[0]
    experts = w_router.shape[1]
    capacity = 3 * rows // experts
    places = experts * capacity
    members = D // local
    share = HEADS * rows // n_ctx
    heads = first_heads(n_ctx, rows)
    gather = functools.partial(lax.all_gather, axis_name="fsdp", axis=0, tiled=True)
    exchange = functools.partial(
        lax.all_to_all, axis_name="ctx", split_axis=0, concat_axis=0, tiled=True
    )
    x = tokens[0]
    length = lengths[0]

    first_pack = jnp.concatenate(
        [
            w_qkv,
            w_router,
            gain_attn[:, None],
            gain_ffn[:, None],
            jnp.zeros((local, LANES - experts - 2), BF16),
        ],
        axis=1,
    )
    qkv_pack = gather(first_pack)
    out_weight = gather(w_out)
    weights = gather(
        jnp.concatenate([w_shared_in, w_expert_in[0], w_expert_out[0].T], axis=1)
    )
    shared_out = gather(w_shared_out)
    bits = members.bit_length() - 1

    query_pos = position_block[ctx_index] * rows + jnp.arange(rows, dtype=jnp.int32)
    live = (query_pos < length).astype(F32)[:, None]
    halves = HEAD_DIM // 2
    inverse = 10000.0 ** (-(jnp.arange(halves, dtype=F32) * 2.0 / HEAD_DIM))
    angles = query_pos.astype(F32)[:, None] * inverse[None, :]
    cos, sin = jnp.cos(angles), jnp.sin(angles)
    cos = jnp.concatenate([cos, cos, cos, cos], axis=1)
    sin = jnp.concatenate([-sin, sin, -sin, sin], axis=1)

    order = jnp.sum(
        jnp.where(
            position_block[None, :] == jnp.arange(n_ctx, dtype=jnp.int32)[:, None],
            jnp.arange(n_ctx, dtype=jnp.int32)[None, :],
            0,
        ),
        axis=1,
    )
    head_of = jnp.minimum(share * ctx_index // rows, HEADS - 2)
    offset = share * ctx_index - rows * head_of
    scalars = jnp.concatenate(
        [order, jnp.stack([offset.astype(jnp.int32), length.astype(jnp.int32)])]
    )

    target, dout, dy_send = call(
        functools.partial(start_kernel, experts, capacity),
        (shape((rows, 2), jnp.int32), shape((rows, D), BF16), shape((places, D), BF16)),
        flops=2 * rows * D * places,
        nbytes=3 << 20,
    )(routes[0], cotangent[0], live)
    dy_rows = exchange(dy_send.reshape(n_ctx, -1, D)).reshape(places, D)

    send, attn_in, tail = call(
        functools.partial(qkv_kernel, heads, experts),
        (
            shape((n_ctx, rows, 3 * LANES), BF16),
            shape((rows, D), BF16),
            shape((LANES, D), F32),
        ),
        flops=2 * rows * D * 3 * D,
        nbytes=6 << 20,
    )(x, qkv_pack, cos, sin)
    send, dy_rows = lax.optimization_barrier((send, dy_rows))
    recv = exchange(send)

    packet = pl.BlockSpec((n_ctx, rows, 3 * LANES), lambda i, sc: (0, 0, 0))
    block_of = lambda i, sc: (i, 0, 0)
    attended, kept, lse = call(
        functools.partial(attend_kernel, n_ctx, share),
        (
            shape((n_ctx, rows, LANES), BF16),
            shape((n_ctx, LANES, share), F32),
            shape((n_ctx, 1, share), F32),
        ),
        flops=2 * share * rows * n_ctx * n_ctx * LANES * 2,
        nbytes=5 << 20,
        grid_spec=pltpu.PrefetchScalarGridSpec(
            num_scalar_prefetch=1,
            grid=(n_ctx,),
            in_specs=[packet],
            out_specs=[
                pl.BlockSpec((1, rows, LANES), lambda i, sc: (sc[i], 0, 0)),
                pl.BlockSpec((1, LANES, share), block_of),
                pl.BlockSpec((1, 1, share), block_of),
            ],
            scratch_shapes=[
                pltpu.VMEM((2 * rows, LANES), BF16),
                pltpu.VMEM((n_ctx, rows, share), F32),
                pltpu.VMEM((2 * rows, LANES), F32),
            ],
        ),
    )(scalars, recv)
    came = exchange(attended)

    whole = pl.BlockSpec(memory_space=pltpu.VMEM)
    out_block = pl.BlockSpec((D, D), lambda *at: (0, 0))

    def full(*dims):
        return pl.BlockSpec(dims, lambda *at: (0,) * len(dims))

    residual, ffn_in, gates, outgoing = call(
        functools.partial(middle_kernel, heads, experts),
        (
            shape((rows, D), F32),
            shape((rows, D), BF16),
            shape((rows, LANES), F32),
            shape((places, D + LANES), BF16),
        ),
        flops=2 * rows * D * (D + 1024 + 2 * places),
        nbytes=5 << 20,
        grid=(1,),
        in_specs=[
            full(n_ctx, rows, LANES),
            out_block,
            full(rows, D),
            full(LANES, D),
            full(rows, 2),
            full(rows, 2),
        ],
        out_specs=[
            full(rows, D),
            full(rows, D),
            full(rows, LANES),
            full(places, D + LANES),
        ],
    )(came, out_weight, x, tail, routes[0], target)
    x_rows = exchange(outgoing.reshape(n_ctx, -1, D + LANES)).reshape(places, D + LANES)

    half, quarter = members // 2, members // 4
    steps = FS // CHUNK
    wide = FF // CHUNK
    expert_dx, expert_res, expert_mid = call(
        expert_kernel,
        (
            shape((places, D + LANES), BF16),
            shape((places, D), BF16),
            shape((3, places, FF), BF16),
        ),
        flops=2 * places * D * FF * 6,
        nbytes=24 << 20,
        grid=(wide,),
        in_specs=[
            full(places, D + LANES),
            full(places, D),
            pl.BlockSpec((D, CHUNK), lambda c: (0, 2 * steps + c)),
            pl.BlockSpec((D, CHUNK), lambda c: (0, 2 * steps + wide + c)),
            pl.BlockSpec((D, CHUNK), lambda c: (0, 2 * steps + 2 * wide + c)),
        ],
        out_specs=[
            full(places, D + LANES),
            full(places, D),
            pl.BlockSpec((3, places, CHUNK), lambda c: (0, 0, c)),
        ],
        scratch_shapes=[
            pltpu.VMEM((places, D), F32),
            pltpu.VMEM((places, D), F32),
            pltpu.VMEM((places, LANES), F32),
        ],
    )(x_rows, dy_rows, weights, weights, weights)
    b_rows = FS // members // 2
    anywhere = pl.BlockSpec(memory_space=pl.ANY)
    (
        branch_recv,
        shared_res,
        dres,
        branch,
        dlogits,
        dgain_two,
        dense_keep,
        dense_give,
        so_keep,
        so_give,
    ) = comm_call(
        functools.partial(shared_kernel, n_ctx, members, heads, experts),
        (
            shape((n_ctx, rows, LANES), BF16),
            shape((rows, D), F32),
            shape((rows, D), F32),
            shape((rows, D), BF16),
            shape((rows, LANES), BF16),
            shape((1, D), F32),
        )
        + (shape((2, quarter, local, FS), BF16),) * 2
        + (shape((2, quarter, b_rows, D), BF16),) * 2,
        2,
        in_specs=[whole] * 9 + [anywhere] * 2,
        out_specs=[whole] * 10,
        scratch_shapes=[
            pltpu.VMEM((places, D + LANES), BF16),
            pltpu.VMEM((n_ctx, rows, LANES), BF16),
            pltpu.VMEM((2 * steps, rows, CHUNK), BF16),
            pltpu.VMEM((rows, D), F32),
            pltpu.VMEM((2, members, local, FS), BF16),
            pltpu.VMEM((2, members, b_rows, D), BF16),
            pltpu.VMEM((2, half, local, FS), BF16),
            pltpu.VMEM((2, half, b_rows, D), BF16),
            pltpu.VMEM((D, rows), BF16),
            pltpu.VMEM((D, rows), BF16),
            pltpu.VMEM((2, D, CHUNK), BF16),
            pltpu.VMEM((2, D, CHUNK), BF16),
            pltpu.VMEM((2, CHUNK, D), BF16),
            pltpu.SemaphoreType.DMA((n_ctx - 1,)),
            pltpu.SemaphoreType.DMA((n_ctx - 1,)),
            pltpu.SemaphoreType.DMA((2,)),
            pltpu.SemaphoreType.DMA((n_ctx - 1,)),
            pltpu.SemaphoreType.DMA((n_ctx - 1,)),
            pltpu.SemaphoreType.DMA((2, 2)),
            pltpu.SemaphoreType.DMA((2, 2)),
            pltpu.SemaphoreType.DMA((2, 3)),
        ],
        nbytes=150 << 20,
    )(
        expert_dx,
        ffn_in,
        dout,
        residual,
        gates,
        routes[0],
        target,
        tail,
        out_weight,
        weights,
        shared_out,
    )

    def gathered(terms):
        return sum(t.astype(F32) for t in terms).astype(BF16)

    def rest_of(keep, give):
        for b in range(1, bits):
            came_in = lax.ppermute(give, "fsdp", [(i, i ^ (1 << b)) for i in range(members)])
            if b + 1 < bits:
                count = keep.shape[1] // 2
                give = gathered([keep[:, count:], came_in[:, count:]])
                keep = gathered([keep[:, :count], came_in[:, :count]])
        return keep[:, 0], came_in[:, 0]

    branch_recv, expert_res = lax.optimization_barrier((branch_recv, expert_res))
    dense_part, dense_other = rest_of(dense_keep, dense_give)
    so_part, so_other = rest_of(so_keep, so_give)

    dsend = call(
        functools.partial(attend_back_kernel, n_ctx, share),
        shape((n_ctx, rows, 3 * LANES), BF16),
        flops=2 * share * rows * n_ctx * n_ctx * LANES * 3,
        nbytes=8 << 20,
        grid_spec=pltpu.PrefetchScalarGridSpec(
            num_scalar_prefetch=1,
            grid=(n_ctx,),
            in_specs=[
                packet,
                pl.BlockSpec((n_ctx, rows, LANES), lambda i, sc: (0, 0, 0)),
                pl.BlockSpec((1, LANES, share), block_of),
                pl.BlockSpec((1, 1, share), block_of),
            ],
            out_specs=packet,
            scratch_shapes=[
                pltpu.VMEM((2 * rows, LANES), BF16),
                pltpu.VMEM((2 * rows, LANES), BF16),
                pltpu.VMEM((n_ctx, rows, LANES), F32),
                pltpu.VMEM((n_ctx, rows, LANES), F32),
                pltpu.VMEM((2 * rows, LANES), F32),
            ],
        ),
    )(scalars, recv, branch_recv, kept, lse)
    res_came = exchange(expert_res.reshape(n_ctx, -1, D)).reshape(places, D)
    drecv, expert_sum, out_grad, grad_router, output = comm_call(
        functools.partial(back_exchange_kernel, n_ctx, members, heads),
        (
            shape((n_ctx, rows, 3 * LANES), BF16),
            shape((3, half, local, FF), BF16),
            shape((members, local, D), BF16),
            shape((D, LANES), F32),
            shape((rows, D), BF16),
        ),
        1,
        in_specs=[whole] * 13 + [pl.BlockSpec(memory_space=pl.ANY)],
        out_specs=[whole] * 5,
        scratch_shapes=[
            pltpu.VMEM((3, half, local, FF), BF16),
            pltpu.VMEM((3, half, local, FF), BF16),
            pltpu.VMEM((members // 4, local, FF), BF16),
            pltpu.VMEM((D, places), BF16),
            pltpu.VMEM((D, places), BF16),
            pltpu.VMEM((D, places), BF16),
            pltpu.VMEM((D, D), F32),
            pltpu.VMEM((2, places, CHUNK), BF16),
            pltpu.SemaphoreType.DMA((n_ctx - 1,)),
            pltpu.SemaphoreType.DMA((n_ctx - 1,)),
            pltpu.SemaphoreType.DMA,
            pltpu.SemaphoreType.DMA((3,)),
            pltpu.SemaphoreType.DMA((3,)),
            pltpu.SemaphoreType.DMA((2,)),
            pltpu.SemaphoreType.DMA((2,)),
        ],
        nbytes=120 << 20,
    )(
        dsend,
        x_rows,
        dy_rows,
        came,
        branch,
        ffn_in,
        dlogits,
        residual,
        shared_res,
        gates,
        target,
        live,
        res_came,
        expert_mid,
    )

    late_width = PACKED + D
    late_widths = [D, D, D, D + LANES]
    sizes = [(local, FS)] * 2 + [(FS // members // 2, D)] * 2
    sizes += [(local, width) for width in late_widths]
    splits = [ring_split(r, c, n_ctx) + (c,) for r, c in sizes]
    tiles = [(n_ctx, t[2], t[3]) for t in splits]
    grad_x, dense_sum, so_sum, last_sum, expert_sum = comm_call(
        functools.partial(last_kernel, n_ctx, members, heads, experts, splits),
        (
            shape((rows, D), F32),
            shape((local, 2 * FS), BF16),
            shape((FS // members, D), BF16),
            shape((local, late_width), BF16),
            shape((3, local, FF), BF16),
        ),
        0,
        in_specs=[whole] * 16,
        out_specs=[whole] * 5,
        scratch_shapes=[pltpu.VMEM(t, BF16) for t in tiles * 4]
        + [pltpu.VMEM((members, local, width), BF16) for width in late_widths]
        + [
            pltpu.VMEM((members >> (b + 1), local, width), BF16)
            for b in range(bits)
            for width in late_widths
        ]
        + [pltpu.VMEM((3, members >> (b + 1), local, FF), BF16) for b in range(1, bits)]
        + [
            pltpu.VMEM((rows, 3 * D), BF16),
            pltpu.VMEM((D, rows), BF16),
            pltpu.VMEM((D, rows), BF16),
            pltpu.VMEM((D, LANES), F32),
            pltpu.SemaphoreType.DMA((8, 2, n_ctx)),
            pltpu.SemaphoreType.DMA((8, 2, n_ctx)),
            pltpu.SemaphoreType.DMA((4, bits)),
            pltpu.SemaphoreType.DMA((4, bits)),
            pltpu.SemaphoreType.DMA((3, max(1, bits - 1))),
            pltpu.SemaphoreType.DMA((3, max(1, bits - 1))),
        ],
        nbytes=200 << 20,
    )(
        drecv,
        cos,
        sin,
        attn_in,
        x,
        qkv_pack,
        tail,
        dres,
        out_grad,
        grad_router,
        dgain_two,
        dense_part,
        dense_other,
        so_part,
        so_other,
        expert_sum,
    )

    quarters = 4 if local % 64 == 0 else 1

    def rows_of(count, width):
        return pl.BlockSpec((count // quarters, width), lambda i: (i, 0))

    grad_qkv, grad_out, grad_si, grad_so, grad_ei, grad_eo, grad_x, grad_router, gains = call(
        functools.partial(widen_kernel, experts),
        (
            shape((local, 3 * D), F32),
            shape((local, D), F32),
            shape((local, 2 * FS), F32),
            shape((FS // members, D), F32),
            shape((local, 2 * FF), F32),
            shape((local, FF), F32),
            shape((rows, D), F32),
            shape((experts, local), F32),
            shape((2, local), F32),
        ),
        flops=0,
        nbytes=22 << 20,
        grid=(quarters,),
        in_specs=[
            rows_of(local, late_width),
            rows_of(local, 2 * FS),
            rows_of(FS // members, D),
            pl.BlockSpec((2, local // quarters, FF), lambda i: (0, i, 0)),
            pl.BlockSpec((1, local // quarters, FF), lambda i: (2, i, 0)),
            rows_of(rows, D),
            pl.BlockSpec((local, LANES), lambda i: (0, 3 * D // LANES)),
        ],
        out_specs=[
            rows_of(local, 3 * D),
            rows_of(local, D),
            rows_of(local, 2 * FS),
            rows_of(FS // members, D),
            rows_of(local, 2 * FF),
            rows_of(local, FF),
            rows_of(rows, D),
            full(experts, local),
            full(2, local),
        ],
    )(last_sum, dense_sum, so_sum, expert_sum, expert_sum, grad_x, last_sum)
    return (
        output[None],
        grad_x[None],
        gains[0],
        grad_qkv,
        grad_out,
        gains[1],
        grad_router.T,
        grad_si,
        grad_so,
        grad_ei[None],
        grad_eo.T[None],
    )


def solution(mesh):
    row_spec = P("fsdp", "ctx", None)
    flat = P("fsdp", None)
    return jax.shard_map(
        on_device,
        mesh=mesh,
        in_specs=(
            row_spec,
            row_spec,
            P("fsdp"),
            P(),
            row_spec,
            P("fsdp"),
            flat,
            flat,
            P("fsdp"),
            flat,
            flat,
            flat,
            P("ctx", "fsdp", None),
            P("ctx", None, "fsdp"),
        ),
        out_specs=(
            row_spec,
            row_spec,
            P("fsdp"),
            flat,
            flat,
            P("fsdp"),
            flat,
            flat,
            flat,
            P("ctx", "fsdp", None),
            P("ctx", None, "fsdp"),
        ),
        check_vma=False,
    )
```

```python
import functools

import jax
import jax.numpy as jnp
from jax import lax
from jax.experimental import pallas as pl
from jax.experimental.pallas import tpu as pltpu
from jax.sharding import PartitionSpec as P

D = 768
HEADS = 12
HEAD_DIM = 64
FF = 2048
FS = 2048
LANES = 128
CHUNK = 256
PACKED = 3 * D + LANES
norm_eps = 1e-06
F32 = jnp.float32
BF16 = jnp.bfloat16


def dot(a, b):
    return jnp.dot(a, b, preferred_element_type=F32)


def dot_nt(a, b):
    return lax.dot_general(a, b, (((1,), (1,)), ((), ())), preferred_element_type=F32)


def dot_tn(a, b):
    return lax.dot_general(a, b, (((0,), (0,)), ((), ())), preferred_element_type=F32)


def call(kernel, outs, *, flops, nbytes, limit=56, **kw):
    return pl.pallas_call(
        kernel,
        out_shape=outs,
        compiler_params=pltpu.CompilerParams(vmem_limit_bytes=limit << 20),
        cost_estimate=pl.CostEstimate(
            flops=int(flops), bytes_accessed=int(nbytes), transcendentals=0
        ),
        **kw,
    )


def comm_call(kernel, outs, number, *, nbytes, limit=60, **kw):
    return pl.pallas_call(
        kernel,
        out_shape=outs,
        compiler_params=pltpu.CompilerParams(
            collective_id=number, has_side_effects=True, vmem_limit_bytes=limit << 20
        ),
        cost_estimate=pl.CostEstimate(flops=0, bytes_accessed=int(nbytes), transcendentals=0),
        **kw,
    )


def shape(dims, dtype):
    return jax.ShapeDtypeStruct(dims, dtype)


def lanes_of(rows, width=LANES):
    return lax.broadcasted_iota(jnp.int32, (rows, width), 1)


def first_heads(n_ctx, slot_dev):
    share = HEADS * slot_dev // n_ctx
    return [min(share * d // slot_dev, HEADS - 2) for d in range(n_ctx)]


def partner(t, lane):
    return jnp.where(lane % 64 < 32, pltpu.roll(t, 96, 1), pltpu.roll(t, 32, 1))


def in_parts(v):
    high = v.astype(BF16)
    rest = v - high.astype(F32)
    mid = rest.astype(BF16)
    low = (rest - mid.astype(F32)).astype(BF16)
    return high.astype(F32), mid.astype(F32), low.astype(F32)


def part_lanes(v, lane):
    high, mid, low = in_parts(v)
    zero = jnp.zeros((), F32)
    return jnp.where(
        lane == 0, high, jnp.where(lane == 1, mid, jnp.where(lane == 2, low, zero))
    ).astype(BF16)


def picks(target_ref, places):
    rows = target_ref.shape[0]
    place = lanes_of(rows, places)
    return tuple(
        jnp.where(place == target_ref[:, k : k + 1], 1.0, 0.0).astype(BF16) for k in range(2)
    )


def flipped(index, mask):
    for b in range(mask.bit_length()):
        if mask >> b & 1:
            index = index + (1 << b) - 2 * (1 << b) * (index // (1 << b) % 2)
    return index


def mirrored(members):
    bits = members.bit_length() - 1
    return [int(format(j, "b").zfill(bits)[::-1], 2) for j in range(members)]


def shard_rows(members, shard):
    fsdp = lax.axis_index("fsdp")
    return [pl.multiple_of(flipped(fsdp, m) * shard, 16) for m in mirrored(members)]


def remote(source, target, send_sem, recv_sem, peer):
    return pltpu.make_async_remote_copy(
        src_ref=source,
        dst_ref=target,
        send_sem=send_sem,
        recv_sem=recv_sem,
        device_id=peer,
        device_id_type=pl.DeviceIdType.MESH,
    )


def greet(peers):
    barrier = pltpu.get_barrier_semaphore()
    for peer in peers:
        pl.semaphore_signal(barrier, inc=1, device_id=peer, device_id_type=pl.DeviceIdType.MESH)
    pl.semaphore_wait(barrier, len(peers))


def mates_of(members):
    ctx, fsdp = lax.axis_index("ctx"), lax.axis_index("fsdp")
    return [(ctx, flipped(fsdp, 1 << b)) for b in range(members.bit_length() - 1)]


def row_peers(n):
    ctx, fsdp = lax.axis_index("ctx"), lax.axis_index("fsdp")
    return [(lax.rem(ctx + d, n), fsdp) for d in range(1, n)]


def loop(body, low, high):
    lax.fori_loop(low, high, lambda s, carry: (body(s), carry)[1], 0)


def add_into(target, j, other):
    target[j] = (target[j].astype(F32) + other[j].astype(F32)).astype(BF16)


def open_kernel(
    n,
    members,
    heads,
    experts,
    capacity,
    early,
    where_ref,
    length_ref,
    routes_ref,
    cot_ref,
    x_ref,
    w_ref,
    router_ref,
    gain_one_ref,
    gain_two_ref,
    cos_ref,
    sin_ref,
    recv_ref,
    in_ref,
    tail_ref,
    target_ref,
    dout_ref,
    dy_ref,
    dy_rest_ref,
    w_all,
    send,
    dy_send,
    small,
    small_all,
    gather_send,
    gather_recv,
    packet_send,
    packet_recv,
    dy_send_sem,
    dy_recv_sem,
    own_sem,
):
    ctx, fsdp = lax.axis_index("ctx"), lax.axis_index("fsdp")
    bits = members.bit_length() - 1
    peers = row_peers(n)
    mates = mates_of(members)
    shard = w_ref.shape[0]
    rows = x_ref.shape[0]
    row = lax.broadcasted_iota(jnp.int32, (LANES, shard), 0)
    gains = jnp.where(
        row == experts,
        gain_one_ref[...].astype(F32),
        jnp.where(row == experts + 1, gain_two_ref[...].astype(F32), 0.0),
    )
    small[...] = gains.T
    small[:, 0:experts] = router_ref[...].astype(F32)
    small_all[fsdp] = small[...].astype(BF16)
    for part in range(3):
        w_all[part, fsdp] = w_ref[:, part * D : (part + 1) * D]
    greet(peers + mates)

    def gather_copy(p, b, mask):
        buffer = small_all if p == 3 else w_all.at[p]
        spot = flipped(fsdp, mask)
        return remote(
            buffer.at[spot],
            buffer.at[spot],
            gather_send.at[p, b, mask],
            gather_recv.at[p, b, mask],
            mates[b],
        )

    def gather_wait(p, b, mask):
        buffer = small_all if p == 3 else w_all.at[p]
        spot = flipped(fsdp, mask | 1 << b)
        remote(
            buffer.at[spot],
            buffer.at[spot],
            gather_send.at[p, b, mask],
            gather_recv.at[p, b, mask],
            mates[b],
        ).wait_recv()

    for p in (3, 0, 1, 2):
        for b in reversed(range(bits)):
            gather_copy(p, b, 0).start()

    def gather_rest(p):
        masks = [0]
        for b in reversed(range(bits)):
            for mask in masks[1:]:
                gather_copy(p, b, mask).start()
            for mask in masks:
                gather_wait(p, b, mask)
            masks = masks + [mask | 1 << b for mask in masks]

    lane = lanes_of(rows)
    hot = [jnp.where(lane == routes_ref[:, k : k + 1], 1.0, 0.0) for k in range(2)]
    below = jnp.where(
        lanes_of(rows, rows) < lax.broadcasted_iota(jnp.int32, (rows, rows), 0), 1.0, 0.0
    )
    before = dot(below.astype(BF16), (hot[0] + hot[1]).astype(BF16))
    place = [
        routes_ref[:, k : k + 1] * capacity
        + jnp.sum(hot[k] * before, axis=-1, keepdims=True).astype(jnp.int32)
        for k in range(2)
    ]
    for k in range(2):
        target_ref[:, k : k + 1] = place[k]
    position = where_ref[ctx] * rows + lax.broadcasted_iota(jnp.int32, (rows, D), 0)
    dout = jnp.where(position < length_ref[0], cot_ref[...].astype(F32), 0.0).astype(BF16)
    dout_ref[...] = dout
    places = experts * capacity
    spot = lanes_of(rows, places)
    pick = jnp.where((spot == place[0]) | (spot == place[1]), 1.0, 0.0).astype(BF16)
    packed = dot_tn(pick, dout).astype(BF16)
    block = places // n
    for p in range(n):
        dy_send[p] = packed[p * block : p * block + early]
        dy_rest_ref[p] = packed[p * block + early : (p + 1) * block]
    own = [
        pltpu.make_async_copy(dy_send.at[ctx], dy_ref.at[ctx], own_sem.at[3]),
    ]
    own[0].start()
    copies = [
        remote(dy_send.at[p[0]], dy_ref.at[ctx], dy_send_sem.at[d], dy_recv_sem.at[d], p)
        for d, p in enumerate(peers)
    ]
    for c in copies:
        c.start()

    x = x_ref[...].astype(F32)
    inv = lax.rsqrt(jnp.mean(x * x, axis=-1, keepdims=True) + norm_eps)
    gather_rest(3)
    tail = small_all[...].reshape(D, LANES).astype(F32).T
    tail_ref[...] = tail
    attn_in = (x * inv * tail[experts : experts + 1, :]).astype(BF16)
    in_ref[...] = attn_in
    cos, sin = cos_ref[...], sin_ref[...]
    for part in range(3):
        gather_rest(part)
        y = dot(attn_in, w_all[part].reshape(D, D))
        groups = []
        for g in range(D // LANES):
            t = y[:, g * LANES : (g + 1) * LANES]
            if part < 2:
                t = t * cos + partner(t, lane) * sin
            groups.append(t)
        turned = [pltpu.roll(t, 64, 1) for t in groups]
        for d, head in enumerate(heads):
            g = head // 2
            if head % 2 == 0:
                packet = groups[g]
            else:
                packet = jnp.where(lane < 64, turned[g], turned[g + 1])
            send[part, d] = packet.astype(BF16)
        own.append(
            pltpu.make_async_copy(
                send.at[part, ctx], recv_ref.at[part, ctx], own_sem.at[part]
            )
        )
        own[-1].start()
        for d, p in enumerate(peers):
            copies.append(
                remote(
                    send.at[part, p[0]],
                    recv_ref.at[part, ctx],
                    packet_send.at[part, d],
                    packet_recv.at[part, d],
                    p,
                )
            )
            copies[-1].start()
    for c in copies + own:
        c.wait()
    for p in range(4):
        masks = [0]
        for b in reversed(range(bits)):
            for mask in masks:
                gather_copy(p, b, mask).wait_send()
            masks = masks + [mask | 1 << b for mask in masks]


def stack_rows(stack_ref, block, lane):
    rows = block.shape[0]
    zero = jnp.zeros((), block.dtype)
    stack_ref[0:rows, :] = jnp.where(lane < 64, block, zero)
    stack_ref[rows : 2 * rows, :] = jnp.where(lane >= 64, block, zero)


def unstack_rows(stack_ref, block, offset, lane):
    rows = stack_ref.shape[0] // 2
    stack_ref[...] = jnp.zeros_like(stack_ref)
    stack_ref[pl.ds(offset, block.shape[0]), :] = block
    return jnp.where(lane < 64, stack_ref[0:rows, :], stack_ref[rows : 2 * rows, :])


def key_limits(share, rows, q_block, offset, length):
    row = lax.broadcasted_iota(jnp.int32, (1, share), 1) + offset
    row = jnp.where(row >= rows, row - rows, row)
    return jnp.minimum(q_block * rows + row + 1, length)


def attend_kernel(n, share, sc, recv_ref, out_ref, keep_ref, lse_ref, stack, scores, back):
    q_block = pl.program_id(0)
    rows = recv_ref.shape[2]
    offset = pl.multiple_of(sc[n], 64)
    length = sc[n + 1]
    lane = lanes_of(rows)
    stack_rows(stack, recv_ref[0, sc[q_block]] * 0.125, lane)
    query = stack[pl.ds(offset, share), :]
    limit = key_limits(share, rows, q_block, offset, length)
    key_row = lax.broadcasted_iota(jnp.int32, (rows, share), 0)
    blocks = jnp.minimum(q_block + 1, (length + rows - 1) // rows)

    def score_step(j, top):
        keys = recv_ref[1, sc[j]]
        s = dot_nt(keys, query)
        s = jnp.where(key_row < limit - j * rows, s, -1e30)
        scores[j] = s
        return jnp.maximum(top, jnp.max(s, axis=0, keepdims=True))

    top = lax.fori_loop(0, blocks, score_step, jnp.full((1, share), -1e30, F32))

    def value_step(j, carry):
        total, acc = carry
        weights = jnp.exp(scores[j] - top)
        total = total + jnp.sum(weights, axis=0, keepdims=True)
        values = recv_ref[2, sc[j]]
        return total, acc + dot_tn(values, weights.astype(BF16))

    total, acc = lax.fori_loop(
        0, blocks, value_step, (jnp.zeros((1, share), F32), jnp.zeros((LANES, share), F32))
    )
    acc = acc / total
    keep_ref[0] = acc
    lse_ref[0] = top + jnp.log(total)
    out_ref[0] = unstack_rows(back, acc.T, offset, lane).astype(BF16)


def attend_back_kernel(
    n, share, sc, recv_ref, grad_ref, keep_ref, lse_ref, out_ref, stack, gstack, dkeys, dvalues, back
):
    q_block = pl.program_id(0)
    rows = recv_ref.shape[2]
    offset = pl.multiple_of(sc[n], 64)
    length = sc[n + 1]
    lane = lanes_of(rows)
    source = sc[q_block]

    @pl.when(q_block == 0)
    def _():
        dkeys[...] = jnp.zeros_like(dkeys)
        dvalues[...] = jnp.zeros_like(dvalues)

    stack_rows(stack, recv_ref[0, source] * 0.125, lane)
    query = stack[pl.ds(offset, share), :]
    stack_rows(gstack, grad_ref[source], lane)
    grad = gstack[pl.ds(offset, share), :]
    lse = lse_ref[0]
    delta = jnp.sum(grad.astype(F32).T * keep_ref[0], axis=0, keepdims=True)
    limit = key_limits(share, rows, q_block, offset, length)
    key_row = lax.broadcasted_iota(jnp.int32, (rows, share), 0)
    blocks = jnp.minimum(q_block + 1, (length + rows - 1) // rows)

    def step(j, acc):
        keys = recv_ref[1, sc[j]]
        values = recv_ref[2, sc[j]]
        s = dot_nt(keys, query)
        weights = jnp.exp(jnp.where(key_row < limit - j * rows, s, -1e30) - lse)
        dweights = dot_nt(values, grad)
        dscores = (weights * (dweights - delta)).astype(BF16)
        dkeys[j] += dot(dscores, query)
        dvalues[j] += dot(weights.astype(BF16), grad)
        return acc + dot_tn(keys, dscores)

    acc = lax.fori_loop(0, blocks, step, jnp.zeros((LANES, share), F32))
    dquery = unstack_rows(back, acc.T * 0.125, offset, lane)
    out_ref[0, source] = dquery.astype(BF16)

    @pl.when(q_block == n - 1)
    def _():
        def flush(j, carry):
            out_ref[1, sc[j]] = dkeys[j].astype(BF16)
            out_ref[2, sc[j]] = dvalues[j].astype(BF16)
            return carry

        lax.fori_loop(0, n, flush, 0)


def middle_kernel(
    n,
    heads,
    experts,
    attended_ref,
    w_ref,
    x_ref,
    tail_ref,
    routes_ref,
    target_ref,
    came_ref,
    residual_ref,
    in_ref,
    gates_ref,
    rows_ref,
    outgoing,
    came_send,
    came_recv,
    send_sem,
    recv_sem,
    own_sem,
):
    ctx = lax.axis_index("ctx")
    peers = row_peers(n)
    greet(peers)
    own = pltpu.make_async_copy(attended_ref.at[ctx], came_ref.at[ctx], own_sem.at[0])
    own.start()
    copies = [
        remote(attended_ref.at[p[0]], came_ref.at[ctx], came_send.at[d], came_recv.at[d], p)
        for d, p in enumerate(peers)
    ]
    for c in copies:
        c.start()
    pick = picks(target_ref, rows_ref.shape[0])
    lane = lanes_of(x_ref.shape[0])
    total = x_ref[...].astype(F32)
    for c in copies:
        c.wait()
    own.wait()
    for d, head in enumerate(heads):
        total = total + dot(came_ref[d], w_ref[64 * head : 64 * head + LANES, :])
    residual_ref[...] = total
    inv = lax.rsqrt(jnp.mean(total * total, axis=-1, keepdims=True) + norm_eps)
    ffn_in = (total * inv * tail_ref[experts + 1 : experts + 2, :]).astype(BF16)
    in_ref[...] = ffn_in
    logits = dot_nt(ffn_in, tail_ref[...].astype(BF16))
    chosen = [
        jnp.sum(jnp.where(lane == routes_ref[:, k : k + 1], logits, 0.0), axis=-1, keepdims=True)
        for k in range(2)
    ]
    top = jnp.maximum(chosen[0], chosen[1])
    raised = [jnp.exp(c - top) for c in chosen]
    gates = [r / (raised[0] + raised[1]) for r in raised]
    gates_ref[...] = jnp.where(lane == 0, gates[0], gates[1])
    outgoing[:, 0:D] = dot_tn(pick[0] + pick[1], ffn_in).astype(BF16)
    outgoing[:, D:] = (
        dot_tn(pick[0], part_lanes(gates[0], lane)) + dot_tn(pick[1], part_lanes(gates[1], lane))
    ).astype(BF16)
    block = outgoing.shape[0] // n

    def block_at(p):
        return pl.ds(pl.multiple_of(p * block, 16), block)

    own = pltpu.make_async_copy(
        outgoing.at[block_at(ctx)], rows_ref.at[block_at(ctx)], own_sem.at[1]
    )
    own.start()
    copies = [
        remote(
            outgoing.at[block_at(p[0])],
            rows_ref.at[block_at(ctx)],
            send_sem.at[d],
            recv_sem.at[d],
            p,
        )
        for d, p in enumerate(peers)
    ]
    for c in copies:
        c.start()
    for c in copies:
        c.wait()
    own.wait()


def gated(g, u, da):
    sig = 1.0 / (1.0 + jnp.exp(-g))
    silu = g * sig
    return silu * u, da * u * sig * (1.0 + g * (1.0 - sig)), da * silu


def expert_kernel(
    x_ref,
    first_ref,
    rest_ref,
    wg_ref,
    wu_ref,
    wt_ref,
    dx_ref,
    res_ref,
    mid_ref,
    dy_ref,
    dx_acc,
    res_acc,
    dgate,
):
    c = pl.program_id(0)

    @pl.when(c == 0)
    def _():
        res_acc[...] = jnp.zeros_like(res_acc)
        dx_acc[...] = jnp.zeros_like(dx_acc)
        dgate[...] = jnp.zeros_like(dgate)
        n, early = first_ref.shape[0:2]
        block = early + rest_ref.shape[1]
        for p in range(n):
            dy_ref[p * block : p * block + early] = first_ref[p]
            dy_ref[p * block + early : (p + 1) * block] = rest_ref[p]

    x, dy = x_ref[:, 0:D], dy_ref[...]
    gate = jnp.sum(x_ref[:, D:].astype(F32), axis=-1, keepdims=True)
    wg, wu, wt = wg_ref[...], wu_ref[...], wt_ref[...]
    da = dot(dy, wt)
    act, dg, du = gated(dot(x, wg), dot(x, wu), da * gate)
    dgate[...] += jnp.sum(act * da, axis=-1, keepdims=True)
    mid_ref[2] = (act * gate).astype(BF16)
    act, dg, du = act.astype(BF16), dg.astype(BF16), du.astype(BF16)
    res_acc[...] += dot_nt(act, wt)
    dx_acc[...] += dot_nt(dg, wg) + dot_nt(du, wu)
    mid_ref[0] = dg
    mid_ref[1] = du

    @pl.when(c == pl.num_programs(0) - 1)
    def _():
        res_ref[...] = res_acc[...].astype(BF16)
        dx_ref[:, 0:D] = dx_acc[...].astype(BF16)
        dx_ref[:, D:] = part_lanes(dgate[:, 0:1], lanes_of(dgate.shape[0]))


def ring_split(rows, columns, pieces):
    down = 1
    while 2 * down <= pieces and rows % (32 * down) == 0:
        down *= 2
    across = pieces // down
    width = -(-columns // (LANES * across)) * LANES
    return down, across, rows // down, width


def ring_place(position, n):
    half = n // 2
    return jnp.where(position < half, 2 * position, 2 * (n - 1 - position) + 1)


def shared_kernel(
    n,
    members,
    heads,
    experts,
    send_ref,
    in_ref,
    dout_ref,
    residual_ref,
    gates_ref,
    routes_ref,
    target_ref,
    tail_ref,
    w_ref,
    wide_ref,
    back_ref,
    recv_ref,
    res_ref,
    dres_ref,
    branch_ref,
    dlogits_ref,
    dgain_ref,
    a_keep,
    a_give,
    b_keep,
    b_give,
    came,
    packets,
    mids,
    dx_acc,
    a_all,
    b_all,
    a_caught,
    b_caught,
    raw,
    xt,
    gate_buf,
    up_buf,
    back_buf,
    send_sem,
    recv_sem,
    own_sem,
    packet_send,
    packet_recv,
    a_sem,
    b_sem,
    w_sem,
):
    ctx, fsdp = lax.axis_index("ctx"), lax.axis_index("fsdp")
    bits = members.bit_length() - 1
    peers = row_peers(n)
    mate = mates_of(members)[0]
    greet(peers + [mate])
    block = send_ref.shape[0] // n

    def block_at(p):
        return pl.ds(pl.multiple_of(p * block, 16), block)

    own = pltpu.make_async_copy(send_ref.at[block_at(ctx)], came.at[block_at(ctx)], own_sem.at[0])
    own.start()
    copies = [
        remote(
            send_ref.at[block_at(p[0])], came.at[block_at(ctx)], send_sem.at[d], recv_sem.at[d], p
        )
        for d, p in enumerate(peers)
    ]
    for c in copies:
        c.start()

    steps = FS // CHUNK

    def fetch(c, slot):
        at = pl.ds(pl.multiple_of(c * CHUNK, CHUNK), CHUNK)
        up = pl.ds(pl.multiple_of(FS + c * CHUNK, CHUNK), CHUNK)
        return [
            pltpu.make_async_copy(wide_ref.at[:, at], gate_buf.at[slot], w_sem.at[slot, 0]),
            pltpu.make_async_copy(wide_ref.at[:, up], up_buf.at[slot], w_sem.at[slot, 1]),
            pltpu.make_async_copy(back_ref.at[at], back_buf.at[slot], w_sem.at[slot, 2]),
        ]

    for f in fetch(0, 0):
        f.start()
    res_ref[...] = jnp.zeros_like(res_ref)
    dx_acc[...] = jnp.zeros_like(dx_acc)
    b_shard = FS // members
    piece = b_all.shape[2]

    def ffn_step(c):
        slot = lax.rem(c, 2)
        for f in fetch(c, slot):
            f.wait()

        @pl.when(c + 1 < steps)
        def _():
            for f in fetch(c + 1, 1 - slot):
                f.start()

        x, dy = in_ref[...], dout_ref[...]
        wg, wu, wo = gate_buf[slot], up_buf[slot], back_buf[slot]
        act, dg, du = gated(dot(x, wg), dot(x, wu), dot_nt(dy, wo))
        act, dg, du = act.astype(BF16), dg.astype(BF16), du.astype(BF16)
        res_ref[...] += dot(act, wo)
        dx_acc[...] += dot_nt(dg, wg) + dot_nt(du, wu)
        mids[c] = dg
        mids[steps + c] = du
        value = dot_tn(act, dy).astype(BF16)
        span = min(piece, CHUNK)
        for u in range(CHUNK // span):
            row = c * CHUNK + u * span
            t = row // b_shard
            j = sum(
                lax.rem(fsdp // (1 << b) + t // (1 << b), 2) * (1 << (bits - 1 - b))
                for b in range(bits)
            )
            inside = lax.rem(row, b_shard)
            top = pl.multiple_of(lax.rem(inside, piece), 16)
            b_all[inside // piece, j, pl.ds(top, span), :] = value[u * span : (u + 1) * span]

    loop(ffn_step, 0, steps)
    half, quarter = members // 2, members // 4

    def a_swap(i):
        return remote(
            a_all.at[i, pl.ds(half, half)], a_caught.at[i], a_sem.at[i, 0], a_sem.at[i, 1], mate
        )

    def b_swap(i):
        return remote(
            b_all.at[i, pl.ds(half, half)], b_caught.at[i], b_sem.at[i, 0], b_sem.at[i, 1], mate
        )

    for i in range(2):
        b_swap(i).start()
    rows = shard_rows(members, D // members)
    shard = D // members
    raw[...] = in_ref[...].T
    for j in range(members):
        xt[j * shard : (j + 1) * shard, :] = raw[pl.ds(rows[j], shard), :]
    for i in range(2):

        def grad_step(c, i=i):
            value = dot(xt[...], mids[i * steps + c]).astype(BF16)
            column = pl.ds(pl.multiple_of(c * CHUNK, CHUNK), CHUNK)
            for j in range(members):
                a_all[i, j, :, column] = value[j * shard : (j + 1) * shard]

        loop(grad_step, 0, steps)
        a_swap(i).start()
    for i in range(2):
        b_swap(i).wait_recv()
        for j in range(half):
            total = (b_all[i, j].astype(F32) + b_caught[i, j].astype(F32)).astype(BF16)
            if j < quarter:
                b_keep[i, j] = total
            else:
                b_give[i, j - quarter] = total
    for c in copies:
        c.wait()
    own.wait()

    pick = picks(target_ref, came.shape[0])
    gates = [gates_ref[:, k : k + 1] for k in range(2)]
    parts = came[:, D:]
    dgate = [jnp.sum(dot(pick[k], parts), axis=-1, keepdims=True) for k in range(2)]
    mean = gates[0] * dgate[0] + gates[1] * dgate[1]
    lane = lanes_of(pick[0].shape[0])
    dlogits = sum(
        jnp.where(lane == routes_ref[:, k : k + 1], gates[k] * (dgate[k] - mean), 0.0)
        for k in range(2)
    ).astype(BF16)
    dlogits_ref[...] = dlogits
    tail = tail_ref[...]
    dffn = dot(pick[0] + pick[1], came[:, 0:D]) + dx_acc[...] + dot(dlogits, tail.astype(BF16))
    residual = residual_ref[...]
    inv = lax.rsqrt(jnp.mean(residual * residual, axis=-1, keepdims=True) + norm_eps)
    scaled = dffn * tail[experts + 1 : experts + 2, :]
    total = jnp.mean(scaled * residual, axis=-1, keepdims=True)
    dres = dout_ref[...].astype(F32) + inv * scaled - residual * inv * inv * inv * total
    branch = dres.astype(BF16)
    branch_ref[...] = branch
    for d, head in enumerate(heads):
        packets[d] = dot_nt(branch, w_ref[64 * head : 64 * head + LANES, :]).astype(BF16)
    own = pltpu.make_async_copy(packets.at[ctx], recv_ref.at[ctx], own_sem.at[1])
    own.start()
    copies = [
        remote(packets.at[p[0]], recv_ref.at[ctx], packet_send.at[d], packet_recv.at[d], p)
        for d, p in enumerate(peers)
    ]
    for c in copies:
        c.start()
    dres_ref[...] = dres
    dgain_ref[...] = jnp.sum(dffn * residual * inv, axis=0, keepdims=True)
    for i in range(2):
        a_swap(i).wait_recv()
        for j in range(half):
            total = (a_all[i, j].astype(F32) + a_caught[i, j].astype(F32)).astype(BF16)
            if j < quarter:
                a_keep[i, j] = total
            else:
                a_give[i, j - quarter] = total
    for c in copies:
        c.wait()
    own.wait()
    for i in range(2):
        a_swap(i).wait_send()
        b_swap(i).wait_send()


def back_exchange_kernel(
    n,
    members,
    heads,
    send_ref,
    x_ref,
    dy_ref,
    came_ref,
    branch_ref,
    in_ref,
    dlogits_ref,
    residual_ref,
    shared_ref,
    gates_ref,
    target_ref,
    live_ref,
    res_ref,
    mid_ref,
    recv_ref,
    sum_ref,
    out_grad_ref,
    router_ref,
    output_ref,
    give,
    caught,
    crossed,
    raw,
    xt,
    dyt,
    acc,
    mids,
    send_sem,
    recv_sem,
    own_sem,
    give_sem,
    caught_sem,
    cross_sem,
    mid_sem,
):
    ctx = lax.axis_index("ctx")
    peers = row_peers(n)
    mates = mates_of(members)
    mate, far = mates[0], mates[1]
    greet(peers + [mate, far])
    own = pltpu.make_async_copy(send_ref.at[:, ctx], recv_ref.at[:, ctx], own_sem)
    own.start()
    copies = [
        remote(send_ref.at[:, p[0]], recv_ref.at[:, ctx], send_sem.at[d], recv_sem.at[d], p)
        for d, p in enumerate(peers)
    ]
    for c in copies:
        c.start()

    steps = mid_ref.shape[2] // CHUNK
    parts = mid_ref.shape[0]

    def fetch(i, c, slot):
        column = pl.multiple_of(c * CHUNK, CHUNK)
        return pltpu.make_async_copy(
            mid_ref.at[i, :, pl.ds(column, CHUNK)], mids.at[slot], mid_sem.at[slot]
        )

    fetch(0, 0, 0).start()
    shard = D // members
    half = members // 2
    rows = shard_rows(members, shard)

    def turned(value, target):
        raw[...] = value.T
        for j in range(members):
            target[j * shard : (j + 1) * shard, :] = raw[pl.ds(rows[j], shard), :]

    turned(x_ref[:, 0:D], xt)
    turned(dy_ref[...], dyt)

    def swap(i):
        return remote(give.at[i], caught.at[i], give_sem.at[i], caught_sem.at[i], mate)

    quarter = members // 4
    cross = remote(
        sum_ref.at[0, pl.ds(quarter, quarter)], crossed, cross_sem.at[0], cross_sem.at[1], far
    )
    for i in range(parts):
        left = xt if i < 2 else dyt

        def step(c, left=left, i=i):
            slot = lax.rem(c, 2)
            fetch(i, c, slot).wait()

            @pl.when(c + 1 < steps)
            def _():
                fetch(i, c + 1, 1 - slot).start()

            value = dot(left[...], mids[slot]).astype(BF16)
            column = pl.ds(pl.multiple_of(c * CHUNK, CHUNK), CHUNK)
            for j in range(half):
                sum_ref[i, j, :, column] = value[j * shard : (j + 1) * shard]
                give[i, j, :, column] = value[(half + j) * shard : (half + j + 1) * shard]

        loop(step, 0, steps)
        if i + 1 < parts:
            fetch(i + 1, 0, 0).start()
        swap(i).start()
        if i > 0:
            swap(i - 1).wait_recv()
            for j in range(half):
                add_into(sum_ref.at[i - 1], j, caught.at[i - 1])
        if i == 1:
            cross.start()

    acc[...] = jnp.zeros_like(acc)
    branch = branch_ref[...]
    for d, head in enumerate(heads):
        acc[64 * head : 64 * head + LANES, :] += dot_tn(came_ref[d], branch)
    for j in range(members):
        out_grad_ref[j] = acc[pl.ds(rows[j], shard), :].astype(BF16)
    router_ref[...] = dot_tn(in_ref[...], dlogits_ref[...])
    pick = picks(target_ref, res_ref.shape[0])
    came = res_ref[...]
    mixture = gates_ref[:, 0:1] * dot(pick[0], came) + gates_ref[:, 1:2] * dot(pick[1], came)
    output_ref[...] = (live_ref[...] * (residual_ref[...] + shared_ref[...] + mixture)).astype(BF16)
    swap(parts - 1).wait_recv()
    for j in range(half):
        add_into(sum_ref.at[parts - 1], j, caught.at[parts - 1])
    for c in copies:
        c.wait()
    own.wait()
    cross.wait()
    for j in range(quarter):
        add_into(sum_ref.at[0], j, crossed)
    for i in range(parts):
        swap(i).wait_send()


def last_kernel(
    n,
    members,
    heads,
    experts,
    splits,
    recv_ref,
    cos_ref,
    sin_ref,
    in_ref,
    x_ref,
    w_ref,
    tail_ref,
    dres_ref,
    out_grad_ref,
    router_ref,
    dgain_ref,
    a_ref,
    a_other,
    b_ref,
    b_other,
    e_ref,
    x_out,
    a_out,
    b_out,
    c_out,
    e_out,
    *scratch,
):
    bits = members.bit_length() - 1
    streams = len(splits)
    own, full, back_up, back_down = (scratch[k * streams : (k + 1) * streams] for k in range(4))
    back = (back_up, back_down)
    scratch = scratch[4 * streams :]
    packs, scratch = scratch[0:4], scratch[4:]
    caught = [scratch[4 * b : 4 * b + 4] for b in range(bits)]
    scratch = scratch[4 * bits :]
    e_caught, scratch = scratch[0 : bits - 1], scratch[bits - 1 :]
    dproj, raw, turned, small = scratch[0:4]
    send_sem, recv_sem, level_send, level_recv, e_send, e_recv = scratch[4:]
    ctx, fsdp = lax.axis_index("ctx"), lax.axis_index("fsdp")
    here = jnp.where(ctx % 2 == 0, ctx // 2, n - 1 - ctx // 2)
    ahead = (ring_place(lax.rem(here + 1, n), n), fsdp)
    behind = (ring_place(lax.rem(here + n - 1, n), n), fsdp)
    mates = mates_of(members)
    greet([ahead, behind] + mates)
    shard = D // members
    parts = e_ref.shape[0]

    def level_copy(p, b):
        count = members >> (b + 1)
        return remote(
            packs[p].at[pl.ds(count, count)],
            caught[b][p],
            level_send.at[p, b],
            level_recv.at[p, b],
            mates[b],
        )

    def level_add(p, b):
        level_copy(p, b).wait_recv()
        for j in range(members >> (b + 1)):
            add_into(packs[p], j, caught[b][p])

    def level_next(p):
        level_add(p, 0)
        level_copy(p, 1).start()

    def e_copy(i, b):
        count = members >> (b + 1)
        source = e_ref if b == 1 or (b == 2 and i == 0) else e_caught[b - 2]
        return remote(
            source.at[i, pl.ds(count, count)],
            e_caught[b - 1].at[i],
            e_send.at[i, b - 1],
            e_recv.at[i, b - 1],
            mates[b],
        )

    def e_add(i, b):
        e_copy(i, b).wait_recv()
        source = e_ref if b == 1 or (b == 2 and i == 0) else e_caught[b - 2]
        for j in range(members >> (b + 1)):
            total = source[i, j].astype(F32) + e_caught[b - 1][i, j].astype(F32)
            if b == bits - 1:
                e_out[i] = total.astype(BF16)
            else:
                e_caught[b - 1][i, j] = total.astype(BF16)

    def tiles(i):
        down, across, height, width = splits[i][0:4]
        columns = splits[i][4]
        for p in range(down * across):
            r, c = p // across, p % across
            yield p, r * height, height, c * width, max(0, min(width, columns - c * width)), width

    def load(i, ref, skip=0, other=None):
        for p, top, height, start, have, width in tiles(i):
            if have > 0:
                value = ref[top : top + height, skip + start : skip + start + have]
                if other is not None:
                    added = other[top : top + height, skip + start : skip + start + have]
                    value = (value.astype(F32) + added.astype(F32)).astype(BF16)
                own[i][p, :, 0:have] = value
            if have < width:
                own[i][p, :, have:] = jnp.zeros((height, width - have), BF16)

    def save(i, ref, skip=0):
        for p, top, height, start, have, width in tiles(i):
            if have > 0:
                ref[top : top + height, skip + start : skip + start + have] = full[i][p, :, 0:have]

    long, short = n // 2, n - 1 - n // 2

    def hops(i, direction):
        return long if direction == i % 2 else short

    def place(direction, steps):
        return lax.rem(here + (steps if direction == 0 else 2 * n - steps), n)

    def copy(i, direction, step, source, target, slot):
        return remote(
            source.at[slot],
            target.at[slot],
            send_sem.at[i, direction, step],
            recv_sem.at[i, direction, step],
            ahead if direction == 0 else behind,
        )

    def first(i):
        for direction in range(2):
            slot = place(direction, hops(i, direction))
            copy(i, direction, 0, own[i], back[direction][i], slot).start()

    def reduce_step(i, s):
        for direction in range(2):
            count = hops(i, direction)
            if s < count:
                slot = place(direction, count - s)
                buffer = back[direction][i]
                copy(i, direction, s - 1, buffer, buffer, slot).wait_recv()
                add_into(buffer, slot, own[i])
                copy(i, direction, s, buffer, buffer, slot).start()

    def turn(i):
        for direction in range(2):
            buffer = back[direction][i]
            copy(i, direction, hops(i, direction) - 1, buffer, buffer, here).wait_recv()
        full[i][here] = (
            own[i][here].astype(F32) + back_up[i][here].astype(F32) + back_down[i][here].astype(F32)
        ).astype(BF16)
        for direction in range(2):
            copy(i, direction, long, full[i], full[i], here).start()

    def gather_step(i, s):
        for direction in range(2):
            if s < hops(i, direction):
                slot = place(1 - direction, s)
                copy(i, direction, long + s - 1, full[i], full[i], slot).wait_recv()
                copy(i, direction, long + s, full[i], full[i], slot).start()

    def end(i):
        for direction in range(2):
            count = hops(i, direction)
            slot = place(1 - direction, count)
            copy(i, direction, long + count - 1, full[i], full[i], slot).wait_recv()

    def drain(i):
        for direction in range(2):

            def sent(step, direction=direction):
                copy(i, direction, step, own[i], full[i], 0).wait_send()

            loop(sent, 0, hops(i, direction))
            loop(sent, long, long + hops(i, direction))

    def steps_of(i):
        done = [functools.partial(reduce_step, i, s) for s in range(1, long)]
        done.append(functools.partial(turn, i))
        done += [functools.partial(gather_step, i, s) for s in range(1, long)]
        done.append(functools.partial(end, i))
        return done

    for i in range(2):
        load(i, a_ref.at[i], 0, a_other.at[i])
        first(i)
    for i in range(2):
        load(2 + i, b_ref.at[i], 0, b_other.at[i])
        first(2 + i)
    waiting = [steps_of(i) for i in range(4)]

    def dense_step():
        for queue in waiting[0:4]:
            if queue:
                queue.pop(0)()

    rows = shard_rows(members, shard)
    raw[...] = in_ref[...].T
    for j in range(members):
        turned[j * shard : (j + 1) * shard, :] = raw[pl.ds(rows[j], shard), :]
    lane = lanes_of(x_ref.shape[0])
    cos, sin = cos_ref[...], sin_ref[...]
    for part in range(3):
        groups = [jnp.zeros(lane.shape, F32) for _ in range(D // LANES)]
        for d, head in enumerate(heads):
            g = head // 2
            packet = recv_ref[part, d].astype(F32)
            if head % 2 == 0:
                groups[g] = groups[g] + packet
            else:
                packet = pltpu.roll(packet, 64, 1)
                groups[g] = groups[g] + jnp.where(lane >= 64, packet, 0.0)
                groups[g + 1] = groups[g + 1] + jnp.where(lane < 64, packet, 0.0)
        for g, t in enumerate(groups):
            if part < 2:
                t = t.astype(BF16).astype(F32)
                t = t * cos - partner(t, lane) * sin
            dproj[:, part * D + g * LANES : part * D + (g + 1) * LANES] = t.astype(BF16)
        value = dot(turned[...], dproj[:, part * D : (part + 1) * D]).astype(BF16)
        for j in range(members):
            packs[part][j] = value[j * shard : (j + 1) * shard]
        level_copy(part, 0).start()
        if part > 0:
            level_next(part - 1)
    dense_step()
    dnorm = sum(
        dot_nt(dproj[:, part * D : (part + 1) * D], w_ref[part].reshape(D, D)) for part in range(3)
    )
    x = x_ref[...].astype(F32)
    gain = tail_ref[experts : experts + 1, :]
    inv = lax.rsqrt(jnp.mean(x * x, axis=-1, keepdims=True) + norm_eps)
    dgain_one = jnp.sum(dnorm * x * inv, axis=0, keepdims=True)
    row = lax.broadcasted_iota(jnp.int32, (LANES, D), 0)
    gains = jnp.where(row == experts, dgain_one, jnp.where(row == experts + 1, dgain_ref[...], 0.0))
    small[...] = router_ref[...] + gains.T
    for j in range(members):
        packs[3][j, :, 0:LANES] = small[pl.ds(rows[j], shard), :].astype(BF16)
        packs[3][j, :, LANES:] = out_grad_ref[j]
    level_copy(3, 0).start()
    level_next(2)
    scaled = dnorm * gain
    total = jnp.mean(scaled * x, axis=-1, keepdims=True)
    x_out[...] = dres_ref[...] + inv * scaled - x * inv * inv * inv * total
    level_next(3)
    for i in range(1, parts):
        e_copy(i, 1).start()

    for p in range(4):
        for b in range(1, bits):
            level_add(p, b)
            if b + 1 < bits:
                level_copy(p, b + 1).start()
        load(4 + p, packs[p].at[0])
        first(4 + p)
        dense_step()
        for queue in waiting[4:]:
            queue.pop(0)()
        waiting.append(steps_of(4 + p))
    while any(waiting):
        for i, queue in enumerate(waiting):
            if queue:
                queue.pop(0)()
                if not queue and i < 4:
                    if i < 2:
                        save(i, a_out, i * splits[0][4])
                    else:
                        height = splits[2][0] * splits[2][2]
                        save(i, b_out.at[pl.ds((i - 2) * height, height)])
        if not any(waiting[0:4]) and parts > 1:
            e_add(1, 1)
            parts = min(parts, 1)
    for p in range(4):
        save(4 + p, c_out, p * D)
    parts = e_ref.shape[0]
    for i in range(2, parts):
        e_add(i, 1)
    if bits == 2:
        e_out[0] = e_ref[0, 0]
    for b in range(2, bits):
        for i in range(parts):
            e_copy(i, b).start()
        for i in range(parts):
            e_add(i, b)
    for b in range(bits):
        for p in range(4):
            level_copy(p, b).wait_send()
    for b in range(1, bits):
        for i in range(1 if b == 1 else 0, parts):
            e_copy(i, b).wait_send()

    for i in range(streams):
        drain(i)


def widen_kernel(
    experts,
    late_ref,
    a_ref,
    b_ref,
    in_ref,
    back_ref,
    x_ref,
    small_ref,
    qkv_out,
    w_out,
    a_out,
    b_out,
    in_out,
    back_out,
    x_out,
    router_out,
    gains_out,
):
    qkv_out[...] = late_ref[:, 0 : 3 * D].astype(F32)
    w_out[...] = late_ref[:, PACKED:].astype(F32)
    a_out[...] = a_ref[...].astype(F32)
    b_out[...] = b_ref[...].astype(F32)
    in_out[:, 0:FF] = in_ref[0].astype(F32)
    in_out[:, FF:] = in_ref[1].astype(F32)
    back_out[...] = back_ref[0].astype(F32)
    x_out[...] = x_ref[...]

    @pl.when(pl.program_id(0) == 0)
    def _():
        small = small_ref[...].astype(F32).T
        router_out[...] = small[0:experts]
        gains_out[...] = small[experts : experts + 2]


def on_device(
    tokens,
    cotangent,
    lengths,
    position_block,
    routes,
    gain_attn,
    w_qkv,
    w_out,
    gain_ffn,
    w_router,
    w_shared_in,
    w_shared_out,
    w_expert_in,
    w_expert_out,
):
    n_ctx = lax.axis_size("ctx")
    ctx_index = lax.axis_index("ctx")
    rows = tokens.shape[1]
    local = w_qkv.shape[0]
    experts = w_router.shape[1]
    capacity = 3 * rows // experts
    places = experts * capacity
    members = D // local
    share = HEADS * rows // n_ctx
    heads = first_heads(n_ctx, rows)
    gather = functools.partial(lax.all_gather, axis_name="fsdp", axis=0, tiled=True)
    exchange = functools.partial(
        lax.all_to_all, axis_name="ctx", split_axis=0, concat_axis=0, tiled=True
    )
    x = tokens[0]
    length = lengths[0]

    out_weight = gather(w_out)
    weights = gather(
        jnp.concatenate([w_shared_in, w_expert_in[0], w_expert_out[0].T], axis=1)
    )
    shared_out = gather(w_shared_out)
    bits = members.bit_length() - 1

    query_pos = position_block[ctx_index] * rows + jnp.arange(rows, dtype=jnp.int32)
    live = (query_pos < length).astype(F32)[:, None]
    halves = HEAD_DIM // 2
    inverse = 10000.0 ** (-(jnp.arange(halves, dtype=F32) * 2.0 / HEAD_DIM))
    angles = query_pos.astype(F32)[:, None] * inverse[None, :]
    cos, sin = jnp.cos(angles), jnp.sin(angles)
    cos = jnp.concatenate([cos, cos, cos, cos], axis=1)
    sin = jnp.concatenate([-sin, sin, -sin, sin], axis=1)

    order = jnp.sum(
        jnp.where(
            position_block[None, :] == jnp.arange(n_ctx, dtype=jnp.int32)[:, None],
            jnp.arange(n_ctx, dtype=jnp.int32)[None, :],
            0,
        ),
        axis=1,
    )
    head_of = jnp.minimum(share * ctx_index // rows, HEADS - 2)
    offset = share * ctx_index - rows * head_of
    scalars = jnp.concatenate(
        [order, jnp.stack([offset.astype(jnp.int32), length.astype(jnp.int32)])]
    )

    whole = pl.BlockSpec(memory_space=pltpu.VMEM)
    scalar = pl.BlockSpec(memory_space=pltpu.SMEM)
    block = places // n_ctx
    early = block // 32 * 16
    recv, attn_in, tail, target, dout, dy_first, dy_rest, qkv_weight = comm_call(
        functools.partial(open_kernel, n_ctx, members, heads, experts, capacity, early),
        (
            shape((3, n_ctx, rows, LANES), BF16),
            shape((rows, D), BF16),
            shape((LANES, D), F32),
            shape((rows, 2), jnp.int32),
            shape((rows, D), BF16),
            shape((n_ctx, early, D), BF16),
            shape((n_ctx, block - early, D), BF16),
            shape((3, members, local, D), BF16),
        ),
        3,
        in_specs=[scalar] * 2 + [whole] * 9,
        out_specs=[whole] * 8,
        scratch_shapes=[
            pltpu.VMEM((3, n_ctx, rows, LANES), BF16),
            pltpu.VMEM((n_ctx, early, D), BF16),
            pltpu.VMEM((local, LANES), F32),
            pltpu.VMEM((members, local, LANES), BF16),
            pltpu.SemaphoreType.DMA((4, bits, members)),
            pltpu.SemaphoreType.DMA((4, bits, members)),
            pltpu.SemaphoreType.DMA((3, n_ctx - 1)),
            pltpu.SemaphoreType.DMA((3, n_ctx - 1)),
            pltpu.SemaphoreType.DMA((n_ctx - 1,)),
            pltpu.SemaphoreType.DMA((n_ctx - 1,)),
            pltpu.SemaphoreType.DMA((4,)),
        ],
        nbytes=150 << 20,
    )(
        position_block,
        lengths,
        routes[0],
        cotangent[0],
        x,
        w_qkv,
        w_router,
        gain_attn[None],
        gain_ffn[None],
        cos,
        sin,
    )
    dy_rest = exchange(dy_rest)

    packet = pl.BlockSpec((3, n_ctx, rows, LANES), lambda i, sc: (0, 0, 0, 0))
    block_of = lambda i, sc: (i, 0, 0)
    attended, kept, lse = call(
        functools.partial(attend_kernel, n_ctx, share),
        (
            shape((n_ctx, rows, LANES), BF16),
            shape((n_ctx, LANES, share), F32),
            shape((n_ctx, 1, share), F32),
        ),
        flops=2 * share * rows * n_ctx * n_ctx * LANES * 2,
        nbytes=5 << 20,
        grid_spec=pltpu.PrefetchScalarGridSpec(
            num_scalar_prefetch=1,
            grid=(n_ctx,),
            in_specs=[packet],
            out_specs=[
                pl.BlockSpec((1, rows, LANES), lambda i, sc: (sc[i], 0, 0)),
                pl.BlockSpec((1, LANES, share), block_of),
                pl.BlockSpec((1, 1, share), block_of),
            ],
            scratch_shapes=[
                pltpu.VMEM((2 * rows, LANES), BF16),
                pltpu.VMEM((n_ctx, rows, share), F32),
                pltpu.VMEM((2 * rows, LANES), F32),
            ],
        ),
    )(scalars, recv)
    attended, dy_rest = lax.optimization_barrier((attended, dy_rest))

    def full(*dims):
        return pl.BlockSpec(dims, lambda *at: (0,) * len(dims))

    came, residual, ffn_in, gates, x_rows = comm_call(
        functools.partial(middle_kernel, n_ctx, heads, experts),
        (
            shape((n_ctx, rows, LANES), BF16),
            shape((rows, D), F32),
            shape((rows, D), BF16),
            shape((rows, LANES), F32),
            shape((places, D + LANES), BF16),
        ),
        4,
        in_specs=[whole] * 6,
        out_specs=[whole] * 5,
        scratch_shapes=[pltpu.VMEM((places, D + LANES), BF16)]
        + [pltpu.SemaphoreType.DMA((n_ctx - 1,)) for _ in range(4)]
        + [pltpu.SemaphoreType.DMA((2,))],
        nbytes=100 << 20,
    )(attended, out_weight, x, tail, routes[0], target)

    half, quarter = members // 2, members // 4
    steps = FS // CHUNK
    wide = FF // CHUNK
    expert_dx, expert_res, expert_mid, dy_rows = call(
        expert_kernel,
        (
            shape((places, D + LANES), BF16),
            shape((places, D), BF16),
            shape((3, places, FF), BF16),
            shape((places, D), BF16),
        ),
        flops=2 * places * D * FF * 6,
        nbytes=24 << 20,
        grid=(wide,),
        in_specs=[
            full(places, D + LANES),
            full(n_ctx, early, D),
            full(n_ctx, block - early, D),
            pl.BlockSpec((D, CHUNK), lambda c: (0, 2 * steps + c)),
            pl.BlockSpec((D, CHUNK), lambda c: (0, 2 * steps + wide + c)),
            pl.BlockSpec((D, CHUNK), lambda c: (0, 2 * steps + 2 * wide + c)),
        ],
        out_specs=[
            full(places, D + LANES),
            full(places, D),
            pl.BlockSpec((3, places, CHUNK), lambda c: (0, 0, c)),
            full(places, D),
        ],
        scratch_shapes=[
            pltpu.VMEM((places, D), F32),
            pltpu.VMEM((places, D), F32),
            pltpu.VMEM((places, LANES), F32),
        ],
    )(x_rows, dy_first, dy_rest, weights, weights, weights)
    b_rows = FS // members // 2
    anywhere = pl.BlockSpec(memory_space=pl.ANY)
    (
        branch_recv,
        shared_res,
        dres,
        branch,
        dlogits,
        dgain_two,
        dense_keep,
        dense_give,
        so_keep,
        so_give,
    ) = comm_call(
        functools.partial(shared_kernel, n_ctx, members, heads, experts),
        (
            shape((n_ctx, rows, LANES), BF16),
            shape((rows, D), F32),
            shape((rows, D), F32),
            shape((rows, D), BF16),
            shape((rows, LANES), BF16),
            shape((1, D), F32),
        )
        + (shape((2, quarter, local, FS), BF16),) * 2
        + (shape((2, quarter, b_rows, D), BF16),) * 2,
        2,
        in_specs=[whole] * 9 + [anywhere] * 2,
        out_specs=[whole] * 10,
        scratch_shapes=[
            pltpu.VMEM((places, D + LANES), BF16),
            pltpu.VMEM((n_ctx, rows, LANES), BF16),
            pltpu.VMEM((2 * steps, rows, CHUNK), BF16),
            pltpu.VMEM((rows, D), F32),
            pltpu.VMEM((2, members, local, FS), BF16),
            pltpu.VMEM((2, members, b_rows, D), BF16),
            pltpu.VMEM((2, half, local, FS), BF16),
            pltpu.VMEM((2, half, b_rows, D), BF16),
            pltpu.VMEM((D, rows), BF16),
            pltpu.VMEM((D, rows), BF16),
            pltpu.VMEM((2, D, CHUNK), BF16),
            pltpu.VMEM((2, D, CHUNK), BF16),
            pltpu.VMEM((2, CHUNK, D), BF16),
            pltpu.SemaphoreType.DMA((n_ctx - 1,)),
            pltpu.SemaphoreType.DMA((n_ctx - 1,)),
            pltpu.SemaphoreType.DMA((2,)),
            pltpu.SemaphoreType.DMA((n_ctx - 1,)),
            pltpu.SemaphoreType.DMA((n_ctx - 1,)),
            pltpu.SemaphoreType.DMA((2, 2)),
            pltpu.SemaphoreType.DMA((2, 2)),
            pltpu.SemaphoreType.DMA((2, 3)),
        ],
        nbytes=150 << 20,
    )(
        expert_dx,
        ffn_in,
        dout,
        residual,
        gates,
        routes[0],
        target,
        tail,
        out_weight,
        weights,
        shared_out,
    )

    def gathered(terms):
        return sum(t.astype(F32) for t in terms).astype(BF16)

    def rest_of(keep, give):
        for b in range(1, bits):
            came_in = lax.ppermute(give, "fsdp", [(i, i ^ (1 << b)) for i in range(members)])
            if b + 1 < bits:
                count = keep.shape[1] // 2
                give = gathered([keep[:, count:], came_in[:, count:]])
                keep = gathered([keep[:, :count], came_in[:, :count]])
        return keep[:, 0], came_in[:, 0]

    branch_recv, expert_res = lax.optimization_barrier((branch_recv, expert_res))
    dense_part, dense_other = rest_of(dense_keep, dense_give)
    so_part, so_other = rest_of(so_keep, so_give)

    dsend = call(
        functools.partial(attend_back_kernel, n_ctx, share),
        shape((3, n_ctx, rows, LANES), BF16),
        flops=2 * share * rows * n_ctx * n_ctx * LANES * 3,
        nbytes=8 << 20,
        grid_spec=pltpu.PrefetchScalarGridSpec(
            num_scalar_prefetch=1,
            grid=(n_ctx,),
            in_specs=[
                packet,
                pl.BlockSpec((n_ctx, rows, LANES), lambda i, sc: (0, 0, 0)),
                pl.BlockSpec((1, LANES, share), block_of),
                pl.BlockSpec((1, 1, share), block_of),
            ],
            out_specs=packet,
            scratch_shapes=[
                pltpu.VMEM((2 * rows, LANES), BF16),
                pltpu.VMEM((2 * rows, LANES), BF16),
                pltpu.VMEM((n_ctx, rows, LANES), F32),
                pltpu.VMEM((n_ctx, rows, LANES), F32),
                pltpu.VMEM((2 * rows, LANES), F32),
            ],
        ),
    )(scalars, recv, branch_recv, kept, lse)
    res_came = exchange(expert_res.reshape(n_ctx, -1, D)).reshape(places, D)
    drecv, expert_sum, out_grad, grad_router, output = comm_call(
        functools.partial(back_exchange_kernel, n_ctx, members, heads),
        (
            shape((3, n_ctx, rows, LANES), BF16),
            shape((3, half, local, FF), BF16),
            shape((members, local, D), BF16),
            shape((D, LANES), F32),
            shape((rows, D), BF16),
        ),
        1,
        in_specs=[whole] * 13 + [pl.BlockSpec(memory_space=pl.ANY)],
        out_specs=[whole] * 5,
        scratch_shapes=[
            pltpu.VMEM((3, half, local, FF), BF16),
            pltpu.VMEM((3, half, local, FF), BF16),
            pltpu.VMEM((members // 4, local, FF), BF16),
            pltpu.VMEM((D, places), BF16),
            pltpu.VMEM((D, places), BF16),
            pltpu.VMEM((D, places), BF16),
            pltpu.VMEM((D, D), F32),
            pltpu.VMEM((2, places, CHUNK), BF16),
            pltpu.SemaphoreType.DMA((n_ctx - 1,)),
            pltpu.SemaphoreType.DMA((n_ctx - 1,)),
            pltpu.SemaphoreType.DMA,
            pltpu.SemaphoreType.DMA((3,)),
            pltpu.SemaphoreType.DMA((3,)),
            pltpu.SemaphoreType.DMA((2,)),
            pltpu.SemaphoreType.DMA((2,)),
        ],
        nbytes=120 << 20,
    )(
        dsend,
        x_rows,
        dy_rows,
        came,
        branch,
        ffn_in,
        dlogits,
        residual,
        shared_res,
        gates,
        target,
        live,
        res_came,
        expert_mid,
    )

    late_width = PACKED + D
    late_widths = [D, D, D, D + LANES]
    sizes = [(local, FS)] * 2 + [(FS // members // 2, D)] * 2
    sizes += [(local, width) for width in late_widths]
    splits = [ring_split(r, c, n_ctx) + (c,) for r, c in sizes]
    tiles = [(n_ctx, t[2], t[3]) for t in splits]
    grad_x, dense_sum, so_sum, last_sum, expert_sum = comm_call(
        functools.partial(last_kernel, n_ctx, members, heads, experts, splits),
        (
            shape((rows, D), F32),
            shape((local, 2 * FS), BF16),
            shape((FS // members, D), BF16),
            shape((local, late_width), BF16),
            shape((3, local, FF), BF16),
        ),
        0,
        in_specs=[whole] * 16,
        out_specs=[whole] * 5,
        scratch_shapes=[pltpu.VMEM(t, BF16) for t in tiles * 4]
        + [pltpu.VMEM((members, local, width), BF16) for width in late_widths]
        + [
            pltpu.VMEM((members >> (b + 1), local, width), BF16)
            for b in range(bits)
            for width in late_widths
        ]
        + [pltpu.VMEM((3, members >> (b + 1), local, FF), BF16) for b in range(1, bits)]
        + [
            pltpu.VMEM((rows, 3 * D), BF16),
            pltpu.VMEM((D, rows), BF16),
            pltpu.VMEM((D, rows), BF16),
            pltpu.VMEM((D, LANES), F32),
            pltpu.SemaphoreType.DMA((8, 2, n_ctx)),
            pltpu.SemaphoreType.DMA((8, 2, n_ctx)),
            pltpu.SemaphoreType.DMA((4, bits)),
            pltpu.SemaphoreType.DMA((4, bits)),
            pltpu.SemaphoreType.DMA((3, max(1, bits - 1))),
            pltpu.SemaphoreType.DMA((3, max(1, bits - 1))),
        ],
        nbytes=200 << 20,
    )(
        drecv,
        cos,
        sin,
        attn_in,
        x,
        qkv_weight,
        tail,
        dres,
        out_grad,
        grad_router,
        dgain_two,
        dense_part,
        dense_other,
        so_part,
        so_other,
        expert_sum,
    )

    quarters = 4 if local % 64 == 0 else 1

    def rows_of(count, width):
        return pl.BlockSpec((count // quarters, width), lambda i: (i, 0))

    grad_qkv, grad_out, grad_si, grad_so, grad_ei, grad_eo, grad_x, grad_router, gains = call(
        functools.partial(widen_kernel, experts),
        (
            shape((local, 3 * D), F32),
            shape((local, D), F32),
            shape((local, 2 * FS), F32),
            shape((FS // members, D), F32),
            shape((local, 2 * FF), F32),
            shape((local, FF), F32),
            shape((rows, D), F32),
            shape((experts, local), F32),
            shape((2, local), F32),
        ),
        flops=0,
        nbytes=22 << 20,
        grid=(quarters,),
        in_specs=[
            rows_of(local, late_width),
            rows_of(local, 2 * FS),
            rows_of(FS // members, D),
            pl.BlockSpec((2, local // quarters, FF), lambda i: (0, i, 0)),
            pl.BlockSpec((1, local // quarters, FF), lambda i: (2, i, 0)),
            rows_of(rows, D),
            pl.BlockSpec((local, LANES), lambda i: (0, 3 * D // LANES)),
        ],
        out_specs=[
            rows_of(local, 3 * D),
            rows_of(local, D),
            rows_of(local, 2 * FS),
            rows_of(FS // members, D),
            rows_of(local, 2 * FF),
            rows_of(local, FF),
            rows_of(rows, D),
            full(experts, local),
            full(2, local),
        ],
    )(last_sum, dense_sum, so_sum, expert_sum, expert_sum, grad_x, last_sum)
    return (
        output[None],
        grad_x[None],
        gains[0],
        grad_qkv,
        grad_out,
        gains[1],
        grad_router.T,
        grad_si,
        grad_so,
        grad_ei[None],
        grad_eo.T[None],
    )


def solution(mesh):
    row_spec = P("fsdp", "ctx", None)
    flat = P("fsdp", None)
    return jax.shard_map(
        on_device,
        mesh=mesh,
        in_specs=(
            row_spec,
            row_spec,
            P("fsdp"),
            P(),
            row_spec,
            P("fsdp"),
            flat,
            flat,
            P("fsdp"),
            flat,
            flat,
            flat,
            P("ctx", "fsdp", None),
            P("ctx", None, "fsdp"),
        ),
        out_specs=(
            row_spec,
            row_spec,
            P("fsdp"),
            flat,
            flat,
            P("fsdp"),
            flat,
            flat,
            flat,
            P("ctx", "fsdp", None),
            P("ctx", None, "fsdp"),
        ),
        check_vma=False,
    )
```

```python
import functools

import jax
import jax.numpy as jnp
import numpy as np
from jax import lax
from jax.experimental import pallas as pl
from jax.experimental.pallas import tpu as pltpu
from jax.sharding import PartitionSpec as P

D = 768
HEADS = 12
HEAD_DIM = 64
FF = 2048
FS = 2048
LANES = 128
CHUNK = 256
BROAD = 512
PACKED = 3 * D + LANES
norm_eps = 1e-06
F32 = jnp.float32
BF16 = jnp.bfloat16


def dot(a, b):
    return jnp.dot(a, b, preferred_element_type=F32)


def dot_nt(a, b):
    return lax.dot_general(a, b, (((1,), (1,)), ((), ())), preferred_element_type=F32)


def dot_tn(a, b):
    return lax.dot_general(a, b, (((0,), (0,)), ((), ())), preferred_element_type=F32)


def call(kernel, outs, *, flops, nbytes, limit=56, **kw):
    return pl.pallas_call(
        kernel,
        out_shape=outs,
        compiler_params=pltpu.CompilerParams(vmem_limit_bytes=limit << 20),
        cost_estimate=pl.CostEstimate(
            flops=int(flops), bytes_accessed=int(nbytes), transcendentals=0
        ),
        **kw,
    )


def comm_call(kernel, outs, number, *, nbytes, limit=60, **kw):
    return pl.pallas_call(
        kernel,
        out_shape=outs,
        compiler_params=pltpu.CompilerParams(
            collective_id=number, has_side_effects=True, vmem_limit_bytes=limit << 20
        ),
        cost_estimate=pl.CostEstimate(flops=0, bytes_accessed=int(nbytes), transcendentals=0),
        **kw,
    )


def shape(dims, dtype):
    return jax.ShapeDtypeStruct(dims, dtype)


def lanes_of(rows, width=LANES):
    return lax.broadcasted_iota(jnp.int32, (rows, width), 1)


def first_heads(n_ctx, slot_dev):
    share = HEADS * slot_dev // n_ctx
    return [min(share * d // slot_dev, HEADS - 2) for d in range(n_ctx)]


def partner(t, lane):
    return jnp.where(lane % 64 < 32, pltpu.roll(t, 96, 1), pltpu.roll(t, 32, 1))


def picks(target_ref, places):
    rows = target_ref.shape[0]
    place = lanes_of(rows, places)
    return tuple(
        jnp.where(place == target_ref[:, k : k + 1], 1.0, 0.0).astype(BF16) for k in range(2)
    )


def flipped(index, mask):
    for b in range(mask.bit_length()):
        if mask >> b & 1:
            index = index + (1 << b) - 2 * (1 << b) * (index // (1 << b) % 2)
    return index


def mirrored(members):
    bits = members.bit_length() - 1
    return [int(format(j, "b").zfill(bits)[::-1], 2) for j in range(members)]


def shard_rows(members, shard):
    fsdp = lax.axis_index("fsdp")
    return [pl.multiple_of(flipped(fsdp, m) * shard, 16) for m in mirrored(members)]


def remote(source, target, send_sem, recv_sem, peer):
    return pltpu.make_async_remote_copy(
        src_ref=source,
        dst_ref=target,
        send_sem=send_sem,
        recv_sem=recv_sem,
        device_id=peer,
        device_id_type=pl.DeviceIdType.MESH,
    )


def greet(peers):
    barrier = pltpu.get_barrier_semaphore()
    for peer in peers:
        pl.semaphore_signal(barrier, inc=1, device_id=peer, device_id_type=pl.DeviceIdType.MESH)
    pl.semaphore_wait(barrier, len(peers))


def mates_of(members):
    ctx, fsdp = lax.axis_index("ctx"), lax.axis_index("fsdp")
    return [(ctx, flipped(fsdp, 1 << b)) for b in range(members.bit_length() - 1)]


def row_peers(n):
    ctx, fsdp = lax.axis_index("ctx"), lax.axis_index("fsdp")
    return [(lax.rem(ctx + d, n), fsdp) for d in range(1, n)]


def loop(body, low, high):
    lax.fori_loop(low, high, lambda s, carry: (body(s), carry)[1], 0)


def add_into(target, j, other):
    target[j] = (target[j].astype(F32) + other[j].astype(F32)).astype(BF16)


def open_kernel(
    n,
    members,
    heads,
    experts,
    capacity,
    early,
    where_ref,
    length_ref,
    routes_ref,
    cot_ref,
    x_ref,
    w_ref,
    router_ref,
    gains_ref,
    turn_ref,
    recv_ref,
    in_ref,
    tail_ref,
    target_ref,
    dout_ref,
    dy_ref,
    dy_rest_ref,
    w_all,
    cos_ref,
    sin_ref,
    send,
    dy_send,
    small,
    small_all,
    gather_send,
    gather_recv,
    packet_send,
    packet_recv,
    dy_send_sem,
    dy_recv_sem,
    own_sem,
):
    ctx, fsdp = lax.axis_index("ctx"), lax.axis_index("fsdp")
    bits = members.bit_length() - 1
    peers = row_peers(n)
    mates = mates_of(members)
    shard = w_ref.shape[0]
    rows = x_ref.shape[0]
    small[...] = jnp.zeros_like(small)
    small[0:experts] = router_ref[...].astype(F32)
    small[experts : experts + 2] = gains_ref[...].astype(F32)
    small_all[fsdp] = small[...].T.astype(BF16)
    for part in range(3):
        w_all[part, fsdp] = w_ref[:, part * D : (part + 1) * D]
    greet(peers + mates)

    def gather_copy(p, b, mask):
        buffer = small_all if p == 3 else w_all.at[p]
        spot = flipped(fsdp, mask)
        return remote(
            buffer.at[spot],
            buffer.at[spot],
            gather_send.at[p, b, mask],
            gather_recv.at[p, b, mask],
            mates[b],
        )

    def gather_wait(p, b, mask):
        buffer = small_all if p == 3 else w_all.at[p]
        spot = flipped(fsdp, mask | 1 << b)
        remote(
            buffer.at[spot],
            buffer.at[spot],
            gather_send.at[p, b, mask],
            gather_recv.at[p, b, mask],
            mates[b],
        ).wait_recv()

    for p in (3, 0, 1, 2):
        for b in reversed(range(bits)):
            gather_copy(p, b, 0).start()

    def gather_rest(p):
        masks = [0]
        for b in reversed(range(bits)):
            for mask in masks[1:]:
                gather_copy(p, b, mask).start()
            for mask in masks:
                gather_wait(p, b, mask)
            masks = masks + [mask | 1 << b for mask in masks]

    lane = lanes_of(rows)
    hot = [jnp.where(lane == routes_ref[:, k : k + 1], 1.0, 0.0) for k in range(2)]
    below = jnp.where(
        lanes_of(rows, rows) < lax.broadcasted_iota(jnp.int32, (rows, rows), 0), 1.0, 0.0
    )
    before = dot(below.astype(BF16), (hot[0] + hot[1]).astype(BF16))
    place = [
        routes_ref[:, k : k + 1] * capacity
        + jnp.sum(hot[k] * before, axis=-1, keepdims=True).astype(jnp.int32)
        for k in range(2)
    ]
    for k in range(2):
        target_ref[:, k : k + 1] = place[k]
    position = where_ref[ctx] * rows + lax.broadcasted_iota(jnp.int32, (rows, D), 0)
    dout = jnp.where(position < length_ref[0], cot_ref[...].astype(F32), 0.0).astype(BF16)
    dout_ref[...] = dout
    places = experts * capacity
    spot = lanes_of(rows, places)
    pick = jnp.where((spot == place[0]) | (spot == place[1]), 1.0, 0.0).astype(BF16)
    packed = dot_tn(pick, dout).astype(BF16)
    block = places // n
    for p in range(n):
        dy_send[p] = packed[p * block : p * block + early]
        dy_rest_ref[p] = packed[p * block + early : (p + 1) * block]
    own = [
        pltpu.make_async_copy(dy_send.at[ctx], dy_ref.at[ctx], own_sem.at[3]),
    ]
    own[0].start()
    copies = [
        remote(dy_send.at[p[0]], dy_ref.at[ctx], dy_send_sem.at[d], dy_recv_sem.at[d], p)
        for d, p in enumerate(peers)
    ]
    for c in copies:
        c.start()

    x = x_ref[...].astype(F32)
    inv = lax.rsqrt(jnp.mean(x * x, axis=-1, keepdims=True) + norm_eps)
    gather_rest(3)
    tail = small_all[...].reshape(D, LANES).astype(F32).T
    tail_ref[...] = tail
    attn_in = (x * inv * tail[experts : experts + 1, :]).astype(BF16)
    in_ref[...] = attn_in
    position = where_ref[ctx] * rows + lax.broadcasted_iota(jnp.int32, (rows, LANES), 0)
    angles = position.astype(F32) * turn_ref[...]
    cos, sin = jnp.cos(angles), jnp.sin(angles)
    sin = jnp.where(lane % 64 < 32, -sin, sin)
    cos_ref[...] = cos
    sin_ref[...] = sin
    for part in range(3):
        gather_rest(part)
        y = dot(attn_in, w_all[part].reshape(D, D))
        groups = []
        for g in range(D // LANES):
            t = y[:, g * LANES : (g + 1) * LANES]
            if part < 2:
                t = t * cos + partner(t, lane) * sin
            groups.append(t)
        turned = [pltpu.roll(t, 64, 1) for t in groups]
        for d, head in enumerate(heads):
            g = head // 2
            if head % 2 == 0:
                packet = groups[g]
            else:
                packet = jnp.where(lane < 64, turned[g], turned[g + 1])
            send[part, d] = packet.astype(BF16)
        own.append(
            pltpu.make_async_copy(
                send.at[part, ctx], recv_ref.at[part, ctx], own_sem.at[part]
            )
        )
        own[-1].start()
        for d, p in enumerate(peers):
            copies.append(
                remote(
                    send.at[part, p[0]],
                    recv_ref.at[part, ctx],
                    packet_send.at[part, d],
                    packet_recv.at[part, d],
                    p,
                )
            )
            copies[-1].start()
    for c in copies + own:
        c.wait()
    for p in range(4):
        masks = [0]
        for b in reversed(range(bits)):
            for mask in masks:
                gather_copy(p, b, mask).wait_send()
            masks = masks + [mask | 1 << b for mask in masks]


def stack_rows(stack_ref, block, lane):
    rows = block.shape[0]
    zero = jnp.zeros((), block.dtype)
    stack_ref[0:rows, :] = jnp.where(lane < 64, block, zero)
    stack_ref[rows : 2 * rows, :] = jnp.where(lane >= 64, block, zero)


def unstack_rows(stack_ref, block, offset, lane):
    rows = stack_ref.shape[0] // 2
    stack_ref[...] = jnp.zeros_like(stack_ref)
    stack_ref[pl.ds(offset, block.shape[0]), :] = block
    return jnp.where(lane < 64, stack_ref[0:rows, :], stack_ref[rows : 2 * rows, :])


def key_limits(share, rows, q_block, offset, length):
    row = lax.broadcasted_iota(jnp.int32, (1, share), 1) + offset
    row = jnp.where(row >= rows, row - rows, row)
    return jnp.minimum(q_block * rows + row + 1, length)


def attend_kernel(n, share, sc, recv_ref, out_ref, keep_ref, lse_ref, stack, scores, back):
    q_block = pl.program_id(0)
    rows = recv_ref.shape[2]
    offset = pl.multiple_of(sc[n], 64)
    length = sc[n + 1]
    lane = lanes_of(rows)
    stack_rows(stack, recv_ref[0, sc[q_block]] * 0.125, lane)
    query = stack[pl.ds(offset, share), :]
    limit = key_limits(share, rows, q_block, offset, length)
    key_row = lax.broadcasted_iota(jnp.int32, (rows, share), 0)
    blocks = jnp.minimum(q_block + 1, (length + rows - 1) // rows)

    def score_step(pair, top):
        found = []
        for j in (2 * pair, 2 * pair + 1):
            s = dot_nt(recv_ref[1, sc[j]], query)
            s = jnp.where(key_row < limit - j * rows, s, -1e30)
            scores[j] = s
            found.append(jnp.max(s, axis=0, keepdims=True))
        return jnp.maximum(top, jnp.maximum(found[0], found[1]))

    pairs = (blocks + 1) // 2
    top = lax.fori_loop(0, pairs, score_step, jnp.full((1, share), -1e30, F32))

    def value_step(pair, carry):
        total, acc = carry
        for j in (2 * pair, 2 * pair + 1):
            weights = jnp.exp(scores[j] - top)
            total = total + jnp.sum(weights, axis=0, keepdims=True)
            acc = acc + dot_tn(recv_ref[2, sc[j]], weights.astype(BF16))
        return total, acc

    total, acc = lax.fori_loop(
        0, pairs, value_step, (jnp.zeros((1, share), F32), jnp.zeros((LANES, share), F32))
    )
    acc = acc / total
    keep_ref[0] = acc
    lse_ref[0] = top + jnp.log(total)
    out_ref[0] = unstack_rows(back, acc.T, offset, lane).astype(BF16)


def attend_back_kernel(
    n, share, sc, recv_ref, grad_ref, keep_ref, lse_ref, out_ref, stack, gstack, dkeys, dvalues, back
):
    q_block = pl.program_id(0)
    rows = recv_ref.shape[2]
    offset = pl.multiple_of(sc[n], 64)
    length = sc[n + 1]
    lane = lanes_of(rows)
    source = sc[q_block]

    @pl.when(q_block == 0)
    def _():
        dkeys[...] = jnp.zeros_like(dkeys)
        dvalues[...] = jnp.zeros_like(dvalues)

    stack_rows(stack, recv_ref[0, source] * 0.125, lane)
    query = stack[pl.ds(offset, share), :]
    stack_rows(gstack, grad_ref[source], lane)
    grad = gstack[pl.ds(offset, share), :]
    lse = lse_ref[0]
    delta = jnp.sum(grad.astype(F32).T * keep_ref[0], axis=0, keepdims=True)
    limit = key_limits(share, rows, q_block, offset, length)
    key_row = lax.broadcasted_iota(jnp.int32, (rows, share), 0)
    blocks = jnp.minimum(q_block + 1, (length + rows - 1) // rows)

    def step(pair, acc):
        for j in (2 * pair, 2 * pair + 1):
            keys = recv_ref[1, sc[j]]
            values = recv_ref[2, sc[j]]
            s = dot_nt(keys, query)
            weights = jnp.exp(jnp.where(key_row < limit - j * rows, s, -1e30) - lse)
            dweights = dot_nt(values, grad)
            dscores = (weights * (dweights - delta)).astype(BF16)
            dkeys[j] += dot(dscores, query)
            dvalues[j] += dot(weights.astype(BF16), grad)
            acc = acc + dot_tn(keys, dscores)
        return acc

    acc = lax.fori_loop(0, (blocks + 1) // 2, step, jnp.zeros((LANES, share), F32))
    dquery = unstack_rows(back, acc.T * 0.125, offset, lane)
    out_ref[0, source] = dquery.astype(BF16)

    @pl.when(q_block == n - 1)
    def _():
        def flush(j, carry):
            out_ref[1, sc[j]] = dkeys[j].astype(BF16)
            out_ref[2, sc[j]] = dvalues[j].astype(BF16)
            return carry

        lax.fori_loop(0, n, flush, 0)


def middle_kernel(
    n,
    heads,
    experts,
    attended_ref,
    w_ref,
    x_ref,
    tail_ref,
    routes_ref,
    target_ref,
    came_ref,
    residual_ref,
    in_ref,
    gates_ref,
    rows_ref,
    row_gates_ref,
    outgoing,
    outgates,
    came_send,
    came_recv,
    send_sem,
    recv_sem,
    gate_send,
    gate_recv,
    own_sem,
):
    ctx = lax.axis_index("ctx")
    peers = row_peers(n)
    greet(peers)
    own = pltpu.make_async_copy(attended_ref.at[ctx], came_ref.at[ctx], own_sem.at[0])
    own.start()
    copies = [
        remote(attended_ref.at[p[0]], came_ref.at[ctx], came_send.at[d], came_recv.at[d], p)
        for d, p in enumerate(peers)
    ]
    for c in copies:
        c.start()
    pick = picks(target_ref, rows_ref.shape[0])
    lane = lanes_of(x_ref.shape[0])
    total = x_ref[...].astype(F32)
    for c in copies:
        c.wait()
    own.wait()
    for d, head in enumerate(heads):
        total = total + dot(came_ref[d], w_ref[64 * head : 64 * head + LANES, :])
    residual_ref[...] = total
    inv = lax.rsqrt(jnp.mean(total * total, axis=-1, keepdims=True) + norm_eps)
    ffn_in = (total * inv * tail_ref[experts + 1 : experts + 2, :]).astype(BF16)
    in_ref[...] = ffn_in
    logits = dot_nt(ffn_in, tail_ref[...].astype(BF16))
    chosen = [
        jnp.sum(jnp.where(lane == routes_ref[:, k : k + 1], logits, 0.0), axis=-1, keepdims=True)
        for k in range(2)
    ]
    top = jnp.maximum(chosen[0], chosen[1])
    raised = [jnp.exp(c - top) for c in chosen]
    gates = [r / (raised[0] + raised[1]) for r in raised]
    gates_ref[...] = jnp.where(lane == 0, gates[0], gates[1])
    outgoing[...] = dot_tn(pick[0] + pick[1], ffn_in).astype(BF16)
    block = outgoing.shape[0] // n

    def block_at(p):
        return pl.ds(pl.multiple_of(p * block, 16), block)

    own = [
        pltpu.make_async_copy(
            outgoing.at[block_at(ctx)], rows_ref.at[block_at(ctx)], own_sem.at[1]
        )
    ]
    copies = [
        remote(
            outgoing.at[block_at(p[0])],
            rows_ref.at[block_at(ctx)],
            send_sem.at[d],
            recv_sem.at[d],
            p,
        )
        for d, p in enumerate(peers)
    ]
    for c in own + copies:
        c.start()
    for p in range(n):
        row = sum(
            jnp.sum(
                jnp.where(lane == target_ref[:, k : k + 1] - p * block, gates[k], 0.0),
                axis=0,
                keepdims=True,
            )
            for k in range(2)
        )
        outgates[p] = jnp.broadcast_to(row, outgates.shape[1:])
    own.append(pltpu.make_async_copy(outgates.at[ctx], row_gates_ref.at[ctx], own_sem.at[2]))
    own[-1].start()
    for d, p in enumerate(peers):
        copies.append(
            remote(
                outgates.at[p[0]], row_gates_ref.at[ctx], gate_send.at[d], gate_recv.at[d], p
            )
        )
        copies[-1].start()
    for c in copies + own:
        c.wait()


def gated(g, u, da):
    sig = 1.0 / (1.0 + jnp.exp(-g))
    silu = g * sig
    return silu * u, da * u * sig * (1.0 + g * (1.0 - sig)), da * silu


def expert_kernel(
    x_ref,
    gates_ref,
    first_ref,
    rest_ref,
    wg_ref,
    wu_ref,
    wt_ref,
    dx_ref,
    dgate_ref,
    res_ref,
    mid_ref,
    dy_ref,
    dx_acc,
    res_acc,
    dgate,
    gate_rows,
):
    c = pl.program_id(0)

    @pl.when(c == 0)
    def _():
        res_acc[...] = jnp.zeros_like(res_acc)
        dx_acc[...] = jnp.zeros_like(dx_acc)
        dgate[...] = jnp.zeros_like(dgate)
        n, early = first_ref.shape[0:2]
        block = early + rest_ref.shape[1]
        for p in range(n):
            dy_ref[p * block : p * block + early] = first_ref[p]
            dy_ref[p * block + early : (p + 1) * block] = rest_ref[p]
            column = gates_ref[p].T[0:block, 0:1]
            gate_rows[p * block : (p + 1) * block] = jnp.broadcast_to(column, (block, LANES))

    x, dy = x_ref[...], dy_ref[...]
    gate = gate_rows[:, 0:1]
    wg, wu, wt = wg_ref[...], wu_ref[...], wt_ref[...]
    da = dot(dy, wt)
    act, dg, du = gated(dot(x, wg), dot(x, wu), da * gate)
    dgate[...] += jnp.sum(act * da, axis=-1, keepdims=True)
    mid_ref[2] = (act * gate).astype(BF16)
    act, dg, du = act.astype(BF16), dg.astype(BF16), du.astype(BF16)
    res_acc[...] += dot_nt(act, wt)
    dx_acc[...] += dot_nt(dg, wg) + dot_nt(du, wu)
    mid_ref[0] = dg
    mid_ref[1] = du

    @pl.when(c == pl.num_programs(0) - 1)
    def _():
        res_ref[...] = res_acc[...].astype(BF16)
        dx_ref[...] = dx_acc[...].astype(BF16)
        n, early = first_ref.shape[0:2]
        block = early + rest_ref.shape[1]
        dgate_ref[...] = jnp.zeros_like(dgate_ref)
        for p in range(n):
            dgate_ref[p, :, 0:block] = dgate[p * block : (p + 1) * block].T[0:8]


def ring_split(rows, columns, pieces):
    down = 1
    while 2 * down <= pieces and rows % (32 * down) == 0:
        down *= 2
    across = pieces // down
    width = -(-columns // (LANES * across)) * LANES
    return down, across, rows // down, width


def ring_place(position, n):
    half = n // 2
    return jnp.where(position < half, 2 * position, 2 * (n - 1 - position) + 1)


def shared_kernel(
    n,
    members,
    heads,
    experts,
    send_ref,
    row_dgates_ref,
    in_ref,
    dout_ref,
    residual_ref,
    gates_ref,
    routes_ref,
    target_ref,
    tail_ref,
    w_ref,
    wide_ref,
    back_ref,
    recv_ref,
    res_ref,
    dres_ref,
    branch_ref,
    dlogits_ref,
    dgain_ref,
    a_keep,
    a_give,
    b_keep,
    b_other,
    came,
    came_dgates,
    packets,
    b_give,
    mids,
    dx_acc,
    a_all,
    b_all,
    a_caught,
    b_caught,
    raw,
    xt,
    gate_buf,
    up_buf,
    back_buf,
    send_sem,
    recv_sem,
    own_sem,
    packet_send,
    packet_recv,
    dgate_send,
    dgate_recv,
    a_sem,
    b_sem,
    far_sem,
    w_sem,
):
    ctx, fsdp = lax.axis_index("ctx"), lax.axis_index("fsdp")
    bits = members.bit_length() - 1
    peers = row_peers(n)
    mate, far = mates_of(members)[0:2]
    greet(peers + [mate, far])
    block = send_ref.shape[0] // n

    def block_at(p):
        return pl.ds(pl.multiple_of(p * block, 16), block)

    copies = [
        pltpu.make_async_copy(send_ref.at[block_at(ctx)], came.at[block_at(ctx)], own_sem.at[0]),
        pltpu.make_async_copy(row_dgates_ref.at[ctx], came_dgates.at[ctx], own_sem.at[2]),
    ]
    for d, p in enumerate(peers):
        copies.append(
            remote(
                row_dgates_ref.at[p[0]],
                came_dgates.at[ctx],
                dgate_send.at[d],
                dgate_recv.at[d],
                p,
            )
        )
        copies.append(
            remote(
                send_ref.at[block_at(p[0])],
                came.at[block_at(ctx)],
                send_sem.at[d],
                recv_sem.at[d],
                p,
            )
        )
    for c in copies:
        c.start()

    steps = FS // CHUNK

    def fetch(c, slot):
        at = pl.ds(pl.multiple_of(c * CHUNK, CHUNK), CHUNK)
        up = pl.ds(pl.multiple_of(FS + c * CHUNK, CHUNK), CHUNK)
        return [
            pltpu.make_async_copy(wide_ref.at[:, at], gate_buf.at[slot], w_sem.at[slot, 0]),
            pltpu.make_async_copy(wide_ref.at[:, up], up_buf.at[slot], w_sem.at[slot, 1]),
            pltpu.make_async_copy(back_ref.at[at], back_buf.at[slot], w_sem.at[slot, 2]),
        ]

    for f in fetch(0, 0):
        f.start()
    res_ref[...] = jnp.zeros_like(res_ref)
    dx_acc[...] = jnp.zeros_like(dx_acc)
    b_shard = FS // members
    piece = b_all.shape[2]

    def ffn_step(c):
        slot = lax.rem(c, 2)
        for f in fetch(c, slot):
            f.wait()

        @pl.when(c + 1 < steps)
        def _():
            for f in fetch(c + 1, 1 - slot):
                f.start()

        x, dy = in_ref[...], dout_ref[...]
        wg, wu, wo = gate_buf[slot], up_buf[slot], back_buf[slot]
        act, dg, du = gated(dot(x, wg), dot(x, wu), dot_nt(dy, wo))
        act, dg, du = act.astype(BF16), dg.astype(BF16), du.astype(BF16)
        res_ref[...] += dot(act, wo)
        dx_acc[...] += dot_nt(dg, wg) + dot_nt(du, wu)
        column = pl.ds(pl.multiple_of(c * CHUNK, CHUNK), CHUNK)
        mids[0, :, column] = dg
        mids[1, :, column] = du
        value = dot_tn(act, dy).astype(BF16)
        span = min(piece, CHUNK)
        for u in range(CHUNK // span):
            row = c * CHUNK + u * span
            t = row // b_shard
            j = sum(
                lax.rem(fsdp // (1 << b) + t // (1 << b), 2) * (1 << (bits - 1 - b))
                for b in range(bits)
            )
            inside = lax.rem(row, b_shard)
            top = pl.multiple_of(lax.rem(inside, piece), 16)
            b_all[inside // piece, j, pl.ds(top, span), :] = value[u * span : (u + 1) * span]

    loop(ffn_step, 0, steps)
    half, quarter = members // 2, members // 4

    def a_swap(i):
        return remote(
            a_all.at[i, pl.ds(half, half)], a_caught.at[i], a_sem.at[i, 0], a_sem.at[i, 1], mate
        )

    def b_swap(i):
        return remote(
            b_all.at[i, pl.ds(half, half)], b_caught.at[i], b_sem.at[i, 0], b_sem.at[i, 1], mate
        )

    def b_cross(i):
        return remote(b_give.at[i], b_other.at[i], far_sem.at[i, 0], far_sem.at[i, 1], far)

    for i in range(2):
        b_swap(i).start()
    rows = shard_rows(members, D // members)
    shard = D // members
    raw[...] = in_ref[...].T
    for j in range(members):
        xt[j * shard : (j + 1) * shard, :] = raw[pl.ds(rows[j], shard), :]
    for i in range(2):

        def grad_step(c, i=i):
            column = pl.ds(pl.multiple_of(c * BROAD, BROAD), BROAD)
            value = dot(xt[...], mids[i, :, column]).astype(BF16)
            for j in range(members):
                a_all[i, j, :, column] = value[j * shard : (j + 1) * shard]

        loop(grad_step, 0, FS // BROAD)
        a_swap(i).start()
        b_swap(i).wait_recv()
        for j in range(half):
            total = (b_all[i, j].astype(F32) + b_caught[i, j].astype(F32)).astype(BF16)
            if j < quarter:
                b_keep[i, j] = total
            else:
                b_give[i, j - quarter] = total
        b_cross(i).start()
    for c in copies:
        c.wait()

    pick = picks(target_ref, came.shape[0])
    gates = [gates_ref[:, k : k + 1] for k in range(2)]
    lane = lanes_of(pick[0].shape[0])
    dgate = [
        jnp.sum(
            sum(
                jnp.where(
                    lane == target_ref[:, k : k + 1] - p * block, came_dgates[p, 0:1, :], 0.0
                )
                for p in range(n)
            ),
            axis=-1,
            keepdims=True,
        )
        for k in range(2)
    ]
    mean = gates[0] * dgate[0] + gates[1] * dgate[1]
    dlogits = sum(
        jnp.where(lane == routes_ref[:, k : k + 1], gates[k] * (dgate[k] - mean), 0.0)
        for k in range(2)
    ).astype(BF16)
    dlogits_ref[...] = dlogits
    tail = tail_ref[...]
    dffn = dot(pick[0] + pick[1], came[...]) + dx_acc[...] + dot(dlogits, tail.astype(BF16))
    residual = residual_ref[...]
    inv = lax.rsqrt(jnp.mean(residual * residual, axis=-1, keepdims=True) + norm_eps)
    scaled = dffn * tail[experts + 1 : experts + 2, :]
    total = jnp.mean(scaled * residual, axis=-1, keepdims=True)
    dres = dout_ref[...].astype(F32) + inv * scaled - residual * inv * inv * inv * total
    branch = dres.astype(BF16)
    branch_ref[...] = branch
    for d, head in enumerate(heads):
        packets[d] = dot_nt(branch, w_ref[64 * head : 64 * head + LANES, :]).astype(BF16)
    own = pltpu.make_async_copy(packets.at[ctx], recv_ref.at[ctx], own_sem.at[1])
    own.start()
    copies = [
        remote(packets.at[p[0]], recv_ref.at[ctx], packet_send.at[d], packet_recv.at[d], p)
        for d, p in enumerate(peers)
    ]
    for c in copies:
        c.start()
    dres_ref[...] = dres
    dgain_ref[...] = jnp.sum(dffn * residual * inv, axis=0, keepdims=True)
    for i in range(2):
        a_swap(i).wait_recv()
        for j in range(half):
            total = (a_all[i, j].astype(F32) + a_caught[i, j].astype(F32)).astype(BF16)
            if j < quarter:
                a_keep[i, j] = total
            else:
                a_give[i, j - quarter] = total
    for c in copies:
        c.wait()
    own.wait()
    for i in range(2):
        a_swap(i).wait_send()
        b_swap(i).wait_send()
        b_cross(i).wait()


def back_exchange_kernel(
    n,
    members,
    heads,
    send_ref,
    x_ref,
    dy_ref,
    came_ref,
    branch_ref,
    in_ref,
    dlogits_ref,
    residual_ref,
    shared_ref,
    gates_ref,
    target_ref,
    live_ref,
    res_ref,
    mid_ref,
    recv_ref,
    sum_ref,
    out_keep,
    out_other,
    router_ref,
    output_ref,
    give,
    caught,
    crossed,
    out_all,
    out_caught,
    raw,
    xt,
    dyt,
    acc,
    mids,
    send_sem,
    recv_sem,
    own_sem,
    give_sem,
    caught_sem,
    cross_sem,
    out_sem,
    mid_sem,
):
    ctx = lax.axis_index("ctx")
    peers = row_peers(n)
    mates = mates_of(members)
    mate, far = mates[0], mates[1]
    greet(peers + [mate, far])
    own = pltpu.make_async_copy(send_ref.at[:, ctx], recv_ref.at[:, ctx], own_sem)
    own.start()
    copies = [
        remote(send_ref.at[:, p[0]], recv_ref.at[:, ctx], send_sem.at[d], recv_sem.at[d], p)
        for d, p in enumerate(peers)
    ]
    for c in copies:
        c.start()

    steps = mid_ref.shape[2] // BROAD
    parts = mid_ref.shape[0]

    def fetch(i, c, slot):
        column = pl.multiple_of(c * BROAD, BROAD)
        return pltpu.make_async_copy(
            mid_ref.at[i, :, pl.ds(column, BROAD)], mids.at[slot], mid_sem.at[slot]
        )

    fetch(0, 0, 0).start()
    shard = D // members
    half = members // 2
    rows = shard_rows(members, shard)

    def turned(value, target):
        raw[...] = value.T
        for j in range(members):
            target[j * shard : (j + 1) * shard, :] = raw[pl.ds(rows[j], shard), :]

    acc[...] = jnp.zeros_like(acc)
    branch = branch_ref[...]
    for d, head in enumerate(heads):
        acc[64 * head : 64 * head + LANES, :] += dot_tn(came_ref[d], branch)
    for j in range(members):
        out_all[j] = acc[pl.ds(rows[j], shard), :].astype(BF16)
    quarter = members // 4
    out_swap = remote(
        out_all.at[pl.ds(half, half)], out_caught, out_sem.at[0], out_sem.at[1], mate
    )
    out_swap.start()
    turned(x_ref[...], xt)
    turned(dy_ref[...], dyt)
    out_swap.wait_recv()
    for j in range(half):
        add_into(out_all, j, out_caught)
    for j in range(quarter):
        out_keep[j] = out_all[j]
    out_cross = remote(
        out_all.at[pl.ds(quarter, quarter)], out_other, out_sem.at[2], out_sem.at[3], far
    )
    out_cross.start()

    def swap(i):
        return remote(give.at[i], caught.at[i], give_sem.at[i], caught_sem.at[i], mate)

    cross = remote(
        sum_ref.at[0, pl.ds(quarter, quarter)], crossed, cross_sem.at[0], cross_sem.at[1], far
    )
    for i in range(parts):
        left = xt if i < 2 else dyt

        def step(c, left=left, i=i):
            slot = lax.rem(c, 2)
            fetch(i, c, slot).wait()

            @pl.when(c + 1 < steps)
            def _():
                fetch(i, c + 1, 1 - slot).start()

            value = dot(left[...], mids[slot]).astype(BF16)
            column = pl.ds(pl.multiple_of(c * BROAD, BROAD), BROAD)
            for j in range(half):
                sum_ref[i, j, :, column] = value[j * shard : (j + 1) * shard]
                give[i, j, :, column] = value[(half + j) * shard : (half + j + 1) * shard]

        loop(step, 0, steps)
        if i + 1 < parts:
            fetch(i + 1, 0, 0).start()
        swap(i).start()
        if i > 0:
            swap(i - 1).wait_recv()
            for j in range(half):
                add_into(sum_ref.at[i - 1], j, caught.at[i - 1])
        if i == 1:
            cross.start()

    router_ref[...] = dot_tn(in_ref[...], dlogits_ref[...])
    pick = picks(target_ref, res_ref.shape[0])
    came = res_ref[...]
    mixture = gates_ref[:, 0:1] * dot(pick[0], came) + gates_ref[:, 1:2] * dot(pick[1], came)
    output_ref[...] = (live_ref[...] * (residual_ref[...] + shared_ref[...] + mixture)).astype(BF16)
    swap(parts - 1).wait_recv()
    for j in range(half):
        add_into(sum_ref.at[parts - 1], j, caught.at[parts - 1])
    for c in copies:
        c.wait()
    own.wait()
    cross.wait()
    for j in range(quarter):
        add_into(sum_ref.at[0], j, crossed)
    for i in range(parts):
        swap(i).wait_send()
    out_swap.wait_send()
    out_cross.wait()


def last_kernel(
    n,
    members,
    heads,
    experts,
    splits,
    recv_ref,
    cos_ref,
    sin_ref,
    in_ref,
    x_ref,
    w_ref,
    tail_ref,
    dres_ref,
    router_ref,
    dgain_ref,
    a_ref,
    a_other,
    b_ref,
    b_other,
    o_ref,
    o_other,
    e_ref,
    x_out,
    a_out,
    b_out,
    c_out,
    e_out,
    *scratch,
):
    bits = members.bit_length() - 1
    streams = len(splits)
    own, full, back_up, back_down = (scratch[k * streams : (k + 1) * streams] for k in range(4))
    back = (back_up, back_down)
    scratch = scratch[4 * streams :]
    packs, scratch = scratch[0:4], scratch[4:]
    caught = [scratch[4 * b : 4 * b + 4] for b in range(bits)]
    scratch = scratch[4 * bits :]
    e_caught, scratch = scratch[0 : bits - 1], scratch[bits - 1 :]
    dproj, raw, turned, small = scratch[0:4]
    send_sem, recv_sem, level_send, level_recv, e_send, e_recv = scratch[4:]
    ctx, fsdp = lax.axis_index("ctx"), lax.axis_index("fsdp")
    here = jnp.where(ctx % 2 == 0, ctx // 2, n - 1 - ctx // 2)
    ahead = (ring_place(lax.rem(here + 1, n), n), fsdp)
    behind = (ring_place(lax.rem(here + n - 1, n), n), fsdp)
    mates = mates_of(members)
    greet([ahead, behind] + mates)
    shard = D // members
    parts = e_ref.shape[0]

    def level_copy(p, b):
        count = members >> (b + 1)
        return remote(
            packs[p].at[pl.ds(count, count)],
            caught[b][p],
            level_send.at[p, b],
            level_recv.at[p, b],
            mates[b],
        )

    def level_add(p, b):
        level_copy(p, b).wait_recv()
        for j in range(members >> (b + 1)):
            add_into(packs[p], j, caught[b][p])

    def level_next(p):
        level_add(p, 0)
        level_copy(p, 1).start()

    def e_copy(i, b):
        count = members >> (b + 1)
        source = e_ref if b == 1 or (b == 2 and i == 0) else e_caught[b - 2]
        return remote(
            source.at[i, pl.ds(count, count)],
            e_caught[b - 1].at[i],
            e_send.at[i, b - 1],
            e_recv.at[i, b - 1],
            mates[b],
        )

    def e_add(i, b):
        e_copy(i, b).wait_recv()
        source = e_ref if b == 1 or (b == 2 and i == 0) else e_caught[b - 2]
        for j in range(members >> (b + 1)):
            total = source[i, j].astype(F32) + e_caught[b - 1][i, j].astype(F32)
            if b == bits - 1:
                e_out[i] = total.astype(BF16)
            else:
                e_caught[b - 1][i, j] = total.astype(BF16)

    def tiles(i):
        down, across, height, width = splits[i][0:4]
        columns = splits[i][4]
        for p in range(down * across):
            r, c = p // across, p % across
            yield p, r * height, height, c * width, max(0, min(width, columns - c * width)), width

    def load(i, ref, skip=0, other=None):
        for p, top, height, start, have, width in tiles(i):
            if have > 0:
                value = ref[top : top + height, skip + start : skip + start + have]
                if other is not None:
                    added = other[top : top + height, skip + start : skip + start + have]
                    value = (value.astype(F32) + added.astype(F32)).astype(BF16)
                own[i][p, :, 0:have] = value
            if have < width:
                own[i][p, :, have:] = jnp.zeros((height, width - have), BF16)

    def save(i, ref, skip=0):
        for p, top, height, start, have, width in tiles(i):
            if have > 0:
                ref[top : top + height, skip + start : skip + start + have] = full[i][p, :, 0:have]

    long, short = n // 2, n - 1 - n // 2

    def hops(i, direction):
        return long if direction == i % 2 else short

    def place(direction, steps):
        return lax.rem(here + (steps if direction == 0 else 2 * n - steps), n)

    def copy(i, direction, step, source, target, slot):
        return remote(
            source.at[slot],
            target.at[slot],
            send_sem.at[i, direction, step],
            recv_sem.at[i, direction, step],
            ahead if direction == 0 else behind,
        )

    def first(i):
        for direction in range(2):
            slot = place(direction, hops(i, direction))
            copy(i, direction, 0, own[i], back[direction][i], slot).start()

    def reduce_step(i, s):
        for direction in range(2):
            count = hops(i, direction)
            if s < count:
                slot = place(direction, count - s)
                buffer = back[direction][i]
                copy(i, direction, s - 1, buffer, buffer, slot).wait_recv()
                add_into(buffer, slot, own[i])
                copy(i, direction, s, buffer, buffer, slot).start()

    def turn(i):
        for direction in range(2):
            buffer = back[direction][i]
            copy(i, direction, hops(i, direction) - 1, buffer, buffer, here).wait_recv()
        full[i][here] = (
            own[i][here].astype(F32) + back_up[i][here].astype(F32) + back_down[i][here].astype(F32)
        ).astype(BF16)
        for direction in range(2):
            copy(i, direction, long, full[i], full[i], here).start()

    def gather_step(i, s):
        for direction in range(2):
            if s < hops(i, direction):
                slot = place(1 - direction, s)
                copy(i, direction, long + s - 1, full[i], full[i], slot).wait_recv()
                copy(i, direction, long + s, full[i], full[i], slot).start()

    def end(i):
        for direction in range(2):
            count = hops(i, direction)
            slot = place(1 - direction, count)
            copy(i, direction, long + count - 1, full[i], full[i], slot).wait_recv()

    def drain(i):
        for direction in range(2):

            def sent(step, direction=direction):
                copy(i, direction, step, own[i], full[i], 0).wait_send()

            loop(sent, 0, hops(i, direction))
            loop(sent, long, long + hops(i, direction))

    def steps_of(i):
        done = [functools.partial(reduce_step, i, s) for s in range(1, long)]
        done.append(functools.partial(turn, i))
        done += [functools.partial(gather_step, i, s) for s in range(1, long)]
        done.append(functools.partial(end, i))
        return done

    for i in range(2):
        load(i, a_ref.at[i], 0, a_other.at[i])
        first(i)
    for i in range(2):
        load(2 + i, b_ref.at[i], 0, b_other.at[i])
        first(2 + i)
    load(4, o_ref, 0, o_other)
    first(4)
    waiting = [steps_of(i) for i in range(5)]

    def dense_step():
        for queue in waiting[0:5]:
            if queue:
                queue.pop(0)()

    rows = shard_rows(members, shard)
    raw[...] = in_ref[...].T
    for j in range(members):
        turned[j * shard : (j + 1) * shard, :] = raw[pl.ds(rows[j], shard), :]
    lane = lanes_of(x_ref.shape[0])
    cos, sin = cos_ref[...], sin_ref[...]
    for part in range(3):
        groups = [jnp.zeros(lane.shape, F32) for _ in range(D // LANES)]
        for d, head in enumerate(heads):
            g = head // 2
            packet = recv_ref[part, d].astype(F32)
            if head % 2 == 0:
                groups[g] = groups[g] + packet
            else:
                packet = pltpu.roll(packet, 64, 1)
                groups[g] = groups[g] + jnp.where(lane >= 64, packet, 0.0)
                groups[g + 1] = groups[g + 1] + jnp.where(lane < 64, packet, 0.0)
        for g, t in enumerate(groups):
            if part < 2:
                t = t.astype(BF16).astype(F32)
                t = t * cos - partner(t, lane) * sin
            dproj[:, part * D + g * LANES : part * D + (g + 1) * LANES] = t.astype(BF16)
        value = dot(turned[...], dproj[:, part * D : (part + 1) * D]).astype(BF16)
        for j in range(members):
            packs[part][j] = value[j * shard : (j + 1) * shard]
        level_copy(part, 0).start()
        if part > 0:
            level_next(part - 1)
    dense_step()
    dnorm = sum(
        dot_nt(dproj[:, part * D : (part + 1) * D], w_ref[part].reshape(D, D)) for part in range(3)
    )
    x = x_ref[...].astype(F32)
    gain = tail_ref[experts : experts + 1, :]
    inv = lax.rsqrt(jnp.mean(x * x, axis=-1, keepdims=True) + norm_eps)
    dgain_one = jnp.sum(dnorm * x * inv, axis=0, keepdims=True)
    row = lax.broadcasted_iota(jnp.int32, (LANES, D), 0)
    gains = jnp.where(row == experts, dgain_one, jnp.where(row == experts + 1, dgain_ref[...], 0.0))
    small[...] = router_ref[...] + gains.T
    for j in range(members):
        packs[3][j] = small[pl.ds(rows[j], shard), :].astype(BF16)
    level_copy(3, 0).start()
    level_next(2)
    scaled = dnorm * gain
    total = jnp.mean(scaled * x, axis=-1, keepdims=True)
    x_out[...] = dres_ref[...] + inv * scaled - x * inv * inv * inv * total
    level_next(3)
    for i in range(1, parts):
        e_copy(i, 1).start()

    for p in range(4):
        for b in range(1, bits):
            level_add(p, b)
            if b + 1 < bits:
                level_copy(p, b + 1).start()
        load(5 + p, packs[p].at[0])
        first(5 + p)
        for queue in waiting[5:]:
            queue.pop(0)()
        if p < 3:
            dense_step()
        waiting.append(steps_of(5 + p))
    turns = 0
    while any(waiting):
        turns += 1
        for i, queue in reversed(list(enumerate(waiting))):
            if queue and (i >= 5 or turns % 2 == 0 or not any(waiting[5:])):
                queue.pop(0)()
                if not queue and i < 5:
                    if i == 4:
                        save(i, c_out, PACKED)
                    elif i < 2:
                        save(i, a_out, i * splits[0][4])
                    else:
                        height = splits[2][0] * splits[2][2]
                        save(i, b_out.at[pl.ds((i - 2) * height, height)])
        if not any(waiting[0:5]) and parts > 1:
            e_add(1, 1)
            parts = min(parts, 1)
    for p in range(4):
        save(5 + p, c_out, p * D)
    parts = e_ref.shape[0]
    for i in range(2, parts):
        e_add(i, 1)
    if bits == 2:
        e_out[0] = e_ref[0, 0]
    for b in range(2, bits):
        for i in range(parts):
            e_copy(i, b).start()
        for i in range(parts):
            e_add(i, b)
    for b in range(bits):
        for p in range(4):
            level_copy(p, b).wait_send()
    for b in range(1, bits):
        for i in range(1 if b == 1 else 0, parts):
            e_copy(i, b).wait_send()

    for i in range(streams):
        drain(i)


def widen_kernel(
    experts,
    late_ref,
    a_ref,
    b_ref,
    in_ref,
    back_ref,
    x_ref,
    small_ref,
    qkv_out,
    w_out,
    a_out,
    b_out,
    in_out,
    back_out,
    x_out,
    router_out,
    gains_out,
):
    qkv_out[...] = late_ref[:, 0 : 3 * D].astype(F32)
    w_out[...] = late_ref[:, PACKED:].astype(F32)
    a_out[...] = a_ref[...].astype(F32)
    b_out[...] = b_ref[...].astype(F32)
    in_out[:, 0:FF] = in_ref[0].astype(F32)
    in_out[:, FF:] = in_ref[1].astype(F32)
    back_out[...] = back_ref[0].astype(F32)
    x_out[...] = x_ref[...]

    @pl.when(pl.program_id(0) == 0)
    def _():
        small = small_ref[...].astype(F32).T
        router_out[...] = small[0:experts]
        gains_out[...] = small[experts : experts + 2]


def on_device(
    tokens,
    cotangent,
    lengths,
    position_block,
    routes,
    gain_attn,
    w_qkv,
    w_out,
    gain_ffn,
    w_router,
    w_shared_in,
    w_shared_out,
    w_expert_in,
    w_expert_out,
):
    n_ctx = lax.axis_size("ctx")
    ctx_index = lax.axis_index("ctx")
    rows = tokens.shape[1]
    local = w_qkv.shape[0]
    experts = w_router.shape[1]
    capacity = 3 * rows // experts
    places = experts * capacity
    members = D // local
    share = HEADS * rows // n_ctx
    heads = first_heads(n_ctx, rows)
    gather = functools.partial(lax.all_gather, axis_name="fsdp", axis=0, tiled=True)
    exchange = functools.partial(
        lax.all_to_all, axis_name="ctx", split_axis=0, concat_axis=0, tiled=True
    )
    x = tokens[0]
    length = lengths[0]

    out_weight = gather(w_out)
    weights = gather(
        jnp.concatenate([w_shared_in, w_expert_in[0], w_expert_out[0].T], axis=1)
    )
    shared_out = gather(w_shared_out)
    bits = members.bit_length() - 1

    query_pos = position_block[ctx_index] * rows + jnp.arange(rows, dtype=jnp.int32)
    live = (query_pos < length).astype(F32)[:, None]
    rates = 10000.0 ** (-(np.arange(HEAD_DIM // 2) * 2.0 / HEAD_DIM))
    rates = jnp.asarray(np.tile(rates.astype(np.float32), 4)[None])

    order = jnp.sum(
        jnp.where(
            position_block[None, :] == jnp.arange(n_ctx, dtype=jnp.int32)[:, None],
            jnp.arange(n_ctx, dtype=jnp.int32)[None, :],
            0,
        ),
        axis=1,
    )
    head_of = jnp.minimum(share * ctx_index // rows, HEADS - 2)
    offset = share * ctx_index - rows * head_of
    scalars = jnp.concatenate(
        [order, jnp.stack([offset.astype(jnp.int32), length.astype(jnp.int32)])]
    )

    whole = pl.BlockSpec(memory_space=pltpu.VMEM)
    scalar = pl.BlockSpec(memory_space=pltpu.SMEM)
    block = places // n_ctx
    early = block // 48 * 16
    recv, attn_in, tail, target, dout, dy_first, dy_rest, qkv_weight, cos, sin = comm_call(
        functools.partial(open_kernel, n_ctx, members, heads, experts, capacity, early),
        (
            shape((3, n_ctx, rows, LANES), BF16),
            shape((rows, D), BF16),
            shape((LANES, D), F32),
            shape((rows, 2), jnp.int32),
            shape((rows, D), BF16),
            shape((n_ctx, early, D), BF16),
            shape((n_ctx, block - early, D), BF16),
            shape((3, members, local, D), BF16),
            shape((rows, LANES), F32),
            shape((rows, LANES), F32),
        ),
        3,
        in_specs=[scalar] * 2 + [whole] * 7,
        out_specs=[whole] * 10,
        scratch_shapes=[
            pltpu.VMEM((3, n_ctx, rows, LANES), BF16),
            pltpu.VMEM((n_ctx, early, D), BF16),
            pltpu.VMEM((LANES, local), F32),
            pltpu.VMEM((members, local, LANES), BF16),
            pltpu.SemaphoreType.DMA((4, bits, members)),
            pltpu.SemaphoreType.DMA((4, bits, members)),
            pltpu.SemaphoreType.DMA((3, n_ctx - 1)),
            pltpu.SemaphoreType.DMA((3, n_ctx - 1)),
            pltpu.SemaphoreType.DMA((n_ctx - 1,)),
            pltpu.SemaphoreType.DMA((n_ctx - 1,)),
            pltpu.SemaphoreType.DMA((4,)),
        ],
        nbytes=150 << 20,
    )(
        position_block,
        lengths,
        routes[0],
        cotangent[0],
        x,
        w_qkv,
        w_router.T,
        jnp.stack([gain_attn, gain_ffn]),
        rates,
    )
    dy_rest = exchange(dy_rest)

    packet = pl.BlockSpec((3, n_ctx, rows, LANES), lambda i, sc: (0, 0, 0, 0))
    block_of = lambda i, sc: (i, 0, 0)
    attended, kept, lse = call(
        functools.partial(attend_kernel, n_ctx, share),
        (
            shape((n_ctx, rows, LANES), BF16),
            shape((n_ctx, LANES, share), F32),
            shape((n_ctx, 1, share), F32),
        ),
        flops=2 * share * rows * n_ctx * n_ctx * LANES * 2,
        nbytes=5 << 20,
        grid_spec=pltpu.PrefetchScalarGridSpec(
            num_scalar_prefetch=1,
            grid=(n_ctx,),
            in_specs=[packet],
            out_specs=[
                pl.BlockSpec((1, rows, LANES), lambda i, sc: (sc[i], 0, 0)),
                pl.BlockSpec((1, LANES, share), block_of),
                pl.BlockSpec((1, 1, share), block_of),
            ],
            scratch_shapes=[
                pltpu.VMEM((2 * rows, LANES), BF16),
                pltpu.VMEM((n_ctx, rows, share), F32),
                pltpu.VMEM((2 * rows, LANES), F32),
            ],
        ),
    )(scalars, recv)
    attended, dy_rest = lax.optimization_barrier((attended, dy_rest))

    def full(*dims):
        return pl.BlockSpec(dims, lambda *at: (0,) * len(dims))

    came, residual, ffn_in, gates, x_rows, row_gates = comm_call(
        functools.partial(middle_kernel, n_ctx, heads, experts),
        (
            shape((n_ctx, rows, LANES), BF16),
            shape((rows, D), F32),
            shape((rows, D), BF16),
            shape((rows, LANES), F32),
            shape((places, D), BF16),
            shape((n_ctx, 8, LANES), F32),
        ),
        4,
        in_specs=[whole] * 6,
        out_specs=[whole] * 6,
        scratch_shapes=[
            pltpu.VMEM((places, D), BF16),
            pltpu.VMEM((n_ctx, 8, LANES), F32),
        ]
        + [pltpu.SemaphoreType.DMA((n_ctx - 1,)) for _ in range(6)]
        + [pltpu.SemaphoreType.DMA((3,))],
        nbytes=100 << 20,
    )(attended, out_weight, x, tail, routes[0], target)

    half, quarter = members // 2, members // 4
    steps = FS // CHUNK
    wide = FF // BROAD
    base = 2 * FS // BROAD
    expert_dx, row_dgates, expert_res, expert_mid, dy_rows = call(
        expert_kernel,
        (
            shape((places, D), BF16),
            shape((n_ctx, 8, LANES), F32),
            shape((places, D), BF16),
            shape((3, places, FF), BF16),
            shape((places, D), BF16),
        ),
        flops=2 * places * D * FF * 6,
        nbytes=24 << 20,
        grid=(wide,),
        in_specs=[
            full(places, D),
            full(n_ctx, 8, LANES),
            full(n_ctx, early, D),
            full(n_ctx, block - early, D),
            pl.BlockSpec((D, BROAD), lambda c: (0, base + c)),
            pl.BlockSpec((D, BROAD), lambda c: (0, base + wide + c)),
            pl.BlockSpec((D, BROAD), lambda c: (0, base + 2 * wide + c)),
        ],
        out_specs=[
            full(places, D),
            full(n_ctx, 8, LANES),
            full(places, D),
            pl.BlockSpec((3, places, BROAD), lambda c: (0, 0, c)),
            full(places, D),
        ],
        scratch_shapes=[
            pltpu.VMEM((places, D), F32),
            pltpu.VMEM((places, D), F32),
            pltpu.VMEM((places, LANES), F32),
            pltpu.VMEM((places, LANES), F32),
        ],
    )(x_rows, row_gates, dy_first, dy_rest, weights, weights, weights)
    b_rows = FS // members // 2
    anywhere = pl.BlockSpec(memory_space=pl.ANY)
    (
        branch_recv,
        shared_res,
        dres,
        branch,
        dlogits,
        dgain_two,
        dense_keep,
        dense_give,
        so_keep,
        so_came,
    ) = comm_call(
        functools.partial(shared_kernel, n_ctx, members, heads, experts),
        (
            shape((n_ctx, rows, LANES), BF16),
            shape((rows, D), F32),
            shape((rows, D), F32),
            shape((rows, D), BF16),
            shape((rows, LANES), BF16),
            shape((1, D), F32),
        )
        + (shape((2, quarter, local, FS), BF16),) * 2
        + (shape((2, quarter, b_rows, D), BF16),) * 2,
        2,
        in_specs=[whole] * 10 + [anywhere] * 2,
        out_specs=[whole] * 10,
        scratch_shapes=[
            pltpu.VMEM((places, D), BF16),
            pltpu.VMEM((n_ctx, 8, LANES), F32),
            pltpu.VMEM((n_ctx, rows, LANES), BF16),
            pltpu.VMEM((2, quarter, b_rows, D), BF16),
            pltpu.VMEM((2, rows, FS), BF16),
            pltpu.VMEM((rows, D), F32),
            pltpu.VMEM((2, members, local, FS), BF16),
            pltpu.VMEM((2, members, b_rows, D), BF16),
            pltpu.VMEM((2, half, local, FS), BF16),
            pltpu.VMEM((2, half, b_rows, D), BF16),
            pltpu.VMEM((D, rows), BF16),
            pltpu.VMEM((D, rows), BF16),
            pltpu.VMEM((2, D, CHUNK), BF16),
            pltpu.VMEM((2, D, CHUNK), BF16),
            pltpu.VMEM((2, CHUNK, D), BF16),
            pltpu.SemaphoreType.DMA((n_ctx - 1,)),
            pltpu.SemaphoreType.DMA((n_ctx - 1,)),
            pltpu.SemaphoreType.DMA((3,)),
            pltpu.SemaphoreType.DMA((n_ctx - 1,)),
            pltpu.SemaphoreType.DMA((n_ctx - 1,)),
            pltpu.SemaphoreType.DMA((n_ctx - 1,)),
            pltpu.SemaphoreType.DMA((n_ctx - 1,)),
            pltpu.SemaphoreType.DMA((2, 2)),
            pltpu.SemaphoreType.DMA((2, 2)),
            pltpu.SemaphoreType.DMA((2, 2)),
            pltpu.SemaphoreType.DMA((2, 3)),
        ],
        nbytes=150 << 20,
    )(
        expert_dx,
        row_dgates,
        ffn_in,
        dout,
        residual,
        gates,
        routes[0],
        target,
        tail,
        out_weight,
        weights,
        shared_out,
    )

    def gathered(terms):
        return sum(t.astype(F32) for t in terms).astype(BF16)

    def cross(give, b):
        return lax.ppermute(give, "fsdp", [(i, i ^ (1 << b)) for i in range(members)])

    def rest_of(keep, came_in):
        for b in range(2, bits):
            count = keep.shape[1] // 2
            give = gathered([keep[:, count:], came_in[:, count:]])
            keep = gathered([keep[:, :count], came_in[:, :count]])
            came_in = cross(give, b)
        return keep[:, 0], came_in[:, 0]

    branch_recv, expert_res = lax.optimization_barrier((branch_recv, expert_res))
    dense_part, dense_other = rest_of(dense_keep, cross(dense_give, 1))
    so_part, so_other = rest_of(so_keep, so_came)

    dsend = call(
        functools.partial(attend_back_kernel, n_ctx, share),
        shape((3, n_ctx, rows, LANES), BF16),
        flops=2 * share * rows * n_ctx * n_ctx * LANES * 3,
        nbytes=8 << 20,
        grid_spec=pltpu.PrefetchScalarGridSpec(
            num_scalar_prefetch=1,
            grid=(n_ctx,),
            in_specs=[
                packet,
                pl.BlockSpec((n_ctx, rows, LANES), lambda i, sc: (0, 0, 0)),
                pl.BlockSpec((1, LANES, share), block_of),
                pl.BlockSpec((1, 1, share), block_of),
            ],
            out_specs=packet,
            scratch_shapes=[
                pltpu.VMEM((2 * rows, LANES), BF16),
                pltpu.VMEM((2 * rows, LANES), BF16),
                pltpu.VMEM((n_ctx, rows, LANES), F32),
                pltpu.VMEM((n_ctx, rows, LANES), F32),
                pltpu.VMEM((2 * rows, LANES), F32),
            ],
        ),
    )(scalars, recv, branch_recv, kept, lse)
    res_came = exchange(expert_res.reshape(n_ctx, -1, D)).reshape(places, D)
    drecv, expert_sum, out_keep, out_came, grad_router, output = comm_call(
        functools.partial(back_exchange_kernel, n_ctx, members, heads),
        (
            shape((3, n_ctx, rows, LANES), BF16),
            shape((3, half, local, FF), BF16),
            shape((quarter, local, D), BF16),
            shape((quarter, local, D), BF16),
            shape((D, LANES), F32),
            shape((rows, D), BF16),
        ),
        1,
        in_specs=[whole] * 13 + [anywhere],
        out_specs=[whole] * 6,
        scratch_shapes=[
            pltpu.VMEM((3, half, local, FF), BF16),
            pltpu.VMEM((3, half, local, FF), BF16),
            pltpu.VMEM((quarter, local, FF), BF16),
            pltpu.VMEM((members, local, D), BF16),
            pltpu.VMEM((half, local, D), BF16),
            pltpu.VMEM((D, places), BF16),
            pltpu.VMEM((D, places), BF16),
            pltpu.VMEM((D, places), BF16),
            pltpu.VMEM((D, D), F32),
            pltpu.VMEM((2, places, BROAD), BF16),
            pltpu.SemaphoreType.DMA((n_ctx - 1,)),
            pltpu.SemaphoreType.DMA((n_ctx - 1,)),
            pltpu.SemaphoreType.DMA,
            pltpu.SemaphoreType.DMA((3,)),
            pltpu.SemaphoreType.DMA((3,)),
            pltpu.SemaphoreType.DMA((2,)),
            pltpu.SemaphoreType.DMA((4,)),
            pltpu.SemaphoreType.DMA((2,)),
        ],
        nbytes=120 << 20,
    )(
        dsend,
        x_rows,
        dy_rows,
        came,
        branch,
        ffn_in,
        dlogits,
        residual,
        shared_res,
        gates,
        target,
        live,
        res_came,
        expert_mid,
    )

    late_width = PACKED + D
    out_part, out_other = rest_of(out_keep[None], out_came[None])
    late_widths = [D, D, D, LANES]
    sizes = [(local, FS)] * 2 + [(FS // members // 2, D)] * 2 + [(local, D)]
    sizes += [(local, width) for width in late_widths]
    splits = [ring_split(r, c, n_ctx) + (c,) for r, c in sizes]
    tiles = [(n_ctx, t[2], t[3]) for t in splits]
    grad_x, dense_sum, so_sum, last_sum, expert_sum = comm_call(
        functools.partial(last_kernel, n_ctx, members, heads, experts, splits),
        (
            shape((rows, D), F32),
            shape((local, 2 * FS), BF16),
            shape((FS // members, D), BF16),
            shape((local, late_width), BF16),
            shape((3, local, FF), BF16),
        ),
        0,
        in_specs=[whole] * 17,
        out_specs=[whole] * 5,
        scratch_shapes=[pltpu.VMEM(t, BF16) for t in tiles * 4]
        + [pltpu.VMEM((members, local, width), BF16) for width in late_widths]
        + [
            pltpu.VMEM((members >> (b + 1), local, width), BF16)
            for b in range(bits)
            for width in late_widths
        ]
        + [pltpu.VMEM((3, members >> (b + 1), local, FF), BF16) for b in range(1, bits)]
        + [
            pltpu.VMEM((rows, 3 * D), BF16),
            pltpu.VMEM((D, rows), BF16),
            pltpu.VMEM((D, rows), BF16),
            pltpu.VMEM((D, LANES), F32),
            pltpu.SemaphoreType.DMA((9, 2, n_ctx)),
            pltpu.SemaphoreType.DMA((9, 2, n_ctx)),
            pltpu.SemaphoreType.DMA((4, bits)),
            pltpu.SemaphoreType.DMA((4, bits)),
            pltpu.SemaphoreType.DMA((3, max(1, bits - 1))),
            pltpu.SemaphoreType.DMA((3, max(1, bits - 1))),
        ],
        nbytes=200 << 20,
    )(
        drecv,
        cos,
        sin,
        attn_in,
        x,
        qkv_weight,
        tail,
        dres,
        grad_router,
        dgain_two,
        dense_part,
        dense_other,
        so_part,
        so_other,
        out_part[0],
        out_other[0],
        expert_sum,
    )

    quarters = 4 if local % 64 == 0 else 1

    def rows_of(count, width):
        return pl.BlockSpec((count // quarters, width), lambda i: (i, 0))

    grad_qkv, grad_out, grad_si, grad_so, grad_ei, grad_eo, grad_x, grad_router, gains = call(
        functools.partial(widen_kernel, experts),
        (
            shape((local, 3 * D), F32),
            shape((local, D), F32),
            shape((local, 2 * FS), F32),
            shape((FS // members, D), F32),
            shape((local, 2 * FF), F32),
            shape((local, FF), F32),
            shape((rows, D), F32),
            shape((experts, local), F32),
            shape((2, local), F32),
        ),
        flops=0,
        nbytes=22 << 20,
        grid=(quarters,),
        in_specs=[
            rows_of(local, late_width),
            rows_of(local, 2 * FS),
            rows_of(FS // members, D),
            pl.BlockSpec((2, local // quarters, FF), lambda i: (0, i, 0)),
            pl.BlockSpec((1, local // quarters, FF), lambda i: (2, i, 0)),
            rows_of(rows, D),
            pl.BlockSpec((local, LANES), lambda i: (0, 3 * D // LANES)),
        ],
        out_specs=[
            rows_of(local, 3 * D),
            rows_of(local, D),
            rows_of(local, 2 * FS),
            rows_of(FS // members, D),
            rows_of(local, 2 * FF),
            rows_of(local, FF),
            rows_of(rows, D),
            full(experts, local),
            full(2, local),
        ],
    )(last_sum, dense_sum, so_sum, expert_sum, expert_sum, grad_x, last_sum)
    return (
        output[None],
        grad_x[None],
        gains[0],
        grad_qkv,
        grad_out,
        gains[1],
        grad_router.T,
        grad_si,
        grad_so,
        grad_ei[None],
        grad_eo.T[None],
    )


def solution(mesh):
    row_spec = P("fsdp", "ctx", None)
    flat = P("fsdp", None)
    return jax.shard_map(
        on_device,
        mesh=mesh,
        in_specs=(
            row_spec,
            row_spec,
            P("fsdp"),
            P(),
            row_spec,
            P("fsdp"),
            flat,
            flat,
            P("fsdp"),
            flat,
            flat,
            flat,
            P("ctx", "fsdp", None),
            P("ctx", None, "fsdp"),
        ),
        out_specs=(
            row_spec,
            row_spec,
            P("fsdp"),
            flat,
            flat,
            P("fsdp"),
            flat,
            flat,
            flat,
            P("ctx", "fsdp", None),
            P("ctx", None, "fsdp"),
        ),
        check_vma=False,
    )
```

```python
import functools

import jax
import jax.numpy as jnp
import numpy as np
from jax import lax
from jax.experimental import pallas as pl
from jax.experimental.pallas import tpu as pltpu
from jax.sharding import PartitionSpec as P

D = 768
HEADS = 12
HEAD_DIM = 64
FF = 2048
FS = 2048
LANES = 128
CHUNK = 256
BROAD = 512
PACKED = 3 * D + LANES
norm_eps = 1e-06
F32 = jnp.float32
BF16 = jnp.bfloat16


def dot(a, b):
    return jnp.dot(a, b, preferred_element_type=F32)


def dot_nt(a, b):
    return lax.dot_general(a, b, (((1,), (1,)), ((), ())), preferred_element_type=F32)


def dot_tn(a, b):
    return lax.dot_general(a, b, (((0,), (0,)), ((), ())), preferred_element_type=F32)


def call(kernel, outs, *, flops, nbytes, limit=56, **kw):
    return pl.pallas_call(
        kernel,
        out_shape=outs,
        compiler_params=pltpu.CompilerParams(vmem_limit_bytes=limit << 20),
        cost_estimate=pl.CostEstimate(
            flops=int(flops), bytes_accessed=int(nbytes), transcendentals=0
        ),
        **kw,
    )


def comm_call(kernel, outs, number, *, nbytes, limit=60, **kw):
    return pl.pallas_call(
        kernel,
        out_shape=outs,
        compiler_params=pltpu.CompilerParams(
            collective_id=number, has_side_effects=True, vmem_limit_bytes=limit << 20
        ),
        cost_estimate=pl.CostEstimate(flops=0, bytes_accessed=int(nbytes), transcendentals=0),
        **kw,
    )


def shape(dims, dtype):
    return jax.ShapeDtypeStruct(dims, dtype)


def lanes_of(rows, width=LANES):
    return lax.broadcasted_iota(jnp.int32, (rows, width), 1)


def first_heads(n_ctx, slot_dev):
    share = HEADS * slot_dev // n_ctx
    return [min(share * d // slot_dev, HEADS - 2) for d in range(n_ctx)]


def partner(t, lane):
    return jnp.where(lane % 64 < 32, pltpu.roll(t, 96, 1), pltpu.roll(t, 32, 1))


def picks(target_ref, places):
    rows = target_ref.shape[0]
    place = lanes_of(rows, places)
    return tuple(
        jnp.where(place == target_ref[:, k : k + 1], 1.0, 0.0).astype(BF16) for k in range(2)
    )


def flipped(index, mask):
    for b in range(mask.bit_length()):
        if mask >> b & 1:
            index = index + (1 << b) - 2 * (1 << b) * (index // (1 << b) % 2)
    return index


def mirrored(members):
    bits = members.bit_length() - 1
    return [int(format(j, "b").zfill(bits)[::-1], 2) for j in range(members)]


def shard_rows(members, shard):
    fsdp = lax.axis_index("fsdp")
    return [pl.multiple_of(flipped(fsdp, m) * shard, 16) for m in mirrored(members)]


def remote(source, target, send_sem, recv_sem, peer):
    return pltpu.make_async_remote_copy(
        src_ref=source,
        dst_ref=target,
        send_sem=send_sem,
        recv_sem=recv_sem,
        device_id=peer,
        device_id_type=pl.DeviceIdType.MESH,
    )


def greet(peers):
    barrier = pltpu.get_barrier_semaphore()
    for peer in peers:
        pl.semaphore_signal(barrier, inc=1, device_id=peer, device_id_type=pl.DeviceIdType.MESH)
    pl.semaphore_wait(barrier, len(peers))


def mates_of(members):
    ctx, fsdp = lax.axis_index("ctx"), lax.axis_index("fsdp")
    return [(ctx, flipped(fsdp, 1 << b)) for b in range(members.bit_length() - 1)]


def row_peers(n):
    ctx, fsdp = lax.axis_index("ctx"), lax.axis_index("fsdp")
    return [(lax.rem(ctx + d, n), fsdp) for d in range(1, n)]


def loop(body, low, high):
    lax.fori_loop(low, high, lambda s, carry: (body(s), carry)[1], 0)


def add_into(target, j, other):
    target[j] = (target[j].astype(F32) + other[j].astype(F32)).astype(BF16)


def open_kernel(
    n,
    members,
    heads,
    experts,
    capacity,
    early,
    where_ref,
    length_ref,
    routes_ref,
    cot_ref,
    x_ref,
    w_ref,
    router_ref,
    gains_ref,
    turn_ref,
    query_ref,
    recv_ref,
    in_ref,
    tail_ref,
    target_ref,
    dout_ref,
    dy_ref,
    dy_rest_ref,
    w_all,
    cos_ref,
    sin_ref,
    query_send,
    send,
    dy_send,
    small,
    small_all,
    gather_send,
    gather_recv,
    packet_send,
    packet_recv,
    dy_send_sem,
    dy_recv_sem,
    own_sem,
):
    ctx, fsdp = lax.axis_index("ctx"), lax.axis_index("fsdp")
    bits = members.bit_length() - 1
    peers = row_peers(n)
    mates = mates_of(members)
    shard = w_ref.shape[0]
    rows = x_ref.shape[0]
    small[...] = jnp.zeros_like(small)
    small[0:experts] = router_ref[...].astype(F32)
    small[experts : experts + 2] = gains_ref[...].astype(F32)
    small_all[fsdp] = small[...].T.astype(BF16)
    for part in range(3):
        w_all[part, fsdp] = w_ref[:, part * D : (part + 1) * D]
    greet(peers + mates)

    def gather_copy(p, b, mask):
        buffer = small_all if p == 3 else w_all.at[p]
        spot = flipped(fsdp, mask)
        return remote(
            buffer.at[spot],
            buffer.at[spot],
            gather_send.at[p, b, mask],
            gather_recv.at[p, b, mask],
            mates[b],
        )

    def gather_wait(p, b, mask):
        buffer = small_all if p == 3 else w_all.at[p]
        spot = flipped(fsdp, mask | 1 << b)
        remote(
            buffer.at[spot],
            buffer.at[spot],
            gather_send.at[p, b, mask],
            gather_recv.at[p, b, mask],
            mates[b],
        ).wait_recv()

    for p in (3, 0, 1, 2):
        for b in reversed(range(bits)):
            gather_copy(p, b, 0).start()

    def gather_rest(p):
        masks = [0]
        for b in reversed(range(bits)):
            for mask in masks[1:]:
                gather_copy(p, b, mask).start()
            for mask in masks:
                gather_wait(p, b, mask)
            masks = masks + [mask | 1 << b for mask in masks]

    lane = lanes_of(rows)
    hot = [jnp.where(lane == routes_ref[:, k : k + 1], 1.0, 0.0) for k in range(2)]
    below = jnp.where(
        lanes_of(rows, rows) < lax.broadcasted_iota(jnp.int32, (rows, rows), 0), 1.0, 0.0
    )
    before = dot(below.astype(BF16), (hot[0] + hot[1]).astype(BF16))
    place = [
        routes_ref[:, k : k + 1] * capacity
        + jnp.sum(hot[k] * before, axis=-1, keepdims=True).astype(jnp.int32)
        for k in range(2)
    ]
    for k in range(2):
        target_ref[:, k : k + 1] = place[k]
    position = where_ref[ctx] * rows + lax.broadcasted_iota(jnp.int32, (rows, D), 0)
    dout = jnp.where(position < length_ref[0], cot_ref[...].astype(F32), 0.0).astype(BF16)
    dout_ref[...] = dout
    places = experts * capacity
    spot = lanes_of(rows, places)
    pick = jnp.where((spot == place[0]) | (spot == place[1]), 1.0, 0.0).astype(BF16)
    packed = dot_tn(pick, dout).astype(BF16)
    block = places // n
    for p in range(n):
        dy_send[p] = packed[p * block : p * block + early]
        dy_rest_ref[p] = packed[p * block + early : (p + 1) * block]
    own = [
        pltpu.make_async_copy(dy_send.at[ctx], dy_ref.at[ctx], own_sem.at[3]),
    ]
    own[0].start()
    copies = [
        remote(dy_send.at[p[0]], dy_ref.at[ctx], dy_send_sem.at[d], dy_recv_sem.at[d], p)
        for d, p in enumerate(peers)
    ]
    for c in copies:
        c.start()

    x = x_ref[...].astype(F32)
    inv = lax.rsqrt(jnp.mean(x * x, axis=-1, keepdims=True) + norm_eps)
    gather_rest(3)
    tail = small_all[...].reshape(D, LANES).astype(F32).T
    tail_ref[...] = tail
    attn_in = (x * inv * tail[experts : experts + 1, :]).astype(BF16)
    in_ref[...] = attn_in
    position = where_ref[ctx] * rows + lax.broadcasted_iota(jnp.int32, (rows, LANES), 0)
    angles = position.astype(F32) * turn_ref[...]
    cos, sin = jnp.cos(angles), jnp.sin(angles)
    sin = jnp.where(lane % 64 < 32, -sin, sin)
    cos_ref[...] = cos
    sin_ref[...] = sin
    for part in range(3):
        gather_rest(part)
        y = dot(attn_in, w_all[part].reshape(D, D))
        groups = []
        for g in range(D // LANES):
            t = y[:, g * LANES : (g + 1) * LANES]
            if part < 2:
                t = t * cos + partner(t, lane) * sin
            groups.append(t)
        turned = [pltpu.roll(t, 64, 1) for t in groups]
        for d, head in enumerate(heads):
            g = head // 2
            if head % 2 == 0:
                packet = groups[g]
            else:
                packet = jnp.where(lane < 64, turned[g], turned[g + 1])
            if part == 0:
                query_send[d] = fold(n, d, packet).astype(BF16)
            else:
                send[part - 1, d] = packet.astype(BF16)
        source = query_send if part == 0 else send.at[part - 1]
        target = query_ref if part == 0 else recv_ref.at[part - 1]
        own.append(
            pltpu.make_async_copy(source.at[ctx], target.at[ctx], own_sem.at[part])
        )
        own[-1].start()
        for d, p in enumerate(peers):
            copies.append(
                remote(
                    source.at[p[0]],
                    target.at[ctx],
                    packet_send.at[part, d],
                    packet_recv.at[part, d],
                    p,
                )
            )
            copies[-1].start()
    for c in copies + own:
        c.wait()
    for p in range(4):
        masks = [0]
        for b in reversed(range(bits)):
            for mask in masks:
                gather_copy(p, b, mask).wait_send()
            masks = masks + [mask | 1 << b for mask in masks]


def folds(n, rows):
    return 2 * HEADS * rows == 3 * n * rows


def packet_rows(n, rows):
    return rows * 3 // 4 if folds(n, rows) else rows


def fold(n, d, block):
    rows = block.shape[0]
    if not folds(n, rows):
        return block
    half, quarter = rows // 2, rows // 4
    lane = lanes_of(quarter)
    if d % 2 == 0:
        both, one = block[0:half], block[half:]
        lone = jnp.where(lane < 64, one[0:quarter], pltpu.roll(one[quarter:], 64, 1))
    else:
        both, one = block[half:], block[0:half]
        lone = jnp.where(lane < 64, pltpu.roll(one[0:quarter], 64, 1), one[quarter:])
    return jnp.concatenate([both, lone], axis=0)


def unfold(n, d, block, rows):
    if not folds(n, rows):
        return block
    half, quarter = rows // 2, rows // 4
    both, lone = block[0:half], block[half:]
    turned = pltpu.roll(lone, 64, 1)
    lane = lanes_of(quarter)
    zero = jnp.zeros((), block.dtype)
    if d % 2 == 0:
        pieces = [both, jnp.where(lane < 64, lone, zero), jnp.where(lane < 64, turned, zero)]
    else:
        pieces = [jnp.where(lane < 64, zero, turned), jnp.where(lane < 64, zero, lone), both]
    return jnp.concatenate(pieces, axis=0)


def stack_folded(stack_ref, block, odd):
    count = block.shape[0]
    half, quarter = count * 2 // 3, count // 3
    lane = lanes_of(half)
    zero = jnp.zeros((), block.dtype)
    both, lone = block[0:half], block[half:]
    stack_ref[0:half, :] = jnp.where(lane < 64, both, zero)
    stack_ref[half : 2 * half, :] = jnp.where(lane < 64, zero, both)
    turned = pltpu.roll(lone, 64, 1)
    lane = lanes_of(quarter)
    low = jnp.where(odd, turned, lone)
    high = jnp.where(odd, lone, turned)
    keep = (lane < 64) != odd
    stack_ref[2 * half : 2 * half + quarter, :] = jnp.where(keep, low, zero)
    stack_ref[2 * half + quarter : 2 * half + 2 * quarter, :] = jnp.where(keep, high, zero)


def fold_stack(block, odd):
    half = block.shape[0] // 3
    quarter = half // 2
    both = jnp.where(lanes_of(half) < 64, block[0:half], block[half : 2 * half])
    low, high = block[2 * half : 2 * half + quarter], block[2 * half + quarter :]
    lane = lanes_of(quarter)
    even_way = jnp.where(lane < 64, low, pltpu.roll(high, 64, 1))
    odd_way = jnp.where(lane < 64, pltpu.roll(low, 64, 1), high)
    return jnp.concatenate([both, jnp.where(odd, odd_way, even_way)], axis=0)


def stack_rows(stack_ref, block, lane):
    rows = block.shape[0]
    zero = jnp.zeros((), block.dtype)
    stack_ref[0:rows, :] = jnp.where(lane < 64, block, zero)
    stack_ref[rows : 2 * rows, :] = jnp.where(lane >= 64, block, zero)


def unstack_rows(stack_ref, block, offset, lane):
    rows = stack_ref.shape[0] // 2
    stack_ref[...] = jnp.zeros_like(stack_ref)
    stack_ref[pl.ds(offset, block.shape[0]), :] = block
    return jnp.where(lane < 64, stack_ref[0:rows, :], stack_ref[rows : 2 * rows, :])


def key_limits(n, share, rows, q_block, offset, length):
    row = lax.broadcasted_iota(jnp.int32, (1, share), 1)
    if folds(n, rows):
        half = rows // 2
        odd = jnp.where(offset > 0, half, 0)
        row = jnp.where(
            row < half, row + odd, jnp.where(row < rows, row - half + odd, row - half - odd)
        )
    else:
        row = row + offset
        row = jnp.where(row >= rows, row - rows, row)
    return jnp.minimum(q_block * rows + row + 1, length)


def attend_kernel(n, share, sc, query_ref, recv_ref, out_ref, keep_ref, lse_ref, stack, scores, back):
    q_block = pl.program_id(0)
    rows = recv_ref.shape[2]
    offset = pl.multiple_of(sc[n], 64)
    length = sc[n + 1]
    lane = lanes_of(rows)
    block = query_ref[sc[q_block]] * 0.125
    if folds(n, rows):
        stack_folded(stack, block, offset > 0)
        query = stack[0:share, :]
    else:
        stack_rows(stack, block, lane)
        query = stack[pl.ds(offset, share), :]
    limit = key_limits(n, share, rows, q_block, offset, length)
    key_row = lax.broadcasted_iota(jnp.int32, (rows, share), 0)
    blocks = jnp.minimum(q_block + 1, (length + rows - 1) // rows)

    def score_step(pair, top):
        found = []
        for j in (2 * pair, 2 * pair + 1):
            s = dot_nt(recv_ref[0, sc[j]], query)
            s = jnp.where(key_row < limit - j * rows, s, -1e30)
            scores[j] = s
            found.append(jnp.max(s, axis=0, keepdims=True))
        return jnp.maximum(top, jnp.maximum(found[0], found[1]))

    pairs = (blocks + 1) // 2
    top = lax.fori_loop(0, pairs, score_step, jnp.full((1, share), -1e30, F32))

    def value_step(pair, carry):
        total, acc = carry
        for j in (2 * pair, 2 * pair + 1):
            weights = jnp.exp(scores[j] - top)
            total = total + jnp.sum(weights, axis=0, keepdims=True)
            acc = acc + dot_tn(recv_ref[1, sc[j]], weights.astype(BF16))
        return total, acc

    total, acc = lax.fori_loop(
        0, pairs, value_step, (jnp.zeros((1, share), F32), jnp.zeros((LANES, share), F32))
    )
    acc = acc / total
    keep_ref[0] = acc
    lse_ref[0] = top + jnp.log(total)
    if folds(n, rows):
        out_ref[0] = fold_stack(acc.T, offset > 0).astype(BF16)
    else:
        out_ref[0] = unstack_rows(back, acc.T, offset, lane).astype(BF16)


def attend_back_kernel(
    n,
    share,
    sc,
    query_ref,
    recv_ref,
    grad_ref,
    keep_ref,
    lse_ref,
    query_out,
    out_ref,
    stack,
    gstack,
    dkeys,
    dvalues,
    back,
):
    q_block = pl.program_id(0)
    rows = recv_ref.shape[2]
    offset = pl.multiple_of(sc[n], 64)
    length = sc[n + 1]
    lane = lanes_of(rows)
    source = sc[q_block]

    @pl.when(q_block == 0)
    def _():
        dkeys[...] = jnp.zeros_like(dkeys)
        dvalues[...] = jnp.zeros_like(dvalues)

    block = query_ref[source] * 0.125
    if folds(n, rows):
        stack_folded(stack, block, offset > 0)
        query = stack[0:share, :]
        stack_folded(gstack, grad_ref[source], offset > 0)
        grad = gstack[0:share, :]
    else:
        stack_rows(stack, block, lane)
        query = stack[pl.ds(offset, share), :]
        stack_rows(gstack, grad_ref[source], lane)
        grad = gstack[pl.ds(offset, share), :]
    lse = lse_ref[0]
    delta = jnp.sum(grad.astype(F32).T * keep_ref[0], axis=0, keepdims=True)
    limit = key_limits(n, share, rows, q_block, offset, length)
    key_row = lax.broadcasted_iota(jnp.int32, (rows, share), 0)
    blocks = jnp.minimum(q_block + 1, (length + rows - 1) // rows)

    def step(pair, acc):
        for j in (2 * pair, 2 * pair + 1):
            keys = recv_ref[0, sc[j]]
            values = recv_ref[1, sc[j]]
            s = dot_nt(keys, query)
            weights = jnp.exp(jnp.where(key_row < limit - j * rows, s, -1e30) - lse)
            dweights = dot_nt(values, grad)
            dscores = (weights * (dweights - delta)).astype(BF16)
            dkeys[j] += dot(dscores, query)
            dvalues[j] += dot(weights.astype(BF16), grad)
            acc = acc + dot_tn(keys, dscores)
        return acc

    acc = lax.fori_loop(0, (blocks + 1) // 2, step, jnp.zeros((LANES, share), F32))
    if folds(n, rows):
        dquery = fold_stack(acc.T * 0.125, offset > 0)
    else:
        dquery = unstack_rows(back, acc.T * 0.125, offset, lane)
    query_out[source] = dquery.astype(BF16)

    @pl.when(q_block == n - 1)
    def _():
        def flush(j, carry):
            out_ref[0, sc[j]] = dkeys[j].astype(BF16)
            out_ref[1, sc[j]] = dvalues[j].astype(BF16)
            return carry

        lax.fori_loop(0, n, flush, 0)


def middle_kernel(
    n,
    heads,
    experts,
    attended_ref,
    w_ref,
    x_ref,
    tail_ref,
    routes_ref,
    target_ref,
    came_ref,
    residual_ref,
    in_ref,
    gates_ref,
    rows_ref,
    row_gates_ref,
    packets,
    outgoing,
    outgates,
    came_send,
    came_recv,
    send_sem,
    recv_sem,
    gate_send,
    gate_recv,
    own_sem,
):
    ctx = lax.axis_index("ctx")
    peers = row_peers(n)
    greet(peers)
    own = pltpu.make_async_copy(attended_ref.at[ctx], packets.at[ctx], own_sem.at[0])
    own.start()
    copies = [
        remote(attended_ref.at[p[0]], packets.at[ctx], came_send.at[d], came_recv.at[d], p)
        for d, p in enumerate(peers)
    ]
    for c in copies:
        c.start()
    pick = picks(target_ref, rows_ref.shape[0])
    lane = lanes_of(x_ref.shape[0])
    total = x_ref[...].astype(F32)
    for c in copies:
        c.wait()
    own.wait()
    for d, head in enumerate(heads):
        came = unfold(n, d, packets[d], total.shape[0])
        came_ref[d] = came
        total = total + dot(came, w_ref[64 * head : 64 * head + LANES, :])
    residual_ref[...] = total
    inv = lax.rsqrt(jnp.mean(total * total, axis=-1, keepdims=True) + norm_eps)
    ffn_in = (total * inv * tail_ref[experts + 1 : experts + 2, :]).astype(BF16)
    in_ref[...] = ffn_in
    logits = dot_nt(ffn_in, tail_ref[...].astype(BF16))
    chosen = [
        jnp.sum(jnp.where(lane == routes_ref[:, k : k + 1], logits, 0.0), axis=-1, keepdims=True)
        for k in range(2)
    ]
    top = jnp.maximum(chosen[0], chosen[1])
    raised = [jnp.exp(c - top) for c in chosen]
    gates = [r / (raised[0] + raised[1]) for r in raised]
    gates_ref[...] = jnp.where(lane == 0, gates[0], gates[1])
    outgoing[...] = dot_tn(pick[0] + pick[1], ffn_in).astype(BF16)
    block = outgoing.shape[0] // n

    def block_at(p):
        return pl.ds(pl.multiple_of(p * block, 16), block)

    own = [
        pltpu.make_async_copy(
            outgoing.at[block_at(ctx)], rows_ref.at[block_at(ctx)], own_sem.at[1]
        )
    ]
    copies = [
        remote(
            outgoing.at[block_at(p[0])],
            rows_ref.at[block_at(ctx)],
            send_sem.at[d],
            recv_sem.at[d],
            p,
        )
        for d, p in enumerate(peers)
    ]
    for c in own + copies:
        c.start()
    for p in range(n):
        row = sum(
            jnp.sum(
                jnp.where(lane == target_ref[:, k : k + 1] - p * block, gates[k], 0.0),
                axis=0,
                keepdims=True,
            )
            for k in range(2)
        )
        outgates[p] = jnp.broadcast_to(row, outgates.shape[1:])
    own.append(pltpu.make_async_copy(outgates.at[ctx], row_gates_ref.at[ctx], own_sem.at[2]))
    own[-1].start()
    for d, p in enumerate(peers):
        copies.append(
            remote(
                outgates.at[p[0]], row_gates_ref.at[ctx], gate_send.at[d], gate_recv.at[d], p
            )
        )
        copies[-1].start()
    for c in copies + own:
        c.wait()


def gated(g, u, da):
    sig = 0.5 * jnp.tanh(0.5 * g) + 0.5
    silu = g * sig
    return silu * u, da * u * sig * (1.0 + g * (1.0 - sig)), da * silu


def expert_kernel(
    x_ref,
    gates_ref,
    first_ref,
    rest_ref,
    wg_ref,
    wu_ref,
    wt_ref,
    dx_ref,
    dgate_ref,
    res_ref,
    mid_ref,
    dy_ref,
    dx_acc,
    res_acc,
    dgate,
    gate_rows,
):
    c = pl.program_id(0)

    @pl.when(c == 0)
    def _():
        res_acc[...] = jnp.zeros_like(res_acc)
        dx_acc[...] = jnp.zeros_like(dx_acc)
        dgate[...] = jnp.zeros_like(dgate)
        n, early = first_ref.shape[0:2]
        block = early + rest_ref.shape[1]
        for p in range(n):
            dy_ref[p * block : p * block + early] = first_ref[p]
            dy_ref[p * block + early : (p + 1) * block] = rest_ref[p]
            column = gates_ref[p].T[0:block, 0:1]
            gate_rows[p * block : (p + 1) * block] = jnp.broadcast_to(column, (block, LANES))

    x, dy = x_ref[...], dy_ref[...]
    gate = gate_rows[:, 0:1]
    wg, wu, wt = wg_ref[...], wu_ref[...], wt_ref[...]
    da = dot(dy, wt)
    act, dg, du = gated(dot(x, wg), dot(x, wu), da * gate)
    dgate[...] += jnp.sum(act * da, axis=-1, keepdims=True)
    mid_ref[2] = (act * gate).astype(BF16)
    act, dg, du = act.astype(BF16), dg.astype(BF16), du.astype(BF16)
    res_acc[...] += dot_nt(act, wt)
    dx_acc[...] += dot_nt(dg, wg) + dot_nt(du, wu)
    mid_ref[0] = dg
    mid_ref[1] = du

    @pl.when(c == pl.num_programs(0) - 1)
    def _():
        res_ref[...] = res_acc[...].astype(BF16)
        dx_ref[...] = dx_acc[...].astype(BF16)
        n, early = first_ref.shape[0:2]
        block = early + rest_ref.shape[1]
        dgate_ref[...] = jnp.zeros_like(dgate_ref)
        for p in range(n):
            dgate_ref[p, :, 0:block] = dgate[p * block : (p + 1) * block].T[0:8]


def ring_split(rows, columns, pieces):
    down = 1
    while 2 * down <= pieces and rows % (32 * down) == 0:
        down *= 2
    across = pieces // down
    width = -(-columns // (LANES * across)) * LANES
    return down, across, rows // down, width


def ring_place(position, n):
    half = n // 2
    return jnp.where(position < half, 2 * position, 2 * (n - 1 - position) + 1)


def shared_kernel(
    n,
    members,
    heads,
    experts,
    send_ref,
    row_dgates_ref,
    in_ref,
    dout_ref,
    residual_ref,
    gates_ref,
    routes_ref,
    target_ref,
    tail_ref,
    w_ref,
    wide_ref,
    back_ref,
    recv_ref,
    res_ref,
    dres_ref,
    branch_ref,
    dlogits_ref,
    dgain_ref,
    a_keep,
    a_give,
    b_keep,
    b_other,
    came,
    came_dgates,
    packets,
    b_give,
    mids,
    dx_acc,
    a_all,
    b_all,
    a_caught,
    b_caught,
    raw,
    xt,
    gate_buf,
    up_buf,
    back_buf,
    send_sem,
    recv_sem,
    own_sem,
    packet_send,
    packet_recv,
    dgate_send,
    dgate_recv,
    a_sem,
    b_sem,
    far_sem,
    w_sem,
):
    ctx, fsdp = lax.axis_index("ctx"), lax.axis_index("fsdp")
    bits = members.bit_length() - 1
    peers = row_peers(n)
    mate, far = mates_of(members)[0:2]
    greet(peers + [mate, far])
    block = send_ref.shape[0] // n

    def block_at(p):
        return pl.ds(pl.multiple_of(p * block, 16), block)

    copies = [
        pltpu.make_async_copy(send_ref.at[block_at(ctx)], came.at[block_at(ctx)], own_sem.at[0]),
        pltpu.make_async_copy(row_dgates_ref.at[ctx], came_dgates.at[ctx], own_sem.at[2]),
    ]
    for d, p in enumerate(peers):
        copies.append(
            remote(
                row_dgates_ref.at[p[0]],
                came_dgates.at[ctx],
                dgate_send.at[d],
                dgate_recv.at[d],
                p,
            )
        )
        copies.append(
            remote(
                send_ref.at[block_at(p[0])],
                came.at[block_at(ctx)],
                send_sem.at[d],
                recv_sem.at[d],
                p,
            )
        )
    for c in copies:
        c.start()

    steps = FS // CHUNK

    def fetch(c, slot):
        at = pl.ds(pl.multiple_of(c * CHUNK, CHUNK), CHUNK)
        up = pl.ds(pl.multiple_of(FS + c * CHUNK, CHUNK), CHUNK)
        return [
            pltpu.make_async_copy(wide_ref.at[:, at], gate_buf.at[slot], w_sem.at[slot, 0]),
            pltpu.make_async_copy(wide_ref.at[:, up], up_buf.at[slot], w_sem.at[slot, 1]),
            pltpu.make_async_copy(back_ref.at[at], back_buf.at[slot], w_sem.at[slot, 2]),
        ]

    for f in fetch(0, 0):
        f.start()
    res_ref[...] = jnp.zeros_like(res_ref)
    dx_acc[...] = jnp.zeros_like(dx_acc)
    b_shard = FS // members
    piece = b_all.shape[2]

    def ffn_step(c):
        slot = lax.rem(c, 2)
        for f in fetch(c, slot):
            f.wait()

        @pl.when(c + 1 < steps)
        def _():
            for f in fetch(c + 1, 1 - slot):
                f.start()

        x, dy = in_ref[...], dout_ref[...]
        wg, wu, wo = gate_buf[slot], up_buf[slot], back_buf[slot]
        act, dg, du = gated(dot(x, wg), dot(x, wu), dot_nt(dy, wo))
        act, dg, du = act.astype(BF16), dg.astype(BF16), du.astype(BF16)
        res_ref[...] += dot(act, wo)
        dx_acc[...] += dot_nt(dg, wg) + dot_nt(du, wu)
        column = pl.ds(pl.multiple_of(c * CHUNK, CHUNK), CHUNK)
        mids[0, :, column] = dg
        mids[1, :, column] = du
        value = dot_tn(act, dy).astype(BF16)
        span = min(piece, CHUNK)
        for u in range(CHUNK // span):
            row = c * CHUNK + u * span
            t = row // b_shard
            j = sum(
                lax.rem(fsdp // (1 << b) + t // (1 << b), 2) * (1 << (bits - 1 - b))
                for b in range(bits)
            )
            inside = lax.rem(row, b_shard)
            top = pl.multiple_of(lax.rem(inside, piece), 16)
            b_all[inside // piece, j, pl.ds(top, span), :] = value[u * span : (u + 1) * span]

    loop(ffn_step, 0, steps)
    half, quarter = members // 2, members // 4

    def a_swap(i):
        return remote(
            a_all.at[i, pl.ds(half, half)], a_caught.at[i], a_sem.at[i, 0], a_sem.at[i, 1], mate
        )

    def b_swap(i):
        return remote(
            b_all.at[i, pl.ds(half, half)], b_caught.at[i], b_sem.at[i, 0], b_sem.at[i, 1], mate
        )

    def b_cross(i):
        return remote(b_give.at[i], b_other.at[i], far_sem.at[i, 0], far_sem.at[i, 1], far)

    for i in range(2):
        b_swap(i).start()
    rows = shard_rows(members, D // members)
    shard = D // members
    raw[...] = in_ref[...].T
    for j in range(members):
        xt[j * shard : (j + 1) * shard, :] = raw[pl.ds(rows[j], shard), :]
    for i in range(2):

        def grad_step(c, i=i):
            column = pl.ds(pl.multiple_of(c * BROAD, BROAD), BROAD)
            value = dot(xt[...], mids[i, :, column]).astype(BF16)
            for j in range(members):
                a_all[i, j, :, column] = value[j * shard : (j + 1) * shard]

        loop(grad_step, 0, FS // BROAD)
        a_swap(i).start()
        b_swap(i).wait_recv()
        for j in range(half):
            total = (b_all[i, j].astype(F32) + b_caught[i, j].astype(F32)).astype(BF16)
            if j < quarter:
                b_keep[i, j] = total
            else:
                b_give[i, j - quarter] = total
        b_cross(i).start()
    for c in copies:
        c.wait()

    pick = picks(target_ref, came.shape[0])
    gates = [gates_ref[:, k : k + 1] for k in range(2)]
    lane = lanes_of(pick[0].shape[0])
    dgate = [
        jnp.sum(
            sum(
                jnp.where(
                    lane == target_ref[:, k : k + 1] - p * block, came_dgates[p, 0:1, :], 0.0
                )
                for p in range(n)
            ),
            axis=-1,
            keepdims=True,
        )
        for k in range(2)
    ]
    mean = gates[0] * dgate[0] + gates[1] * dgate[1]
    dlogits = sum(
        jnp.where(lane == routes_ref[:, k : k + 1], gates[k] * (dgate[k] - mean), 0.0)
        for k in range(2)
    ).astype(BF16)
    dlogits_ref[...] = dlogits
    tail = tail_ref[...]
    dffn = dot(pick[0] + pick[1], came[...]) + dx_acc[...] + dot(dlogits, tail.astype(BF16))
    residual = residual_ref[...]
    inv = lax.rsqrt(jnp.mean(residual * residual, axis=-1, keepdims=True) + norm_eps)
    scaled = dffn * tail[experts + 1 : experts + 2, :]
    total = jnp.mean(scaled * residual, axis=-1, keepdims=True)
    dres = dout_ref[...].astype(F32) + inv * scaled - residual * inv * inv * inv * total
    branch = dres.astype(BF16)
    branch_ref[...] = branch
    for d, head in enumerate(heads):
        packet = dot_nt(branch, w_ref[64 * head : 64 * head + LANES, :])
        packets[d] = fold(n, d, packet).astype(BF16)
    own = pltpu.make_async_copy(packets.at[ctx], recv_ref.at[ctx], own_sem.at[1])
    own.start()
    copies = [
        remote(packets.at[p[0]], recv_ref.at[ctx], packet_send.at[d], packet_recv.at[d], p)
        for d, p in enumerate(peers)
    ]
    for c in copies:
        c.start()
    dres_ref[...] = dres
    dgain_ref[...] = jnp.sum(dffn * residual * inv, axis=0, keepdims=True)
    for i in range(2):
        a_swap(i).wait_recv()
        for j in range(half):
            total = (a_all[i, j].astype(F32) + a_caught[i, j].astype(F32)).astype(BF16)
            if j < quarter:
                a_keep[i, j] = total
            else:
                a_give[i, j - quarter] = total
    for c in copies:
        c.wait()
    own.wait()
    for i in range(2):
        a_swap(i).wait_send()
        b_swap(i).wait_send()
        b_cross(i).wait()


def back_exchange_kernel(
    n,
    members,
    heads,
    query_ref,
    send_ref,
    x_ref,
    dy_ref,
    came_ref,
    branch_ref,
    in_ref,
    dlogits_ref,
    residual_ref,
    shared_ref,
    gates_ref,
    target_ref,
    res_ref,
    where_ref,
    length_ref,
    mid_ref,
    query_out,
    recv_ref,
    sum_ref,
    out_keep,
    out_other,
    router_ref,
    output_ref,
    give,
    caught,
    crossed,
    out_all,
    out_caught,
    raw,
    xt,
    dyt,
    acc,
    mids,
    query_send,
    query_recv,
    send_sem,
    recv_sem,
    own_sem,
    give_sem,
    caught_sem,
    cross_sem,
    out_sem,
    mid_sem,
):
    ctx = lax.axis_index("ctx")
    peers = row_peers(n)
    mates = mates_of(members)
    mate, far = mates[0], mates[1]
    greet(peers + [mate, far])
    own = [
        pltpu.make_async_copy(send_ref.at[:, ctx], recv_ref.at[:, ctx], own_sem.at[0]),
        pltpu.make_async_copy(query_ref.at[ctx], query_out.at[ctx], own_sem.at[1]),
    ]
    for c in own:
        c.start()
    copies = [
        remote(query_ref.at[p[0]], query_out.at[ctx], query_send.at[d], query_recv.at[d], p)
        for d, p in enumerate(peers)
    ]
    copies += [
        remote(send_ref.at[:, p[0]], recv_ref.at[:, ctx], send_sem.at[d], recv_sem.at[d], p)
        for d, p in enumerate(peers)
    ]
    for c in copies:
        c.start()

    steps = mid_ref.shape[2] // BROAD
    parts = mid_ref.shape[0]

    def fetch(i, c, slot):
        column = pl.multiple_of(c * BROAD, BROAD)
        return pltpu.make_async_copy(
            mid_ref.at[i, :, pl.ds(column, BROAD)], mids.at[slot], mid_sem.at[slot]
        )

    fetch(0, 0, 0).start()
    shard = D // members
    half = members // 2
    rows = shard_rows(members, shard)

    def turned(value, target):
        raw[...] = value.T
        for j in range(members):
            target[j * shard : (j + 1) * shard, :] = raw[pl.ds(rows[j], shard), :]

    acc[...] = jnp.zeros_like(acc)
    branch = branch_ref[...]
    for d, head in enumerate(heads):
        acc[64 * head : 64 * head + LANES, :] += dot_tn(came_ref[d], branch)
    for j in range(members):
        out_all[j] = acc[pl.ds(rows[j], shard), :].astype(BF16)
    quarter = members // 4
    out_swap = remote(
        out_all.at[pl.ds(half, half)], out_caught, out_sem.at[0], out_sem.at[1], mate
    )
    out_swap.start()
    turned(x_ref[...], xt)
    turned(dy_ref[...], dyt)
    out_swap.wait_recv()
    for j in range(half):
        add_into(out_all, j, out_caught)
    for j in range(quarter):
        out_keep[j] = out_all[j]
    out_cross = remote(
        out_all.at[pl.ds(quarter, quarter)], out_other, out_sem.at[2], out_sem.at[3], far
    )
    out_cross.start()

    def swap(i):
        return remote(give.at[i], caught.at[i], give_sem.at[i], caught_sem.at[i], mate)

    cross = remote(
        sum_ref.at[0, pl.ds(quarter, quarter)], crossed, cross_sem.at[0], cross_sem.at[1], far
    )
    for i in range(parts):
        left = xt if i < 2 else dyt

        def step(c, left=left, i=i):
            slot = lax.rem(c, 2)
            fetch(i, c, slot).wait()

            @pl.when(c + 1 < steps)
            def _():
                fetch(i, c + 1, 1 - slot).start()

            value = dot(left[...], mids[slot]).astype(BF16)
            column = pl.ds(pl.multiple_of(c * BROAD, BROAD), BROAD)
            for j in range(half):
                sum_ref[i, j, :, column] = value[j * shard : (j + 1) * shard]
                give[i, j, :, column] = value[(half + j) * shard : (half + j + 1) * shard]

        loop(step, 0, steps)
        if i + 1 < parts:
            fetch(i + 1, 0, 0).start()
        swap(i).start()
        if i > 0:
            swap(i - 1).wait_recv()
            for j in range(half):
                add_into(sum_ref.at[i - 1], j, caught.at[i - 1])
        if i == 1:
            cross.start()

    router_ref[...] = dot_tn(in_ref[...], dlogits_ref[...])
    pick = picks(target_ref, res_ref.shape[0])
    came = res_ref[...]
    mixture = gates_ref[:, 0:1] * dot(pick[0], came) + gates_ref[:, 1:2] * dot(pick[1], came)
    total = residual_ref[...] + shared_ref[...] + mixture
    position = where_ref[ctx] * total.shape[0] + lax.broadcasted_iota(jnp.int32, total.shape, 0)
    output_ref[...] = jnp.where(position < length_ref[0], total, 0.0).astype(BF16)
    swap(parts - 1).wait_recv()
    for j in range(half):
        add_into(sum_ref.at[parts - 1], j, caught.at[parts - 1])
    for c in copies + own:
        c.wait()
    cross.wait()
    for j in range(quarter):
        add_into(sum_ref.at[0], j, crossed)
    for i in range(parts):
        swap(i).wait_send()
    out_swap.wait_send()
    out_cross.wait()


def last_kernel(
    n,
    members,
    heads,
    experts,
    splits,
    query_ref,
    recv_ref,
    cos_ref,
    sin_ref,
    in_ref,
    x_ref,
    w_ref,
    tail_ref,
    dres_ref,
    router_ref,
    dgain_ref,
    a_ref,
    a_other,
    b_ref,
    b_other,
    o_ref,
    o_other,
    e_ref,
    x_out,
    a_out,
    b_out,
    c_out,
    e_out,
    *scratch,
):
    bits = members.bit_length() - 1
    streams = len(splits)
    own, full, back_up, back_down = (scratch[k * streams : (k + 1) * streams] for k in range(4))
    back = (back_up, back_down)
    scratch = scratch[4 * streams :]
    packs, scratch = scratch[0:4], scratch[4:]
    caught = [scratch[4 * b : 4 * b + 4] for b in range(bits)]
    scratch = scratch[4 * bits :]
    e_caught, scratch = scratch[0 : bits - 1], scratch[bits - 1 :]
    dproj, raw, turned, small = scratch[0:4]
    send_sem, recv_sem, level_send, level_recv, e_send, e_recv = scratch[4:]
    ctx, fsdp = lax.axis_index("ctx"), lax.axis_index("fsdp")
    here = jnp.where(ctx % 2 == 0, ctx // 2, n - 1 - ctx // 2)
    ahead = (ring_place(lax.rem(here + 1, n), n), fsdp)
    behind = (ring_place(lax.rem(here + n - 1, n), n), fsdp)
    mates = mates_of(members)
    barrier = pltpu.get_barrier_semaphore()
    for peer in [ahead, behind] + mates:
        pl.semaphore_signal(barrier, inc=1, device_id=peer, device_id_type=pl.DeviceIdType.MESH)
    shard = D // members
    parts = e_ref.shape[0]

    def level_copy(p, b):
        count = members >> (b + 1)
        return remote(
            packs[p].at[pl.ds(count, count)],
            caught[b][p],
            level_send.at[p, b],
            level_recv.at[p, b],
            mates[b],
        )

    def level_add(p, b):
        level_copy(p, b).wait_recv()
        for j in range(members >> (b + 1)):
            add_into(packs[p], j, caught[b][p])

    def level_next(p):
        level_add(p, 0)
        level_copy(p, 1).start()

    def e_copy(i, b):
        count = members >> (b + 1)
        source = e_ref if b == 1 or (b == 2 and i == 0) else e_caught[b - 2]
        return remote(
            source.at[i, pl.ds(count, count)],
            e_caught[b - 1].at[i],
            e_send.at[i, b - 1],
            e_recv.at[i, b - 1],
            mates[b],
        )

    def e_add(i, b):
        e_copy(i, b).wait_recv()
        source = e_ref if b == 1 or (b == 2 and i == 0) else e_caught[b - 2]
        for j in range(members >> (b + 1)):
            total = source[i, j].astype(F32) + e_caught[b - 1][i, j].astype(F32)
            if b == bits - 1:
                e_out[i] = total.astype(BF16)
            else:
                e_caught[b - 1][i, j] = total.astype(BF16)

    def tiles(i):
        down, across, height, width = splits[i][0:4]
        columns = splits[i][4]
        for p in range(down * across):
            r, c = p // across, p % across
            yield p, r * height, height, c * width, max(0, min(width, columns - c * width)), width

    def load(i, ref, skip=0, other=None):
        for p, top, height, start, have, width in tiles(i):
            if have > 0:
                value = ref[top : top + height, skip + start : skip + start + have]
                if other is not None:
                    added = other[top : top + height, skip + start : skip + start + have]
                    value = (value.astype(F32) + added.astype(F32)).astype(BF16)
                own[i][p, :, 0:have] = value
            if have < width:
                own[i][p, :, have:] = jnp.zeros((height, width - have), BF16)

    def save(i, ref, skip=0):
        for p, top, height, start, have, width in tiles(i):
            if have > 0:
                ref[top : top + height, skip + start : skip + start + have] = full[i][p, :, 0:have]

    long, short = n // 2, n - 1 - n // 2

    def hops(i, direction):
        return long if direction == i % 2 else short

    def place(direction, steps):
        return lax.rem(here + (steps if direction == 0 else 2 * n - steps), n)

    def copy(i, direction, step, source, target, slot):
        return remote(
            source.at[slot],
            target.at[slot],
            send_sem.at[i, direction, step],
            recv_sem.at[i, direction, step],
            ahead if direction == 0 else behind,
        )

    def first(i):
        for direction in range(2):
            slot = place(direction, hops(i, direction))
            copy(i, direction, 0, own[i], back[direction][i], slot).start()

    def reduce_step(i, s):
        for direction in range(2):
            count = hops(i, direction)
            if s < count:
                slot = place(direction, count - s)
                buffer = back[direction][i]
                copy(i, direction, s - 1, buffer, buffer, slot).wait_recv()
                add_into(buffer, slot, own[i])
                copy(i, direction, s, buffer, buffer, slot).start()

    def turn(i):
        for direction in range(2):
            buffer = back[direction][i]
            copy(i, direction, hops(i, direction) - 1, buffer, buffer, here).wait_recv()
        full[i][here] = (
            own[i][here].astype(F32) + back_up[i][here].astype(F32) + back_down[i][here].astype(F32)
        ).astype(BF16)
        for direction in range(2):
            copy(i, direction, long, full[i], full[i], here).start()

    def gather_step(i, s):
        for direction in range(2):
            if s < hops(i, direction):
                slot = place(1 - direction, s)
                copy(i, direction, long + s - 1, full[i], full[i], slot).wait_recv()
                copy(i, direction, long + s, full[i], full[i], slot).start()

    def end(i):
        for direction in range(2):
            count = hops(i, direction)
            slot = place(1 - direction, count)
            copy(i, direction, long + count - 1, full[i], full[i], slot).wait_recv()

    def drain(i):
        for direction in range(2):

            def sent(step, direction=direction):
                copy(i, direction, step, own[i], full[i], 0).wait_send()

            loop(sent, 0, hops(i, direction))
            loop(sent, long, long + hops(i, direction))

    def steps_of(i):
        done = [functools.partial(reduce_step, i, s) for s in range(1, long)]
        done.append(functools.partial(turn, i))
        done += [functools.partial(gather_step, i, s) for s in range(1, long)]
        done.append(functools.partial(end, i))
        return done

    for i in range(2):
        load(i, a_ref.at[i], 0, a_other.at[i])
    pl.semaphore_wait(barrier, 2 + bits)
    first(0)
    first(1)
    for i in range(2):
        load(2 + i, b_ref.at[i], 0, b_other.at[i])
        first(2 + i)
    load(4, o_ref, 0, o_other)
    first(4)
    waiting = [steps_of(i) for i in range(5)]

    def dense_step(picked=range(5)):
        for i in picked:
            if waiting[i]:
                waiting[i].pop(0)()

    rows = shard_rows(members, shard)
    raw[...] = in_ref[...].T
    for j in range(members):
        turned[j * shard : (j + 1) * shard, :] = raw[pl.ds(rows[j], shard), :]
    lane = lanes_of(x_ref.shape[0])
    cos, sin = cos_ref[...], sin_ref[...]
    for part in range(3):
        groups = [jnp.zeros(lane.shape, F32) for _ in range(D // LANES)]
        for d, head in enumerate(heads):
            g = head // 2
            if part == 0:
                packet = unfold(n, d, query_ref[d].astype(F32), lane.shape[0])
            else:
                packet = recv_ref[part - 1, d].astype(F32)
            if head % 2 == 0:
                groups[g] = groups[g] + packet
            else:
                packet = pltpu.roll(packet, 64, 1)
                groups[g] = groups[g] + jnp.where(lane >= 64, packet, 0.0)
                groups[g + 1] = groups[g + 1] + jnp.where(lane < 64, packet, 0.0)
        for g, t in enumerate(groups):
            if part < 2:
                t = t.astype(BF16).astype(F32)
                t = t * cos - partner(t, lane) * sin
            dproj[:, part * D + g * LANES : part * D + (g + 1) * LANES] = t.astype(BF16)
        value = dot(turned[...], dproj[:, part * D : (part + 1) * D]).astype(BF16)
        for j in range(members):
            packs[part][j] = value[j * shard : (j + 1) * shard]
        level_copy(part, 0).start()
        if part > 0:
            level_next(part - 1)
    dense_step()
    dnorm = sum(
        dot_nt(dproj[:, part * D : (part + 1) * D], w_ref[part].reshape(D, D)) for part in range(3)
    )
    x = x_ref[...].astype(F32)
    gain = tail_ref[experts : experts + 1, :]
    inv = lax.rsqrt(jnp.mean(x * x, axis=-1, keepdims=True) + norm_eps)
    dgain_one = jnp.sum(dnorm * x * inv, axis=0, keepdims=True)
    row = lax.broadcasted_iota(jnp.int32, (LANES, D), 0)
    gains = jnp.where(row == experts, dgain_one, jnp.where(row == experts + 1, dgain_ref[...], 0.0))
    small[...] = router_ref[...] + gains.T
    for j in range(members):
        packs[3][j] = small[pl.ds(rows[j], shard), :].astype(BF16)
    level_copy(3, 0).start()
    level_next(2)
    scaled = dnorm * gain
    total = jnp.mean(scaled * x, axis=-1, keepdims=True)
    x_out[...] = dres_ref[...] + inv * scaled - x * inv * inv * inv * total
    level_next(3)
    for i in range(1, parts):
        e_copy(i, 1).start()

    for p in range(4):
        if p < 3:
            dense_step((0, 2))
        for b in range(1, bits):
            level_add(p, b)
            if b + 1 < bits:
                level_copy(p, b + 1).start()
        load(5 + p, packs[p].at[0])
        first(5 + p)
        for queue in waiting[5:]:
            queue.pop(0)()
        if p < 3:
            dense_step((1, 3, 4))
        waiting.append(steps_of(5 + p))
    turns = 0
    while any(waiting):
        turns += 1
        for i, queue in reversed(list(enumerate(waiting))):
            if queue and (i >= 5 or turns % 2 == (i in (1, 3, 4))):
                queue.pop(0)()
                if not queue and i < 5:
                    if i == 4:
                        save(i, c_out, PACKED)
                    elif i < 2:
                        save(i, a_out, i * splits[0][4])
                    else:
                        height = splits[2][0] * splits[2][2]
                        save(i, b_out.at[pl.ds((i - 2) * height, height)])
        if not any(waiting[0:5]) and parts > 1:
            e_add(1, 1)
            parts = min(parts, 1)
    for p in range(4):
        save(5 + p, c_out, p * D)
    parts = e_ref.shape[0]
    for i in range(2, parts):
        e_add(i, 1)
    if bits == 2:
        e_out[0] = e_ref[0, 0]
    for b in range(2, bits):
        for i in range(parts):
            e_copy(i, b).start()
        for i in range(parts):
            e_add(i, b)
    for b in range(bits):
        for p in range(4):
            level_copy(p, b).wait_send()
    for b in range(1, bits):
        for i in range(1 if b == 1 else 0, parts):
            e_copy(i, b).wait_send()

    for i in range(streams):
        drain(i)


def widen_kernel(
    experts,
    late_ref,
    a_ref,
    b_ref,
    in_ref,
    back_ref,
    x_ref,
    small_ref,
    qkv_out,
    w_out,
    a_out,
    b_out,
    in_out,
    back_out,
    x_out,
    router_out,
    gains_out,
):
    qkv_out[...] = late_ref[:, 0 : 3 * D].astype(F32)
    w_out[...] = late_ref[:, PACKED:].astype(F32)
    a_out[...] = a_ref[...].astype(F32)
    b_out[...] = b_ref[...].astype(F32)
    in_out[:, 0:FF] = in_ref[0].astype(F32)
    in_out[:, FF:] = in_ref[1].astype(F32)
    back_out[...] = back_ref[0].astype(F32)
    x_out[...] = x_ref[...]

    @pl.when(pl.program_id(0) == 0)
    def _():
        small = small_ref[...].astype(F32).T
        router_out[...] = small[0:experts]
        gains_out[...] = small[experts : experts + 2]


def on_device(
    tokens,
    cotangent,
    lengths,
    position_block,
    routes,
    gain_attn,
    w_qkv,
    w_out,
    gain_ffn,
    w_router,
    w_shared_in,
    w_shared_out,
    w_expert_in,
    w_expert_out,
):
    n_ctx = lax.axis_size("ctx")
    ctx_index = lax.axis_index("ctx")
    rows = tokens.shape[1]
    local = w_qkv.shape[0]
    experts = w_router.shape[1]
    capacity = 3 * rows // experts
    places = experts * capacity
    members = D // local
    share = HEADS * rows // n_ctx
    heads = first_heads(n_ctx, rows)
    gather = functools.partial(lax.all_gather, axis_name="fsdp", axis=0, tiled=True)
    exchange = functools.partial(
        lax.all_to_all, axis_name="ctx", split_axis=0, concat_axis=0, tiled=True
    )
    x = tokens[0]
    length = lengths[0]

    out_weight = gather(w_out)
    weights = gather(
        jnp.concatenate([w_shared_in, w_expert_in[0], w_expert_out[0].T], axis=1)
    )
    shared_out = gather(w_shared_out)
    bits = members.bit_length() - 1

    rates = 10000.0 ** (-(np.arange(HEAD_DIM // 2) * 2.0 / HEAD_DIM))
    rates = jnp.asarray(np.tile(rates.astype(np.float32), 4)[None])

    order = jnp.sum(
        jnp.where(
            position_block[None, :] == jnp.arange(n_ctx, dtype=jnp.int32)[:, None],
            jnp.arange(n_ctx, dtype=jnp.int32)[None, :],
            0,
        ),
        axis=1,
    )
    head_of = jnp.minimum(share * ctx_index // rows, HEADS - 2)
    offset = share * ctx_index - rows * head_of
    scalars = jnp.concatenate(
        [order, jnp.stack([offset.astype(jnp.int32), length.astype(jnp.int32)])]
    )

    whole = pl.BlockSpec(memory_space=pltpu.VMEM)
    scalar = pl.BlockSpec(memory_space=pltpu.SMEM)
    block = places // n_ctx
    early = block // 48 * 16
    thin = packet_rows(n_ctx, rows)
    queries, recv, attn_in, tail, target, dout, dy_first, dy_rest, qkv_weight, cos, sin = comm_call(
        functools.partial(open_kernel, n_ctx, members, heads, experts, capacity, early),
        (
            shape((n_ctx, thin, LANES), BF16),
            shape((2, n_ctx, rows, LANES), BF16),
            shape((rows, D), BF16),
            shape((LANES, D), F32),
            shape((rows, 2), jnp.int32),
            shape((rows, D), BF16),
            shape((n_ctx, early, D), BF16),
            shape((n_ctx, block - early, D), BF16),
            shape((3, members, local, D), BF16),
            shape((rows, LANES), F32),
            shape((rows, LANES), F32),
        ),
        3,
        in_specs=[scalar] * 2 + [whole] * 7,
        out_specs=[whole] * 11,
        scratch_shapes=[
            pltpu.VMEM((n_ctx, thin, LANES), BF16),
            pltpu.VMEM((2, n_ctx, rows, LANES), BF16),
            pltpu.VMEM((n_ctx, early, D), BF16),
            pltpu.VMEM((LANES, local), F32),
            pltpu.VMEM((members, local, LANES), BF16),
            pltpu.SemaphoreType.DMA((4, bits, members)),
            pltpu.SemaphoreType.DMA((4, bits, members)),
            pltpu.SemaphoreType.DMA((3, n_ctx - 1)),
            pltpu.SemaphoreType.DMA((3, n_ctx - 1)),
            pltpu.SemaphoreType.DMA((n_ctx - 1,)),
            pltpu.SemaphoreType.DMA((n_ctx - 1,)),
            pltpu.SemaphoreType.DMA((4,)),
        ],
        nbytes=150 << 20,
    )(
        position_block,
        lengths,
        routes[0],
        cotangent[0],
        x,
        w_qkv,
        w_router.T,
        jnp.stack([gain_attn, gain_ffn]),
        rates,
    )
    dy_rest = exchange(dy_rest)

    packet = pl.BlockSpec((2, n_ctx, rows, LANES), lambda i, sc: (0, 0, 0, 0))
    thin_packet = pl.BlockSpec((n_ctx, thin, LANES), lambda i, sc: (0, 0, 0))
    block_of = lambda i, sc: (i, 0, 0)
    attended, kept, lse = call(
        functools.partial(attend_kernel, n_ctx, share),
        (
            shape((n_ctx, thin, LANES), BF16),
            shape((n_ctx, LANES, share), F32),
            shape((n_ctx, 1, share), F32),
        ),
        flops=2 * share * rows * n_ctx * n_ctx * LANES * 2,
        nbytes=5 << 20,
        grid_spec=pltpu.PrefetchScalarGridSpec(
            num_scalar_prefetch=1,
            grid=(n_ctx,),
            in_specs=[thin_packet, packet],
            out_specs=[
                pl.BlockSpec((1, thin, LANES), lambda i, sc: (sc[i], 0, 0)),
                pl.BlockSpec((1, LANES, share), block_of),
                pl.BlockSpec((1, 1, share), block_of),
            ],
            scratch_shapes=[
                pltpu.VMEM((2 * rows, LANES), BF16),
                pltpu.VMEM((n_ctx, rows, share), F32),
                pltpu.VMEM((2 * rows, LANES), F32),
            ],
        ),
    )(scalars, queries, recv)
    attended, dy_rest = lax.optimization_barrier((attended, dy_rest))

    def full(*dims):
        return pl.BlockSpec(dims, lambda *at: (0,) * len(dims))

    came, residual, ffn_in, gates, x_rows, row_gates = comm_call(
        functools.partial(middle_kernel, n_ctx, heads, experts),
        (
            shape((n_ctx, rows, LANES), BF16),
            shape((rows, D), F32),
            shape((rows, D), BF16),
            shape((rows, LANES), F32),
            shape((places, D), BF16),
            shape((n_ctx, 8, LANES), F32),
        ),
        4,
        in_specs=[whole] * 6,
        out_specs=[whole] * 6,
        scratch_shapes=[
            pltpu.VMEM((n_ctx, thin, LANES), BF16),
            pltpu.VMEM((places, D), BF16),
            pltpu.VMEM((n_ctx, 8, LANES), F32),
        ]
        + [pltpu.SemaphoreType.DMA((n_ctx - 1,)) for _ in range(6)]
        + [pltpu.SemaphoreType.DMA((3,))],
        nbytes=100 << 20,
    )(attended, out_weight, x, tail, routes[0], target)

    half, quarter = members // 2, members // 4
    steps = FS // CHUNK
    wide = FF // BROAD
    base = 2 * FS // BROAD
    expert_dx, row_dgates, expert_res, expert_mid, dy_rows = call(
        expert_kernel,
        (
            shape((places, D), BF16),
            shape((n_ctx, 8, LANES), F32),
            shape((places, D), BF16),
            shape((3, places, FF), BF16),
            shape((places, D), BF16),
        ),
        flops=2 * places * D * FF * 6,
        nbytes=24 << 20,
        grid=(wide,),
        in_specs=[
            full(places, D),
            full(n_ctx, 8, LANES),
            full(n_ctx, early, D),
            full(n_ctx, block - early, D),
            pl.BlockSpec((D, BROAD), lambda c: (0, base + c)),
            pl.BlockSpec((D, BROAD), lambda c: (0, base + wide + c)),
            pl.BlockSpec((D, BROAD), lambda c: (0, base + 2 * wide + c)),
        ],
        out_specs=[
            full(places, D),
            full(n_ctx, 8, LANES),
            full(places, D),
            pl.BlockSpec((3, places, BROAD), lambda c: (0, 0, c)),
            full(places, D),
        ],
        scratch_shapes=[
            pltpu.VMEM((places, D), F32),
            pltpu.VMEM((places, D), F32),
            pltpu.VMEM((places, LANES), F32),
            pltpu.VMEM((places, LANES), F32),
        ],
    )(x_rows, row_gates, dy_first, dy_rest, weights, weights, weights)
    b_rows = FS // members // 2
    anywhere = pl.BlockSpec(memory_space=pl.ANY)
    (
        branch_recv,
        shared_res,
        dres,
        branch,
        dlogits,
        dgain_two,
        dense_keep,
        dense_give,
        so_keep,
        so_came,
    ) = comm_call(
        functools.partial(shared_kernel, n_ctx, members, heads, experts),
        (
            shape((n_ctx, thin, LANES), BF16),
            shape((rows, D), F32),
            shape((rows, D), F32),
            shape((rows, D), BF16),
            shape((rows, LANES), BF16),
            shape((1, D), F32),
        )
        + (shape((2, quarter, local, FS), BF16),) * 2
        + (shape((2, quarter, b_rows, D), BF16),) * 2,
        2,
        in_specs=[whole] * 10 + [anywhere] * 2,
        out_specs=[whole] * 10,
        scratch_shapes=[
            pltpu.VMEM((places, D), BF16),
            pltpu.VMEM((n_ctx, 8, LANES), F32),
            pltpu.VMEM((n_ctx, thin, LANES), BF16),
            pltpu.VMEM((2, quarter, b_rows, D), BF16),
            pltpu.VMEM((2, rows, FS), BF16),
            pltpu.VMEM((rows, D), F32),
            pltpu.VMEM((2, members, local, FS), BF16),
            pltpu.VMEM((2, members, b_rows, D), BF16),
            pltpu.VMEM((2, half, local, FS), BF16),
            pltpu.VMEM((2, half, b_rows, D), BF16),
            pltpu.VMEM((D, rows), BF16),
            pltpu.VMEM((D, rows), BF16),
            pltpu.VMEM((2, D, CHUNK), BF16),
            pltpu.VMEM((2, D, CHUNK), BF16),
            pltpu.VMEM((2, CHUNK, D), BF16),
            pltpu.SemaphoreType.DMA((n_ctx - 1,)),
            pltpu.SemaphoreType.DMA((n_ctx - 1,)),
            pltpu.SemaphoreType.DMA((3,)),
            pltpu.SemaphoreType.DMA((n_ctx - 1,)),
            pltpu.SemaphoreType.DMA((n_ctx - 1,)),
            pltpu.SemaphoreType.DMA((n_ctx - 1,)),
            pltpu.SemaphoreType.DMA((n_ctx - 1,)),
            pltpu.SemaphoreType.DMA((2, 2)),
            pltpu.SemaphoreType.DMA((2, 2)),
            pltpu.SemaphoreType.DMA((2, 2)),
            pltpu.SemaphoreType.DMA((2, 3)),
        ],
        nbytes=150 << 20,
    )(
        expert_dx,
        row_dgates,
        ffn_in,
        dout,
        residual,
        gates,
        routes[0],
        target,
        tail,
        out_weight,
        weights,
        shared_out,
    )

    def gathered(terms):
        return sum(t.astype(F32) for t in terms).astype(BF16)

    def cross(give, b):
        return lax.ppermute(give, "fsdp", [(i, i ^ (1 << b)) for i in range(members)])

    def rest_of(keep, came_in):
        for b in range(2, bits):
            count = keep.shape[1] // 2
            give = gathered([keep[:, count:], came_in[:, count:]])
            keep = gathered([keep[:, :count], came_in[:, :count]])
            came_in = cross(give, b)
        return keep[:, 0], came_in[:, 0]

    branch_recv, expert_res = lax.optimization_barrier((branch_recv, expert_res))
    dense_part, dense_other = rest_of(dense_keep, cross(dense_give, 1))
    so_part, so_other = rest_of(so_keep, so_came)

    dquery, dsend = call(
        functools.partial(attend_back_kernel, n_ctx, share),
        (shape((n_ctx, thin, LANES), BF16), shape((2, n_ctx, rows, LANES), BF16)),
        flops=2 * share * rows * n_ctx * n_ctx * LANES * 3,
        nbytes=8 << 20,
        grid_spec=pltpu.PrefetchScalarGridSpec(
            num_scalar_prefetch=1,
            grid=(n_ctx,),
            in_specs=[
                thin_packet,
                packet,
                thin_packet,
                pl.BlockSpec((1, LANES, share), block_of),
                pl.BlockSpec((1, 1, share), block_of),
            ],
            out_specs=[thin_packet, packet],
            scratch_shapes=[
                pltpu.VMEM((2 * rows, LANES), BF16),
                pltpu.VMEM((2 * rows, LANES), BF16),
                pltpu.VMEM((n_ctx, rows, LANES), F32),
                pltpu.VMEM((n_ctx, rows, LANES), F32),
                pltpu.VMEM((2 * rows, LANES), F32),
            ],
        ),
    )(scalars, queries, recv, branch_recv, kept, lse)
    res_came = exchange(expert_res.reshape(n_ctx, -1, D)).reshape(places, D)
    dquery, drecv, expert_sum, out_keep, out_came, grad_router, output = comm_call(
        functools.partial(back_exchange_kernel, n_ctx, members, heads),
        (
            shape((n_ctx, thin, LANES), BF16),
            shape((2, n_ctx, rows, LANES), BF16),
            shape((3, half, local, FF), BF16),
            shape((quarter, local, D), BF16),
            shape((quarter, local, D), BF16),
            shape((D, LANES), F32),
            shape((rows, D), BF16),
        ),
        1,
        in_specs=[whole] * 13 + [scalar] * 2 + [anywhere],
        out_specs=[whole] * 7,
        scratch_shapes=[
            pltpu.VMEM((3, half, local, FF), BF16),
            pltpu.VMEM((3, half, local, FF), BF16),
            pltpu.VMEM((quarter, local, FF), BF16),
            pltpu.VMEM((members, local, D), BF16),
            pltpu.VMEM((half, local, D), BF16),
            pltpu.VMEM((D, places), BF16),
            pltpu.VMEM((D, places), BF16),
            pltpu.VMEM((D, places), BF16),
            pltpu.VMEM((D, D), F32),
            pltpu.VMEM((2, places, BROAD), BF16),
            pltpu.SemaphoreType.DMA((n_ctx - 1,)),
            pltpu.SemaphoreType.DMA((n_ctx - 1,)),
            pltpu.SemaphoreType.DMA((n_ctx - 1,)),
            pltpu.SemaphoreType.DMA((n_ctx - 1,)),
            pltpu.SemaphoreType.DMA((2,)),
            pltpu.SemaphoreType.DMA((3,)),
            pltpu.SemaphoreType.DMA((3,)),
            pltpu.SemaphoreType.DMA((2,)),
            pltpu.SemaphoreType.DMA((4,)),
            pltpu.SemaphoreType.DMA((2,)),
        ],
        nbytes=120 << 20,
    )(
        dquery,
        dsend,
        x_rows,
        dy_rows,
        came,
        branch,
        ffn_in,
        dlogits,
        residual,
        shared_res,
        gates,
        target,
        res_came,
        position_block,
        lengths,
        expert_mid,
    )

    late_width = PACKED + D
    out_part, out_other = rest_of(out_keep[None], out_came[None])
    late_widths = [D, D, D, LANES]
    sizes = [(local, FS)] * 2 + [(FS // members // 2, D)] * 2 + [(local, D)]
    sizes += [(local, width) for width in late_widths]
    splits = [ring_split(r, c, n_ctx) + (c,) for r, c in sizes]
    tiles = [(n_ctx, t[2], t[3]) for t in splits]
    grad_x, dense_sum, so_sum, last_sum, expert_sum = comm_call(
        functools.partial(last_kernel, n_ctx, members, heads, experts, splits),
        (
            shape((rows, D), F32),
            shape((local, 2 * FS), BF16),
            shape((FS // members, D), BF16),
            shape((local, late_width), BF16),
            shape((3, local, FF), BF16),
        ),
        0,
        in_specs=[whole] * 18,
        out_specs=[whole] * 5,
        scratch_shapes=[pltpu.VMEM(t, BF16) for t in tiles * 4]
        + [pltpu.VMEM((members, local, width), BF16) for width in late_widths]
        + [
            pltpu.VMEM((members >> (b + 1), local, width), BF16)
            for b in range(bits)
            for width in late_widths
        ]
        + [pltpu.VMEM((3, members >> (b + 1), local, FF), BF16) for b in range(1, bits)]
        + [
            pltpu.VMEM((rows, 3 * D), BF16),
            pltpu.VMEM((D, rows), BF16),
            pltpu.VMEM((D, rows), BF16),
            pltpu.VMEM((D, LANES), F32),
            pltpu.SemaphoreType.DMA((9, 2, n_ctx)),
            pltpu.SemaphoreType.DMA((9, 2, n_ctx)),
            pltpu.SemaphoreType.DMA((4, bits)),
            pltpu.SemaphoreType.DMA((4, bits)),
            pltpu.SemaphoreType.DMA((3, max(1, bits - 1))),
            pltpu.SemaphoreType.DMA((3, max(1, bits - 1))),
        ],
        nbytes=200 << 20,
    )(
        dquery,
        drecv,
        cos,
        sin,
        attn_in,
        x,
        qkv_weight,
        tail,
        dres,
        grad_router,
        dgain_two,
        dense_part,
        dense_other,
        so_part,
        so_other,
        out_part[0],
        out_other[0],
        expert_sum,
    )

    quarters = 4 if local % 64 == 0 else 1

    def rows_of(count, width):
        return pl.BlockSpec((count // quarters, width), lambda i: (i, 0))

    grad_qkv, grad_out, grad_si, grad_so, grad_ei, grad_eo, grad_x, grad_router, gains = call(
        functools.partial(widen_kernel, experts),
        (
            shape((local, 3 * D), F32),
            shape((local, D), F32),
            shape((local, 2 * FS), F32),
            shape((FS // members, D), F32),
            shape((local, 2 * FF), F32),
            shape((local, FF), F32),
            shape((rows, D), F32),
            shape((experts, local), F32),
            shape((2, local), F32),
        ),
        flops=0,
        nbytes=22 << 20,
        grid=(quarters,),
        in_specs=[
            rows_of(local, late_width),
            rows_of(local, 2 * FS),
            rows_of(FS // members, D),
            pl.BlockSpec((2, local // quarters, FF), lambda i: (0, i, 0)),
            pl.BlockSpec((1, local // quarters, FF), lambda i: (2, i, 0)),
            rows_of(rows, D),
            pl.BlockSpec((local, LANES), lambda i: (0, 3 * D // LANES)),
        ],
        out_specs=[
            rows_of(local, 3 * D),
            rows_of(local, D),
            rows_of(local, 2 * FS),
            rows_of(FS // members, D),
            rows_of(local, 2 * FF),
            rows_of(local, FF),
            rows_of(rows, D),
            full(experts, local),
            full(2, local),
        ],
    )(last_sum, dense_sum, so_sum, expert_sum, expert_sum, grad_x, last_sum)
    return (
        output[None],
        grad_x[None],
        gains[0],
        grad_qkv,
        grad_out,
        gains[1],
        grad_router.T,
        grad_si,
        grad_so,
        grad_ei[None],
        grad_eo.T[None],
    )


def solution(mesh):
    row_spec = P("fsdp", "ctx", None)
    flat = P("fsdp", None)
    return jax.shard_map(
        on_device,
        mesh=mesh,
        in_specs=(
            row_spec,
            row_spec,
            P("fsdp"),
            P(),
            row_spec,
            P("fsdp"),
            flat,
            flat,
            P("fsdp"),
            flat,
            flat,
            flat,
            P("ctx", "fsdp", None),
            P("ctx", None, "fsdp"),
        ),
        out_specs=(
            row_spec,
            row_spec,
            P("fsdp"),
            flat,
            flat,
            P("fsdp"),
            flat,
            flat,
            flat,
            P("ctx", "fsdp", None),
            P("ctx", None, "fsdp"),
        ),
        check_vma=False,
    )
```

```python
import functools

import jax
import jax.numpy as jnp
import numpy as np
from jax import lax
from jax.experimental import pallas as pl
from jax.experimental.pallas import tpu as pltpu
from jax.sharding import PartitionSpec as P

D = 768
HEADS = 12
HEAD_DIM = 64
FF = 2048
FS = 2048
LANES = 128
CHUNK = 256
BROAD = 512
PACKED = 3 * D + LANES
norm_eps = 1e-06
F32 = jnp.float32
BF16 = jnp.bfloat16


def dot(a, b):
    return jnp.dot(a, b, preferred_element_type=F32)


def dot_nt(a, b):
    return lax.dot_general(a, b, (((1,), (1,)), ((), ())), preferred_element_type=F32)


def dot_tn(a, b):
    return lax.dot_general(a, b, (((0,), (0,)), ((), ())), preferred_element_type=F32)


def call(kernel, outs, *, flops, nbytes, limit=56, **kw):
    return pl.pallas_call(
        kernel,
        out_shape=outs,
        compiler_params=pltpu.CompilerParams(vmem_limit_bytes=limit << 20),
        cost_estimate=pl.CostEstimate(
            flops=int(flops), bytes_accessed=int(nbytes), transcendentals=0
        ),
        **kw,
    )


def comm_call(kernel, outs, number, *, nbytes, limit=60, **kw):
    return pl.pallas_call(
        kernel,
        out_shape=outs,
        compiler_params=pltpu.CompilerParams(
            collective_id=number, has_side_effects=True, vmem_limit_bytes=limit << 20
        ),
        cost_estimate=pl.CostEstimate(flops=0, bytes_accessed=int(nbytes), transcendentals=0),
        **kw,
    )


def shape(dims, dtype):
    return jax.ShapeDtypeStruct(dims, dtype)


def lanes_of(rows, width=LANES):
    return lax.broadcasted_iota(jnp.int32, (rows, width), 1)


def first_heads(n_ctx, slot_dev):
    share = HEADS * slot_dev // n_ctx
    return [min(share * d // slot_dev, HEADS - 2) for d in range(n_ctx)]


def partner(t, lane):
    return jnp.where(lane % 64 < 32, pltpu.roll(t, 96, 1), pltpu.roll(t, 32, 1))


def picks(target_ref, places):
    rows = target_ref.shape[0]
    place = lanes_of(rows, places)
    return tuple(
        jnp.where(place == target_ref[:, k : k + 1], 1.0, 0.0).astype(BF16) for k in range(2)
    )


def flipped(index, mask):
    for b in range(mask.bit_length()):
        if mask >> b & 1:
            index = index + (1 << b) - 2 * (1 << b) * (index // (1 << b) % 2)
    return index


def mirrored(members):
    bits = members.bit_length() - 1
    return [int(format(j, "b").zfill(bits)[::-1], 2) for j in range(members)]


def shard_rows(members, shard):
    fsdp = lax.axis_index("fsdp")
    return [pl.multiple_of(flipped(fsdp, m) * shard, 16) for m in mirrored(members)]


def remote(source, target, send_sem, recv_sem, peer):
    return pltpu.make_async_remote_copy(
        src_ref=source,
        dst_ref=target,
        send_sem=send_sem,
        recv_sem=recv_sem,
        device_id=peer,
        device_id_type=pl.DeviceIdType.MESH,
    )


def greet(peers):
    barrier = pltpu.get_barrier_semaphore()
    for peer in peers:
        pl.semaphore_signal(barrier, inc=1, device_id=peer, device_id_type=pl.DeviceIdType.MESH)
    pl.semaphore_wait(barrier, len(peers))


def mates_of(members):
    ctx, fsdp = lax.axis_index("ctx"), lax.axis_index("fsdp")
    return [(ctx, flipped(fsdp, 1 << b)) for b in range(members.bit_length() - 1)]


def row_peers(n):
    ctx, fsdp = lax.axis_index("ctx"), lax.axis_index("fsdp")
    return [(lax.rem(ctx + d, n), fsdp) for d in range(1, n)]


def loop(body, low, high):
    lax.fori_loop(low, high, lambda s, carry: (body(s), carry)[1], 0)


def add_into(target, j, other):
    target[j] = (target[j].astype(F32) + other[j].astype(F32)).astype(BF16)


def open_kernel(
    n,
    members,
    heads,
    experts,
    capacity,
    early,
    where_ref,
    length_ref,
    routes_ref,
    cot_ref,
    x_ref,
    w_ref,
    router_ref,
    gains_ref,
    turn_ref,
    query_ref,
    recv_ref,
    in_ref,
    tail_ref,
    target_ref,
    dout_ref,
    dy_ref,
    dy_rest_ref,
    w_all,
    cos_ref,
    sin_ref,
    query_send,
    send,
    dy_send,
    small,
    small_all,
    gather_send,
    gather_recv,
    packet_send,
    packet_recv,
    dy_send_sem,
    dy_recv_sem,
    own_sem,
):
    ctx, fsdp = lax.axis_index("ctx"), lax.axis_index("fsdp")
    bits = members.bit_length() - 1
    peers = row_peers(n)
    mates = mates_of(members)
    shard = w_ref.shape[0]
    rows = x_ref.shape[0]
    small[...] = jnp.zeros_like(small)
    small[0:experts] = router_ref[...].astype(F32)
    small[experts : experts + 2] = gains_ref[...].astype(F32)
    small_all[fsdp] = small[...].T.astype(BF16)
    for part in range(3):
        w_all[part, fsdp] = w_ref[:, part * D : (part + 1) * D]
    greet(peers + mates)

    def gather_copy(p, b, mask):
        buffer = small_all if p == 3 else w_all.at[p]
        spot = flipped(fsdp, mask)
        return remote(
            buffer.at[spot],
            buffer.at[spot],
            gather_send.at[p, b, mask],
            gather_recv.at[p, b, mask],
            mates[b],
        )

    def gather_wait(p, b, mask):
        buffer = small_all if p == 3 else w_all.at[p]
        spot = flipped(fsdp, mask | 1 << b)
        remote(
            buffer.at[spot],
            buffer.at[spot],
            gather_send.at[p, b, mask],
            gather_recv.at[p, b, mask],
            mates[b],
        ).wait_recv()

    for p in (3, 0, 1, 2):
        for b in reversed(range(bits)):
            gather_copy(p, b, 0).start()

    def gather_rest(p):
        masks = [0]
        for b in reversed(range(bits)):
            for mask in masks[1:]:
                gather_copy(p, b, mask).start()
            for mask in masks:
                gather_wait(p, b, mask)
            masks = masks + [mask | 1 << b for mask in masks]

    lane = lanes_of(rows)
    hot = [jnp.where(lane == routes_ref[:, k : k + 1], 1.0, 0.0) for k in range(2)]
    below = jnp.where(
        lanes_of(rows, rows) < lax.broadcasted_iota(jnp.int32, (rows, rows), 0), 1.0, 0.0
    )
    before = dot(below.astype(BF16), (hot[0] + hot[1]).astype(BF16))
    place = [
        routes_ref[:, k : k + 1] * capacity
        + jnp.sum(hot[k] * before, axis=-1, keepdims=True).astype(jnp.int32)
        for k in range(2)
    ]
    for k in range(2):
        target_ref[:, k : k + 1] = place[k]
    position = where_ref[ctx] * rows + lax.broadcasted_iota(jnp.int32, (rows, D), 0)
    dout = jnp.where(position < length_ref[0], cot_ref[...].astype(F32), 0.0).astype(BF16)
    dout_ref[...] = dout
    places = experts * capacity
    spot = lanes_of(rows, places)
    pick = jnp.where((spot == place[0]) | (spot == place[1]), 1.0, 0.0).astype(BF16)
    packed = dot_tn(pick, dout).astype(BF16)
    block = places // n
    for p in range(n):
        dy_send[p] = packed[p * block : p * block + early]
        dy_rest_ref[p] = packed[p * block + early : (p + 1) * block]
    own = [
        pltpu.make_async_copy(dy_send.at[ctx], dy_ref.at[ctx], own_sem.at[3]),
    ]
    own[0].start()
    copies = [
        remote(dy_send.at[p[0]], dy_ref.at[ctx], dy_send_sem.at[d], dy_recv_sem.at[d], p)
        for d, p in enumerate(peers)
    ]
    for c in copies:
        c.start()

    x = x_ref[...].astype(F32)
    inv = lax.rsqrt(jnp.mean(x * x, axis=-1, keepdims=True) + norm_eps)
    gather_rest(3)
    tail = small_all[...].reshape(D, LANES).astype(F32).T
    tail_ref[...] = tail
    attn_in = (x * inv * tail[experts : experts + 1, :]).astype(BF16)
    in_ref[...] = attn_in
    position = where_ref[ctx] * rows + lax.broadcasted_iota(jnp.int32, (rows, LANES), 0)
    angles = position.astype(F32) * turn_ref[...]
    cos, sin = jnp.cos(angles), jnp.sin(angles)
    sin = jnp.where(lane % 64 < 32, -sin, sin)
    cos_ref[...] = cos
    sin_ref[...] = sin
    for part in range(3):
        gather_rest(part)
        y = dot(attn_in, w_all[part].reshape(D, D))
        groups = []
        for g in range(D // LANES):
            t = y[:, g * LANES : (g + 1) * LANES]
            if part < 2:
                t = t * cos + partner(t, lane) * sin
            groups.append(t)
        turned = [pltpu.roll(t, 64, 1) for t in groups]
        for d, head in enumerate(heads):
            g = head // 2
            if head % 2 == 0:
                packet = groups[g]
            else:
                packet = jnp.where(lane < 64, turned[g], turned[g + 1])
            if part == 0:
                query_send[d] = fold(n, d, packet).astype(BF16)
            else:
                send[part - 1, d] = packet.astype(BF16)
        source = query_send if part == 0 else send.at[part - 1]
        target = query_ref if part == 0 else recv_ref.at[part - 1]
        own.append(
            pltpu.make_async_copy(source.at[ctx], target.at[ctx], own_sem.at[part])
        )
        own[-1].start()
        for d, p in enumerate(peers):
            copies.append(
                remote(
                    source.at[p[0]],
                    target.at[ctx],
                    packet_send.at[part, d],
                    packet_recv.at[part, d],
                    p,
                )
            )
            copies[-1].start()
    for c in copies + own:
        c.wait()
    for p in range(4):
        masks = [0]
        for b in reversed(range(bits)):
            for mask in masks:
                gather_copy(p, b, mask).wait_send()
            masks = masks + [mask | 1 << b for mask in masks]


def folds(n, rows):
    return 2 * HEADS * rows == 3 * n * rows


def packet_rows(n, rows):
    return rows * 3 // 4 if folds(n, rows) else rows


def fold(n, d, block):
    rows = block.shape[0]
    if not folds(n, rows):
        return block
    half, quarter = rows // 2, rows // 4
    lane = lanes_of(quarter)
    if d % 2 == 0:
        both, one = block[0:half], block[half:]
        lone = jnp.where(lane < 64, one[0:quarter], pltpu.roll(one[quarter:], 64, 1))
    else:
        both, one = block[half:], block[0:half]
        lone = jnp.where(lane < 64, pltpu.roll(one[0:quarter], 64, 1), one[quarter:])
    return jnp.concatenate([both, lone], axis=0)


def unfold(n, d, block, rows):
    if not folds(n, rows):
        return block
    half, quarter = rows // 2, rows // 4
    both, lone = block[0:half], block[half:]
    turned = pltpu.roll(lone, 64, 1)
    lane = lanes_of(quarter)
    zero = jnp.zeros((), block.dtype)
    if d % 2 == 0:
        pieces = [both, jnp.where(lane < 64, lone, zero), jnp.where(lane < 64, turned, zero)]
    else:
        pieces = [jnp.where(lane < 64, zero, turned), jnp.where(lane < 64, zero, lone), both]
    return jnp.concatenate(pieces, axis=0)


def stack_folded(stack_ref, block, odd):
    count = block.shape[0]
    half, quarter = count * 2 // 3, count // 3
    lane = lanes_of(half)
    zero = jnp.zeros((), block.dtype)
    both, lone = block[0:half], block[half:]
    stack_ref[0:half, :] = jnp.where(lane < 64, both, zero)
    stack_ref[half : 2 * half, :] = jnp.where(lane < 64, zero, both)
    turned = pltpu.roll(lone, 64, 1)
    lane = lanes_of(quarter)
    low = jnp.where(odd, turned, lone)
    high = jnp.where(odd, lone, turned)
    keep = (lane < 64) != odd
    stack_ref[2 * half : 2 * half + quarter, :] = jnp.where(keep, low, zero)
    stack_ref[2 * half + quarter : 2 * half + 2 * quarter, :] = jnp.where(keep, high, zero)


def fold_stack(block, odd):
    half = block.shape[0] // 3
    quarter = half // 2
    both = jnp.where(lanes_of(half) < 64, block[0:half], block[half : 2 * half])
    low, high = block[2 * half : 2 * half + quarter], block[2 * half + quarter :]
    lane = lanes_of(quarter)
    even_way = jnp.where(lane < 64, low, pltpu.roll(high, 64, 1))
    odd_way = jnp.where(lane < 64, pltpu.roll(low, 64, 1), high)
    return jnp.concatenate([both, jnp.where(odd, odd_way, even_way)], axis=0)


def stack_rows(stack_ref, block, lane):
    rows = block.shape[0]
    zero = jnp.zeros((), block.dtype)
    stack_ref[0:rows, :] = jnp.where(lane < 64, block, zero)
    stack_ref[rows : 2 * rows, :] = jnp.where(lane >= 64, block, zero)


def unstack_rows(stack_ref, block, offset, lane):
    rows = stack_ref.shape[0] // 2
    stack_ref[...] = jnp.zeros_like(stack_ref)
    stack_ref[pl.ds(offset, block.shape[0]), :] = block
    return jnp.where(lane < 64, stack_ref[0:rows, :], stack_ref[rows : 2 * rows, :])


def key_limits(n, share, rows, q_block, offset, length):
    row = lax.broadcasted_iota(jnp.int32, (1, share), 1)
    if folds(n, rows):
        half = rows // 2
        odd = jnp.where(offset > 0, half, 0)
        row = jnp.where(
            row < half, row + odd, jnp.where(row < rows, row - half + odd, row - half - odd)
        )
    else:
        row = row + offset
        row = jnp.where(row >= rows, row - rows, row)
    return jnp.minimum(q_block * rows + row + 1, length)


def attend_kernel(n, share, sc, query_ref, recv_ref, out_ref, keep_ref, lse_ref, stack, scores, back):
    q_block = pl.program_id(0)
    rows = recv_ref.shape[2]
    offset = pl.multiple_of(sc[n], 64)
    length = sc[n + 1]
    lane = lanes_of(rows)
    block = query_ref[sc[q_block]] * 0.125
    if folds(n, rows):
        stack_folded(stack, block, offset > 0)
        query = stack[0:share, :]
    else:
        stack_rows(stack, block, lane)
        query = stack[pl.ds(offset, share), :]
    limit = key_limits(n, share, rows, q_block, offset, length)
    key_row = lax.broadcasted_iota(jnp.int32, (rows, share), 0)
    blocks = jnp.minimum(q_block + 1, (length + rows - 1) // rows)

    def score_step(pair, top):
        found = []
        for j in (2 * pair, 2 * pair + 1):
            s = dot_nt(recv_ref[0, sc[j]], query)
            s = jnp.where(key_row < limit - j * rows, s, -1e30)
            scores[j] = s
            found.append(jnp.max(s, axis=0, keepdims=True))
        return jnp.maximum(top, jnp.maximum(found[0], found[1]))

    pairs = (blocks + 1) // 2
    top = lax.fori_loop(0, pairs, score_step, jnp.full((1, share), -1e30, F32))

    def value_step(pair, carry):
        total, acc = carry
        for j in (2 * pair, 2 * pair + 1):
            weights = jnp.exp(scores[j] - top)
            total = total + jnp.sum(weights, axis=0, keepdims=True)
            acc = acc + dot_tn(recv_ref[1, sc[j]], weights.astype(BF16))
        return total, acc

    total, acc = lax.fori_loop(
        0, pairs, value_step, (jnp.zeros((1, share), F32), jnp.zeros((LANES, share), F32))
    )
    acc = acc / total
    keep_ref[0] = acc
    lse_ref[0] = top + jnp.log(total)
    if folds(n, rows):
        out_ref[0] = fold_stack(acc.T, offset > 0).astype(BF16)
    else:
        out_ref[0] = unstack_rows(back, acc.T, offset, lane).astype(BF16)


def attend_back_kernel(
    n,
    share,
    sc,
    query_ref,
    recv_ref,
    grad_ref,
    keep_ref,
    lse_ref,
    query_out,
    out_ref,
    stack,
    gstack,
    dkeys,
    dvalues,
    back,
):
    q_block = pl.program_id(0)
    rows = recv_ref.shape[2]
    offset = pl.multiple_of(sc[n], 64)
    length = sc[n + 1]
    lane = lanes_of(rows)
    source = sc[q_block]

    @pl.when(q_block == 0)
    def _():
        dkeys[...] = jnp.zeros_like(dkeys)
        dvalues[...] = jnp.zeros_like(dvalues)

    block = query_ref[source] * 0.125
    if folds(n, rows):
        stack_folded(stack, block, offset > 0)
        query = stack[0:share, :]
        stack_folded(gstack, grad_ref[source], offset > 0)
        grad = gstack[0:share, :]
    else:
        stack_rows(stack, block, lane)
        query = stack[pl.ds(offset, share), :]
        stack_rows(gstack, grad_ref[source], lane)
        grad = gstack[pl.ds(offset, share), :]
    lse = lse_ref[0]
    delta = jnp.sum(grad.astype(F32).T * keep_ref[0], axis=0, keepdims=True)
    limit = key_limits(n, share, rows, q_block, offset, length)
    key_row = lax.broadcasted_iota(jnp.int32, (rows, share), 0)
    blocks = jnp.minimum(q_block + 1, (length + rows - 1) // rows)

    def step(pair, acc):
        for j in (2 * pair, 2 * pair + 1):
            keys = recv_ref[0, sc[j]]
            values = recv_ref[1, sc[j]]
            s = dot_nt(keys, query)
            weights = jnp.exp(jnp.where(key_row < limit - j * rows, s, -1e30) - lse)
            dweights = dot_nt(values, grad)
            dscores = (weights * (dweights - delta)).astype(BF16)
            dkeys[j] += dot(dscores, query)
            dvalues[j] += dot(weights.astype(BF16), grad)
            acc = acc + dot_tn(keys, dscores)
        return acc

    acc = lax.fori_loop(0, (blocks + 1) // 2, step, jnp.zeros((LANES, share), F32))
    if folds(n, rows):
        dquery = fold_stack(acc.T * 0.125, offset > 0)
    else:
        dquery = unstack_rows(back, acc.T * 0.125, offset, lane)
    query_out[source] = dquery.astype(BF16)

    @pl.when(q_block == n - 1)
    def _():
        def flush(j, carry):
            out_ref[0, sc[j]] = dkeys[j].astype(BF16)
            out_ref[1, sc[j]] = dvalues[j].astype(BF16)
            return carry

        lax.fori_loop(0, n, flush, 0)


def middle_kernel(
    n,
    heads,
    experts,
    attended_ref,
    w_ref,
    x_ref,
    tail_ref,
    routes_ref,
    target_ref,
    came_ref,
    residual_ref,
    in_ref,
    gates_ref,
    rows_ref,
    row_gates_ref,
    packets,
    outgoing,
    outgates,
    came_send,
    came_recv,
    send_sem,
    recv_sem,
    gate_send,
    gate_recv,
    own_sem,
):
    ctx = lax.axis_index("ctx")
    peers = row_peers(n)
    greet(peers)
    own = pltpu.make_async_copy(attended_ref.at[ctx], packets.at[ctx], own_sem.at[0])
    own.start()
    copies = [
        remote(attended_ref.at[p[0]], packets.at[ctx], came_send.at[d], came_recv.at[d], p)
        for d, p in enumerate(peers)
    ]
    for c in copies:
        c.start()
    pick = picks(target_ref, rows_ref.shape[0])
    lane = lanes_of(x_ref.shape[0])
    total = x_ref[...].astype(F32)
    for c in copies:
        c.wait()
    own.wait()
    for d, head in enumerate(heads):
        came = unfold(n, d, packets[d], total.shape[0])
        came_ref[d] = came
        total = total + dot(came, w_ref[64 * head : 64 * head + LANES, :])
    residual_ref[...] = total
    inv = lax.rsqrt(jnp.mean(total * total, axis=-1, keepdims=True) + norm_eps)
    ffn_in = (total * inv * tail_ref[experts + 1 : experts + 2, :]).astype(BF16)
    in_ref[...] = ffn_in
    logits = dot_nt(ffn_in, tail_ref[...].astype(BF16))
    chosen = [
        jnp.sum(jnp.where(lane == routes_ref[:, k : k + 1], logits, 0.0), axis=-1, keepdims=True)
        for k in range(2)
    ]
    top = jnp.maximum(chosen[0], chosen[1])
    raised = [jnp.exp(c - top) for c in chosen]
    gates = [r / (raised[0] + raised[1]) for r in raised]
    gates_ref[...] = jnp.where(lane == 0, gates[0], gates[1])
    outgoing[...] = dot_tn(pick[0] + pick[1], ffn_in).astype(BF16)
    block = outgoing.shape[0] // n

    def block_at(p):
        return pl.ds(pl.multiple_of(p * block, 16), block)

    own = [
        pltpu.make_async_copy(
            outgoing.at[block_at(ctx)], rows_ref.at[block_at(ctx)], own_sem.at[1]
        )
    ]
    copies = [
        remote(
            outgoing.at[block_at(p[0])],
            rows_ref.at[block_at(ctx)],
            send_sem.at[d],
            recv_sem.at[d],
            p,
        )
        for d, p in enumerate(peers)
    ]
    for c in own + copies:
        c.start()
    for p in range(n):
        row = sum(
            jnp.sum(
                jnp.where(lane == target_ref[:, k : k + 1] - p * block, gates[k], 0.0),
                axis=0,
                keepdims=True,
            )
            for k in range(2)
        )
        outgates[p] = jnp.broadcast_to(row, outgates.shape[1:])
    own.append(pltpu.make_async_copy(outgates.at[ctx], row_gates_ref.at[ctx], own_sem.at[2]))
    own[-1].start()
    for d, p in enumerate(peers):
        copies.append(
            remote(
                outgates.at[p[0]], row_gates_ref.at[ctx], gate_send.at[d], gate_recv.at[d], p
            )
        )
        copies[-1].start()
    for c in copies + own:
        c.wait()


def gated(g, u, da):
    sig = 0.5 * jnp.tanh(0.5 * g) + 0.5
    silu = g * sig
    return silu * u, da * u * sig * (1.0 + g * (1.0 - sig)), da * silu


def expert_kernel(
    x_ref,
    gates_ref,
    first_ref,
    rest_ref,
    wg_ref,
    wu_ref,
    wt_ref,
    dx_ref,
    dgate_ref,
    res_ref,
    mid_ref,
    dy_ref,
    dx_acc,
    res_acc,
    dgate,
    gate_rows,
):
    c = pl.program_id(0)

    @pl.when(c == 0)
    def _():
        res_acc[...] = jnp.zeros_like(res_acc)
        dx_acc[...] = jnp.zeros_like(dx_acc)
        dgate[...] = jnp.zeros_like(dgate)
        n, early = first_ref.shape[0:2]
        block = early + rest_ref.shape[1]
        for p in range(n):
            dy_ref[p * block : p * block + early] = first_ref[p]
            dy_ref[p * block + early : (p + 1) * block] = rest_ref[p]
            column = gates_ref[p].T[0:block, 0:1]
            gate_rows[p * block : (p + 1) * block] = jnp.broadcast_to(column, (block, LANES))

    x, dy = x_ref[...], dy_ref[...]
    gate = gate_rows[:, 0:1]
    wg, wu, wt = wg_ref[...], wu_ref[...], wt_ref[...]
    da = dot(dy, wt)
    act, dg, du = gated(dot(x, wg), dot(x, wu), da * gate)
    dgate[...] += jnp.sum(act * da, axis=-1, keepdims=True)
    mid_ref[2] = (act * gate).astype(BF16)
    act, dg, du = act.astype(BF16), dg.astype(BF16), du.astype(BF16)
    res_acc[...] += dot_nt(act, wt)
    dx_acc[...] += dot_nt(dg, wg) + dot_nt(du, wu)
    mid_ref[0] = dg
    mid_ref[1] = du

    @pl.when(c == pl.num_programs(0) - 1)
    def _():
        res_ref[...] = res_acc[...].astype(BF16)
        dx_ref[...] = dx_acc[...].astype(BF16)
        n, early = first_ref.shape[0:2]
        block = early + rest_ref.shape[1]
        dgate_ref[...] = jnp.zeros_like(dgate_ref)
        for p in range(n):
            dgate_ref[p, :, 0:block] = dgate[p * block : (p + 1) * block].T[0:8]


def ring_split(rows, columns, pieces):
    down = 1
    while 2 * down <= pieces and rows % (32 * down) == 0:
        down *= 2
    across = pieces // down
    width = -(-columns // (LANES * across)) * LANES
    return down, across, rows // down, width


def ring_place(position, n):
    half = n // 2
    return jnp.where(position < half, 2 * position, 2 * (n - 1 - position) + 1)


def shared_kernel(
    n,
    members,
    heads,
    experts,
    send_ref,
    row_dgates_ref,
    in_ref,
    dout_ref,
    residual_ref,
    gates_ref,
    routes_ref,
    target_ref,
    tail_ref,
    w_ref,
    wide_ref,
    back_ref,
    recv_ref,
    res_ref,
    dres_ref,
    branch_ref,
    dlogits_ref,
    dgain_ref,
    a_keep,
    a_give,
    b_keep,
    b_other,
    came,
    came_dgates,
    packets,
    b_give,
    mids,
    dx_acc,
    a_all,
    b_all,
    a_caught,
    b_caught,
    raw,
    xt,
    gate_buf,
    up_buf,
    back_buf,
    send_sem,
    recv_sem,
    own_sem,
    packet_send,
    packet_recv,
    dgate_send,
    dgate_recv,
    a_sem,
    b_sem,
    far_sem,
    w_sem,
):
    ctx, fsdp = lax.axis_index("ctx"), lax.axis_index("fsdp")
    bits = members.bit_length() - 1
    peers = row_peers(n)
    mate, far = mates_of(members)[0:2]
    greet(peers + [mate, far])
    block = send_ref.shape[0] // n

    def block_at(p):
        return pl.ds(pl.multiple_of(p * block, 16), block)

    copies = [
        pltpu.make_async_copy(send_ref.at[block_at(ctx)], came.at[block_at(ctx)], own_sem.at[0]),
        pltpu.make_async_copy(row_dgates_ref.at[ctx], came_dgates.at[ctx], own_sem.at[2]),
    ]
    for d, p in enumerate(peers):
        copies.append(
            remote(
                row_dgates_ref.at[p[0]],
                came_dgates.at[ctx],
                dgate_send.at[d],
                dgate_recv.at[d],
                p,
            )
        )
        copies.append(
            remote(
                send_ref.at[block_at(p[0])],
                came.at[block_at(ctx)],
                send_sem.at[d],
                recv_sem.at[d],
                p,
            )
        )
    for c in copies:
        c.start()

    steps = FS // CHUNK

    def fetch(c, slot):
        at = pl.ds(pl.multiple_of(c * CHUNK, CHUNK), CHUNK)
        up = pl.ds(pl.multiple_of(FS + c * CHUNK, CHUNK), CHUNK)
        return [
            pltpu.make_async_copy(wide_ref.at[:, at], gate_buf.at[slot], w_sem.at[slot, 0]),
            pltpu.make_async_copy(wide_ref.at[:, up], up_buf.at[slot], w_sem.at[slot, 1]),
            pltpu.make_async_copy(back_ref.at[at], back_buf.at[slot], w_sem.at[slot, 2]),
        ]

    for f in fetch(0, 0):
        f.start()
    res_ref[...] = jnp.zeros_like(res_ref)
    dx_acc[...] = jnp.zeros_like(dx_acc)
    b_shard = FS // members
    piece = b_all.shape[2]

    def ffn_step(c):
        slot = lax.rem(c, 2)
        for f in fetch(c, slot):
            f.wait()

        @pl.when(c + 1 < steps)
        def _():
            for f in fetch(c + 1, 1 - slot):
                f.start()

        x, dy = in_ref[...], dout_ref[...]
        wg, wu, wo = gate_buf[slot], up_buf[slot], back_buf[slot]
        act, dg, du = gated(dot(x, wg), dot(x, wu), dot_nt(dy, wo))
        act, dg, du = act.astype(BF16), dg.astype(BF16), du.astype(BF16)
        res_ref[...] += dot(act, wo)
        dx_acc[...] += dot_nt(dg, wg) + dot_nt(du, wu)
        column = pl.ds(pl.multiple_of(c * CHUNK, CHUNK), CHUNK)
        mids[0, :, column] = dg
        mids[1, :, column] = du
        value = dot_tn(act, dy).astype(BF16)
        span = min(piece, CHUNK)
        for u in range(CHUNK // span):
            row = c * CHUNK + u * span
            t = row // b_shard
            j = sum(
                lax.rem(fsdp // (1 << b) + t // (1 << b), 2) * (1 << (bits - 1 - b))
                for b in range(bits)
            )
            inside = lax.rem(row, b_shard)
            top = pl.multiple_of(lax.rem(inside, piece), 16)
            b_all[inside // piece, j, pl.ds(top, span), :] = value[u * span : (u + 1) * span]

    loop(ffn_step, 0, steps)
    half, quarter = members // 2, members // 4

    def a_swap(i):
        return remote(
            a_all.at[i, pl.ds(half, half)], a_caught.at[i], a_sem.at[i, 0], a_sem.at[i, 1], mate
        )

    def b_swap(i):
        return remote(
            b_all.at[i, pl.ds(half, half)], b_caught.at[i], b_sem.at[i, 0], b_sem.at[i, 1], mate
        )

    def b_cross(i):
        return remote(b_give.at[i], b_other.at[i], far_sem.at[i, 0], far_sem.at[i, 1], far)

    for i in range(2):
        b_swap(i).start()
    rows = shard_rows(members, D // members)
    shard = D // members
    raw[...] = in_ref[...].T
    for j in range(members):
        xt[j * shard : (j + 1) * shard, :] = raw[pl.ds(rows[j], shard), :]
    for i in range(2):

        def grad_step(c, i=i):
            column = pl.ds(pl.multiple_of(c * BROAD, BROAD), BROAD)
            value = dot(xt[...], mids[i, :, column]).astype(BF16)
            for j in range(members):
                a_all[i, j, :, column] = value[j * shard : (j + 1) * shard]

        loop(grad_step, 0, FS // BROAD)
        a_swap(i).start()
        b_swap(i).wait_recv()
        for j in range(half):
            total = (b_all[i, j].astype(F32) + b_caught[i, j].astype(F32)).astype(BF16)
            if j < quarter:
                b_keep[i, j] = total
            else:
                b_give[i, j - quarter] = total
        b_cross(i).start()
    for c in copies:
        c.wait()

    pick = picks(target_ref, came.shape[0])
    gates = [gates_ref[:, k : k + 1] for k in range(2)]
    lane = lanes_of(pick[0].shape[0])
    dgate = [
        jnp.sum(
            sum(
                jnp.where(
                    lane == target_ref[:, k : k + 1] - p * block, came_dgates[p, 0:1, :], 0.0
                )
                for p in range(n)
            ),
            axis=-1,
            keepdims=True,
        )
        for k in range(2)
    ]
    mean = gates[0] * dgate[0] + gates[1] * dgate[1]
    dlogits = sum(
        jnp.where(lane == routes_ref[:, k : k + 1], gates[k] * (dgate[k] - mean), 0.0)
        for k in range(2)
    ).astype(BF16)
    dlogits_ref[...] = dlogits
    tail = tail_ref[...]
    dffn = dot(pick[0] + pick[1], came[...]) + dx_acc[...] + dot(dlogits, tail.astype(BF16))
    residual = residual_ref[...]
    inv = lax.rsqrt(jnp.mean(residual * residual, axis=-1, keepdims=True) + norm_eps)
    scaled = dffn * tail[experts + 1 : experts + 2, :]
    total = jnp.mean(scaled * residual, axis=-1, keepdims=True)
    dres = dout_ref[...].astype(F32) + inv * scaled - residual * inv * inv * inv * total
    branch = dres.astype(BF16)
    branch_ref[...] = branch
    for d, head in enumerate(heads):
        packet = dot_nt(branch, w_ref[64 * head : 64 * head + LANES, :])
        packets[d] = fold(n, d, packet).astype(BF16)
    own = pltpu.make_async_copy(packets.at[ctx], recv_ref.at[ctx], own_sem.at[1])
    own.start()
    copies = [
        remote(packets.at[p[0]], recv_ref.at[ctx], packet_send.at[d], packet_recv.at[d], p)
        for d, p in enumerate(peers)
    ]
    for c in copies:
        c.start()
    dres_ref[...] = dres
    dgain_ref[...] = jnp.sum(dffn * residual * inv, axis=0, keepdims=True)
    for i in range(2):
        a_swap(i).wait_recv()
        for j in range(half):
            total = (a_all[i, j].astype(F32) + a_caught[i, j].astype(F32)).astype(BF16)
            if j < quarter:
                a_keep[i, j] = total
            else:
                a_give[i, j - quarter] = total
    for c in copies:
        c.wait()
    own.wait()
    for i in range(2):
        a_swap(i).wait_send()
        b_swap(i).wait_send()
        b_cross(i).wait()


def back_exchange_kernel(
    n,
    members,
    heads,
    query_ref,
    send_ref,
    x_ref,
    dy_ref,
    came_ref,
    branch_ref,
    in_ref,
    dlogits_ref,
    residual_ref,
    shared_ref,
    gates_ref,
    target_ref,
    res_ref,
    where_ref,
    length_ref,
    mid_ref,
    query_out,
    recv_ref,
    sum_ref,
    out_keep,
    out_other,
    router_ref,
    output_ref,
    give,
    caught,
    crossed,
    out_all,
    out_caught,
    raw,
    xt,
    dyt,
    acc,
    mids,
    query_send,
    query_recv,
    send_sem,
    recv_sem,
    own_sem,
    give_sem,
    caught_sem,
    cross_sem,
    out_sem,
    mid_sem,
):
    ctx = lax.axis_index("ctx")
    peers = row_peers(n)
    mates = mates_of(members)
    mate, far = mates[0], mates[1]
    greet(peers + [mate, far])
    own = [
        pltpu.make_async_copy(send_ref.at[:, ctx], recv_ref.at[:, ctx], own_sem.at[0]),
        pltpu.make_async_copy(query_ref.at[ctx], query_out.at[ctx], own_sem.at[1]),
    ]
    for c in own:
        c.start()
    copies = [
        remote(query_ref.at[p[0]], query_out.at[ctx], query_send.at[d], query_recv.at[d], p)
        for d, p in enumerate(peers)
    ]
    copies += [
        remote(send_ref.at[:, p[0]], recv_ref.at[:, ctx], send_sem.at[d], recv_sem.at[d], p)
        for d, p in enumerate(peers)
    ]
    for c in copies:
        c.start()

    steps = mid_ref.shape[2] // BROAD
    parts = mid_ref.shape[0]

    def fetch(i, c, slot):
        column = pl.multiple_of(c * BROAD, BROAD)
        return pltpu.make_async_copy(
            mid_ref.at[i, :, pl.ds(column, BROAD)], mids.at[slot], mid_sem.at[slot]
        )

    fetch(0, 0, 0).start()
    shard = D // members
    half = members // 2
    rows = shard_rows(members, shard)

    def turned(value, target):
        raw[...] = value.T
        for j in range(members):
            target[j * shard : (j + 1) * shard, :] = raw[pl.ds(rows[j], shard), :]

    acc[...] = jnp.zeros_like(acc)
    branch = branch_ref[...]
    for d, head in enumerate(heads):
        acc[64 * head : 64 * head + LANES, :] += dot_tn(came_ref[d], branch)
    for j in range(members):
        out_all[j] = acc[pl.ds(rows[j], shard), :].astype(BF16)
    quarter = members // 4
    out_swap = remote(
        out_all.at[pl.ds(half, half)], out_caught, out_sem.at[0], out_sem.at[1], mate
    )
    out_swap.start()
    turned(x_ref[...], xt)
    turned(dy_ref[...], dyt)
    out_swap.wait_recv()
    for j in range(half):
        add_into(out_all, j, out_caught)
    for j in range(quarter):
        out_keep[j] = out_all[j]
    out_cross = remote(
        out_all.at[pl.ds(quarter, quarter)], out_other, out_sem.at[2], out_sem.at[3], far
    )
    out_cross.start()

    def swap(i):
        return remote(give.at[i], caught.at[i], give_sem.at[i], caught_sem.at[i], mate)

    cross = remote(
        sum_ref.at[0, pl.ds(quarter, quarter)], crossed, cross_sem.at[0], cross_sem.at[1], far
    )
    for i in range(parts):
        left = xt if i < 2 else dyt

        def step(c, left=left, i=i):
            slot = lax.rem(c, 2)
            fetch(i, c, slot).wait()

            @pl.when(c + 1 < steps)
            def _():
                fetch(i, c + 1, 1 - slot).start()

            value = dot(left[...], mids[slot]).astype(BF16)
            column = pl.ds(pl.multiple_of(c * BROAD, BROAD), BROAD)
            for j in range(half):
                sum_ref[i, j, :, column] = value[j * shard : (j + 1) * shard]
                give[i, j, :, column] = value[(half + j) * shard : (half + j + 1) * shard]

        loop(step, 0, steps)
        if i + 1 < parts:
            fetch(i + 1, 0, 0).start()
        swap(i).start()
        if i > 0:
            swap(i - 1).wait_recv()
            for j in range(half):
                add_into(sum_ref.at[i - 1], j, caught.at[i - 1])
        if i == 1:
            cross.start()

    router_ref[...] = dot_tn(in_ref[...], dlogits_ref[...])
    pick = picks(target_ref, res_ref.shape[0])
    came = res_ref[...]
    mixture = gates_ref[:, 0:1] * dot(pick[0], came) + gates_ref[:, 1:2] * dot(pick[1], came)
    total = residual_ref[...] + shared_ref[...] + mixture
    position = where_ref[ctx] * total.shape[0] + lax.broadcasted_iota(jnp.int32, total.shape, 0)
    output_ref[...] = jnp.where(position < length_ref[0], total, 0.0).astype(BF16)
    swap(parts - 1).wait_recv()
    for j in range(half):
        add_into(sum_ref.at[parts - 1], j, caught.at[parts - 1])
    for c in copies + own:
        c.wait()
    cross.wait()
    for j in range(quarter):
        add_into(sum_ref.at[0], j, crossed)
    for i in range(parts):
        swap(i).wait_send()
    out_swap.wait_send()
    out_cross.wait()


def last_kernel(
    n,
    members,
    heads,
    experts,
    splits,
    query_ref,
    recv_ref,
    cos_ref,
    sin_ref,
    in_ref,
    x_ref,
    w_ref,
    tail_ref,
    dres_ref,
    router_ref,
    dgain_ref,
    a_ref,
    a_other,
    b_ref,
    b_other,
    o_ref,
    o_other,
    e_ref,
    x_out,
    a_out,
    b_out,
    c_out,
    e_out,
    *scratch,
):
    bits = members.bit_length() - 1
    streams = len(splits)
    own, full, back_up, back_down = (scratch[k * streams : (k + 1) * streams] for k in range(4))
    back = (back_up, back_down)
    scratch = scratch[4 * streams :]
    packs, scratch = scratch[0:4], scratch[4:]
    caught = [scratch[4 * b : 4 * b + 4] for b in range(bits)]
    scratch = scratch[4 * bits :]
    e_caught, scratch = scratch[0 : bits - 1], scratch[bits - 1 :]
    dproj, raw, turned, small = scratch[0:4]
    send_sem, recv_sem, level_send, level_recv, e_send, e_recv = scratch[4:]
    ctx, fsdp = lax.axis_index("ctx"), lax.axis_index("fsdp")
    here = jnp.where(ctx % 2 == 0, ctx // 2, n - 1 - ctx // 2)
    ahead = (ring_place(lax.rem(here + 1, n), n), fsdp)
    behind = (ring_place(lax.rem(here + n - 1, n), n), fsdp)
    mates = mates_of(members)
    barrier = pltpu.get_barrier_semaphore()
    for peer in [ahead, behind] + mates:
        pl.semaphore_signal(barrier, inc=1, device_id=peer, device_id_type=pl.DeviceIdType.MESH)
    shard = D // members
    parts = e_ref.shape[0]

    def level_copy(p, b):
        count = members >> (b + 1)
        return remote(
            packs[p].at[pl.ds(count, count)],
            caught[b][p],
            level_send.at[p, b],
            level_recv.at[p, b],
            mates[b],
        )

    def level_add(p, b):
        level_copy(p, b).wait_recv()
        for j in range(members >> (b + 1)):
            add_into(packs[p], j, caught[b][p])

    def level_next(p):
        level_add(p, 0)
        level_copy(p, 1).start()

    def e_copy(i, b):
        count = members >> (b + 1)
        source = e_ref if b == 1 or (b == 2 and i == 0) else e_caught[b - 2]
        return remote(
            source.at[i, pl.ds(count, count)],
            e_caught[b - 1].at[i],
            e_send.at[i, b - 1],
            e_recv.at[i, b - 1],
            mates[b],
        )

    def e_add(i, b):
        e_copy(i, b).wait_recv()
        source = e_ref if b == 1 or (b == 2 and i == 0) else e_caught[b - 2]
        for j in range(members >> (b + 1)):
            total = source[i, j].astype(F32) + e_caught[b - 1][i, j].astype(F32)
            if b == bits - 1:
                e_out[i] = total.astype(BF16)
            else:
                e_caught[b - 1][i, j] = total.astype(BF16)

    def tiles(i):
        down, across, height, width = splits[i][0:4]
        columns = splits[i][4]
        for p in range(down * across):
            r, c = p // across, p % across
            yield p, r * height, height, c * width, max(0, min(width, columns - c * width)), width

    def load(i, ref, skip=0, other=None):
        for p, top, height, start, have, width in tiles(i):
            if have > 0:
                value = ref[top : top + height, skip + start : skip + start + have]
                if other is not None:
                    added = other[top : top + height, skip + start : skip + start + have]
                    value = (value.astype(F32) + added.astype(F32)).astype(BF16)
                own[i][p, :, 0:have] = value
            if have < width:
                own[i][p, :, have:] = jnp.zeros((height, width - have), BF16)

    def save(i, ref, skip=0):
        for p, top, height, start, have, width in tiles(i):
            if have > 0:
                ref[top : top + height, skip + start : skip + start + have] = full[i][p, :, 0:have]

    long, short = n // 2, n - 1 - n // 2

    def hops(i, direction):
        return long if direction == i % 2 else short

    def place(direction, steps):
        return lax.rem(here + (steps if direction == 0 else 2 * n - steps), n)

    def copy(i, direction, step, source, target, slot):
        return remote(
            source.at[slot],
            target.at[slot],
            send_sem.at[i, direction, step],
            recv_sem.at[i, direction, step],
            ahead if direction == 0 else behind,
        )

    def first(i):
        for direction in range(2):
            slot = place(direction, hops(i, direction))
            copy(i, direction, 0, own[i], back[direction][i], slot).start()

    def reduce_step(i, s):
        for direction in range(2):
            count = hops(i, direction)
            if s < count:
                slot = place(direction, count - s)
                buffer = back[direction][i]
                copy(i, direction, s - 1, buffer, buffer, slot).wait_recv()
                add_into(buffer, slot, own[i])
                copy(i, direction, s, buffer, buffer, slot).start()

    def turn(i):
        for direction in range(2):
            buffer = back[direction][i]
            copy(i, direction, hops(i, direction) - 1, buffer, buffer, here).wait_recv()
        full[i][here] = (
            own[i][here].astype(F32) + back_up[i][here].astype(F32) + back_down[i][here].astype(F32)
        ).astype(BF16)
        for direction in range(2):
            copy(i, direction, long, full[i], full[i], here).start()

    def gather_step(i, s):
        for direction in range(2):
            if s < hops(i, direction):
                slot = place(1 - direction, s)
                copy(i, direction, long + s - 1, full[i], full[i], slot).wait_recv()
                copy(i, direction, long + s, full[i], full[i], slot).start()

    def end(i):
        for direction in range(2):
            count = hops(i, direction)
            slot = place(1 - direction, count)
            copy(i, direction, long + count - 1, full[i], full[i], slot).wait_recv()

    def drain(i):
        for direction in range(2):

            def sent(step, direction=direction):
                copy(i, direction, step, own[i], full[i], 0).wait_send()

            loop(sent, 0, hops(i, direction))
            loop(sent, long, long + hops(i, direction))

    def steps_of(i):
        done = [functools.partial(reduce_step, i, s) for s in range(1, long)]
        done.append(functools.partial(turn, i))
        done += [functools.partial(gather_step, i, s) for s in range(1, long)]
        done.append(functools.partial(end, i))
        return done

    for i in range(2):
        load(i, a_ref.at[i], 0, a_other.at[i])
    pl.semaphore_wait(barrier, 2 + bits)
    first(0)
    first(1)
    for i in range(2):
        load(2 + i, b_ref.at[i], 0, b_other.at[i])
        first(2 + i)
    load(4, o_ref, 0, o_other)
    first(4)
    waiting = [steps_of(i) for i in range(5)]

    def dense_step(picked=range(5)):
        for i in picked:
            if waiting[i]:
                waiting[i].pop(0)()

    rows = shard_rows(members, shard)
    raw[...] = in_ref[...].T
    for j in range(members):
        turned[j * shard : (j + 1) * shard, :] = raw[pl.ds(rows[j], shard), :]
    lane = lanes_of(x_ref.shape[0])
    cos, sin = cos_ref[...], sin_ref[...]
    for part in range(3):
        groups = [jnp.zeros(lane.shape, F32) for _ in range(D // LANES)]
        for d, head in enumerate(heads):
            g = head // 2
            if part == 0:
                packet = unfold(n, d, query_ref[d].astype(F32), lane.shape[0])
            else:
                packet = recv_ref[part - 1, d].astype(F32)
            if head % 2 == 0:
                groups[g] = groups[g] + packet
            else:
                packet = pltpu.roll(packet, 64, 1)
                groups[g] = groups[g] + jnp.where(lane >= 64, packet, 0.0)
                groups[g + 1] = groups[g + 1] + jnp.where(lane < 64, packet, 0.0)
        for g, t in enumerate(groups):
            if part < 2:
                t = t.astype(BF16).astype(F32)
                t = t * cos - partner(t, lane) * sin
            dproj[:, part * D + g * LANES : part * D + (g + 1) * LANES] = t.astype(BF16)
        value = dot(turned[...], dproj[:, part * D : (part + 1) * D]).astype(BF16)
        for j in range(members):
            packs[part][j] = value[j * shard : (j + 1) * shard]
        level_copy(part, 0).start()
        if part > 0:
            level_next(part - 1)
    dense_step()
    dnorm = sum(
        dot_nt(dproj[:, part * D : (part + 1) * D], w_ref[part].reshape(D, D)) for part in range(3)
    )
    x = x_ref[...].astype(F32)
    gain = tail_ref[experts : experts + 1, :]
    inv = lax.rsqrt(jnp.mean(x * x, axis=-1, keepdims=True) + norm_eps)
    dgain_one = jnp.sum(dnorm * x * inv, axis=0, keepdims=True)
    row = lax.broadcasted_iota(jnp.int32, (LANES, D), 0)
    gains = jnp.where(row == experts, dgain_one, jnp.where(row == experts + 1, dgain_ref[...], 0.0))
    small[...] = router_ref[...] + gains.T
    for j in range(members):
        packs[3][j] = small[pl.ds(rows[j], shard), :].astype(BF16)
    level_copy(3, 0).start()
    level_next(2)
    scaled = dnorm * gain
    total = jnp.mean(scaled * x, axis=-1, keepdims=True)
    x_out[...] = dres_ref[...] + inv * scaled - x * inv * inv * inv * total
    level_next(3)
    for i in range(1, parts):
        e_copy(i, 1).start()

    for p in range(4):
        if p < 3:
            dense_step((0, 2))
        for b in range(1, bits):
            level_add(p, b)
            if b + 1 < bits:
                level_copy(p, b + 1).start()
        load(5 + p, packs[p].at[0])
        first(5 + p)
        for queue in waiting[5:]:
            queue.pop(0)()
        if p < 3:
            dense_step((1, 3, 4))
        waiting.append(steps_of(5 + p))
    turns = 0
    while any(waiting):
        turns += 1
        for i, queue in reversed(list(enumerate(waiting))):
            if queue and (i >= 5 or turns % 2 == (i in (1, 3, 4))):
                queue.pop(0)()
                if not queue and i < 5:
                    if i == 4:
                        save(i, c_out, PACKED)
                    elif i < 2:
                        save(i, a_out, i * splits[0][4])
                    else:
                        height = splits[2][0] * splits[2][2]
                        save(i, b_out.at[pl.ds((i - 2) * height, height)])
        if not any(waiting[0:5]) and parts > 1:
            e_add(1, 1)
            parts = min(parts, 1)
    for p in range(4):
        save(5 + p, c_out, p * D)
    parts = e_ref.shape[0]
    for i in range(2, parts):
        e_add(i, 1)
    if bits == 2:
        e_out[0] = e_ref[0, 0]
    for b in range(2, bits):
        for i in range(parts):
            e_copy(i, b).start()
        for i in range(parts):
            e_add(i, b)
    for b in range(bits):
        for p in range(4):
            level_copy(p, b).wait_send()
    for b in range(1, bits):
        for i in range(1 if b == 1 else 0, parts):
            e_copy(i, b).wait_send()

    for i in range(streams):
        drain(i)


def widen_kernel(
    experts,
    late_ref,
    a_ref,
    b_ref,
    in_ref,
    back_ref,
    x_ref,
    small_ref,
    output_ref,
    qkv_out,
    w_out,
    a_out,
    b_out,
    in_out,
    back_out,
    x_out,
    router_out,
    gain_one_out,
    gain_two_out,
    output_out,
):
    qkv_out[...] = late_ref[:, 0 : 3 * D].astype(F32)
    w_out[...] = late_ref[:, PACKED:].astype(F32)
    a_out[...] = a_ref[...].astype(F32)
    b_out[...] = b_ref[...].astype(F32)
    in_out[:, 0:FF] = in_ref[0].astype(F32)
    in_out[:, FF:] = in_ref[1].astype(F32)
    back_out[...] = back_ref[0].astype(F32)
    x_out[...] = x_ref[...]
    output_out[...] = output_ref[...]

    @pl.when(pl.program_id(0) == 0)
    def _():
        small = small_ref[...].astype(F32).T
        router_out[...] = small[0:experts]
        gain_one_out[...] = small[experts]
        gain_two_out[...] = small[experts + 1]


def on_device(
    tokens,
    cotangent,
    lengths,
    position_block,
    routes,
    gain_attn,
    w_qkv,
    w_out,
    gain_ffn,
    w_router,
    w_shared_in,
    w_shared_out,
    w_expert_in,
    w_expert_out,
):
    n_ctx = lax.axis_size("ctx")
    ctx_index = lax.axis_index("ctx")
    rows = tokens.shape[1]
    local = w_qkv.shape[0]
    experts = w_router.shape[1]
    capacity = 3 * rows // experts
    places = experts * capacity
    members = D // local
    share = HEADS * rows // n_ctx
    heads = first_heads(n_ctx, rows)
    gather = functools.partial(lax.all_gather, axis_name="fsdp", axis=0, tiled=True)
    exchange = functools.partial(
        lax.all_to_all, axis_name="ctx", split_axis=0, concat_axis=0, tiled=True
    )
    x = tokens[0]
    length = lengths[0]

    out_weight = gather(w_out)
    weights = gather(
        jnp.concatenate([w_shared_in, w_expert_in[0], w_expert_out[0].T], axis=1)
    )
    shared_out = gather(w_shared_out)
    bits = members.bit_length() - 1

    rates = 10000.0 ** (-(np.arange(HEAD_DIM // 2) * 2.0 / HEAD_DIM))
    rates = jnp.asarray(np.tile(rates.astype(np.float32), 4)[None])

    order = jnp.sum(
        jnp.where(
            position_block[None, :] == jnp.arange(n_ctx, dtype=jnp.int32)[:, None],
            jnp.arange(n_ctx, dtype=jnp.int32)[None, :],
            0,
        ),
        axis=1,
    )
    head_of = jnp.minimum(share * ctx_index // rows, HEADS - 2)
    offset = share * ctx_index - rows * head_of
    scalars = jnp.concatenate(
        [order, jnp.stack([offset.astype(jnp.int32), length.astype(jnp.int32)])]
    )

    whole = pl.BlockSpec(memory_space=pltpu.VMEM)
    scalar = pl.BlockSpec(memory_space=pltpu.SMEM)
    block = places // n_ctx
    early = block // 48 * 16
    thin = packet_rows(n_ctx, rows)
    queries, recv, attn_in, tail, target, dout, dy_first, dy_rest, qkv_weight, cos, sin = comm_call(
        functools.partial(open_kernel, n_ctx, members, heads, experts, capacity, early),
        (
            shape((n_ctx, thin, LANES), BF16),
            shape((2, n_ctx, rows, LANES), BF16),
            shape((rows, D), BF16),
            shape((LANES, D), F32),
            shape((rows, 2), jnp.int32),
            shape((rows, D), BF16),
            shape((n_ctx, early, D), BF16),
            shape((n_ctx, block - early, D), BF16),
            shape((3, members, local, D), BF16),
            shape((rows, LANES), F32),
            shape((rows, LANES), F32),
        ),
        3,
        in_specs=[scalar] * 2 + [whole] * 7,
        out_specs=[whole] * 11,
        scratch_shapes=[
            pltpu.VMEM((n_ctx, thin, LANES), BF16),
            pltpu.VMEM((2, n_ctx, rows, LANES), BF16),
            pltpu.VMEM((n_ctx, early, D), BF16),
            pltpu.VMEM((LANES, local), F32),
            pltpu.VMEM((members, local, LANES), BF16),
            pltpu.SemaphoreType.DMA((4, bits, members)),
            pltpu.SemaphoreType.DMA((4, bits, members)),
            pltpu.SemaphoreType.DMA((3, n_ctx - 1)),
            pltpu.SemaphoreType.DMA((3, n_ctx - 1)),
            pltpu.SemaphoreType.DMA((n_ctx - 1,)),
            pltpu.SemaphoreType.DMA((n_ctx - 1,)),
            pltpu.SemaphoreType.DMA((4,)),
        ],
        nbytes=150 << 20,
    )(
        position_block,
        lengths,
        routes[0],
        cotangent[0],
        x,
        w_qkv,
        w_router.T,
        jnp.stack([gain_attn, gain_ffn]),
        rates,
    )
    dy_rest = exchange(dy_rest)

    packet = pl.BlockSpec((2, n_ctx, rows, LANES), lambda i, sc: (0, 0, 0, 0))
    thin_packet = pl.BlockSpec((n_ctx, thin, LANES), lambda i, sc: (0, 0, 0))
    block_of = lambda i, sc: (i, 0, 0)
    attended, kept, lse = call(
        functools.partial(attend_kernel, n_ctx, share),
        (
            shape((n_ctx, thin, LANES), BF16),
            shape((n_ctx, LANES, share), F32),
            shape((n_ctx, 1, share), F32),
        ),
        flops=2 * share * rows * n_ctx * n_ctx * LANES * 2,
        nbytes=5 << 20,
        grid_spec=pltpu.PrefetchScalarGridSpec(
            num_scalar_prefetch=1,
            grid=(n_ctx,),
            in_specs=[thin_packet, packet],
            out_specs=[
                pl.BlockSpec((1, thin, LANES), lambda i, sc: (sc[i], 0, 0)),
                pl.BlockSpec((1, LANES, share), block_of),
                pl.BlockSpec((1, 1, share), block_of),
            ],
            scratch_shapes=[
                pltpu.VMEM((2 * rows, LANES), BF16),
                pltpu.VMEM((n_ctx, rows, share), F32),
                pltpu.VMEM((2 * rows, LANES), F32),
            ],
        ),
    )(scalars, queries, recv)
    attended, dy_rest = lax.optimization_barrier((attended, dy_rest))

    def full(*dims):
        return pl.BlockSpec(dims, lambda *at: (0,) * len(dims))

    came, residual, ffn_in, gates, x_rows, row_gates = comm_call(
        functools.partial(middle_kernel, n_ctx, heads, experts),
        (
            shape((n_ctx, rows, LANES), BF16),
            shape((rows, D), F32),
            shape((rows, D), BF16),
            shape((rows, LANES), F32),
            shape((places, D), BF16),
            shape((n_ctx, 8, LANES), F32),
        ),
        4,
        in_specs=[whole] * 6,
        out_specs=[whole] * 6,
        scratch_shapes=[
            pltpu.VMEM((n_ctx, thin, LANES), BF16),
            pltpu.VMEM((places, D), BF16),
            pltpu.VMEM((n_ctx, 8, LANES), F32),
        ]
        + [pltpu.SemaphoreType.DMA((n_ctx - 1,)) for _ in range(6)]
        + [pltpu.SemaphoreType.DMA((3,))],
        nbytes=100 << 20,
    )(attended, out_weight, x, tail, routes[0], target)

    half, quarter = members // 2, members // 4
    steps = FS // CHUNK
    wide = FF // BROAD
    base = 2 * FS // BROAD
    expert_dx, row_dgates, expert_res, expert_mid, dy_rows = call(
        expert_kernel,
        (
            shape((places, D), BF16),
            shape((n_ctx, 8, LANES), F32),
            shape((places, D), BF16),
            shape((3, places, FF), BF16),
            shape((places, D), BF16),
        ),
        flops=2 * places * D * FF * 6,
        nbytes=24 << 20,
        grid=(wide,),
        in_specs=[
            full(places, D),
            full(n_ctx, 8, LANES),
            full(n_ctx, early, D),
            full(n_ctx, block - early, D),
            pl.BlockSpec((D, BROAD), lambda c: (0, base + c)),
            pl.BlockSpec((D, BROAD), lambda c: (0, base + wide + c)),
            pl.BlockSpec((D, BROAD), lambda c: (0, base + 2 * wide + c)),
        ],
        out_specs=[
            full(places, D),
            full(n_ctx, 8, LANES),
            full(places, D),
            pl.BlockSpec((3, places, BROAD), lambda c: (0, 0, c)),
            full(places, D),
        ],
        scratch_shapes=[
            pltpu.VMEM((places, D), F32),
            pltpu.VMEM((places, D), F32),
            pltpu.VMEM((places, LANES), F32),
            pltpu.VMEM((places, LANES), F32),
        ],
    )(x_rows, row_gates, dy_first, dy_rest, weights, weights, weights)
    b_rows = FS // members // 2
    anywhere = pl.BlockSpec(memory_space=pl.ANY)
    (
        branch_recv,
        shared_res,
        dres,
        branch,
        dlogits,
        dgain_two,
        dense_keep,
        dense_give,
        so_keep,
        so_came,
    ) = comm_call(
        functools.partial(shared_kernel, n_ctx, members, heads, experts),
        (
            shape((n_ctx, thin, LANES), BF16),
            shape((rows, D), F32),
            shape((rows, D), F32),
            shape((rows, D), BF16),
            shape((rows, LANES), BF16),
            shape((1, D), F32),
        )
        + (shape((2, quarter, local, FS), BF16),) * 2
        + (shape((2, quarter, b_rows, D), BF16),) * 2,
        2,
        in_specs=[whole] * 10 + [anywhere] * 2,
        out_specs=[whole] * 10,
        scratch_shapes=[
            pltpu.VMEM((places, D), BF16),
            pltpu.VMEM((n_ctx, 8, LANES), F32),
            pltpu.VMEM((n_ctx, thin, LANES), BF16),
            pltpu.VMEM((2, quarter, b_rows, D), BF16),
            pltpu.VMEM((2, rows, FS), BF16),
            pltpu.VMEM((rows, D), F32),
            pltpu.VMEM((2, members, local, FS), BF16),
            pltpu.VMEM((2, members, b_rows, D), BF16),
            pltpu.VMEM((2, half, local, FS), BF16),
            pltpu.VMEM((2, half, b_rows, D), BF16),
            pltpu.VMEM((D, rows), BF16),
            pltpu.VMEM((D, rows), BF16),
            pltpu.VMEM((2, D, CHUNK), BF16),
            pltpu.VMEM((2, D, CHUNK), BF16),
            pltpu.VMEM((2, CHUNK, D), BF16),
            pltpu.SemaphoreType.DMA((n_ctx - 1,)),
            pltpu.SemaphoreType.DMA((n_ctx - 1,)),
            pltpu.SemaphoreType.DMA((3,)),
            pltpu.SemaphoreType.DMA((n_ctx - 1,)),
            pltpu.SemaphoreType.DMA((n_ctx - 1,)),
            pltpu.SemaphoreType.DMA((n_ctx - 1,)),
            pltpu.SemaphoreType.DMA((n_ctx - 1,)),
            pltpu.SemaphoreType.DMA((2, 2)),
            pltpu.SemaphoreType.DMA((2, 2)),
            pltpu.SemaphoreType.DMA((2, 2)),
            pltpu.SemaphoreType.DMA((2, 3)),
        ],
        nbytes=150 << 20,
    )(
        expert_dx,
        row_dgates,
        ffn_in,
        dout,
        residual,
        gates,
        routes[0],
        target,
        tail,
        out_weight,
        weights,
        shared_out,
    )

    def gathered(terms):
        return sum(t.astype(F32) for t in terms).astype(BF16)

    def cross(give, b):
        return lax.ppermute(give, "fsdp", [(i, i ^ (1 << b)) for i in range(members)])

    def rest_of(keep, came_in):
        for b in range(2, bits):
            count = keep.shape[1] // 2
            give = gathered([keep[:, count:], came_in[:, count:]])
            keep = gathered([keep[:, :count], came_in[:, :count]])
            came_in = cross(give, b)
        return keep[:, 0], came_in[:, 0]

    branch_recv, expert_res = lax.optimization_barrier((branch_recv, expert_res))
    dense_part, dense_other = rest_of(dense_keep, cross(dense_give, 1))
    so_part, so_other = rest_of(so_keep, so_came)

    dquery, dsend = call(
        functools.partial(attend_back_kernel, n_ctx, share),
        (shape((n_ctx, thin, LANES), BF16), shape((2, n_ctx, rows, LANES), BF16)),
        flops=2 * share * rows * n_ctx * n_ctx * LANES * 3,
        nbytes=8 << 20,
        grid_spec=pltpu.PrefetchScalarGridSpec(
            num_scalar_prefetch=1,
            grid=(n_ctx,),
            in_specs=[
                thin_packet,
                packet,
                thin_packet,
                pl.BlockSpec((1, LANES, share), block_of),
                pl.BlockSpec((1, 1, share), block_of),
            ],
            out_specs=[thin_packet, packet],
            scratch_shapes=[
                pltpu.VMEM((2 * rows, LANES), BF16),
                pltpu.VMEM((2 * rows, LANES), BF16),
                pltpu.VMEM((n_ctx, rows, LANES), F32),
                pltpu.VMEM((n_ctx, rows, LANES), F32),
                pltpu.VMEM((2 * rows, LANES), F32),
            ],
        ),
    )(scalars, queries, recv, branch_recv, kept, lse)
    res_came = exchange(expert_res.reshape(n_ctx, -1, D)).reshape(places, D)
    dquery, drecv, expert_sum, out_keep, out_came, grad_router, output = comm_call(
        functools.partial(back_exchange_kernel, n_ctx, members, heads),
        (
            shape((n_ctx, thin, LANES), BF16),
            shape((2, n_ctx, rows, LANES), BF16),
            shape((3, half, local, FF), BF16),
            shape((quarter, local, D), BF16),
            shape((quarter, local, D), BF16),
            shape((D, LANES), F32),
            shape((rows, D), BF16),
        ),
        1,
        in_specs=[whole] * 13 + [scalar] * 2 + [anywhere],
        out_specs=[whole] * 7,
        scratch_shapes=[
            pltpu.VMEM((3, half, local, FF), BF16),
            pltpu.VMEM((3, half, local, FF), BF16),
            pltpu.VMEM((quarter, local, FF), BF16),
            pltpu.VMEM((members, local, D), BF16),
            pltpu.VMEM((half, local, D), BF16),
            pltpu.VMEM((D, places), BF16),
            pltpu.VMEM((D, places), BF16),
            pltpu.VMEM((D, places), BF16),
            pltpu.VMEM((D, D), F32),
            pltpu.VMEM((2, places, BROAD), BF16),
            pltpu.SemaphoreType.DMA((n_ctx - 1,)),
            pltpu.SemaphoreType.DMA((n_ctx - 1,)),
            pltpu.SemaphoreType.DMA((n_ctx - 1,)),
            pltpu.SemaphoreType.DMA((n_ctx - 1,)),
            pltpu.SemaphoreType.DMA((2,)),
            pltpu.SemaphoreType.DMA((3,)),
            pltpu.SemaphoreType.DMA((3,)),
            pltpu.SemaphoreType.DMA((2,)),
            pltpu.SemaphoreType.DMA((4,)),
            pltpu.SemaphoreType.DMA((2,)),
        ],
        nbytes=120 << 20,
    )(
        dquery,
        dsend,
        x_rows,
        dy_rows,
        came,
        branch,
        ffn_in,
        dlogits,
        residual,
        shared_res,
        gates,
        target,
        res_came,
        position_block,
        lengths,
        expert_mid,
    )

    late_width = PACKED + D
    out_part, out_other = rest_of(out_keep[None], out_came[None])
    late_widths = [D, D, D, LANES]
    sizes = [(local, FS)] * 2 + [(FS // members // 2, D)] * 2 + [(local, D)]
    sizes += [(local, width) for width in late_widths]
    splits = [ring_split(r, c, n_ctx) + (c,) for r, c in sizes]
    tiles = [(n_ctx, t[2], t[3]) for t in splits]
    grad_x, dense_sum, so_sum, last_sum, expert_sum = comm_call(
        functools.partial(last_kernel, n_ctx, members, heads, experts, splits),
        (
            shape((rows, D), F32),
            shape((local, 2 * FS), BF16),
            shape((FS // members, D), BF16),
            shape((local, late_width), BF16),
            shape((3, local, FF), BF16),
        ),
        0,
        in_specs=[whole] * 18,
        out_specs=[whole] * 5,
        scratch_shapes=[pltpu.VMEM(t, BF16) for t in tiles * 4]
        + [pltpu.VMEM((members, local, width), BF16) for width in late_widths]
        + [
            pltpu.VMEM((members >> (b + 1), local, width), BF16)
            for b in range(bits)
            for width in late_widths
        ]
        + [pltpu.VMEM((3, members >> (b + 1), local, FF), BF16) for b in range(1, bits)]
        + [
            pltpu.VMEM((rows, 3 * D), BF16),
            pltpu.VMEM((D, rows), BF16),
            pltpu.VMEM((D, rows), BF16),
            pltpu.VMEM((D, LANES), F32),
            pltpu.SemaphoreType.DMA((9, 2, n_ctx)),
            pltpu.SemaphoreType.DMA((9, 2, n_ctx)),
            pltpu.SemaphoreType.DMA((4, bits)),
            pltpu.SemaphoreType.DMA((4, bits)),
            pltpu.SemaphoreType.DMA((3, max(1, bits - 1))),
            pltpu.SemaphoreType.DMA((3, max(1, bits - 1))),
        ],
        nbytes=200 << 20,
    )(
        dquery,
        drecv,
        cos,
        sin,
        attn_in,
        x,
        qkv_weight,
        tail,
        dres,
        grad_router,
        dgain_two,
        dense_part,
        dense_other,
        so_part,
        so_other,
        out_part[0],
        out_other[0],
        expert_sum,
    )

    quarters = 4 if local % 64 == 0 else 1

    def rows_of(count, width):
        return pl.BlockSpec((count // quarters, width), lambda i: (i, 0))

    grad_qkv, grad_out, grad_si, grad_so, grad_ei, grad_eo, grad_x, grad_router, gain_one, gain_two, output = call(
        functools.partial(widen_kernel, experts),
        (
            shape((local, 3 * D), F32),
            shape((local, D), F32),
            shape((local, 2 * FS), F32),
            shape((FS // members, D), F32),
            shape((local, 2 * FF), F32),
            shape((local, FF), F32),
            shape((rows, D), F32),
            shape((experts, local), F32),
            shape((local,), F32),
            shape((local,), F32),
            shape((rows, D), BF16),
        ),
        flops=0,
        nbytes=22 << 20,
        grid=(quarters,),
        in_specs=[
            rows_of(local, late_width),
            rows_of(local, 2 * FS),
            rows_of(FS // members, D),
            pl.BlockSpec((2, local // quarters, FF), lambda i: (0, i, 0)),
            pl.BlockSpec((1, local // quarters, FF), lambda i: (2, i, 0)),
            rows_of(rows, D),
            pl.BlockSpec((local, LANES), lambda i: (0, 3 * D // LANES)),
            rows_of(rows, D),
        ],
        out_specs=[
            rows_of(local, 3 * D),
            rows_of(local, D),
            rows_of(local, 2 * FS),
            rows_of(FS // members, D),
            rows_of(local, 2 * FF),
            rows_of(local, FF),
            rows_of(rows, D),
            full(experts, local),
            full(local),
            full(local),
            rows_of(rows, D),
        ],
    )(last_sum, dense_sum, so_sum, expert_sum, expert_sum, grad_x, last_sum, output)
    return (
        output[None],
        grad_x[None],
        gain_one,
        grad_qkv,
        grad_out,
        gain_two,
        grad_router.T,
        grad_si,
        grad_so,
        grad_ei[None],
        grad_eo.T[None],
    )


def solution(mesh):
    row_spec = P("fsdp", "ctx", None)
    flat = P("fsdp", None)
    return jax.shard_map(
        on_device,
        mesh=mesh,
        in_specs=(
            row_spec,
            row_spec,
            P("fsdp"),
            P(),
            row_spec,
            P("fsdp"),
            flat,
            flat,
            P("fsdp"),
            flat,
            flat,
            flat,
            P("ctx", "fsdp", None),
            P("ctx", None, "fsdp"),
        ),
        out_specs=(
            row_spec,
            row_spec,
            P("fsdp"),
            flat,
            flat,
            P("fsdp"),
            flat,
            flat,
            flat,
            P("ctx", "fsdp", None),
            P("ctx", None, "fsdp"),
        ),
        check_vma=False,
    )
```
